32 devices in a mesh: dp: 8 (over z, y), mp: 4 (over x, core).
Axes of the slice: x: 2, y: 2, z: 4, core: 2. Of those that a mesh axis runs over, the one named last changes fastest.
Arguments:
- pixels: float32 [8, 48, 16, 384], P('dp'), may hold values from -6 to 6
- dataset_id: int32 [8], P('dp'), may hold values from 0 to 5
- variable_mask: int32 [6, 48], replicated, may hold values from 0 to 1, as said below
- lead_hours: int32 [8], P('dp'), may hold values from 6 to 168
- token_counts: int32 [8], P('dp'), may hold values from 128 to 2048
- dataset_weight: int32 [6], replicated, may hold values from 1 to 4
- patch_weight: bfloat16 [48, 16, 1024], replicated, may hold values from -1.5 to 1.5
- variable_embed: float32 [48, 1024], replicated, may hold values from -4 to 4
- position_embed: float32 [384, 1024], replicated, may hold values from -4 to 4
- pool_query: float32 [1024], replicated, may hold values from -6 to 6
- pool_query_weight: bfloat16 [1024, 1024], P(None, 'mp'), may hold values from -0.1875 to 0.1875
- pool_key_weight: bfloat16 [1024, 1024], P(None, 'mp'), may hold values from -0.1875 to 0.1875
- pool_value_weight: bfloat16 [1024, 1024], P(None, 'mp'), may hold values from -0.1875 to 0.1875
- pool_value_bias: float32 [1024], P('mp'), may hold values from -2 to 2
- pool_output_weight: bfloat16 [1024, 1024], P('mp'), may hold values from -0.75 to 0.75
- pool_output_bias: float32 [1024], replicated, may hold values from -2 to 2
- lead_weight: float32 [1024], replicated, may hold values from -0.6 to 0.6
- lead_bias: float32 [1024], replicated, may hold values from -2 to 2
- norm_gain: float32 [2, 2, 1024], replicated, may hold values from 0.5 to 1.5
- norm_bias: float32 [2, 2, 1024], replicated, may hold values from -1.2 to 1.2
- attention_weight: bfloat16 [2, 3, 1024, 1024], P(None, None, None, 'mp'), may hold values from -0.1875 to 0.1875
- attention_bias: float32 [2, 2, 1024], P(None, None, 'mp'), may hold values from -2 to 2
- output_weight: bfloat16 [2, 1024, 1024], P(None, 'mp'), may hold values from -0.75 to 0.75
- output_bias: float32 [2, 1024], replicated, may hold values from -1.2 to 1.2
- up_weight: bfloat16 [2, 1024, 4096], P(None, None, 'mp'), may hold values from -0.1875 to 0.1875
- up_bias: float32 [2, 4096], P(None, 'mp'), may hold values from -2 to 2
- down_weight: bfloat16 [2, 4096, 1024], P(None, 'mp'), may hold values from -0.1875 to 0.1875
- down_bias: float32 [2, 1024], replicated, may hold values from -1.2 to 1.2
- cotangent: float32 [8, 384, 1024], P('dp'), may hold values from -6 to 6
Outputs:
- layer_out: float32 [8, 384, 1024], P('dp')
- pixel_grad: float32 [8, 48, 16, 384], P('dp')
- grad_patch_weight: float32 [48, 16, 1024], P(None, None, ('dp', 'mp'))
- grad_variable_embed: float32 [48, 1024], P(None, ('dp', 'mp'))
- grad_position_embed: float32 [384, 1024], P(None, 'dp')
- grad_pool_query: float32 [1024], P(('dp', 'mp'))
- grad_pool_query_weight: float32 [1024, 1024], P('dp', 'mp')
- grad_pool_key_weight: float32 [1024, 1024], P('dp', 'mp')
- grad_pool_value_weight: float32 [1024, 1024], P('dp', 'mp')
- grad_pool_value_bias: float32 [1024], P(('mp', 'dp'))
- grad_pool_output_weight: float32 [1024, 1024], P('mp', 'dp')
- grad_pool_output_bias: float32 [1024], P('dp')
- grad_lead_weight: float32 [1024], P('dp')
- grad_lead_bias: float32 [1024], P('dp')
- grad_norm_gain: float32 [2, 2, 1024], P(None, None, 'dp')
- grad_norm_bias: float32 [2, 2, 1024], P(None, None, 'dp')
- grad_attention_weight: float32 [2, 3, 1024, 1024], P(None, None, 'dp', 'mp')
- grad_attention_bias: float32 [2, 2, 1024], P(None, None, ('mp', 'dp'))
- grad_output_weight: float32 [2, 1024, 1024], P(None, 'mp', 'dp')
- grad_output_bias: float32 [2, 1024], P(None, 'dp')
- grad_up_weight: float32 [2, 1024, 4096], P(None, 'dp', 'mp')
- grad_up_bias: float32 [2, 4096], P(None, ('mp', 'dp'))
- grad_down_weight: float32 [2, 4096, 1024], P(None, 'mp', 'dp')
- grad_down_bias: float32 [2, 1024], P(None, 'dp')
The draws below stay inside these ranges and needn't reach their ends.
Inputs may be any that keep to these rules, and one draw needn't show every extreme that they name: `variable_mask`: each dataset's row has at least one 1.
All inputs are finite; a program needn't handle non-finite values.
Results may differ from the reference program's by a relative error of at most 0.035.
Values sent between devices are 32-bit elements; how exact they have to be, the bound alone decides.
No kernel may reach another device: no remote copies, remote signals or barrier semaphores. Data moves between devices by JAX's collectives and lax.ppermute only.
A program may use at most 192 MiB of HBM per device.

```python
import math
import jax
import jax.numpy as jnp
from jax import lax

D = 1024
HEADS = 16
HEAD_DIM = 64
FF = 4096
VARS = 48
PATCH_PIX = 16
PATCHES = 384
DATASETS = 6
LAYERS = 2
ITEMS = 8


def draw_variable_mask(key, part):
    random_bits = jax.random.randint(jax.random.fold_in(key, 11), (DATASETS, VARS), 0, 2)
    chosen = jax.random.randint(jax.random.fold_in(key, 12), (DATASETS, 1), 0, VARS)
    forced = (jnp.arange(VARS, dtype=jnp.int32)[None, :] == chosen).astype(jnp.int32)
    return jnp.maximum(random_bits, forced).astype(jnp.int32)


def with_ends(entries, rng, least, top_value):
    extent = entries.shape
    index_at = [jax.random.randint(jax.random.fold_in(rng, axis), (), 0, extent[axis]) for axis in range(len(extent))]
    entries = entries.at[tuple(index_at)].set(least)
    longest = extent.index(max(extent))
    index_at[longest] = (index_at[longest] + 1) % extent[longest]
    return entries.at[tuple(index_at)].set(top_value)


def level_of(own_key, shape, shards, least, top_value):
    def one(dim, parts):
        steps = jax.random.uniform(jax.random.fold_in(jax.random.fold_in(own_key, 6), dim), (parts,), jnp.float32, least / len(shards), top_value / len(shards))
        return jnp.repeat(jnp.exp(steps), shape[dim] // parts).reshape((-1,) + (1,) * (len(shape) - dim - 1))

    factor_of = one(*shards[0])
    for cut in shards[1:]:
        factor_of = factor_of * one(*cut)
    return factor_of


def scatter_about(stream_key, dims, scale, limit, pieces=(), kind=jnp.bfloat16):
    array = scale * jax.random.normal(stream_key, dims, jnp.float32)
    if pieces:
        array = array * level_of(stream_key, dims, pieces, -0.22, 0.18)
    return jnp.clip(array, -limit, limit).astype(kind)


def setup_inputs(seed: int = 0) -> dict:
    key_list = jax.random.split(jax.random.key(seed), 30)
    return {
        "pixels": scatter_about(key_list[0], (ITEMS, VARS, PATCH_PIX, PATCHES), 1.0, 6.0, ((0, 8),), jnp.float32),
        "dataset_id": with_ends(jax.random.randint(key_list[1], (ITEMS,), 0, DATASETS), jax.random.fold_in(key_list[1], 1), 0, DATASETS - 1).astype(jnp.int32),
        "variable_mask": draw_variable_mask(jax.random.fold_in(key_list[29], 71), 0),
        "lead_hours": with_ends(jax.random.randint(key_list[3], (ITEMS,), 6, 169), jax.random.fold_in(key_list[3], 1), 6, 168).astype(jnp.int32),
        "token_counts": with_ends(jax.random.randint(key_list[4], (ITEMS,), 128, 2049), jax.random.fold_in(key_list[4], 1), 128, 2048).astype(jnp.int32),
        "dataset_weight": with_ends(jax.random.randint(key_list[5], (DATASETS,), 1, 5), jax.random.fold_in(key_list[5], 1), 1, 4).astype(jnp.int32),
        "patch_weight": scatter_about(key_list[6], (VARS, PATCH_PIX, D), PATCH_PIX ** -0.5, 1.5),
        "variable_embed": scatter_about(key_list[7], (VARS, D), 0.5, 4.0, (), jnp.float32),
        "position_embed": scatter_about(key_list[8], (PATCHES, D), 0.5, 4.0, (), jnp.float32),
        "pool_query": scatter_about(key_list[9], (D,), 1.0, 6.0, (), jnp.float32),
        "pool_query_weight": scatter_about(key_list[10], (D, D), D ** -0.5, 0.1875, ((1, 4),)),
        "pool_key_weight": scatter_about(key_list[11], (D, D), D ** -0.5, 0.1875, ((1, 4),)),
        "pool_value_weight": scatter_about(key_list[12], (D, D), D ** -0.5, 0.1875, ((1, 4),)),
        "pool_value_bias": scatter_about(key_list[13], (D,), 0.3, 2.0, ((0, 4),), jnp.float32),
        "pool_output_weight": scatter_about(key_list[14], (D, D), (D // 16) ** -0.5, 0.75, ((0, 4),)),
        "pool_output_bias": scatter_about(key_list[15], (D,), 0.3, 2.0, (), jnp.float32),
        "lead_weight": scatter_about(key_list[16], (D,), 0.1, 0.6, (), jnp.float32),
        "lead_bias": scatter_about(key_list[17], (D,), 0.3, 2.0, (), jnp.float32),
        "norm_gain": jnp.clip(1.0 + 0.1 * jax.random.normal(key_list[18], (LAYERS, 2, D), jnp.float32), 0.5, 1.5),
        "norm_bias": scatter_about(key_list[19], (LAYERS, 2, D), 0.2, 1.2, (), jnp.float32),
        "attention_weight": scatter_about(key_list[20], (LAYERS, 3, D, D), D ** -0.5, 0.1875, ((3, 4),)),
        "attention_bias": scatter_about(key_list[21], (LAYERS, 2, D), 0.3, 2.0, ((2, 4),), jnp.float32),
        "output_weight": scatter_about(key_list[22], (LAYERS, D, D), (D // 16) ** -0.5, 0.75, ((1, 4),)),
        "output_bias": scatter_about(key_list[23], (LAYERS, D), 0.2, 1.2, (), jnp.float32),
        "up_weight": scatter_about(key_list[24], (LAYERS, D, FF), D ** -0.5, 0.1875, ((2, 4),)),
        "up_bias": scatter_about(key_list[25], (LAYERS, FF), 0.3, 2.0, ((1, 4),), jnp.float32),
        "down_weight": scatter_about(key_list[26], (LAYERS, FF, D), (FF // 4) ** -0.5, 0.1875, ((1, 4),)),
        "down_bias": scatter_about(key_list[27], (LAYERS, D), 0.2, 1.2, (), jnp.float32),
        "cotangent": scatter_about(key_list[28], (ITEMS, PATCHES, D), 1.0, 6.0, ((0, 8),), jnp.float32),
    }


HIGHEST = lax.Precision.HIGHEST

@jax.custom_vjp
def low(v):
    return lax.optimization_barrier(v.astype(jnp.bfloat16)).astype(jnp.float32)

@jax.custom_vjp
def low_back(v):
    return v

def low_keep(v):
    return (low(v), None)

def low_pass(kept, grad):
    return (grad,)

def back_keep(v):
    return (v, None)

def back_low(kept, grad):
    return (low(grad),)
low.defvjp(low_keep, low_pass)
low_back.defvjp(back_keep, back_low)

def rounded_both(tensor):
    return low(low_back(tensor))

def norm_layer(inputs, gain_vec, bias_vec):
    row_mean = lax.optimization_barrier(jnp.mean(inputs, axis=-1, keepdims=True))
    centred = inputs - row_mean
    spread = lax.optimization_barrier(jnp.mean(centred * centred, axis=-1, keepdims=True))
    return centred * lax.rsqrt(spread + 1e-05) * gain_vec + bias_vec

def softmax_last(scores):
    row_max = lax.optimization_barrier(jnp.max(scores, axis=-1, keepdims=True))
    exponent = jnp.exp(scores - row_max)
    return exponent / lax.optimization_barrier(jnp.sum(exponent, axis=-1, keepdims=True))

def item_forward(params, pixel_item, mask_row, hour_value):
    patch_weight, variable_embed, position_embed, pool_query, pool_query_weight, pool_key_weight, pool_value_weight, pool_value_bias, pool_output_weight, pool_output_bias, lead_weight, lead_bias, norm_gain, norm_bias, attention_weight, attention_bias, output_weight, output_bias, up_weight, up_bias, down_weight, down_bias = params
    root_dim = math.sqrt(HEAD_DIM)
    pixel_low = low(pixel_item)
    embedded = jnp.einsum('vkp,vkd->vpd', pixel_low, patch_weight, precision=HIGHEST) + variable_embed[:, None, :]
    embed_low = low(embedded)
    query_vec = rounded_both(jnp.dot(low(pool_query), pool_query_weight, precision=HIGHEST))
    key_rows = rounded_both(jnp.einsum('vpd,de->vpe', embed_low, pool_key_weight, precision=HIGHEST))
    value_rows = low(low_back(jnp.einsum('vpd,de->vpe', embed_low, pool_value_weight, precision=HIGHEST)) + pool_value_bias)
    key_heads = key_rows.reshape(VARS, PATCHES, HEADS, HEAD_DIM)
    value_heads = value_rows.reshape(VARS, PATCHES, HEADS, HEAD_DIM)
    pool_scores = jnp.einsum('vphd,hd->phv', key_heads, query_vec.reshape(HEADS, HEAD_DIM), precision=HIGHEST) / root_dim
    pool_scores = jnp.where(mask_row[None, None, :] > 0, pool_scores, -1000000000.0)
    pool_low = low(softmax_last(pool_scores))
    pooled = rounded_both(jnp.einsum('phv,vphd->phd', pool_low, value_heads, precision=HIGHEST).reshape(PATCHES, D))
    hidden = low_back(jnp.dot(pooled, pool_output_weight, precision=HIGHEST)) + pool_output_bias
    hidden = hidden + position_embed + hour_value.astype(jnp.float32) / 24.0 * lead_weight + lead_bias
    for layer_num in range(LAYERS):
        normed = low(norm_layer(hidden, norm_gain[layer_num, 0], norm_bias[layer_num, 0]))
        queries = low(low_back(jnp.dot(normed, attention_weight[layer_num, 0], precision=HIGHEST)) + attention_bias[layer_num, 0])
        keys_new = rounded_both(jnp.dot(normed, attention_weight[layer_num, 1], precision=HIGHEST))
        values_new = low(low_back(jnp.dot(normed, attention_weight[layer_num, 2], precision=HIGHEST)) + attention_bias[layer_num, 1])
        query_three = queries.reshape(PATCHES, HEADS, HEAD_DIM)
        key_three = keys_new.reshape(PATCHES, HEADS, HEAD_DIM)
        value_three = values_new.reshape(PATCHES, HEADS, HEAD_DIM)
        scores = low_back(jnp.einsum('phd,khd->hpk', query_three, key_three, precision=HIGHEST) / root_dim)
        attend = low(softmax_last(scores))
        mixed_heads = rounded_both(jnp.einsum('hpk,khd->phd', attend, value_three, precision=HIGHEST).reshape(PATCHES, D))
        hidden = hidden + low_back(jnp.dot(mixed_heads, output_weight[layer_num], precision=HIGHEST)) + output_bias[layer_num]
        normed_two = low(norm_layer(hidden, norm_gain[layer_num, 1], norm_bias[layer_num, 1]))
        pre_act = low_back(jnp.dot(normed_two, up_weight[layer_num], precision=HIGHEST)) + up_bias[layer_num]
        activation = low(jax.nn.gelu(pre_act, approximate=False))
        hidden = hidden + low_back(jnp.dot(activation, down_weight[layer_num], precision=HIGHEST)) + down_bias[layer_num]
    return hidden

def reference(pixels, dataset_id, variable_mask, lead_hours, token_counts, dataset_weight, patch_weight, variable_embed, position_embed, pool_query, pool_query_weight, pool_key_weight, pool_value_weight, pool_value_bias, pool_output_weight, pool_output_bias, lead_weight, lead_bias, norm_gain, norm_bias, attention_weight, attention_bias, output_weight, output_bias, up_weight, up_bias, down_weight, down_bias, cotangent):
    params = tuple((tensor.astype(jnp.float32) for tensor in (patch_weight, variable_embed, position_embed, pool_query, pool_query_weight, pool_key_weight, pool_value_weight, pool_value_bias, pool_output_weight, pool_output_bias, lead_weight, lead_bias, norm_gain, norm_bias, attention_weight, attention_bias, output_weight, output_bias, up_weight, up_bias, down_weight, down_bias)))
    count_total = jnp.sum(token_counts).astype(jnp.float32)
    masks = variable_mask[dataset_id]
    scales = dataset_weight[dataset_id].astype(jnp.float32) * token_counts.astype(jnp.float32) / count_total
    zeros = jax.tree.map(jnp.zeros_like, params)

    def one_item(running, inputs):
        pixel_item, mask_row, hour_value, item_scale, cotangent_item = inputs
        result, pull_back = jax.vjp(lambda weights, pixel_in: item_forward(weights, pixel_in, mask_row, hour_value), params, pixel_item.astype(jnp.float32))
        weight_grads, pixel_grad = pull_back(cotangent_item)
        running = jax.tree.map(lambda total, term: total + item_scale * term, running, weight_grads)
        return (running, (result, pixel_grad))
    merged, (outputs, pixel_grads) = lax.scan(one_item, zeros, (pixels, masks, lead_hours, scales, cotangent))
    return (outputs, pixel_grads) + tuple(merged)
```

```python
import math

import jax
import jax.numpy as jnp
from jax import lax
from jax.sharding import PartitionSpec as P

HEAD_DIM = 64
ROOT_DIM = math.sqrt(HEAD_DIM)
BF = jnp.bfloat16
F32 = jnp.float32


def matmul(left, right):
    return jnp.dot(left, right, preferred_element_type=F32)


def matmul_tn(left, right):
    return lax.dot_general(left, right, (((0,), (0,)), ((), ())), preferred_element_type=F32)


def matmul_nt(left, right):
    return lax.dot_general(left, right, (((1,), (1,)), ((), ())), preferred_element_type=F32)


def two_part(tensor):
    high = tensor.astype(BF)
    return high, (tensor - high.astype(F32)).astype(BF)


def gelu_exact(pre_act):
    return jax.nn.gelu(pre_act, approximate=False)


def bit_count(size):
    bits = size.bit_length() - 1
    assert 1 << bits == size
    return bits


def exchange(tensor, axis, size, bit):
    return lax.ppermute(tensor, axis, [(i, i ^ (1 << bit)) for i in range(size)])


def pick(tensor, index, axis):
    return lax.dynamic_index_in_dim(tensor, index, axis, keepdims=False)


class Links:
    def __init__(self, dp, mp):
        self.dp, self.mp = dp, mp
        self.dp_index = lax.axis_index("dp")
        self.mp_index = lax.axis_index("mp")

    def dp_bit(self, bit):
        return (self.dp_index >> bit) & 1

    def mp_bit(self, bit):
        return (self.mp_index >> bit) & 1

    def sum_rows(self, partial):
        half = partial.shape[0] // 2
        total = partial[:half] + exchange(partial[half:], "mp", self.mp, 0)
        for bit in range(1, bit_count(self.mp)):
            total = total + exchange(total, "mp", self.mp, bit)
        return total

    def other_rows(self, own):
        return exchange(own, "mp", self.mp, 0)

    def both_rows(self, own):
        return jnp.concatenate([own, self.other_rows(own)], axis=0)

    def split_rows(self, tensor):
        half = tensor.shape[0] // 2
        core = self.mp_bit(0)
        own = lax.dynamic_slice_in_dim(tensor, core * half, half, 0)
        other = lax.dynamic_slice_in_dim(tensor, (1 - core) * half, half, 0)
        return own, other

    def global_rows(self, own, other):
        core = self.mp_bit(0)
        return jnp.concatenate(
            [jnp.where(core == 0, own, other), jnp.where(core == 0, other, own)], axis=0
        )

    def finish_scatter(self, shards, first_bit):
        for bit in range(first_bit, bit_count(self.dp)):
            count = shards.shape[0] // 2
            pairs = shards.reshape((count, 2) + shards.shape[1:])
            own = self.dp_bit(bit)
            got = exchange(pick(pairs, 1 - own, 1), "dp", self.dp, bit)
            shards = pick(pairs, own, 1) + got
        return shards[0]

    def scatter_sum(self, shards):
        return self.finish_scatter(shards, 0)

    def scatter_product(self, left, right, scale):
        width = left.shape[1]
        parts = left.reshape(left.shape[0], self.dp // 2, 2, width // self.dp)
        own = self.dp_bit(0)
        keep_left = jnp.where(own == 0, parts[:, :, 0], parts[:, :, 1])
        send_left = jnp.where(own == 0, parts[:, :, 1], parts[:, :, 0])
        flat = (left.shape[0], width // 2)
        send = matmul_tn(send_left.reshape(flat), right) * scale
        got = exchange(send, "dp", self.dp, 0)
        total = matmul_tn(keep_left.reshape(flat), right) * scale + got
        return self.finish_scatter(
            total.reshape(self.dp // 2, width // self.dp, right.shape[1]), 1
        )


def norm_parts(rows):
    row_mean = jnp.mean(rows, axis=-1, keepdims=True)
    centred = rows - row_mean
    spread = jnp.mean(centred * centred, axis=-1, keepdims=True)
    inverse = lax.rsqrt(spread + 1e-05)
    return centred * inverse, inverse


def norm_back(grad, gain, unit, inverse):
    scaled = grad * gain
    first = jnp.mean(scaled, axis=-1, keepdims=True)
    second = jnp.mean(scaled * unit, axis=-1, keepdims=True)
    return inverse * (scaled - first - unit * second)


def make_per_device(dp, mp):
    def per_device(
        pixels,
        dataset_id,
        variable_mask,
        lead_hours,
        token_counts,
        dataset_weight,
        patch_weight,
        variable_embed,
        position_embed,
        pool_query,
        pool_query_weight,
        pool_key_weight,
        pool_value_weight,
        pool_value_bias,
        pool_output_weight,
        pool_output_bias,
        lead_weight,
        lead_bias,
        norm_gain,
        norm_bias,
        attention_weight,
        attention_bias,
        output_weight,
        output_bias,
        up_weight,
        up_bias,
        down_weight,
        down_bias,
        cotangent,
    ):
        links = Links(dp, mp)
        var_count, pix_count, row_count = pixels.shape[1:]
        flat_count = var_count * pix_count
        model_width = patch_weight.shape[2]
        local_width = pool_query_weight.shape[1]
        head_count = local_width // HEAD_DIM
        layer_count = attention_weight.shape[0]
        shard = model_width // dp

        def heads_first(tensor):
            return tensor.reshape(row_count, head_count, HEAD_DIM).transpose(1, 0, 2)

        def heads_last(tensor):
            return tensor.transpose(1, 0, 2).reshape(row_count, local_width)

        dataset_pick = jnp.arange(variable_mask.shape[0], dtype=jnp.int32) == dataset_id[0]
        mask_row = jnp.sum(jnp.where(dataset_pick[:, None], variable_mask, 0), axis=0)
        item_weight = jnp.sum(jnp.where(dataset_pick, dataset_weight, 0)).astype(F32)
        own_count = token_counts[0].astype(F32)
        count_total = jnp.full((8, 128), own_count, F32)
        for bit in range(bit_count(dp)):
            count_total = count_total + exchange(count_total, "dp", dp, bit)
        item_scale = item_weight * own_count / count_total[0, 0]
        lead_scale = lead_hours[0].astype(F32) / 24.0

        pix_rows = pixels[0].reshape(flat_count, row_count).T
        pix_own, pix_other = links.split_rows(pix_rows)
        pix_low = jnp.concatenate([pix_own, pix_other], axis=0).astype(BF)
        pix_value = pix_low.astype(F32)
        embed_high, embed_rest = two_part(variable_embed)
        embed_all = jnp.concatenate(
            [patch_weight.reshape(flat_count, model_width), embed_high, embed_rest], axis=0
        )
        query_low = pool_query.astype(BF)
        query_vec = matmul(query_low[None, :], pool_query_weight)[0].astype(BF)
        head_of = jnp.arange(local_width, dtype=jnp.int32) // HEAD_DIM
        head_pick = head_of[:, None] == jnp.arange(head_count, dtype=jnp.int32)[None, :]
        query_heads = jnp.where(head_pick, query_vec[:, None], 0).astype(BF)
        key_query = matmul(pool_key_weight, query_heads) / ROOT_DIM
        key_high, key_rest = two_part(key_query)
        projected = matmul(
            embed_all, jnp.concatenate([pool_value_weight, key_high, key_rest], axis=1)
        )
        tail = projected[flat_count : flat_count + var_count] + projected[flat_count + var_count :]
        score_flat = (
            projected[:flat_count, local_width : local_width + head_count]
            + projected[:flat_count, local_width + head_count :]
        )
        score_var = tail[:, local_width : local_width + head_count] + tail[:, local_width + head_count :]
        value_flat = projected[:flat_count, :local_width].astype(BF)
        value_var = (tail[:, :local_width] + pool_value_bias).astype(BF)
        value_flat = value_flat.reshape(flat_count, head_count, HEAD_DIM).transpose(1, 0, 2)
        value_var = value_var.reshape(var_count, head_count, HEAD_DIM).transpose(1, 0, 2)

        var_of = jnp.arange(flat_count, dtype=jnp.int32) // pix_count
        segment = (
            var_of[None, :] == jnp.arange(var_count, dtype=jnp.int32)[:, None]
        )
        segment_low = segment.astype(BF)
        score_block = jnp.where(segment.T[None], score_flat.T[:, :, None], 0.0)
        block_high, block_rest = two_part(score_block)
        block_both = jnp.concatenate([block_high, block_rest], axis=2)
        pool_scores = jnp.einsum(
            "rk,hkv->hrv", pix_low, block_both, preferred_element_type=F32
        )
        pool_scores = (
            pool_scores[:, :, :var_count] + pool_scores[:, :, var_count:] + score_var.T[:, None, :]
        )
        pool_scores = jnp.where(mask_row[None, None, :] > 0, pool_scores, -1000000000.0)
        pool_top = jnp.max(pool_scores, axis=-1, keepdims=True)
        pool_exp = jnp.exp(pool_scores - pool_top)
        pool_probs = pool_exp / jnp.sum(pool_exp, axis=-1, keepdims=True)
        probs_low = pool_probs.astype(BF)
        probs_wide = jnp.einsum("hrv,vk->hrk", probs_low, segment_low, preferred_element_type=F32)
        mixed_pixels = (probs_wide * pix_value[None]).astype(BF)
        pooled = jnp.einsum(
            "hrk,hkd->hrd", mixed_pixels, value_flat, preferred_element_type=F32
        ) + jnp.einsum("hrv,hvd->hrd", probs_low, value_var, preferred_element_type=F32)
        pooled = heads_last(pooled).astype(BF)

        hidden = links.sum_rows(matmul(pooled, pool_output_weight)) + pool_output_bias
        position_own = links.split_rows(position_embed)[0]
        hidden = hidden + position_own + lead_scale * lead_weight + lead_bias

        kept = []
        for layer in range(layer_count):
            unit_one, inverse_one = norm_parts(hidden)
            normed = links.both_rows(unit_one) * norm_gain[layer, 0] + norm_bias[layer, 0]
            normed = normed.astype(BF)
            queries = (
                matmul(normed, attention_weight[layer, 0]) + attention_bias[layer, 0]
            ).astype(BF)
            keys_new = matmul(normed, attention_weight[layer, 1]).astype(BF)
            values_new = (
                matmul(normed, attention_weight[layer, 2]) + attention_bias[layer, 1]
            ).astype(BF)
            query_three = heads_first(queries)
            key_three = heads_first(keys_new)
            value_three = heads_first(values_new)
            scores = (
                jnp.einsum("hpd,hkd->hpk", query_three, key_three, preferred_element_type=F32)
                / ROOT_DIM
            )
            row_max = jnp.max(scores, axis=-1, keepdims=True)
            exponent = jnp.exp(scores - row_max)
            attend = exponent / jnp.sum(exponent, axis=-1, keepdims=True)
            attend_low = attend.astype(BF)
            mixed = heads_last(
                jnp.einsum("hpk,hkd->hpd", attend_low, value_three, preferred_element_type=F32)
            ).astype(BF)
            hidden = (
                hidden
                + links.sum_rows(matmul(mixed, output_weight[layer]))
                + output_bias[layer]
            )
            unit_two, inverse_two = norm_parts(hidden)
            normed_two = links.both_rows(unit_two) * norm_gain[layer, 1] + norm_bias[layer, 1]
            normed_two = normed_two.astype(BF)
            pre_act = matmul(normed_two, up_weight[layer]) + up_bias[layer]
            activation = gelu_exact(pre_act).astype(BF)
            hidden = (
                hidden
                + links.sum_rows(matmul(activation, down_weight[layer]))
                + down_bias[layer]
            )
            kept.append(
                (
                    unit_one,
                    inverse_one,
                    normed,
                    query_three,
                    key_three,
                    value_three,
                    attend,
                    attend_low,
                    mixed,
                    unit_two,
                    inverse_two,
                    normed_two,
                    pre_act,
                    activation,
                )
            )
        layer_out = links.global_rows(hidden, links.other_rows(hidden))

        grad_own, grad_other = links.split_rows(cotangent[0])
        row_sums = {}
        local_sums = {}
        weight_grads = [None] * layer_count
        for layer in reversed(range(layer_count)):
            (
                unit_one,
                inverse_one,
                normed,
                query_three,
                key_three,
                value_three,
                attend,
                attend_low,
                mixed,
                unit_two,
                inverse_two,
                normed_two,
                pre_act,
                activation,
            ) = kept[layer]
            down_low = jnp.concatenate([grad_own, grad_other], axis=0).astype(BF)
            row_sums["down_bias", layer] = jnp.sum(grad_own, axis=0)
            grad_activation = matmul_nt(down_low, down_weight[layer])
            grad_pre = jax.vjp(gelu_exact, pre_act)[1](grad_activation)[0]
            local_sums["up_bias", layer] = jnp.sum(grad_pre, axis=0)
            pre_low = grad_pre.astype(BF)
            grad_two = links.sum_rows(matmul_nt(pre_low, up_weight[layer]))
            down_grad = links.scatter_product(down_low, activation, item_scale)
            up_grad = links.scatter_product(normed_two, pre_low, item_scale)
            row_sums["gain", layer, 1] = jnp.sum(grad_two * unit_two, axis=0)
            row_sums["bias", layer, 1] = jnp.sum(grad_two, axis=0)
            change = norm_back(grad_two, norm_gain[layer, 1], unit_two, inverse_two)
            grad_own = grad_own + change
            grad_other = grad_other + links.other_rows(change)
            out_low = jnp.concatenate([grad_own, grad_other], axis=0).astype(BF)
            row_sums["out_bias", layer] = jnp.sum(grad_own, axis=0)
            grad_mixed = heads_first(matmul_nt(out_low, output_weight[layer]).astype(BF))
            grad_attend = jnp.einsum(
                "hpd,hkd->hpk", grad_mixed, value_three, preferred_element_type=F32
            )
            grad_values = heads_last(
                jnp.einsum("hpk,hpd->hkd", attend_low, grad_mixed, preferred_element_type=F32)
            )
            grad_scores = attend * (
                grad_attend - jnp.sum(attend * grad_attend, axis=-1, keepdims=True)
            )
            score_low = grad_scores.astype(BF)
            grad_queries = heads_last(
                jnp.einsum("hpk,hkd->hpd", score_low, key_three, preferred_element_type=F32)
                / ROOT_DIM
            )
            grad_keys = heads_last(
                jnp.einsum("hpk,hpd->hkd", score_low, query_three, preferred_element_type=F32)
                / ROOT_DIM
            )
            local_sums["qv", layer, 0] = jnp.sum(grad_queries, axis=0)
            local_sums["qv", layer, 1] = jnp.sum(grad_values, axis=0)
            grad_three = [part.astype(BF) for part in (grad_queries, grad_keys, grad_values)]
            partial = matmul_nt(grad_three[0], attention_weight[layer, 0])
            partial = partial + matmul_nt(grad_three[1], attention_weight[layer, 1])
            partial = partial + matmul_nt(grad_three[2], attention_weight[layer, 2])
            grad_one = links.sum_rows(partial)
            out_grad = links.scatter_product(out_low, mixed, item_scale)
            qkv_grad = links.scatter_product(
                normed, jnp.concatenate(grad_three, axis=1), item_scale
            )
            row_sums["gain", layer, 0] = jnp.sum(grad_one * unit_one, axis=0)
            row_sums["bias", layer, 0] = jnp.sum(grad_one, axis=0)
            change = norm_back(grad_one, norm_gain[layer, 0], unit_one, inverse_one)
            grad_own = grad_own + change
            grad_other = grad_other + links.other_rows(change)
            weight_grads[layer] = (down_grad, up_grad, out_grad, qkv_grad)

        column_sum = jnp.sum(grad_own, axis=0)
        row_sums["column"] = column_sum
        row_sums["lead"] = lead_scale * column_sum
        pool_grad_low = jnp.concatenate([grad_own, grad_other], axis=0).astype(BF)
        grad_pooled = heads_first(matmul_nt(pool_grad_low, pool_output_weight).astype(BF))
        pull_flat = jnp.einsum("hrd,hkd->hrk", grad_pooled, value_flat, preferred_element_type=F32)
        pull_high, pull_rest = two_part(pull_flat * pix_value[None])
        grad_probs = (
            jnp.einsum("hrk,vk->hrv", pull_high, segment_low, preferred_element_type=F32)
            + jnp.einsum("hrk,vk->hrv", pull_rest, segment_low, preferred_element_type=F32)
            + jnp.einsum("hrd,hvd->hrv", grad_pooled, value_var, preferred_element_type=F32)
        )
        grad_pool_scores = pool_probs * (
            grad_probs - jnp.sum(pool_probs * grad_probs, axis=-1, keepdims=True)
        )
        score_high, score_rest = two_part(grad_pool_scores)
        pixel_part = jnp.einsum(
            "hrv,hkv->rk", score_high, block_high, preferred_element_type=F32
        ) + jnp.sum(probs_wide * pull_flat, axis=0)

        turned = jnp.einsum(
            "rk,hrv->hkv", pix_low, score_high, preferred_element_type=F32
        ) + jnp.einsum("rk,hrv->hkv", pix_low, score_rest, preferred_element_type=F32)
        key_flat = jnp.sum(jnp.where(segment.T[None], turned, 0.0), axis=2).T * item_scale
        key_var = jnp.sum(grad_pool_scores, axis=1).T * item_scale
        value_grad_flat = jnp.einsum(
            "hrk,hrd->khd", mixed_pixels, grad_pooled, preferred_element_type=F32
        ).reshape(flat_count, local_width)
        value_grad_var = jnp.einsum(
            "hrv,hrd->vhd", probs_low, grad_pooled, preferred_element_type=F32
        ).reshape(var_count, local_width)
        local_sums["pool_bias"] = jnp.sum(value_grad_var, axis=0)
        value_grad_flat = (value_grad_flat * item_scale).astype(BF)
        value_grad_var = (value_grad_var * item_scale).astype(BF)

        key_grad = jnp.concatenate([key_flat, key_var, key_var], axis=0)
        key_grad_high, key_grad_rest = two_part(key_grad)
        summed_key = matmul_tn(
            embed_all, jnp.concatenate([key_grad_high, key_grad_rest], axis=1)
        )
        summed_key = summed_key[:, :head_count] + summed_key[:, head_count:]
        summed_high, summed_rest = two_part(summed_key)
        query_grad = matmul_tn(
            jnp.concatenate([summed_high, summed_rest], axis=1), pool_key_weight
        )
        query_grad = query_grad[:head_count] + query_grad[head_count:]
        query_grad = jnp.sum(jnp.where(head_pick.T, query_grad, 0.0), axis=0) / ROOT_DIM
        query_part = jnp.sum(pool_query_weight.astype(F32) * query_grad[None, :], axis=1)

        flat_all = flat_count + var_count
        grad_rows = jnp.concatenate([value_grad_flat, value_grad_var], axis=0)
        key_rows_high, key_rows_rest = two_part(jnp.concatenate([key_flat, key_var], axis=0))
        right_side = jnp.concatenate([grad_rows, key_rows_high, key_rows_rest, key_rows_high], axis=1)
        left_side = jnp.concatenate([pool_value_weight, key_high, key_high, key_rest], axis=1)
        sub = shard // mp
        sides = left_side.reshape(dp, mp // 2, 2, sub, left_side.shape[1])
        parts = query_part.reshape(dp, mp // 2, 2, sub)
        core = links.mp_bit(0)

        def embed_side(which):
            side = pick(sides, which, 2).transpose(1, 0, 2, 3)
            part = pick(parts, which, 2).transpose(1, 0, 2)
            block = matmul_nt(side.reshape(model_width // 2, left_side.shape[1]), right_side)
            block = jnp.concatenate([block, part.reshape(model_width // 2, 1)], axis=1)
            return block.reshape(mp // 2, dp, sub, flat_all + 1)

        embed_grad = embed_side(core) + exchange(embed_side(1 - core), "mp", mp, 0)
        for bit in range(1, bit_count(mp)):
            own = links.mp_bit(bit)
            count = embed_grad.shape[0] // 2
            pairs = embed_grad.reshape((count, 2) + embed_grad.shape[1:])
            embed_grad = pick(pairs, own, 1) + exchange(pick(pairs, 1 - own, 1), "mp", mp, bit)
        embed_grad = links.scatter_sum(embed_grad[0])

        pool_out_grad = links.scatter_product(pool_grad_low, pooled, item_scale)
        value_weight_grad = links.scatter_product(
            embed_all,
            jnp.concatenate([value_grad_flat, value_grad_var, value_grad_var], axis=0),
            jnp.float32(1.0),
        )
        position = (grad_own * item_scale).reshape(row_count // 2, dp, shard).transpose(1, 0, 2)
        position = links.scatter_sum(position)
        position = links.global_rows(position, links.other_rows(position))

        pixel_own = links.sum_rows(pixel_part)
        pixel_grad = links.global_rows(pixel_own, links.other_rows(pixel_own))
        pixel_grad = pixel_grad.T.reshape(1, var_count, pix_count, row_count)

        names = []
        for layer in range(layer_count):
            names += [("gain", layer, 0), ("gain", layer, 1), ("bias", layer, 0), ("bias", layer, 1)]
        for layer in range(layer_count):
            names += [("out_bias", layer), ("down_bias", layer)]
        names += ["column", "lead"]
        own_sums = jnp.stack([row_sums[name] for name in names]) * item_scale
        full_sums = own_sums + exchange(own_sums, "mp", mp, 0)
        local = jnp.stack([local_sums["up_bias", layer] for layer in range(layer_count)]) * item_scale
        thin = [local_sums["qv", layer, which] for layer in range(layer_count) for which in range(2)]
        thin = jnp.stack(thin + [local_sums["pool_bias"]]) * item_scale
        packed = jnp.concatenate(
            [
                full_sums.reshape(len(names), dp, shard).transpose(1, 0, 2).reshape(dp, -1),
                summed_key.reshape(dp, -1),
                local.reshape(layer_count, dp, -1).transpose(1, 0, 2).reshape(dp, -1),
                thin.reshape(2 * layer_count + 1, dp, -1).transpose(1, 0, 2).reshape(dp, -1),
                jnp.broadcast_to(query_grad[None, :], (dp, local_width)),
            ],
            axis=1,
        )
        packed = links.scatter_sum(packed[:, None, :])[0]
        offset = 0

        def take(*shape):
            nonlocal offset
            size = math.prod(shape)
            piece = packed[offset : offset + size].reshape(shape)
            offset += size
            return piece

        gains = take(layer_count, 2, shard)
        biases = []
        gain_list = []
        offset = 0
        norm_all = take(layer_count, 2, 2, shard)
        gain_list = norm_all[:, 0]
        biases = norm_all[:, 1]
        dense_bias = take(layer_count, 2, shard)
        column_total = take(shard)
        lead_total = take(shard)
        key_shard = take(shard, head_count)
        up_bias_total = take(layer_count, local.shape[1] // dp)
        thin_total = take(2 * layer_count + 1, local_width // dp)
        query_total = take(local_width)

        query_rows = lax.dynamic_slice_in_dim(query_low, links.dp_index * shard, shard, 0)
        query_weight_grad = query_rows.astype(F32)[:, None] * query_total[None, :]
        key_weight_grad = (
            jnp.repeat(key_shard, HEAD_DIM, axis=1) * query_vec.astype(F32)[None, :] / ROOT_DIM
        )
        embed_turned = embed_grad.T
        hidden_width = weight_grads[0][0].shape[1]
        return (
            layer_out[None],
            pixel_grad,
            embed_turned[:flat_count].reshape(var_count, pix_count, sub),
            embed_turned[flat_count:flat_all],
            position,
            embed_turned[flat_all],
            query_weight_grad,
            key_weight_grad,
            value_weight_grad,
            thin_total[-1],
            pool_out_grad.T,
            column_total,
            lead_total,
            column_total,
            gain_list,
            biases,
            jnp.stack(
                [
                    grads[3].reshape(shard, 3, local_width).transpose(1, 0, 2)
                    for grads in weight_grads
                ]
            ),
            thin_total[:-1].reshape(layer_count, 2, local_width // dp),
            jnp.stack([grads[2].T for grads in weight_grads]),
            dense_bias[:, 0],
            jnp.stack([grads[1] for grads in weight_grads]),
            up_bias_total,
            jnp.stack([grads[0].T for grads in weight_grads]),
            dense_bias[:, 1],
        )

    return per_device


def solution(mesh):
    return jax.shard_map(
        make_per_device(mesh.shape["dp"], mesh.shape["mp"]),
        mesh=mesh,
        in_specs=(
            P("dp", None, None, None),
            P("dp"),
            P(),
            P("dp"),
            P("dp"),
            P(),
            P(),
            P(),
            P(),
            P(),
            P(None, "mp"),
            P(None, "mp"),
            P(None, "mp"),
            P("mp"),
            P("mp", None),
            P(),
            P(),
            P(),
            P(),
            P(),
            P(None, None, None, "mp"),
            P(None, None, "mp"),
            P(None, "mp", None),
            P(),
            P(None, None, "mp"),
            P(None, "mp"),
            P(None, "mp", None),
            P(),
            P("dp", None, None),
        ),
        out_specs=(
            P("dp", None, None),
            P("dp", None, None, None),
            P(None, None, ("dp", "mp")),
            P(None, ("dp", "mp")),
            P(None, "dp"),
            P(("dp", "mp")),
            P("dp", "mp"),
            P("dp", "mp"),
            P("dp", "mp"),
            P(("mp", "dp")),
            P("mp", "dp"),
            P("dp"),
            P("dp"),
            P("dp"),
            P(None, None, "dp"),
            P(None, None, "dp"),
            P(None, None, "dp", "mp"),
            P(None, None, ("mp", "dp")),
            P(None, "mp", "dp"),
            P(None, "dp"),
            P(None, "dp", "mp"),
            P(None, ("mp", "dp")),
            P(None, "mp", "dp"),
            P(None, "dp"),
        ),
        check_vma=False,
    )
```

```python
import math

import jax
import jax.numpy as jnp
from jax import lax
from jax.experimental import pallas as pl
from jax.experimental.pallas import tpu as pltpu
from jax.sharding import PartitionSpec as P

HEAD_DIM = 64
Z_FIRST = {("down", 0)}
PLAN = {
    ("pre", 0): [("down", 0), ("up", 0)],
    ("wait_two", 0): [],
    ("mid", 0): [("out", 0)],
    ("wait_one", 0): [("down", 0), ("qkv", 0)],
    ("end", 0): [("up", 0), ("out", 0)],
    ("pre", 1): [("down", 1)],
    ("wait_two", 1): [("down", 0), ("qkv", 0), ("up", 0), ("out", 0)],
    ("mid", 1): [("up", 1), ("out", 1)],
    ("wait_one", 1): [("qkv", 0), ("down", 1), ("qkv", 1), ("out", 1)],
    ("end", 1): [("down", 0), ("up", 0), ("out", 0)],
    "pool": [("qkv", 0), ("up", 1), ("pool_out"), ("pool_value")],
}
DRAIN = [
    ("down", 1),
    ("qkv", 1),
    ("out", 1),
    ("up", 1),
    ("down", 1),
    "pool_out",
    "pool_value",
    ("qkv", 1),
    ("out", 1),
    ("up", 1),
    "pool_out",
    "pool_value",
    ("qkv", 1),
    "pool_out",
    "pool_value",
]
ROOT_DIM = math.sqrt(HEAD_DIM)
BF = jnp.bfloat16
F32 = jnp.float32


def matmul(left, right):
    return jnp.dot(left, right, preferred_element_type=F32)


def matmul_tn(left, right):
    return lax.dot_general(left, right, (((0,), (0,)), ((), ())), preferred_element_type=F32)


def matmul_nt(left, right):
    return lax.dot_general(left, right, (((1,), (1,)), ((), ())), preferred_element_type=F32)


def two_part(tensor):
    high = tensor.astype(BF)
    return high, (tensor - high.astype(F32)).astype(BF)


def gelu_exact(pre_act):
    return jax.nn.gelu(pre_act, approximate=False)


def bit_count(size):
    bits = size.bit_length() - 1
    assert 1 << bits == size
    return bits


def exchange(tensor, axis, size, bit):
    return lax.ppermute(tensor, axis, [(i, i ^ (1 << bit)) for i in range(size)])


def pick(tensor, index, axis):
    return lax.dynamic_index_in_dim(tensor, index, axis, keepdims=False)


def after(value, *earlier):
    return lax.optimization_barrier((value,) + earlier)[0]


def spread(index, bits):
    return sum(((index >> place) & 1) << bit for place, bit in enumerate(bits))


def gradient_blocks(left, right, scale, columns, shard, got=None, got_index=None):
    count = columns.shape[0]
    rows, width = right.shape
    has_got = got is not None

    def kernel(columns_ref, index_ref, scale_ref, left_ref, right_ref, *refs):
        block = (
            lax.dot_general(
                left_ref[...], right_ref[...], (((0,), (0,)), ((), ())), preferred_element_type=F32
            )
            * scale_ref[0, 0]
        )
        if has_got:
            block = block + refs[0][0]
        refs[-1][0] = block

    in_specs = [
        pl.BlockSpec(memory_space=pltpu.SMEM),
        pl.BlockSpec((rows, shard), lambda j, columns_ref, index_ref: (0, columns_ref[j])),
        pl.BlockSpec((rows, width), lambda j, columns_ref, index_ref: (0, 0)),
    ]
    operands = [scale, left, right]
    if has_got:
        in_specs.append(
            pl.BlockSpec((1, shard, width), lambda j, columns_ref, index_ref: (index_ref[j], 0, 0))
        )
        operands.append(got)
    return pl.pallas_call(
        kernel,
        out_shape=jax.ShapeDtypeStruct((count, shard, width), F32),
        grid_spec=pltpu.PrefetchScalarGridSpec(
            num_scalar_prefetch=2,
            grid=(count,),
            in_specs=in_specs,
            out_specs=pl.BlockSpec(
                (1, shard, width), lambda j, columns_ref, index_ref: (j, 0, 0)
            ),
        ),
        cost_estimate=pl.CostEstimate(
            flops=2 * count * shard * rows * width,
            bytes_accessed=4 * count * shard * width * (2 if has_got else 1) + 2 * rows * width,
            transcendentals=0,
        ),
        name="gradient_blocks",
    )(columns, columns if got_index is None else got_index, *operands)


def add_blocks(first, first_index, second, second_index):
    count = first_index.shape[0]
    rows, width = first.shape[1:]

    def kernel(first_index_ref, second_index_ref, first_ref, second_ref, out_ref):
        out_ref[...] = first_ref[...] + second_ref[...]

    block = (1, rows, width)
    return pl.pallas_call(
        kernel,
        out_shape=jax.ShapeDtypeStruct((count, rows, width), F32),
        grid_spec=pltpu.PrefetchScalarGridSpec(
            num_scalar_prefetch=2,
            grid=(count,),
            in_specs=[
                pl.BlockSpec(block, lambda j, one, two: (one[j], 0, 0)),
                pl.BlockSpec(block, lambda j, one, two: (two[j], 0, 0)),
            ],
            out_specs=pl.BlockSpec(block, lambda j, one, two: (j, 0, 0)),
        ),
        cost_estimate=pl.CostEstimate(
            flops=count * rows * width, bytes_accessed=12 * count * rows * width, transcendentals=0
        ),
        name="add_blocks",
    )(first_index, second_index, first, second)


def norm_rows(own, other, gain, bias):
    half, width = own.shape

    def kernel(own_ref, other_ref, gain_ref, bias_ref, out_ref):
        out_ref[:half] = (own_ref[...] * gain_ref[...] + bias_ref[...]).astype(BF)
        out_ref[half:] = (other_ref[...] * gain_ref[...] + bias_ref[...]).astype(BF)

    return pl.pallas_call(
        kernel,
        out_shape=jax.ShapeDtypeStruct((2 * half, width), BF),
        cost_estimate=pl.CostEstimate(
            flops=4 * half * width, bytes_accessed=12 * half * width, transcendentals=0
        ),
        name="norm_rows",
    )(own, other, gain[None], bias[None])


def merge_rows(own, other, change):
    half, width = own.shape

    def kernel(own_ref, other_ref, change_ref, other_out, low_out):
        low_out[:half] = own_ref[...].astype(BF)
        total = other_ref[...] + change_ref[...]
        other_out[...] = total
        low_out[half:] = total.astype(BF)

    return pl.pallas_call(
        kernel,
        out_shape=(
            jax.ShapeDtypeStruct((half, width), F32),
            jax.ShapeDtypeStruct((2 * half, width), BF),
        ),
        cost_estimate=pl.CostEstimate(
            flops=2 * half * width, bytes_accessed=20 * half * width, transcendentals=0
        ),
        name="merge_rows",
    )(own, other, change)


def norm_back(mine, got, unit, inverse, gain, grad):
    half, width = mine.shape

    def kernel(mine_ref, got_ref, unit_ref, inverse_ref, gain_ref, grad_ref, change_out, grad_out, sums_out):
        pull = mine_ref[...] + got_ref[...]
        unit_rows = unit_ref[...]
        scaled = pull * gain_ref[...]
        first = jnp.mean(scaled, axis=-1, keepdims=True)
        second = jnp.mean(scaled * unit_rows, axis=-1, keepdims=True)
        change = inverse_ref[...] * (scaled - first - unit_rows * second)
        change_out[...] = change
        total = grad_ref[...] + change
        grad_out[...] = total
        sums_out[0:1] = jnp.sum(pull * unit_rows, axis=0, keepdims=True)
        sums_out[1:2] = jnp.sum(pull, axis=0, keepdims=True)
        sums_out[2:3] = jnp.sum(total, axis=0, keepdims=True)

    rows = jax.ShapeDtypeStruct((half, width), F32)
    return pl.pallas_call(
        kernel,
        out_shape=(rows, rows, jax.ShapeDtypeStruct((3, width), F32)),
        cost_estimate=pl.CostEstimate(
            flops=14 * half * width, bytes_accessed=24 * half * width, transcendentals=0
        ),
        name="norm_back",
    )(mine, got, unit, inverse, gain[None], grad)


class Links:
    def __init__(self, dp, mp):
        self.dp, self.mp = dp, mp
        self.dp_index = lax.axis_index("dp")
        self.mp_index = lax.axis_index("mp")

    def dp_bit(self, bit):
        return (self.dp_index >> bit) & 1

    def mp_bit(self, bit):
        return (self.mp_index >> bit) & 1

    def begin_sum(self, partial):
        half = partial.shape[0] // 2
        mine = partial[:half] + exchange(partial[half:], "mp", self.mp, 0)
        last = bit_count(self.mp) - 1
        for bit in range(1, last):
            mine = mine + exchange(mine, "mp", self.mp, bit)
        return mine, exchange(mine, "mp", self.mp, last)

    def sum_rows(self, partial):
        mine, got = self.begin_sum(partial)
        return mine + got

    def other_rows(self, own):
        return exchange(own, "mp", self.mp, 0)

    def split_rows(self, tensor):
        half = tensor.shape[0] // 2
        core = self.mp_bit(0)
        own = lax.dynamic_slice_in_dim(tensor, core * half, half, 0)
        other = lax.dynamic_slice_in_dim(tensor, (1 - core) * half, half, 0)
        return own, other

    def global_rows(self, own, other):
        core = self.mp_bit(0)
        return jnp.concatenate(
            [jnp.where(core == 0, own, other), jnp.where(core == 0, other, own)], axis=0
        )

    def scatter_sum(self, shards):
        for bit in range(bit_count(self.dp)):
            count = shards.shape[0] // 2
            pairs = shards.reshape((count, 2) + shards.shape[1:])
            own = self.dp_bit(bit)
            got = exchange(pick(pairs, 1 - own, 1), "dp", self.dp, bit)
            shards = pick(pairs, own, 1) + got
        return shards[0]


class Merge:
    def __init__(self, links, left, right, scale, order):
        self.links, self.left, self.right, self.scale = links, left, right, scale
        self.order = list(order)
        self.shard = left.shape[1] // links.dp
        self.step = 0
        self.got = None
        self.keep = None

    def entries(self, fixed, left_bits):
        count = 1 << len(left_bits)
        return jnp.array([spread(j, left_bits) for j in range(count)], jnp.int32) + fixed

    def advance(self, *earlier):
        links = self.links
        done = self.order[: self.step]
        bits = sorted(self.order[self.step - 1 :] if self.step else self.order)
        fixed = sum((links.dp_bit(bit) << bit for bit in done), jnp.int32(0))
        if self.step == 0:
            bit = self.order[0]
            rest = sorted(b for b in self.order if b != bit)
            left = after(self.left, *earlier) if earlier else self.left
            send = self.blocks(left, self.entries((1 - links.dp_bit(bit)) << bit, rest))
        elif self.step < len(self.order):
            bit = self.order[self.step]
            before = sorted(self.order[self.step :])
            place = before.index(bit)
            rest = [b for b in before if b != bit]
            slots = [before.index(b) for b in rest]
            other = self.entries((1 - links.dp_bit(bit)) << place, slots)
            same = self.entries(links.dp_bit(bit) << place, slots)
            got = after(self.got, *earlier) if earlier else self.got
            if self.step == 1:
                first = self.order[0]
                base = links.dp_bit(first) << first
                flip = (1 - links.dp_bit(bit)) << bit
                send = self.blocks(self.left, self.entries(base + flip, rest), got, other)
                hold = links.dp_bit(bit) << bit
                self.keep = self.blocks(
                    self.left, self.entries(base + hold, rest), after(got, send), same
                )
            else:
                send = add_blocks(self.keep, other, got, other)
                self.keep = add_blocks(self.keep, same, after(got, send), same)
        else:
            got = after(self.got, *earlier) if earlier else self.got
            self.step += 1
            self.result = self.keep[0] + got[0]
            return self.result
        self.got = exchange(send, "dp", links.dp, self.order[self.step])
        self.step += 1
        return send

    def blocks(self, left, columns, got=None, got_index=None):
        if self.shard % 128 == 0:
            return gradient_blocks(
                left, self.right, self.scale, columns, self.shard, got, got_index
            )
        rows = left.reshape(left.shape[0], -1, self.shard)[:, columns]
        block = (
            jnp.einsum("rcs,rn->csn", rows, self.right, preferred_element_type=F32)
            * self.scale[0, 0]
        )
        return block if got is None else block + got[got_index]


def norm_parts(rows):
    row_mean = jnp.mean(rows, axis=-1, keepdims=True)
    centred = rows - row_mean
    spread = jnp.mean(centred * centred, axis=-1, keepdims=True)
    inverse = lax.rsqrt(spread + 1e-05)
    return centred * inverse, inverse


def make_per_device(dp, mp):
    def per_device(
        pixels,
        dataset_id,
        variable_mask,
        lead_hours,
        token_counts,
        dataset_weight,
        patch_weight,
        variable_embed,
        position_embed,
        pool_query,
        pool_query_weight,
        pool_key_weight,
        pool_value_weight,
        pool_value_bias,
        pool_output_weight,
        pool_output_bias,
        lead_weight,
        lead_bias,
        norm_gain,
        norm_bias,
        attention_weight,
        attention_bias,
        output_weight,
        output_bias,
        up_weight,
        up_bias,
        down_weight,
        down_bias,
        cotangent,
    ):
        links = Links(dp, mp)
        var_count, pix_count, row_count = pixels.shape[1:]
        flat_count = var_count * pix_count
        model_width = patch_weight.shape[2]
        local_width = pool_query_weight.shape[1]
        head_count = local_width // HEAD_DIM
        layer_count = attention_weight.shape[0]
        shard = model_width // dp

        def heads_first(tensor):
            return tensor.reshape(row_count, head_count, HEAD_DIM).transpose(1, 0, 2)

        def heads_last(tensor):
            return tensor.transpose(1, 0, 2).reshape(row_count, local_width)

        dataset_pick = jnp.arange(variable_mask.shape[0], dtype=jnp.int32) == dataset_id[0]
        mask_row = jnp.sum(jnp.where(dataset_pick[:, None], variable_mask, 0), axis=0)
        item_weight = jnp.sum(jnp.where(dataset_pick, dataset_weight, 0)).astype(F32)
        own_count = token_counts[0].astype(F32)
        lead_scale = lead_hours[0].astype(F32) / 24.0

        pix_rows = pixels[0].reshape(flat_count, row_count).T
        pix_own, pix_other = links.split_rows(pix_rows)
        pix_low = jnp.concatenate([pix_own, pix_other], axis=0).astype(BF)
        pix_value = pix_low.astype(F32)
        embed_high, embed_rest = two_part(variable_embed)
        embed_all = jnp.concatenate(
            [patch_weight.reshape(flat_count, model_width), embed_high, embed_rest], axis=0
        )
        query_low = pool_query.astype(BF)
        query_vec = matmul(query_low[None, :], pool_query_weight)[0].astype(BF)
        head_of = jnp.arange(local_width, dtype=jnp.int32) // HEAD_DIM
        head_pick = head_of[:, None] == jnp.arange(head_count, dtype=jnp.int32)[None, :]
        query_heads = jnp.where(head_pick, query_vec[:, None], 0).astype(BF)
        key_query = matmul(pool_key_weight, query_heads) / ROOT_DIM
        key_high, key_rest = two_part(key_query)
        projected = matmul(
            embed_all, jnp.concatenate([pool_value_weight, key_high, key_rest], axis=1)
        )
        tail = projected[flat_count : flat_count + var_count] + projected[flat_count + var_count :]
        score_flat = (
            projected[:flat_count, local_width : local_width + head_count]
            + projected[:flat_count, local_width + head_count :]
        )
        score_var = tail[:, local_width : local_width + head_count] + tail[:, local_width + head_count :]
        value_flat = projected[:flat_count, :local_width].astype(BF)
        value_var = (tail[:, :local_width] + pool_value_bias).astype(BF)
        value_flat = value_flat.reshape(flat_count, head_count, HEAD_DIM).transpose(1, 0, 2)
        value_var = value_var.reshape(var_count, head_count, HEAD_DIM).transpose(1, 0, 2)

        var_of = jnp.arange(flat_count, dtype=jnp.int32) // pix_count
        segment = (
            var_of[None, :] == jnp.arange(var_count, dtype=jnp.int32)[:, None]
        )
        segment_low = segment.astype(BF)
        score_block = jnp.where(segment.T[None], score_flat.T[:, :, None], 0.0)
        block_high, block_rest = two_part(score_block)
        block_both = jnp.concatenate([block_high, block_rest], axis=2)
        pool_scores = jnp.einsum(
            "rk,hkv->hrv", pix_low, block_both, preferred_element_type=F32
        )
        pool_scores = (
            pool_scores[:, :, :var_count] + pool_scores[:, :, var_count:] + score_var.T[:, None, :]
        )
        pool_scores = jnp.where(mask_row[None, None, :] > 0, pool_scores, -1000000000.0)
        pool_top = jnp.max(pool_scores, axis=-1, keepdims=True)
        pool_exp = jnp.exp(pool_scores - pool_top)
        pool_probs = pool_exp / jnp.sum(pool_exp, axis=-1, keepdims=True)
        probs_low = pool_probs.astype(BF)
        probs_wide = jnp.einsum("hrv,vk->hrk", probs_low, segment_low, preferred_element_type=F32)
        mixed_pixels = (probs_wide * pix_value[None]).astype(BF)
        pooled = jnp.einsum(
            "hrk,hkd->hrd", mixed_pixels, value_flat, preferred_element_type=F32
        ) + jnp.einsum("hrv,hvd->hrd", probs_low, value_var, preferred_element_type=F32)
        pooled = heads_last(pooled).astype(BF)

        mine, got = links.begin_sum(matmul(pooled, pool_output_weight))
        count_total = after(jnp.full((8, 128), own_count, F32), mine)
        for bit in range(bit_count(dp)):
            count_total = count_total + exchange(count_total, "dp", dp, bit)
        item_scale = item_weight * own_count / count_total[0, 0]
        scale_cell = item_scale.reshape(1, 1)
        position_own = links.split_rows(position_embed)[0]
        offset_rows = pool_output_bias + position_own + lead_scale * lead_weight + lead_bias
        mine, scale_cell = lax.optimization_barrier((mine, scale_cell))
        hidden = mine + got + offset_rows

        kept = []
        for layer in range(layer_count):
            last = layer == layer_count - 1
            unit_one, inverse_one = norm_parts(hidden)
            normed = norm_rows(
                unit_one, links.other_rows(unit_one), norm_gain[layer, 0], norm_bias[layer, 0]
            )
            queries = (
                matmul(normed, attention_weight[layer, 0]) + attention_bias[layer, 0]
            ).astype(BF)
            keys_new = matmul(normed, attention_weight[layer, 1]).astype(BF)
            values_new = (
                matmul(normed, attention_weight[layer, 2]) + attention_bias[layer, 1]
            ).astype(BF)
            query_three = heads_first(queries)
            key_three = heads_first(keys_new)
            value_three = heads_first(values_new)
            scores = (
                jnp.einsum("hpd,hkd->hpk", query_three, key_three, preferred_element_type=F32)
                / ROOT_DIM
            )
            row_max = jnp.max(scores, axis=-1, keepdims=True)
            exponent = jnp.exp(scores - row_max)
            attend = exponent / jnp.sum(exponent, axis=-1, keepdims=True)
            attend_low = attend.astype(BF)
            mixed = heads_last(
                jnp.einsum("hpk,hkd->hpd", attend_low, value_three, preferred_element_type=F32)
            ).astype(BF)
            mine, got = links.begin_sum(matmul(mixed, output_weight[layer]))
            if layer == 0:
                grad_own, grad_other = links.split_rows(after(cotangent[0], mine))
                ones = jnp.ones((model_width,), F32)
                down_low = norm_rows(grad_own, grad_other, ones, jnp.zeros_like(ones))
                mine, down_low = lax.optimization_barrier((mine, down_low))
            hidden = hidden + (mine + got) + output_bias[layer]
            unit_two, inverse_two = norm_parts(hidden)
            normed_two = norm_rows(
                unit_two, links.other_rows(unit_two), norm_gain[layer, 1], norm_bias[layer, 1]
            )
            pre_act = matmul(normed_two, up_weight[layer]) + up_bias[layer]
            activation = gelu_exact(pre_act).astype(BF)
            if not last:
                mine, got = links.begin_sum(matmul(activation, down_weight[layer]))
                if layer == 0:
                    top_grad = matmul_nt(after(down_low, mine), down_weight[layer_count - 1])
                    mine, top_grad = lax.optimization_barrier((mine, top_grad))
                hidden = hidden + (mine + got) + down_bias[layer]
            kept.append(
                (
                    unit_one,
                    inverse_one,
                    normed,
                    query_three,
                    key_three,
                    value_three,
                    attend,
                    attend_low,
                    mixed,
                    unit_two,
                    inverse_two,
                    normed_two,
                    pre_act,
                    activation,
                )
            )
        last_partial = matmul(activation, down_weight[layer_count - 1])

        row_sums = {}
        local_sums = {}
        merges = {}
        top = layer_count - 1
        row_sums["down_bias", top] = jnp.sum(grad_own, axis=0)

        def add_merge(name, left, right):
            order = list(range(bit_count(dp)))
            if name in Z_FIRST:
                order = order[1:] + order[:1]
            merges[name] = Merge(links, left, right, scale_cell, order)

        def advance(spot, critical):
            for name in PLAN.get(spot, ()):
                if name in merges:
                    critical = after(critical, merges[name].advance(critical))
            return critical

        for layer in reversed(range(layer_count)):
            depth = top - layer
            (
                unit_one,
                inverse_one,
                normed,
                query_three,
                key_three,
                value_three,
                attend,
                attend_low,
                mixed,
                unit_two,
                inverse_two,
                normed_two,
                pre_act,
                activation,
            ) = kept[layer]
            grad_activation = top_grad if layer == top else matmul_nt(down_low, down_weight[layer])
            grad_pre = jax.vjp(gelu_exact, pre_act)[1](grad_activation)[0]
            local_sums["up_bias", layer] = jnp.sum(grad_pre, axis=0)
            pre_low = grad_pre.astype(BF)
            add_merge(("down", depth), down_low, activation)
            add_merge(("up", depth), normed_two, pre_low)
            pre_low = advance(("pre", depth), pre_low)
            mine, got = links.begin_sum(matmul_nt(pre_low, up_weight[layer]))
            mine = advance(("wait_two", depth), mine)
            change, grad_own, sums = norm_back(
                mine, got, unit_two, inverse_two, norm_gain[layer, 1], grad_own
            )
            row_sums["gain", layer, 1] = sums[0]
            row_sums["bias", layer, 1] = sums[1]
            row_sums["out_bias", layer] = sums[2]
            grad_other, out_low = merge_rows(grad_own, grad_other, links.other_rows(change))
            add_merge(("out", depth), out_low, mixed)
            out_low = advance(("mid", depth), out_low)
            grad_mixed = heads_first(matmul_nt(out_low, output_weight[layer]).astype(BF))
            grad_attend = jnp.einsum(
                "hpd,hkd->hpk", grad_mixed, value_three, preferred_element_type=F32
            )
            grad_values = heads_last(
                jnp.einsum("hpk,hpd->hkd", attend_low, grad_mixed, preferred_element_type=F32)
            )
            grad_scores = attend * (
                grad_attend - jnp.sum(attend * grad_attend, axis=-1, keepdims=True)
            )
            score_low = grad_scores.astype(BF)
            grad_queries = heads_last(
                jnp.einsum("hpk,hkd->hpd", score_low, key_three, preferred_element_type=F32)
                / ROOT_DIM
            )
            grad_keys = heads_last(
                jnp.einsum("hpk,hpd->hkd", score_low, query_three, preferred_element_type=F32)
                / ROOT_DIM
            )
            local_sums["qv", layer, 0] = jnp.sum(grad_queries, axis=0)
            local_sums["qv", layer, 1] = jnp.sum(grad_values, axis=0)
            grad_three = [part.astype(BF) for part in (grad_queries, grad_keys, grad_values)]
            partial = matmul_nt(grad_three[0], attention_weight[layer, 0])
            partial = partial + matmul_nt(grad_three[1], attention_weight[layer, 1])
            partial = partial + matmul_nt(grad_three[2], attention_weight[layer, 2])
            mine, got = links.begin_sum(partial)
            add_merge(("qkv", depth), normed, jnp.concatenate(grad_three, axis=1))
            mine = advance(("wait_one", depth), mine)
            change, grad_own, sums = norm_back(
                mine, got, unit_one, inverse_one, norm_gain[layer, 0], grad_own
            )
            row_sums["gain", layer, 0] = sums[0]
            row_sums["bias", layer, 0] = sums[1]
            if layer:
                row_sums["down_bias", layer - 1] = sums[2]
            grad_other, down_low = merge_rows(grad_own, grad_other, links.other_rows(change))
            down_low = advance(("end", depth), down_low)

        row_sums["column"] = sums[2]
        row_sums["lead"] = lead_scale * sums[2]
        pool_grad_low = down_low
        grad_pooled = heads_first(matmul_nt(pool_grad_low, pool_output_weight).astype(BF))
        pull_flat = jnp.einsum("hrd,hkd->hrk", grad_pooled, value_flat, preferred_element_type=F32)
        pull_high, pull_rest = two_part(pull_flat * pix_value[None])
        grad_probs = (
            jnp.einsum("hrk,vk->hrv", pull_high, segment_low, preferred_element_type=F32)
            + jnp.einsum("hrk,vk->hrv", pull_rest, segment_low, preferred_element_type=F32)
            + jnp.einsum("hrd,hvd->hrv", grad_pooled, value_var, preferred_element_type=F32)
        )
        grad_pool_scores = pool_probs * (
            grad_probs - jnp.sum(pool_probs * grad_probs, axis=-1, keepdims=True)
        )
        score_high, score_rest = two_part(grad_pool_scores)
        pixel_part = jnp.einsum(
            "hrv,hkv->rk", score_high, block_high, preferred_element_type=F32
        ) + jnp.sum(probs_wide * pull_flat, axis=0)

        turned = jnp.einsum(
            "rk,hrv->hkv", pix_low, score_high, preferred_element_type=F32
        ) + jnp.einsum("rk,hrv->hkv", pix_low, score_rest, preferred_element_type=F32)
        key_flat = jnp.sum(jnp.where(segment.T[None], turned, 0.0), axis=2).T * item_scale
        key_var = jnp.sum(grad_pool_scores, axis=1).T * item_scale
        value_grad_flat = jnp.einsum(
            "hrk,hrd->khd", mixed_pixels, grad_pooled, preferred_element_type=F32
        ).reshape(flat_count, local_width)
        value_grad_var = jnp.einsum(
            "hrv,hrd->vhd", probs_low, grad_pooled, preferred_element_type=F32
        ).reshape(var_count, local_width)
        local_sums["pool_bias"] = jnp.sum(value_grad_var, axis=0)
        value_grad_flat = (value_grad_flat * item_scale).astype(BF)
        value_grad_var = (value_grad_var * item_scale).astype(BF)

        key_grad = jnp.concatenate([key_flat, key_var, key_var], axis=0)
        key_grad_high, key_grad_rest = two_part(key_grad)
        summed_key = matmul_tn(
            embed_all, jnp.concatenate([key_grad_high, key_grad_rest], axis=1)
        )
        summed_key = summed_key[:, :head_count] + summed_key[:, head_count:]
        summed_high, summed_rest = two_part(summed_key)
        query_grad = matmul_tn(
            jnp.concatenate([summed_high, summed_rest], axis=1), pool_key_weight
        )
        query_grad = query_grad[:head_count] + query_grad[head_count:]
        query_grad = jnp.sum(jnp.where(head_pick.T, query_grad, 0.0), axis=0) / ROOT_DIM
        query_part = jnp.sum(pool_query_weight.astype(F32) * query_grad[None, :], axis=1)

        flat_all = flat_count + var_count
        grad_rows = jnp.concatenate([value_grad_flat, value_grad_var], axis=0)
        key_rows_high, key_rows_rest = two_part(jnp.concatenate([key_flat, key_var], axis=0))
        right_side = jnp.concatenate([grad_rows, key_rows_high, key_rows_rest, key_rows_high], axis=1)
        left_side = jnp.concatenate([pool_value_weight, key_high, key_high, key_rest], axis=1)
        sub = shard // mp
        sides = left_side.reshape(dp, mp // 2, 2, sub, left_side.shape[1])
        parts = query_part.reshape(dp, mp // 2, 2, sub)
        core = links.mp_bit(0)

        def embed_side(which):
            side = pick(sides, which, 2).transpose(1, 0, 2, 3)
            part = pick(parts, which, 2).transpose(1, 0, 2)
            block = matmul_nt(side.reshape(model_width // 2, left_side.shape[1]), right_side)
            block = jnp.concatenate([block, part.reshape(model_width // 2, 1)], axis=1)
            return block.reshape(mp // 2, dp, sub, flat_all + 1)

        embed_grad = embed_side(core) + exchange(embed_side(1 - core), "mp", mp, 0)
        for bit in range(1, bit_count(mp)):
            own = links.mp_bit(bit)
            count = embed_grad.shape[0] // 2
            pairs = embed_grad.reshape((count, 2) + embed_grad.shape[1:])
            embed_grad = pick(pairs, own, 1) + exchange(pick(pairs, 1 - own, 1), "mp", mp, bit)
        embed_grad = links.scatter_sum(embed_grad[0])

        add_merge("pool_out", pool_grad_low, pooled)
        merges["pool_value"] = Merge(
            links,
            embed_all,
            jnp.concatenate([value_grad_flat, value_grad_var, value_grad_var], axis=0),
            jnp.ones((1, 1), F32),
            list(range(bit_count(dp))),
        )
        marker = value_grad_flat
        marker = advance("pool", marker)
        for name in DRAIN:
            marker = after(marker, merges[name].advance(marker))
        weight_grads = {}
        for name, merge in merges.items():
            while merge.step <= bit_count(dp):
                result = merge.advance()
            weight_grads[name] = merge.result
        last_mine, last_got = links.begin_sum(last_partial)
        hidden = hidden + (last_mine + last_got) + down_bias[top]
        layer_out = links.global_rows(hidden, links.other_rows(hidden))
        position = (grad_own * item_scale).reshape(row_count // 2, dp, shard).transpose(1, 0, 2)
        position = links.scatter_sum(position)
        position = links.global_rows(position, links.other_rows(position))

        pixel_own = links.sum_rows(pixel_part)
        pixel_grad = links.global_rows(pixel_own, links.other_rows(pixel_own))
        pixel_grad = pixel_grad.T.reshape(1, var_count, pix_count, row_count)

        names = []
        for layer in range(layer_count):
            names += [("gain", layer, 0), ("gain", layer, 1), ("bias", layer, 0), ("bias", layer, 1)]
        for layer in range(layer_count):
            names += [("out_bias", layer), ("down_bias", layer)]
        names += ["column", "lead"]
        own_sums = jnp.stack([row_sums[name] for name in names]) * item_scale
        full_sums = own_sums + exchange(own_sums, "mp", mp, 0)
        local = jnp.stack([local_sums["up_bias", layer] for layer in range(layer_count)]) * item_scale
        thin = [local_sums["qv", layer, which] for layer in range(layer_count) for which in range(2)]
        thin = jnp.stack(thin + [local_sums["pool_bias"]]) * item_scale
        packed = jnp.concatenate(
            [
                full_sums.reshape(len(names), dp, shard).transpose(1, 0, 2).reshape(dp, -1),
                summed_key.reshape(dp, -1),
                local.reshape(layer_count, dp, -1).transpose(1, 0, 2).reshape(dp, -1),
                thin.reshape(2 * layer_count + 1, dp, -1).transpose(1, 0, 2).reshape(dp, -1),
                jnp.broadcast_to(query_grad[None, :], (dp, local_width)),
            ],
            axis=1,
        )
        packed = links.scatter_sum(packed[:, None, :])[0]
        offset = 0

        def take(*shape):
            nonlocal offset
            size = math.prod(shape)
            piece = packed[offset : offset + size].reshape(shape)
            offset += size
            return piece

        gains = take(layer_count, 2, shard)
        biases = []
        gain_list = []
        offset = 0
        norm_all = take(layer_count, 2, 2, shard)
        gain_list = norm_all[:, 0]
        biases = norm_all[:, 1]
        dense_bias = take(layer_count, 2, shard)
        column_total = take(shard)
        lead_total = take(shard)
        key_shard = take(shard, head_count)
        up_bias_total = take(layer_count, local.shape[1] // dp)
        thin_total = take(2 * layer_count + 1, local_width // dp)
        query_total = take(local_width)

        query_rows = lax.dynamic_slice_in_dim(query_low, links.dp_index * shard, shard, 0)
        query_weight_grad = query_rows.astype(F32)[:, None] * query_total[None, :]
        key_weight_grad = (
            jnp.repeat(key_shard, HEAD_DIM, axis=1) * query_vec.astype(F32)[None, :] / ROOT_DIM
        )
        embed_turned = embed_grad.T
        return (
            layer_out[None],
            pixel_grad,
            embed_turned[:flat_count].reshape(var_count, pix_count, sub),
            embed_turned[flat_count:flat_all],
            position,
            embed_turned[flat_all],
            query_weight_grad,
            key_weight_grad,
            weight_grads["pool_value"],
            thin_total[-1],
            weight_grads["pool_out"].T,
            column_total,
            lead_total,
            column_total,
            gain_list,
            biases,
            jnp.stack(
                [
                    weight_grads["qkv", top - layer]
                    .reshape(shard, 3, local_width)
                    .transpose(1, 0, 2)
                    for layer in range(layer_count)
                ]
            ),
            thin_total[:-1].reshape(layer_count, 2, local_width // dp),
            jnp.stack(
                [weight_grads["out", top - layer].T for layer in range(layer_count)]
            ),
            dense_bias[:, 0],
            jnp.stack(
                [weight_grads["up", top - layer] for layer in range(layer_count)]
            ),
            up_bias_total,
            jnp.stack(
                [weight_grads["down", top - layer].T for layer in range(layer_count)]
            ),
            dense_bias[:, 1],
        )

    return per_device


def solution(mesh):
    return jax.shard_map(
        make_per_device(mesh.shape["dp"], mesh.shape["mp"]),
        mesh=mesh,
        in_specs=(
            P("dp", None, None, None),
            P("dp"),
            P(),
            P("dp"),
            P("dp"),
            P(),
            P(),
            P(),
            P(),
            P(),
            P(None, "mp"),
            P(None, "mp"),
            P(None, "mp"),
            P("mp"),
            P("mp", None),
            P(),
            P(),
            P(),
            P(),
            P(),
            P(None, None, None, "mp"),
            P(None, None, "mp"),
            P(None, "mp", None),
            P(),
            P(None, None, "mp"),
            P(None, "mp"),
            P(None, "mp", None),
            P(),
            P("dp", None, None),
        ),
        out_specs=(
            P("dp", None, None),
            P("dp", None, None, None),
            P(None, None, ("dp", "mp")),
            P(None, ("dp", "mp")),
            P(None, "dp"),
            P(("dp", "mp")),
            P("dp", "mp"),
            P("dp", "mp"),
            P("dp", "mp"),
            P(("mp", "dp")),
            P("mp", "dp"),
            P("dp"),
            P("dp"),
            P("dp"),
            P(None, None, "dp"),
            P(None, None, "dp"),
            P(None, None, "dp", "mp"),
            P(None, None, ("mp", "dp")),
            P(None, "mp", "dp"),
            P(None, "dp"),
            P(None, "dp", "mp"),
            P(None, ("mp", "dp")),
            P(None, "mp", "dp"),
            P(None, "dp"),
        ),
        check_vma=False,
    )
```

```python
import math

import jax
import jax.numpy as jnp
from jax import lax
from jax.experimental import pallas as pl
from jax.experimental.pallas import tpu as pltpu
from jax.sharding import PartitionSpec as P

HEAD_DIM = 64
PLAN = {
    ("pre", 0): [("down", 0), ("up", 0)],
    ("wait_one", 0): [("att", 0), ("down", 0), ("up", 0)],
    ("wait_two", 1): [("down", 1)],
    ("mid", 1): [("up", 0), ("att", 0)],
    ("wait_one", 1): [("up", 1), ("down", 0), ("att", 0)],
    ("end", 1): [("down", 1), ("att", 1)],
    "scores": [("up", 1), ("down", 1)],
    "values": ["tail"],
}
DRAIN = [("att", 1), ("up", 1), "position", "vectors", "embed", "tail", ("att", 1),
         "position", "vectors", "embed", "tail", "position", "vectors", "embed"]
ROOT_DIM = math.sqrt(HEAD_DIM)
BF = jnp.bfloat16
F32 = jnp.float32


def matmul(left, right):
    return jnp.dot(left, right, preferred_element_type=F32)


def matmul_tn(left, right):
    return lax.dot_general(left, right, (((0,), (0,)), ((), ())), preferred_element_type=F32)


def matmul_nt(left, right):
    return lax.dot_general(left, right, (((1,), (1,)), ((), ())), preferred_element_type=F32)


def two_part(tensor):
    high = tensor.astype(BF)
    return high, (tensor - high.astype(F32)).astype(BF)


def gelu_exact(pre_act):
    return jax.nn.gelu(pre_act, approximate=False)


def bit_count(size):
    bits = size.bit_length() - 1
    assert 1 << bits == size
    return bits


def exchange(tensor, axis, size, bit):
    return lax.ppermute(tensor, axis, [(i, i ^ (1 << bit)) for i in range(size)])


def pick(tensor, index, axis):
    return lax.dynamic_index_in_dim(tensor, index, axis, keepdims=False)


def after(value, *earlier):
    return lax.optimization_barrier((value,) + earlier)[0]


def vmem_limit(size):
    return pltpu.CompilerParams(vmem_limit_bytes=int(size * 1.25) + (2 << 20))


LONG = pl.CostEstimate(flops=10**12, bytes_accessed=8, transcendentals=0)


def step_cell(cell):
    def kernel(cell_ref, out_ref):
        out_ref[...] = cell_ref[...]

    return pl.pallas_call(
        kernel,
        out_shape=jax.ShapeDtypeStruct(cell.shape, F32),
        cost_estimate=LONG,
        compiler_params=vmem_limit(0),
        name="step_cell",
    )(cell)


class Clock:
    def __init__(self, cell):
        self.cell = cell

    def both(self, *values):
        *values, self.cell = lax.optimization_barrier((*values, self.cell))
        return values

    def one(self, value):
        return self.both(value)[0]

    def hold(self):
        self.cell = step_cell(self.cell)


def ordered_columns(source, target, shards_ref, count, shard):
    for place in range(count):
        column = pl.multiple_of(shards_ref[place] * shard, shard)
        target[:, place * shard : (place + 1) * shard] = source[:, pl.ds(column, shard)]


def take_columns(rows, shards, shard):
    pieces = rows.reshape(rows.shape[0], -1, shard)[:, shards]
    return pieces.reshape(rows.shape)


def norm_rows(own, other, gain, bias, shards):
    half, width = own.shape
    count = shards.shape[0]
    shard = width // count
    if shard % 128:
        rows = jnp.concatenate([own, other], axis=0) * gain + bias
        return take_columns(rows.astype(BF), shards, shard)

    def kernel(shards_ref, own_ref, other_ref, gain_ref, bias_ref, out_ref, low_ref):
        low_ref[:half] = (own_ref[...] * gain_ref[...] + bias_ref[...]).astype(BF)
        low_ref[half:] = (other_ref[...] * gain_ref[...] + bias_ref[...]).astype(BF)
        ordered_columns(low_ref, out_ref, shards_ref, count, shard)

    return pl.pallas_call(
        kernel,
        out_shape=jax.ShapeDtypeStruct((2 * half, width), BF),
        in_specs=[pl.BlockSpec(memory_space=pltpu.SMEM)] + [pl.BlockSpec()] * 4,
        scratch_shapes=[pltpu.VMEM((2 * half, width), BF)],
        cost_estimate=pl.CostEstimate(
            flops=4 * half * width, bytes_accessed=12 * half * width, transcendentals=0
        ),
        compiler_params=vmem_limit(16 * half * width),
        name="norm_rows",
    )(shards, own, other, gain[None], bias[None])


def merge_rows(own, other, change, shards):
    half, width = own.shape
    count = shards.shape[0]
    shard = width // count
    if shard % 128:
        total = other + change
        low = jnp.concatenate([own, total], axis=0).astype(BF)
        return total, low, take_columns(low, shards, shard)

    def kernel(shards_ref, own_ref, other_ref, change_ref, other_out, low_out, ordered_out):
        low_out[:half] = own_ref[...].astype(BF)
        total = other_ref[...] + change_ref[...]
        other_out[...] = total
        low_out[half:] = total.astype(BF)
        ordered_columns(low_out, ordered_out, shards_ref, count, shard)

    return pl.pallas_call(
        kernel,
        out_shape=(
            jax.ShapeDtypeStruct((half, width), F32),
            jax.ShapeDtypeStruct((2 * half, width), BF),
            jax.ShapeDtypeStruct((2 * half, width), BF),
        ),
        in_specs=[pl.BlockSpec(memory_space=pltpu.SMEM)] + [pl.BlockSpec()] * 3,
        cost_estimate=LONG,
        compiler_params=vmem_limit(26 * half * width),
        name="merge_rows",
    )(shards, own, other, change)


def norm_back(mine, got, unit, inverse, gain, grad):
    half, width = mine.shape

    def kernel(mine_ref, got_ref, unit_ref, inverse_ref, gain_ref, grad_ref, change_out, grad_out, sums_out):
        pull = mine_ref[...] + got_ref[...]
        unit_rows = unit_ref[...]
        scaled = pull * gain_ref[...]
        first = jnp.mean(scaled, axis=-1, keepdims=True)
        second = jnp.mean(scaled * unit_rows, axis=-1, keepdims=True)
        change = inverse_ref[:, :1] * (scaled - first - unit_rows * second)
        change_out[...] = change
        total = grad_ref[...] + change
        grad_out[...] = total
        sums_out[0:1] = jnp.sum(pull * unit_rows, axis=0, keepdims=True)
        sums_out[1:2] = jnp.sum(pull, axis=0, keepdims=True)
        sums_out[2:3] = jnp.sum(total, axis=0, keepdims=True)

    rows = jax.ShapeDtypeStruct((half, width), F32)
    return pl.pallas_call(
        kernel,
        out_shape=(rows, rows, jax.ShapeDtypeStruct((3, width), F32)),
        cost_estimate=LONG,
        compiler_params=vmem_limit(30 * half * width),
        name="norm_back",
    )(mine, got, unit, inverse, gain[None], grad)


def product_rows(pairs, scale, start, first, second, got=None):
    widths = [right.shape[1] for _, right in pairs]
    total = sum(widths)
    has_got = got is not None
    count = first + second

    def kernel(scale_ref, *refs):
        ins = refs[: 2 * len(pairs)]
        outs = refs[2 * len(pairs) + has_got :]
        step = pl.program_id(0)

        def fill(out_ref):
            column = 0
            for i, width in enumerate(widths):
                block = (
                    lax.dot_general(
                        ins[2 * i][...],
                        ins[2 * i + 1][...],
                        (((0,), (0,)), ((), ())),
                        preferred_element_type=F32,
                    )
                    * scale_ref[0:1, 0:1]
                )
                if has_got:
                    block = block + refs[2 * len(pairs)][:, column : column + width]
                out_ref[:, column : column + width] = block
                column += width

        if second:
            pl.when(step < first)(lambda: fill(outs[0]))
            pl.when(step >= first)(lambda: fill(outs[1]))
        else:
            fill(outs[0])

    in_specs = [pl.BlockSpec(scale.shape, lambda j: (0, 0))]
    operands = [scale]
    traffic = 0
    for left, right in pairs:
        rows = left.shape[0]
        in_specs.append(pl.BlockSpec((rows, 128), lambda j: (0, start + j)))
        in_specs.append(pl.BlockSpec(right.shape, lambda j: (0, 0)))
        operands += [left, right]
        traffic += 2 * 2 * rows * (128 + right.shape[1])
    if has_got:
        in_specs.append(pl.BlockSpec((128, total), lambda j: (j, 0)))
        operands.append(got)
    out_shape = [jax.ShapeDtypeStruct((first * 128, total), F32)]
    out_specs = [pl.BlockSpec((128, total), lambda j: (jnp.minimum(j, first - 1), 0))]
    if second:
        out_shape.append(jax.ShapeDtypeStruct((second * 128, total), F32))
        out_specs.append(pl.BlockSpec((128, total), lambda j: (jnp.maximum(j - first, 0), 0)))
    return pl.pallas_call(
        kernel,
        out_shape=out_shape,
        grid=(count,),
        in_specs=in_specs,
        out_specs=out_specs,
        cost_estimate=LONG,
        compiler_params=vmem_limit(traffic + 2 * 4 * 128 * total * 3),
        name="product_rows",
    )(*operands)


def add_split(keep, got):
    rows, width = keep.shape
    half = rows // 2
    size = min(64, half)
    count = half // size

    def kernel(keep_ref, got_ref, first_out, second_out):
        total = keep_ref[...] + got_ref[...]

        @pl.when(pl.program_id(0) < count)
        def _():
            first_out[...] = total

        @pl.when(pl.program_id(0) >= count)
        def _():
            second_out[...] = total

    block = (size, width)
    return pl.pallas_call(
        kernel,
        out_shape=[jax.ShapeDtypeStruct((half, width), F32)] * 2,
        grid=(2 * count,),
        in_specs=[pl.BlockSpec(block, lambda j: (j, 0))] * 2,
        out_specs=[
            pl.BlockSpec(block, lambda j: (jnp.minimum(j, count - 1), 0)),
            pl.BlockSpec(block, lambda j: (jnp.maximum(j - count, 0), 0)),
        ],
        cost_estimate=LONG,
        compiler_params=vmem_limit(32 * size * width),
        name="add_split",
    )(keep, got)


def attend_forward(unit_own, unit_other, gain, bias, weights, biases, out_weight):
    half, model_width = unit_own.shape
    rows = 2 * half
    local_width = weights.shape[2]
    head_count = local_width // HEAD_DIM

    def kernel(own_ref, other_ref, gain_ref, bias_ref, weight_ref, biases_ref, out_weight_ref,
               qkv_out, mixed_out, total_out, own_out, send_out, normed_ref):
        normed_ref[:half] = (own_ref[...] * gain_ref[...] + bias_ref[...]).astype(BF)
        normed_ref[half:] = (other_ref[...] * gain_ref[...] + bias_ref[...]).astype(BF)
        normed = normed_ref[...]
        qkv_out[:, :local_width] = (matmul(normed, weight_ref[0]) + biases_ref[0:1]).astype(BF)
        qkv_out[:, local_width : 2 * local_width] = matmul(normed, weight_ref[1]).astype(BF)
        qkv_out[:, 2 * local_width :] = (matmul(normed, weight_ref[2]) + biases_ref[1:2]).astype(BF)
        for head in range(head_count):
            one = slice(head * HEAD_DIM, (head + 1) * HEAD_DIM)
            query = qkv_out[:, one]
            key = qkv_out[:, local_width + head * HEAD_DIM : local_width + (head + 1) * HEAD_DIM]
            value = qkv_out[:, 2 * local_width + head * HEAD_DIM : 2 * local_width + (head + 1) * HEAD_DIM]
            scores = matmul_nt(query, key) / ROOT_DIM
            top = jnp.max(scores, axis=-1, keepdims=True)
            exponent = jnp.exp(scores - top)
            row_sum = jnp.sum(exponent, axis=-1, keepdims=True)
            attend = (exponent / row_sum).astype(BF)
            mixed_out[:, one] = matmul(attend, value).astype(BF)
            total_out[:, head : head + 1] = top + jnp.log(row_sum)
        send_out[...] = matmul(mixed_out[half:], out_weight_ref[...])
        own_out[...] = matmul(mixed_out[:half], out_weight_ref[...])

    piece = jax.ShapeDtypeStruct((half, model_width), F32)
    return pl.pallas_call(
        kernel,
        out_shape=(
            jax.ShapeDtypeStruct((rows, 3 * local_width), BF),
            jax.ShapeDtypeStruct((rows, local_width), BF),
            jax.ShapeDtypeStruct((rows, 128), F32),
            piece,
            piece,
        ),
        scratch_shapes=[pltpu.VMEM((rows, model_width), BF)],
        cost_estimate=pl.CostEstimate(
            flops=2 * rows * local_width * (4 * model_width + 2 * rows),
            bytes_accessed=8 * rows * model_width + 8 * local_width * model_width,
            transcendentals=rows * rows * head_count,
        ),
        compiler_params=vmem_limit(22 * rows * model_width),
        name="attend_forward",
    )(unit_own, unit_other, gain[None], bias[None], weights, biases, out_weight)


def attend_back(low, qkv, totals, weights, out_weight):
    rows, model_width = low.shape
    half = rows // 2
    local_width = weights.shape[2]
    head_count = local_width // HEAD_DIM

    def kernel(low_ref, qkv_ref, total_ref, weight_ref, out_weight_ref,
               grads_out, sums_out, own_out, send_out, mix_ref):
        mix_ref[...] = matmul_nt(low_ref[...], out_weight_ref[...]).astype(BF)
        for head in range(head_count):
            one = slice(head * HEAD_DIM, (head + 1) * HEAD_DIM)
            two = slice(local_width + head * HEAD_DIM, local_width + (head + 1) * HEAD_DIM)
            three = slice(2 * local_width + head * HEAD_DIM, 2 * local_width + (head + 1) * HEAD_DIM)
            query, key, value = qkv_ref[:, one], qkv_ref[:, two], qkv_ref[:, three]
            mix = mix_ref[:, one]
            attend = jnp.exp(matmul_nt(query, key) / ROOT_DIM - total_ref[:, head : head + 1])
            grad_attend = matmul_nt(mix, value)
            grad_value = matmul_tn(attend.astype(BF), mix)
            weighted = attend * grad_attend
            grad_scores = weighted - attend * jnp.sum(weighted, axis=-1, keepdims=True)
            grad_low = grad_scores.astype(BF)
            grad_query = matmul(grad_low, key) / ROOT_DIM
            grad_key = matmul_tn(grad_low, query) / ROOT_DIM
            grads_out[:, one] = grad_query.astype(BF)
            grads_out[:, two] = grad_key.astype(BF)
            grads_out[:, three] = grad_value.astype(BF)
            sums_out[0:1, one] = jnp.sum(grad_query, axis=0, keepdims=True)
            sums_out[1:2, one] = jnp.sum(grad_value, axis=0, keepdims=True)

        def pull(part):
            total = matmul_nt(grads_out[part, :local_width], weight_ref[0])
            total = total + matmul_nt(grads_out[part, local_width : 2 * local_width], weight_ref[1])
            return total + matmul_nt(grads_out[part, 2 * local_width :], weight_ref[2])

        send_out[...] = pull(slice(half, rows))
        own_out[...] = pull(slice(0, half))

    piece = jax.ShapeDtypeStruct((half, model_width), F32)
    return pl.pallas_call(
        kernel,
        out_shape=(
            jax.ShapeDtypeStruct((rows, 3 * local_width), BF),
            jax.ShapeDtypeStruct((2, local_width), F32),
            piece,
            piece,
        ),
        scratch_shapes=[pltpu.VMEM((rows, local_width), BF)],
        cost_estimate=LONG,
        compiler_params=vmem_limit(24 * rows * model_width),
        name="attend_back",
    )(low, qkv, totals, weights, out_weight)


def finish_layers(kind, pieces, layer_count, shard, local_width):
    width = pieces[0].shape[1]
    shapes = {
        "down": [(layer_count, width, shard)],
        "up": [(layer_count, shard, width)],
        "att": [
            (layer_count, local_width, shard),
            (layer_count, 3, shard, local_width),
        ],
    }[kind]

    def store(values, outs):
        for layer, value in enumerate(values):
            if kind == "down":
                outs[0][layer] = value.T
            elif kind == "up":
                outs[0][layer] = value
            else:
                outs[0][layer] = value[:, :local_width].T
                for which in range(3):
                    begin = (1 + which) * local_width
                    outs[1][layer, which] = value[:, begin : begin + local_width]

    if shard % 128:
        values = [pieces[2 * i] + pieces[2 * i + 1] for i in range(layer_count)]
        if kind == "down":
            return [jnp.stack([value.T for value in values])]
        if kind == "up":
            return [jnp.stack(values)]
        rest = [
            value[:, local_width:].reshape(shard, 3, local_width).transpose(1, 0, 2)
            for value in values
        ]
        return [jnp.stack([value[:, :local_width].T for value in values]), jnp.stack(rest)]

    def kernel(*refs):
        ins = refs[: 2 * layer_count]
        store(
            [ins[2 * i][...] + ins[2 * i + 1][...] for i in range(layer_count)],
            refs[2 * layer_count :],
        )

    return pl.pallas_call(
        kernel,
        out_shape=[jax.ShapeDtypeStruct(shape, F32) for shape in shapes],
        cost_estimate=pl.CostEstimate(
            flops=layer_count * shard * width,
            bytes_accessed=12 * layer_count * shard * width,
            transcendentals=0,
        ),
        compiler_params=vmem_limit(20 * layer_count * shard * width),
        name="finish_layers",
    )(*pieces)


class Links:
    def __init__(self, dp, mp):
        self.dp, self.mp = dp, mp
        self.dp_index = lax.axis_index("dp")
        self.mp_index = lax.axis_index("mp")

    def dp_bit(self, bit):
        return (self.dp_index >> bit) & 1

    def mp_bit(self, bit):
        return (self.mp_index >> bit) & 1

    def ordered_sum(self, clock, own, send):
        send = clock.one(send)
        got = exchange(send, "mp", self.mp, 0)
        clock.hold()
        mine = clock.one(own() + clock.one(got))
        last = bit_count(self.mp) - 1
        for bit in range(1, last):
            mine = clock.one(mine + exchange(mine, "mp", self.mp, bit))
        return mine, exchange(mine, "mp", self.mp, last)

    def begin_sum(self, own, send):
        mine = own + exchange(send, "mp", self.mp, 0)
        last = bit_count(self.mp) - 1
        for bit in range(1, last):
            mine = mine + exchange(mine, "mp", self.mp, bit)
        return mine, exchange(mine, "mp", self.mp, last)

    def begin_product(self, left, right, product=matmul):
        half = left.shape[0] // 2
        send = product(left[half:], right)
        return self.begin_sum(product(left[:half], right), send)

    def sum_rows(self, partial):
        half = partial.shape[0] // 2
        mine, got = self.begin_sum(partial[:half], partial[half:])
        return mine + got

    def other_rows(self, own):
        return exchange(own, "mp", self.mp, 0)

    def split_rows(self, tensor):
        half = tensor.shape[0] // 2
        core = self.mp_bit(0)
        own = lax.dynamic_slice_in_dim(tensor, core * half, half, 0)
        other = lax.dynamic_slice_in_dim(tensor, (1 - core) * half, half, 0)
        return own, other

    def global_rows(self, own, other):
        core = self.mp_bit(0)
        return jnp.concatenate(
            [jnp.where(core == 0, own, other), jnp.where(core == 0, other, own)], axis=0
        )

    def order(self, bits):
        masks = []
        for place in range(self.dp):
            mask = 0
            for i, bit in enumerate(bits):
                if not (place >> (len(bits) - 1 - i)) & 1:
                    mask |= 1 << bit
            masks.append(mask)
        return jnp.array(masks, jnp.int32) ^ self.dp_index


class Merge:
    def __init__(self, links, pairs, bits):
        self.links, self.pairs, self.bits = links, pairs, bits
        self.blocks = pairs[0][0].shape[1] // 128
        self.step = 0

    def advance(self, clock):
        got, pairs = None, self.pairs
        if self.step:
            got = clock.one(self.got)
        else:
            pairs = [(clock.one(pairs[0][0]), pairs[0][1])] + pairs[1:]
        if self.step == 0:
            send = product_rows(pairs, clock.cell, 0, self.blocks // 2, 0)[0]
        elif self.step == 1:
            send, self.keep = product_rows(
                pairs, clock.cell, self.blocks // 2, self.blocks // 4, self.blocks // 4, got
            )
        else:
            send, self.keep = add_split(self.keep, got)
        send = clock.one(send)
        self.got = exchange(send, "dp", self.links.dp, self.bits[self.step])
        self.step += 1

    @property
    def open(self):
        return self.step < len(self.bits)


class ShardMerge:
    def __init__(self, links, shards):
        self.links, self.shards = links, shards
        self.step = 0

    def split(self, total):
        pairs = total.reshape((total.shape[0] // 2, 2) + total.shape[1:])
        own = self.links.dp_bit(self.step)
        self.keep = pick(pairs, own, 1)
        return pick(pairs, 1 - own, 1)

    def advance(self, clock):
        total = self.shards
        if self.step:
            total = self.keep + clock.one(self.got)
        send = clock.one(self.split(clock.one(total)))
        self.got = exchange(send, "dp", self.links.dp, self.step)
        clock.hold()
        self.step += 1

    @property
    def open(self):
        return self.step < bit_count(self.links.dp)


def norm_parts(rows):
    row_mean = jnp.mean(rows, axis=-1, keepdims=True)
    centred = rows - row_mean
    spread = jnp.mean(centred * centred, axis=-1, keepdims=True)
    inverse = lax.rsqrt(spread + 1e-05)
    return centred * inverse, jnp.broadcast_to(inverse, (rows.shape[0], 128))


def make_per_device(dp, mp):
    def per_device(
        pixels,
        dataset_id,
        variable_mask,
        lead_hours,
        token_counts,
        dataset_weight,
        patch_weight,
        variable_embed,
        position_embed,
        pool_query,
        pool_query_weight,
        pool_key_weight,
        pool_value_weight,
        pool_value_bias,
        pool_output_weight,
        pool_output_bias,
        lead_weight,
        lead_bias,
        norm_gain,
        norm_bias,
        attention_weight,
        attention_bias,
        output_weight,
        output_bias,
        up_weight,
        up_bias,
        down_weight,
        down_bias,
        cotangent,
    ):
        links = Links(dp, mp)
        var_count, pix_count, row_count = pixels.shape[1:]
        flat_count = var_count * pix_count
        model_width = patch_weight.shape[2]
        local_width = pool_query_weight.shape[1]
        head_count = local_width // HEAD_DIM
        layer_count = attention_weight.shape[0]
        shard = model_width // dp

        def heads_first(tensor):
            return tensor.reshape(row_count, head_count, HEAD_DIM).transpose(1, 0, 2)

        def heads_last(tensor):
            return tensor.transpose(1, 0, 2).reshape(row_count, local_width)

        dataset_pick = jnp.arange(variable_mask.shape[0], dtype=jnp.int32) == dataset_id[0]
        mask_row = jnp.sum(jnp.where(dataset_pick[:, None], variable_mask, 0), axis=0)
        item_weight = jnp.sum(jnp.where(dataset_pick, dataset_weight, 0)).astype(F32)
        own_count = token_counts[0].astype(F32)
        lead_scale = lead_hours[0].astype(F32) / 24.0

        pix_rows = pixels[0].reshape(flat_count, row_count).T
        pix_own, pix_other = links.split_rows(pix_rows)
        pix_low = jnp.concatenate([pix_own, pix_other], axis=0).astype(BF)
        pix_value = pix_low.astype(F32)
        embed_high, embed_rest = two_part(variable_embed)
        embed_all = jnp.concatenate(
            [patch_weight.reshape(flat_count, model_width), embed_high, embed_rest], axis=0
        )
        embed_left = take_columns(embed_all, links.order(list(range(bit_count(dp)))), shard)
        query_low = pool_query.astype(BF)
        query_vec = matmul(query_low[None, :], pool_query_weight)[0].astype(BF)
        head_of = jnp.arange(local_width, dtype=jnp.int32) // HEAD_DIM
        head_pick = head_of[:, None] == jnp.arange(head_count, dtype=jnp.int32)[None, :]
        query_heads = jnp.where(head_pick, query_vec[:, None], 0).astype(BF)
        key_query = matmul(pool_key_weight, query_heads) / ROOT_DIM
        key_high, key_rest = two_part(key_query)
        projected = matmul(
            embed_all, jnp.concatenate([pool_value_weight, key_high, key_rest], axis=1)
        )
        tail = projected[flat_count : flat_count + var_count] + projected[flat_count + var_count :]
        score_flat = (
            projected[:flat_count, local_width : local_width + head_count]
            + projected[:flat_count, local_width + head_count :]
        )
        score_var = tail[:, local_width : local_width + head_count] + tail[:, local_width + head_count :]
        value_flat = projected[:flat_count, :local_width].astype(BF)
        value_var = (tail[:, :local_width] + pool_value_bias).astype(BF)
        value_flat = value_flat.reshape(flat_count, head_count, HEAD_DIM).transpose(1, 0, 2)
        value_var = value_var.reshape(var_count, head_count, HEAD_DIM).transpose(1, 0, 2)

        var_of = jnp.arange(flat_count, dtype=jnp.int32) // pix_count
        segment = (
            var_of[None, :] == jnp.arange(var_count, dtype=jnp.int32)[:, None]
        )
        segment_low = segment.astype(BF)
        score_block = jnp.where(segment.T[None], score_flat.T[:, :, None], 0.0)
        block_high, block_rest = two_part(score_block)
        block_both = jnp.concatenate([block_high, block_rest], axis=2)
        pool_scores = jnp.einsum(
            "rk,hkv->hrv", pix_low, block_both, preferred_element_type=F32
        )
        pool_scores = (
            pool_scores[:, :, :var_count] + pool_scores[:, :, var_count:] + score_var.T[:, None, :]
        )
        pool_scores = jnp.where(mask_row[None, None, :] > 0, pool_scores, -1000000000.0)
        pool_top = jnp.max(pool_scores, axis=-1, keepdims=True)
        pool_exp = jnp.exp(pool_scores - pool_top)
        pool_probs = pool_exp / jnp.sum(pool_exp, axis=-1, keepdims=True)
        probs_low = pool_probs.astype(BF)
        probs_wide = jnp.einsum("hrv,vk->hrk", probs_low, segment_low, preferred_element_type=F32)
        mixed_pixels = (probs_wide * pix_value[None]).astype(BF)
        pooled = jnp.einsum(
            "hrk,hkd->hrd", mixed_pixels, value_flat, preferred_element_type=F32
        ) + jnp.einsum("hrv,hvd->hrd", probs_low, value_var, preferred_element_type=F32)
        pooled = heads_last(pooled).astype(BF)

        mine, got = links.begin_product(pooled, pool_output_weight)
        count_total = after(jnp.full((8, 128), own_count, F32), mine)
        for bit in range(bit_count(dp)):
            count_total = count_total + exchange(count_total, "dp", dp, bit)
        scale_cell = item_weight * own_count / count_total
        item_scale = scale_cell[0, 0]
        position_own = links.split_rows(position_embed)[0]
        offset_rows = pool_output_bias + position_own + lead_scale * lead_weight + lead_bias
        mine, scale_cell = lax.optimization_barrier((mine, scale_cell))
        hidden = mine + got + offset_rows

        bits = list(range(bit_count(dp)))
        bits_late = bits[1:] + bits[:1]
        shards, shards_late = links.order(bits), links.order(bits_late)
        top = layer_count - 1
        kept = []
        for layer in range(layer_count):
            unit_one, inverse_one = norm_parts(hidden)
            unit_other = links.other_rows(unit_one)
            qkv, mixed, totals, part_own, part_send = attend_forward(
                unit_one,
                unit_other,
                norm_gain[layer, 0],
                norm_bias[layer, 0],
                attention_weight[layer],
                attention_bias[layer],
                output_weight[layer],
            )
            mine, got = links.begin_sum(part_own, part_send)
            normed = norm_rows(
                after(unit_one, mine), unit_other, norm_gain[layer, 0], norm_bias[layer, 0], shards
            )
            mine, normed = lax.optimization_barrier((mine, normed))
            if layer == 0:
                grad_own, grad_other = links.split_rows(after(cotangent[0], mine))
                grad_other, down_low, down_left = merge_rows(
                    grad_own, grad_other, jnp.zeros_like(grad_other), shards_late
                )
                mine, down_low = lax.optimization_barrier((mine, down_low))
            hidden = hidden + (mine + got) + output_bias[layer]
            unit_two, inverse_two = norm_parts(hidden)
            unit_other = links.other_rows(unit_two)
            normed_two = jnp.concatenate([unit_two, unit_other], axis=0)
            normed_two = (normed_two * norm_gain[layer, 1] + norm_bias[layer, 1]).astype(BF)
            pre_act = matmul(normed_two, up_weight[layer]) + up_bias[layer]
            activation = gelu_exact(pre_act).astype(BF)
            marker = activation
            if layer < top:
                mine, got = links.begin_product(activation, down_weight[layer])
                marker = mine
            normed_two = norm_rows(
                after(unit_two, marker), unit_other, norm_gain[layer, 1], norm_bias[layer, 1], shards
            )
            if layer < top:
                if layer == 0:
                    top_grad = matmul_nt(after(down_low, mine), down_weight[top])
                    mine, top_grad = lax.optimization_barrier((mine, top_grad))
                mine, normed_two = lax.optimization_barrier((mine, normed_two))
                hidden = hidden + (mine + got) + down_bias[layer]
            kept.append(
                (
                    unit_one,
                    inverse_one,
                    normed,
                    qkv,
                    totals,
                    mixed,
                    unit_two,
                    inverse_two,
                    normed_two,
                    pre_act,
                    activation,
                )
            )

        activation_top = kept[top][-1]
        row_sums = {}
        local_sums = {}
        merges = {}
        row_sums["down_bias", top] = jnp.sum(grad_own, axis=0)

        clock = Clock(scale_cell)

        def advance(spot):
            for name in PLAN.get(spot, ()):
                if name in merges and merges[name].open:
                    merges[name].advance(clock)

        for layer in reversed(range(layer_count)):
            depth = top - layer
            (
                unit_one,
                inverse_one,
                normed,
                qkv,
                totals,
                mixed,
                unit_two,
                inverse_two,
                normed_two,
                pre_act,
                activation,
            ) = kept[layer]
            merges["down", depth] = Merge(
                links, [(down_left, activation)], bits if depth else bits_late
            )
            grad_activation = top_grad if layer == top else matmul_nt(down_low, down_weight[layer])
            grad_pre = jax.vjp(gelu_exact, pre_act)[1](grad_activation)[0]
            local_sums["up_bias", layer] = jnp.sum(grad_pre, axis=0)
            pre_low = clock.one(grad_pre.astype(BF))
            merges["up", depth] = Merge(links, [(normed_two, pre_low)], bits)
            advance(("pre", depth))
            pre_low = clock.one(pre_low)
            half = row_count // 2
            mine, got = links.ordered_sum(
                clock,
                lambda: matmul_nt(pre_low[:half], up_weight[layer]),
                matmul_nt(pre_low[half:], up_weight[layer]),
            )
            if not PLAN.get(("wait_two", depth)):
                clock.hold()
            advance(("wait_two", depth))
            mine, got = clock.both(mine, got)
            change, grad_own, sums = norm_back(
                mine, got, unit_two, inverse_two, norm_gain[layer, 1], grad_own
            )
            change, sums = clock.both(change, sums)
            row_sums["gain", layer, 1] = sums[0]
            row_sums["bias", layer, 1] = sums[1]
            row_sums["out_bias", layer] = sums[2]
            other_change = links.other_rows(change)
            clock.hold()
            grad_other, out_low, out_left = merge_rows(
                grad_own, grad_other, clock.one(other_change), shards
            )
            out_low = clock.one(out_low)
            advance(("mid", depth))
            grads, qv_sums, part_own, part_send = attend_back(
                clock.one(out_low), qkv, totals, attention_weight[layer], output_weight[layer]
            )
            local_sums["qv", layer] = qv_sums
            mine, got = links.ordered_sum(clock, lambda: part_own, part_send)
            if not PLAN.get(("wait_one", depth)):
                clock.hold()
            merges["att", depth] = Merge(links, [(out_left, mixed), (normed, grads)], bits)
            advance(("wait_one", depth))
            mine, got = clock.both(mine, got)
            change, grad_own, sums = norm_back(
                mine, got, unit_one, inverse_one, norm_gain[layer, 0], grad_own
            )
            change, sums = clock.both(change, sums)
            row_sums["gain", layer, 0] = sums[0]
            row_sums["bias", layer, 0] = sums[1]
            if layer:
                row_sums["down_bias", layer - 1] = sums[2]
            other_change = links.other_rows(change)
            clock.hold()
            grad_other, down_low, down_left = merge_rows(
                grad_own, grad_other, clock.one(other_change), shards
            )
            down_low = clock.one(down_low)
            advance(("end", depth))
            down_low = clock.one(down_low)

        activation_top = clock.one(activation_top)
        half = row_count // 2
        last_mine, last_got = links.ordered_sum(
            clock,
            lambda: matmul(activation_top[:half], down_weight[top]),
            matmul(activation_top[half:], down_weight[top]),
        )
        clock.hold()
        row_sums["column"] = sums[2]
        row_sums["lead"] = lead_scale * sums[2]
        pool_grad_low = down_low
        grad_pooled = heads_first(matmul_nt(pool_grad_low, pool_output_weight).astype(BF))
        pull_flat = jnp.einsum("hrd,hkd->hrk", grad_pooled, value_flat, preferred_element_type=F32)
        pull_high, pull_rest = two_part(pull_flat * pix_value[None])
        grad_probs = (
            jnp.einsum("hrk,vk->hrv", pull_high, segment_low, preferred_element_type=F32)
            + jnp.einsum("hrk,vk->hrv", pull_rest, segment_low, preferred_element_type=F32)
            + jnp.einsum("hrd,hvd->hrv", grad_pooled, value_var, preferred_element_type=F32)
        )
        grad_pool_scores = pool_probs * (
            grad_probs - jnp.sum(pool_probs * grad_probs, axis=-1, keepdims=True)
        )
        grad_pool_scores = clock.one(grad_pool_scores)
        advance("scores")
        grad_pool_scores = clock.one(grad_pool_scores)
        score_high, score_rest = two_part(grad_pool_scores)
        pixel_part = jnp.einsum(
            "hrv,hkv->rk", score_high, block_high, preferred_element_type=F32
        ) + jnp.sum(probs_wide * pull_flat, axis=0)

        turned = jnp.einsum(
            "rk,hrv->hkv", pix_low, score_high, preferred_element_type=F32
        ) + jnp.einsum("rk,hrv->hkv", pix_low, score_rest, preferred_element_type=F32)
        key_flat = jnp.sum(jnp.where(segment.T[None], turned, 0.0), axis=2).T * item_scale
        key_var = jnp.sum(grad_pool_scores, axis=1).T * item_scale
        value_grad_flat = jnp.einsum(
            "hrk,hrd->khd", mixed_pixels, grad_pooled, preferred_element_type=F32
        ).reshape(flat_count, local_width)
        value_grad_var = jnp.einsum(
            "hrv,hrd->vhd", probs_low, grad_pooled, preferred_element_type=F32
        ).reshape(var_count, local_width)
        local_sums["pool_bias"] = jnp.sum(value_grad_var, axis=0)
        value_rows_grad = jnp.concatenate(
            [part.astype(BF) for part in (value_grad_flat, value_grad_var, value_grad_var)], axis=0
        )
        merges["tail"] = Merge(
            links,
            [(down_left, pooled), (embed_left, value_rows_grad)],
            bits,
        )
        advance("values")
        value_grad_flat = (clock.one(value_grad_flat) * item_scale).astype(BF)
        value_grad_var = (value_grad_var * item_scale).astype(BF)

        key_grad = jnp.concatenate([key_flat, key_var, key_var], axis=0)
        key_grad_high, key_grad_rest = two_part(key_grad)
        summed_key = matmul_tn(
            embed_all, jnp.concatenate([key_grad_high, key_grad_rest], axis=1)
        )
        summed_key = summed_key[:, :head_count] + summed_key[:, head_count:]
        summed_high, summed_rest = two_part(summed_key)
        query_grad = matmul_tn(
            jnp.concatenate([summed_high, summed_rest], axis=1), pool_key_weight
        )
        query_grad = query_grad[:head_count] + query_grad[head_count:]
        query_grad = jnp.sum(jnp.where(head_pick.T, query_grad, 0.0), axis=0) / ROOT_DIM
        query_part = jnp.sum(pool_query_weight.astype(F32) * query_grad[None, :], axis=1)

        flat_all = flat_count + var_count
        grad_rows = jnp.concatenate([value_grad_flat, value_grad_var], axis=0)
        key_rows_high, key_rows_rest = two_part(jnp.concatenate([key_flat, key_var], axis=0))
        right_side = jnp.concatenate([grad_rows, key_rows_high, key_rows_rest, key_rows_high], axis=1)
        left_side = jnp.concatenate([pool_value_weight, key_high, key_high, key_rest], axis=1)
        sub = shard // mp
        sides = left_side.reshape(dp, mp // 2, 2, sub, left_side.shape[1])
        parts = query_part.reshape(dp, mp // 2, 2, sub)
        core = links.mp_bit(0)

        def embed_side(which):
            side = pick(sides, which, 2).transpose(1, 0, 2, 3)
            part = pick(parts, which, 2).transpose(1, 0, 2)
            block = matmul_nt(side.reshape(model_width // 2, left_side.shape[1]), right_side)
            block = jnp.concatenate([block, part.reshape(model_width // 2, 1)], axis=1)
            return block.reshape(mp // 2, dp, sub, flat_all + 1)

        embed_grad = embed_side(core) + exchange(embed_side(1 - core), "mp", mp, 0)
        for bit in range(1, bit_count(mp)):
            own = links.mp_bit(bit)
            count = embed_grad.shape[0] // 2
            pairs = embed_grad.reshape((count, 2) + embed_grad.shape[1:])
            embed_grad = pick(pairs, own, 1) + exchange(pick(pairs, 1 - own, 1), "mp", mp, bit)
        merges["embed"] = ShardMerge(links, embed_grad[0])
        position = (grad_own * item_scale).reshape(row_count // 2, dp, shard).transpose(1, 0, 2)
        merges["position"] = ShardMerge(links, position)
        pixel_own = links.sum_rows(pixel_part)
        pixel_grad = links.global_rows(pixel_own, links.other_rows(pixel_own))
        pixel_grad = pixel_grad.T.reshape(1, var_count, pix_count, row_count)

        names = []
        for layer in range(layer_count):
            names += [("gain", layer, 0), ("gain", layer, 1), ("bias", layer, 0), ("bias", layer, 1)]
        for layer in range(layer_count):
            names += [("out_bias", layer), ("down_bias", layer)]
        names += ["column", "lead"]
        own_sums = jnp.stack([row_sums[name] for name in names]) * item_scale
        full_sums = own_sums + exchange(own_sums, "mp", mp, 0)
        local = jnp.stack([local_sums["up_bias", layer] for layer in range(layer_count)]) * item_scale
        thin = [local_sums["qv", layer] for layer in range(layer_count)]
        thin = jnp.concatenate(thin + [local_sums["pool_bias"][None]], axis=0) * item_scale
        packed = jnp.concatenate(
            [
                full_sums.reshape(len(names), dp, shard).transpose(1, 0, 2).reshape(dp, -1),
                summed_key.reshape(dp, -1),
                local.reshape(layer_count, dp, -1).transpose(1, 0, 2).reshape(dp, -1),
                thin.reshape(2 * layer_count + 1, dp, -1).transpose(1, 0, 2).reshape(dp, -1),
                jnp.broadcast_to(query_grad[None, :], (dp, local_width)),
            ],
            axis=1,
        )
        merges["vectors"] = ShardMerge(links, packed[:, None, :])
        for name in DRAIN:
            if merges[name].open:
                merges[name].advance(clock)
        for merge in merges.values():
            while merge.open:
                merge.advance(clock)
        hidden = hidden + (last_mine + last_got) + down_bias[top]
        layer_out = links.global_rows(hidden, links.other_rows(hidden))
        finished = {
            kind: finish_layers(
                kind,
                [
                    part
                    for layer in range(layer_count)
                    for part in (merges[kind, top - layer].keep, merges[kind, top - layer].got)
                ],
                layer_count,
                shard,
                local_width,
            )
            for kind in ("down", "up", "att")
        }
        tail_total = merges["tail"].keep + merges["tail"].got
        embed_grad = (merges["embed"].keep + merges["embed"].got)[0]
        position = (merges["position"].keep + merges["position"].got)[0]
        position = links.global_rows(position, links.other_rows(position))
        packed, _ = lax.optimization_barrier(
            ((merges["vectors"].keep + merges["vectors"].got)[0, 0], clock.cell)
        )
        offset = 0

        def take(*shape):
            nonlocal offset
            size = math.prod(shape)
            piece = packed[offset : offset + size].reshape(shape)
            offset += size
            return piece

        gains = take(layer_count, 2, shard)
        biases = []
        gain_list = []
        offset = 0
        norm_all = take(layer_count, 2, 2, shard)
        gain_list = norm_all[:, 0]
        biases = norm_all[:, 1]
        dense_bias = take(layer_count, 2, shard)
        column_total = take(shard)
        lead_total = take(shard)
        key_shard = take(shard, head_count)
        up_bias_total = take(layer_count, local.shape[1] // dp)
        thin_total = take(2 * layer_count + 1, local_width // dp)
        query_total = take(local_width)

        query_rows = lax.dynamic_slice_in_dim(query_low, links.dp_index * shard, shard, 0)
        query_weight_grad = query_rows.astype(F32)[:, None] * query_total[None, :]
        key_weight_grad = (
            jnp.repeat(key_shard, HEAD_DIM, axis=1) * query_vec.astype(F32)[None, :] / ROOT_DIM
        )
        embed_turned = embed_grad.T
        return (
            layer_out[None],
            pixel_grad,
            embed_turned[:flat_count].reshape(var_count, pix_count, sub),
            embed_turned[flat_count:flat_all],
            position,
            embed_turned[flat_all],
            query_weight_grad,
            key_weight_grad,
            tail_total[:, local_width:],
            thin_total[-1],
            tail_total[:, :local_width].T,
            column_total,
            lead_total,
            column_total,
            gain_list,
            biases,
            finished["att"][1],
            thin_total[:-1].reshape(layer_count, 2, local_width // dp),
            finished["att"][0],
            dense_bias[:, 0],
            finished["up"][0],
            up_bias_total,
            finished["down"][0],
            dense_bias[:, 1],
        )

    return per_device


def solution(mesh):
    return jax.shard_map(
        make_per_device(mesh.shape["dp"], mesh.shape["mp"]),
        mesh=mesh,
        in_specs=(
            P("dp", None, None, None),
            P("dp"),
            P(),
            P("dp"),
            P("dp"),
            P(),
            P(),
            P(),
            P(),
            P(),
            P(None, "mp"),
            P(None, "mp"),
            P(None, "mp"),
            P("mp"),
            P("mp", None),
            P(),
            P(),
            P(),
            P(),
            P(),
            P(None, None, None, "mp"),
            P(None, None, "mp"),
            P(None, "mp", None),
            P(),
            P(None, None, "mp"),
            P(None, "mp"),
            P(None, "mp", None),
            P(),
            P("dp", None, None),
        ),
        out_specs=(
            P("dp", None, None),
            P("dp", None, None, None),
            P(None, None, ("dp", "mp")),
            P(None, ("dp", "mp")),
            P(None, "dp"),
            P(("dp", "mp")),
            P("dp", "mp"),
            P("dp", "mp"),
            P("dp", "mp"),
            P(("mp", "dp")),
            P("mp", "dp"),
            P("dp"),
            P("dp"),
            P("dp"),
            P(None, None, "dp"),
            P(None, None, "dp"),
            P(None, None, "dp", "mp"),
            P(None, None, ("mp", "dp")),
            P(None, "mp", "dp"),
            P(None, "dp"),
            P(None, "dp", "mp"),
            P(None, ("mp", "dp")),
            P(None, "mp", "dp"),
            P(None, "dp"),
        ),
        check_vma=False,
    )
```

```python
import math

import jax
import jax.numpy as jnp
from jax import lax
from jax.experimental import pallas as pl
from jax.experimental.pallas import tpu as pltpu
from jax.sharding import PartitionSpec as P

HEAD_DIM = 64
PLAN = {
    ("pre", 0): [("down", 0), ("up", 0)],
    ("wait_one", 0): [("att", 0), ("down", 0), ("up", 0)],
    ("wait_two", 1): [("down", 1)],
    ("mid", 1): [("up", 0), ("att", 0)],
    ("wait_one", 1): [("up", 1), ("down", 0), ("att", 0)],
    ("end", 1): [("up", 0), ("down", 1), ("down", 0), ("att", 1)],
    "values": [("up", 1), ("att", 0), ("down", 1), "tail"],
    "vectors": [("att", 1), ("down", 1), ("up", 1)],
    "small": ["small"],
    "output": ["tail"],
    "pixels": [("att", 1), ("up", 1)],
    "rows": ["tail", "small"],
}
DRAIN = [("att", 1), "small", "tail", "small"]
ROOT_DIM = math.sqrt(HEAD_DIM)
BF = jnp.bfloat16
F32 = jnp.float32


def matmul(left, right):
    return jnp.dot(left, right, preferred_element_type=F32)


def matmul_tn(left, right):
    return lax.dot_general(left, right, (((0,), (0,)), ((), ())), preferred_element_type=F32)


def matmul_nt(left, right):
    return lax.dot_general(left, right, (((1,), (1,)), ((), ())), preferred_element_type=F32)


def two_part(tensor):
    high = tensor.astype(BF)
    return high, (tensor - high.astype(F32)).astype(BF)


def gelu_exact(pre_act):
    return jax.nn.gelu(pre_act, approximate=False)


def bit_count(size):
    bits = size.bit_length() - 1
    assert 1 << bits == size
    return bits


def exchange(tensor, axis, size, bit):
    return lax.ppermute(tensor, axis, [(i, i ^ (1 << bit)) for i in range(size)])


def pick(tensor, index, axis):
    return lax.dynamic_index_in_dim(tensor, index, axis, keepdims=False)


def after(value, *earlier):
    return lax.optimization_barrier((value,) + earlier)[0]


def vmem_limit(size):
    return pltpu.CompilerParams(vmem_limit_bytes=int(size * 1.25) + (2 << 20))


LONG = pl.CostEstimate(flops=10**12, bytes_accessed=8, transcendentals=0)


def step_cell(cell):
    def kernel(cell_ref, out_ref):
        out_ref[...] = cell_ref[...]

    return pl.pallas_call(
        kernel,
        out_shape=jax.ShapeDtypeStruct(cell.shape, F32),
        cost_estimate=LONG,
        compiler_params=vmem_limit(0),
        name="step_cell",
    )(cell)


class Clock:
    def __init__(self, cell):
        self.cell = cell

    def both(self, *values):
        *values, self.cell = lax.optimization_barrier((*values, self.cell))
        return values

    def one(self, value):
        return self.both(value)[0]

    def hold(self):
        self.cell = step_cell(self.cell)


def ordered_columns(source, target, shards_ref, count, shard):
    for place in range(count):
        column = pl.multiple_of(shards_ref[place] * shard, shard)
        target[:, place * shard : (place + 1) * shard] = source[:, pl.ds(column, shard)]


def take_columns(rows, shards, shard):
    pieces = rows.reshape(rows.shape[0], -1, shard)[:, shards]
    return pieces.reshape(rows.shape)


def norm_rows(own, other, gain, bias, shards):
    half, width = own.shape
    count = shards.shape[0]
    shard = width // count
    if shard % 128:
        rows = jnp.concatenate([own, other], axis=0) * gain + bias
        return take_columns(rows.astype(BF), shards, shard)

    def kernel(shards_ref, own_ref, other_ref, gain_ref, bias_ref, out_ref, low_ref):
        low_ref[:half] = (own_ref[...] * gain_ref[...] + bias_ref[...]).astype(BF)
        low_ref[half:] = (other_ref[...] * gain_ref[...] + bias_ref[...]).astype(BF)
        ordered_columns(low_ref, out_ref, shards_ref, count, shard)

    return pl.pallas_call(
        kernel,
        out_shape=jax.ShapeDtypeStruct((2 * half, width), BF),
        in_specs=[pl.BlockSpec(memory_space=pltpu.SMEM)] + [pl.BlockSpec()] * 4,
        scratch_shapes=[pltpu.VMEM((2 * half, width), BF)],
        cost_estimate=pl.CostEstimate(
            flops=4 * half * width, bytes_accessed=12 * half * width, transcendentals=0
        ),
        compiler_params=vmem_limit(16 * half * width),
        name="norm_rows",
    )(shards, own, other, gain[None], bias[None])


def merge_rows(own, other, change, shards):
    half, width = own.shape
    count = shards.shape[0]
    shard = width // count
    if shard % 128:
        total = other + change
        low = jnp.concatenate([own, total], axis=0).astype(BF)
        return total, low, take_columns(low, shards, shard)

    def kernel(shards_ref, own_ref, other_ref, change_ref, other_out, low_out, ordered_out):
        low_out[:half] = own_ref[...].astype(BF)
        total = other_ref[...] + change_ref[...]
        other_out[...] = total
        low_out[half:] = total.astype(BF)
        ordered_columns(low_out, ordered_out, shards_ref, count, shard)

    return pl.pallas_call(
        kernel,
        out_shape=(
            jax.ShapeDtypeStruct((half, width), F32),
            jax.ShapeDtypeStruct((2 * half, width), BF),
            jax.ShapeDtypeStruct((2 * half, width), BF),
        ),
        in_specs=[pl.BlockSpec(memory_space=pltpu.SMEM)] + [pl.BlockSpec()] * 3,
        cost_estimate=LONG,
        compiler_params=vmem_limit(26 * half * width),
        name="merge_rows",
    )(shards, own, other, change)


def norm_back(mine, got, unit, inverse, gain, grad):
    half, width = mine.shape

    def kernel(mine_ref, got_ref, unit_ref, inverse_ref, gain_ref, grad_ref, change_out, grad_out, sums_out):
        pull = mine_ref[...] + got_ref[...]
        unit_rows = unit_ref[...]
        scaled = pull * gain_ref[...]
        first = jnp.mean(scaled, axis=-1, keepdims=True)
        second = jnp.mean(scaled * unit_rows, axis=-1, keepdims=True)
        change = inverse_ref[:, :1] * (scaled - first - unit_rows * second)
        change_out[...] = change
        total = grad_ref[...] + change
        grad_out[...] = total
        sums_out[0:1] = jnp.sum(pull * unit_rows, axis=0, keepdims=True)
        sums_out[1:2] = jnp.sum(pull, axis=0, keepdims=True)
        sums_out[2:3] = jnp.sum(total, axis=0, keepdims=True)

    rows = jax.ShapeDtypeStruct((half, width), F32)
    return pl.pallas_call(
        kernel,
        out_shape=(rows, rows, jax.ShapeDtypeStruct((3, width), F32)),
        cost_estimate=LONG,
        compiler_params=vmem_limit(30 * half * width),
        name="norm_back",
    )(mine, got, unit, inverse, gain[None], grad)


def product_rows(pairs, scale, start, first, second, got=None):
    widths = [right.shape[1] for _, right in pairs]
    total = sum(widths)
    has_got = got is not None
    count = first + second

    def kernel(scale_ref, *refs):
        ins = refs[: 2 * len(pairs)]
        outs = refs[2 * len(pairs) + has_got :]
        step = pl.program_id(0)

        def fill(out_ref):
            column = 0
            for i, width in enumerate(widths):
                block = (
                    lax.dot_general(
                        ins[2 * i][...],
                        ins[2 * i + 1][...],
                        (((0,), (0,)), ((), ())),
                        preferred_element_type=F32,
                    )
                    * scale_ref[0:1, 0:1]
                )
                if has_got:
                    block = block + refs[2 * len(pairs)][:, column : column + width]
                out_ref[:, column : column + width] = block
                column += width

        if second:
            pl.when(step < first)(lambda: fill(outs[0]))
            pl.when(step >= first)(lambda: fill(outs[1]))
        else:
            fill(outs[0])

    in_specs = [pl.BlockSpec(scale.shape, lambda j: (0, 0))]
    operands = [scale]
    traffic = 0
    for left, right in pairs:
        rows = left.shape[0]
        in_specs.append(pl.BlockSpec((rows, 128), lambda j: (0, start + j)))
        in_specs.append(pl.BlockSpec(right.shape, lambda j: (0, 0)))
        operands += [left, right]
        traffic += 2 * 2 * rows * (128 + right.shape[1])
    if has_got:
        in_specs.append(pl.BlockSpec((128, total), lambda j: (j, 0)))
        operands.append(got)
    out_shape = [jax.ShapeDtypeStruct((first * 128, total), F32)]
    out_specs = [pl.BlockSpec((128, total), lambda j: (jnp.minimum(j, first - 1), 0))]
    if second:
        out_shape.append(jax.ShapeDtypeStruct((second * 128, total), F32))
        out_specs.append(pl.BlockSpec((128, total), lambda j: (jnp.maximum(j - first, 0), 0)))
    return pl.pallas_call(
        kernel,
        out_shape=out_shape,
        grid=(count,),
        in_specs=in_specs,
        out_specs=out_specs,
        cost_estimate=LONG,
        compiler_params=vmem_limit(traffic + 2 * 4 * 128 * total * 3),
        name="product_rows",
    )(*operands)


def add_split(keep, got):
    rows, width = keep.shape
    half = rows // 2
    size = min(64, half)
    count = half // size

    def kernel(keep_ref, got_ref, first_out, second_out):
        total = keep_ref[...] + got_ref[...]

        @pl.when(pl.program_id(0) < count)
        def _():
            first_out[...] = total

        @pl.when(pl.program_id(0) >= count)
        def _():
            second_out[...] = total

    block = (size, width)
    return pl.pallas_call(
        kernel,
        out_shape=[jax.ShapeDtypeStruct((half, width), F32)] * 2,
        grid=(2 * count,),
        in_specs=[pl.BlockSpec(block, lambda j: (j, 0))] * 2,
        out_specs=[
            pl.BlockSpec(block, lambda j: (jnp.minimum(j, count - 1), 0)),
            pl.BlockSpec(block, lambda j: (jnp.maximum(j - count, 0), 0)),
        ],
        cost_estimate=LONG,
        compiler_params=vmem_limit(32 * size * width),
        name="add_split",
    )(keep, got)


def attend_forward(unit_own, unit_other, gain, bias, weights, biases, out_weight):
    half, model_width = unit_own.shape
    rows = 2 * half
    local_width = weights.shape[2]
    head_count = local_width // HEAD_DIM

    def kernel(own_ref, other_ref, gain_ref, bias_ref, weight_ref, biases_ref, out_weight_ref,
               qkv_out, mixed_out, total_out, own_out, send_out, normed_ref):
        normed_ref[:half] = (own_ref[...] * gain_ref[...] + bias_ref[...]).astype(BF)
        normed_ref[half:] = (other_ref[...] * gain_ref[...] + bias_ref[...]).astype(BF)
        normed = normed_ref[...]
        qkv_out[:, :local_width] = (matmul(normed, weight_ref[0]) + biases_ref[0:1]).astype(BF)
        qkv_out[:, local_width : 2 * local_width] = matmul(normed, weight_ref[1]).astype(BF)
        qkv_out[:, 2 * local_width :] = (matmul(normed, weight_ref[2]) + biases_ref[1:2]).astype(BF)
        for head in range(head_count):
            one = slice(head * HEAD_DIM, (head + 1) * HEAD_DIM)
            query = qkv_out[:, one]
            key = qkv_out[:, local_width + head * HEAD_DIM : local_width + (head + 1) * HEAD_DIM]
            value = qkv_out[:, 2 * local_width + head * HEAD_DIM : 2 * local_width + (head + 1) * HEAD_DIM]
            scores = matmul_nt(query, key) / ROOT_DIM
            top = jnp.max(scores, axis=-1, keepdims=True)
            exponent = jnp.exp(scores - top)
            row_sum = jnp.sum(exponent, axis=-1, keepdims=True)
            attend = (exponent / row_sum).astype(BF)
            mixed_out[:, one] = matmul(attend, value).astype(BF)
            total_out[:, head : head + 1] = top + jnp.log(row_sum)
        send_out[...] = matmul(mixed_out[half:], out_weight_ref[...])
        own_out[...] = matmul(mixed_out[:half], out_weight_ref[...])

    piece = jax.ShapeDtypeStruct((half, model_width), F32)
    return pl.pallas_call(
        kernel,
        out_shape=(
            jax.ShapeDtypeStruct((rows, 3 * local_width), BF),
            jax.ShapeDtypeStruct((rows, local_width), BF),
            jax.ShapeDtypeStruct((rows, 128), F32),
            piece,
            piece,
        ),
        scratch_shapes=[pltpu.VMEM((rows, model_width), BF)],
        cost_estimate=pl.CostEstimate(
            flops=2 * rows * local_width * (4 * model_width + 2 * rows),
            bytes_accessed=8 * rows * model_width + 8 * local_width * model_width,
            transcendentals=rows * rows * head_count,
        ),
        compiler_params=vmem_limit(22 * rows * model_width),
        name="attend_forward",
    )(unit_own, unit_other, gain[None], bias[None], weights, biases, out_weight)


def attend_back(low, qkv, totals, weights, out_weight):
    rows, model_width = low.shape
    half = rows // 2
    local_width = weights.shape[2]
    head_count = local_width // HEAD_DIM

    def kernel(low_ref, qkv_ref, total_ref, weight_ref, out_weight_ref,
               grads_out, sums_out, own_out, send_out, mix_ref):
        mix_ref[...] = matmul_nt(low_ref[...], out_weight_ref[...]).astype(BF)
        for head in range(head_count):
            one = slice(head * HEAD_DIM, (head + 1) * HEAD_DIM)
            two = slice(local_width + head * HEAD_DIM, local_width + (head + 1) * HEAD_DIM)
            three = slice(2 * local_width + head * HEAD_DIM, 2 * local_width + (head + 1) * HEAD_DIM)
            query, key, value = qkv_ref[:, one], qkv_ref[:, two], qkv_ref[:, three]
            mix = mix_ref[:, one]
            attend = jnp.exp(matmul_nt(query, key) / ROOT_DIM - total_ref[:, head : head + 1])
            grad_attend = matmul_nt(mix, value)
            grad_value = matmul_tn(attend.astype(BF), mix)
            weighted = attend * grad_attend
            grad_scores = weighted - attend * jnp.sum(weighted, axis=-1, keepdims=True)
            grad_low = grad_scores.astype(BF)
            grad_query = matmul(grad_low, key) / ROOT_DIM
            grad_key = matmul_tn(grad_low, query) / ROOT_DIM
            grads_out[:, one] = grad_query.astype(BF)
            grads_out[:, two] = grad_key.astype(BF)
            grads_out[:, three] = grad_value.astype(BF)
            sums_out[0:1, one] = jnp.sum(grad_query, axis=0, keepdims=True)
            sums_out[1:2, one] = jnp.sum(grad_value, axis=0, keepdims=True)

        def pull(part):
            total = matmul_nt(grads_out[part, :local_width], weight_ref[0])
            total = total + matmul_nt(grads_out[part, local_width : 2 * local_width], weight_ref[1])
            return total + matmul_nt(grads_out[part, 2 * local_width :], weight_ref[2])

        send_out[...] = pull(slice(half, rows))
        own_out[...] = pull(slice(0, half))

    piece = jax.ShapeDtypeStruct((half, model_width), F32)
    return pl.pallas_call(
        kernel,
        out_shape=(
            jax.ShapeDtypeStruct((rows, 3 * local_width), BF),
            jax.ShapeDtypeStruct((2, local_width), F32),
            piece,
            piece,
        ),
        scratch_shapes=[pltpu.VMEM((rows, local_width), BF)],
        cost_estimate=LONG,
        compiler_params=vmem_limit(24 * rows * model_width),
        name="attend_back",
    )(low, qkv, totals, weights, out_weight)


def finish_layers(kind, pieces, layer_count, shard, local_width):
    width = pieces[0].shape[1]
    shapes = {
        "down": [(layer_count, width, shard)],
        "up": [(layer_count, shard, width)],
        "att": [
            (layer_count, local_width, shard),
            (layer_count, 3, shard, local_width),
        ],
    }[kind]

    def store(values, outs):
        for layer, value in enumerate(values):
            if kind == "down":
                outs[0][layer] = value.T
            elif kind == "up":
                outs[0][layer] = value
            else:
                outs[0][layer] = value[:, :local_width].T
                for which in range(3):
                    begin = (1 + which) * local_width
                    outs[1][layer, which] = value[:, begin : begin + local_width]

    if shard % 128:
        values = pieces
        if kind == "down":
            return [jnp.stack([value.T for value in values])]
        if kind == "up":
            return [jnp.stack(values)]
        rest = [
            value[:, local_width:].reshape(shard, 3, local_width).transpose(1, 0, 2)
            for value in values
        ]
        return [jnp.stack([value[:, :local_width].T for value in values]), jnp.stack(rest)]

    def kernel(*refs):
        store([ref[...] for ref in refs[:layer_count]], refs[layer_count:])

    return pl.pallas_call(
        kernel,
        out_shape=[jax.ShapeDtypeStruct(shape, F32) for shape in shapes],
        cost_estimate=pl.CostEstimate(
            flops=layer_count * shard * width,
            bytes_accessed=12 * layer_count * shard * width,
            transcendentals=0,
        ),
        compiler_params=vmem_limit(20 * layer_count * shard * width),
        name="finish_layers",
    )(*pieces)


def one_hot_segments(var_count, pix_count):
    flat = var_count * pix_count
    rows = lax.broadcasted_iota(jnp.int32, (var_count, flat), 0)
    columns = lax.broadcasted_iota(jnp.int32, (var_count, flat), 1)
    inside = (columns >= rows * pix_count) & (columns < (rows + 1) * pix_count)
    return jnp.where(inside, 1.0, 0.0).astype(BF)


def pool_front(core, pixels, patch, embed, query, query_weight, key_weight, value_weight,
               value_bias, mask, out_weight):
    var_count = embed.shape[0]
    flat, rows = pixels.shape
    pix_count = flat // var_count
    model_width, local_width = key_weight.shape
    head_count = local_width // HEAD_DIM
    half = rows // 2

    def kernel(core_ref, pixels_ref, patch_ref, embed_ref, query_ref, query_weight_ref, key_weight_ref,
               value_weight_ref, bias_ref, mask_ref, out_weight_ref,
               low_out, query_out, key_out, score_out, flat_out, var_out, probs_out, pooled_out,
               own_out, send_out, turned_ref):
        turned_ref[...] = pixels_ref[...].T
        mine = pl.multiple_of(core_ref[0] * half, 8)
        theirs = pl.multiple_of(half - core_ref[0] * half, 8)
        low_out[:half] = turned_ref[pl.ds(mine, half)].astype(BF)
        low_out[half:] = turned_ref[pl.ds(theirs, half)].astype(BF)
        query = matmul(query_ref[...].astype(BF), query_weight_ref[...]).astype(BF)
        query_out[...] = query.astype(F32)
        for head in range(head_count):
            one = slice(head * HEAD_DIM, (head + 1) * HEAD_DIM)
            key_out[head : head + 1] = matmul_nt(query[:, one], key_weight_ref[:, one]) / ROOT_DIM
        key_high, key_rest = two_part(key_out[...])
        embed_high, embed_rest = two_part(embed_ref[...])
        score_out[...] = matmul_nt(key_high, patch_ref[...]) + matmul_nt(key_rest, patch_ref[...])
        score_var = (
            matmul_nt(key_high, embed_high)
            + matmul_nt(key_rest, embed_high)
            + matmul_nt(key_high, embed_rest)
        )
        flat_out[...] = matmul(patch_ref[...], value_weight_ref[...]).astype(BF)
        value_var = matmul(embed_high, value_weight_ref[...]) + matmul(embed_rest, value_weight_ref[...])
        var_out[...] = (value_var + bias_ref[...]).astype(BF)
        segment = one_hot_segments(var_count, pix_count)
        for head in range(head_count):
            one = slice(head * HEAD_DIM, (head + 1) * HEAD_DIM)
            pix = low_out[...].astype(F32)
            high, rest = two_part(pix * score_out[head : head + 1])
            scores = matmul_nt(high, segment) + matmul_nt(rest, segment) + score_var[head : head + 1]
            scores = jnp.where(mask_ref[...] > 0, scores, -1000000000.0)
            exponent = jnp.exp(scores - jnp.max(scores, axis=-1, keepdims=True))
            probs = exponent / jnp.sum(exponent, axis=-1, keepdims=True)
            probs_out[head] = probs
            low = probs.astype(BF)
            mixed = (matmul(low, segment) * pix).astype(BF)
            pooled_out[:, one] = (matmul(mixed, flat_out[:, one]) + matmul(low, var_out[:, one])).astype(BF)
        send_out[...] = matmul(pooled_out[half:], out_weight_ref[...])
        own_out[...] = matmul(pooled_out[:half], out_weight_ref[...])

    piece = jax.ShapeDtypeStruct((half, model_width), F32)
    return pl.pallas_call(
        kernel,
        out_shape=(
            jax.ShapeDtypeStruct((rows, flat), BF),
            jax.ShapeDtypeStruct((1, local_width), F32),
            jax.ShapeDtypeStruct((head_count, model_width), F32),
            jax.ShapeDtypeStruct((head_count, flat), F32),
            jax.ShapeDtypeStruct((flat, local_width), BF),
            jax.ShapeDtypeStruct((var_count, local_width), BF),
            jax.ShapeDtypeStruct((head_count, rows, var_count), F32),
            jax.ShapeDtypeStruct((rows, local_width), BF),
            piece,
            piece,
        ),
        in_specs=[pl.BlockSpec(memory_space=pltpu.SMEM)] + [pl.BlockSpec()] * 10,
        scratch_shapes=[pltpu.VMEM((rows, flat), F32)],
        cost_estimate=LONG,
        compiler_params=vmem_limit(20 << 20),
        name="pool_front",
    )(core, pixels, patch, embed, query, query_weight, key_weight, value_weight, value_bias, mask, out_weight)


def pool_back(low, out_weight, value_flat, value_var, pix_low, probs, scores):
    rows, flat = pix_low.shape
    head_count, _, var_count = probs.shape
    pix_count = flat // var_count
    local_width = value_flat.shape[1]
    half = rows // 2

    def kernel(low_ref, out_weight_ref, flat_ref, var_ref, pix_ref, probs_ref, score_ref,
               value_out, key_out, key_var_out, own_out, send_out, pooled_ref, pixel_ref):
        pooled_ref[...] = matmul_nt(low_ref[...], out_weight_ref[...]).astype(BF)
        segment = one_hot_segments(var_count, pix_count)
        for head in range(head_count):
            one = slice(head * HEAD_DIM, (head + 1) * HEAD_DIM)
            pix = pix_ref[...].astype(F32)
            pooled = pooled_ref[:, one]
            pull = matmul_nt(pooled, flat_ref[:, one])
            high, rest = two_part(pull * pix)
            grad_probs = (
                matmul_nt(high, segment) + matmul_nt(rest, segment) + matmul_nt(pooled, var_ref[:, one])
            )
            probs_one = probs_ref[head]
            weighted = probs_one * grad_probs
            grad_scores = weighted - probs_one * jnp.sum(weighted, axis=-1, keepdims=True)
            high, rest = two_part(grad_scores)
            wide = matmul(high, segment) + matmul(rest, segment)
            key_out[head : head + 1] = jnp.sum(wide * pix, axis=0, keepdims=True)
            key_var_out[head : head + 1] = jnp.sum(grad_scores, axis=0, keepdims=True)
            probs_low = probs_one.astype(BF)
            probs_wide = matmul(probs_low, segment)
            term = wide * score_ref[head : head + 1] + probs_wide * pull
            if head:
                pixel_ref[...] += term
            else:
                pixel_ref[...] = term
            mixed = (probs_wide * pix).astype(BF)
            value_out[:flat, one] = matmul_tn(mixed, pooled)
            value_out[flat:, one] = matmul_tn(probs_low, pooled)
        own_out[...] = pixel_ref[:half]
        send_out[...] = pixel_ref[half:]

    piece = jax.ShapeDtypeStruct((half, flat), F32)
    return pl.pallas_call(
        kernel,
        out_shape=(
            jax.ShapeDtypeStruct((flat + var_count, local_width), F32),
            jax.ShapeDtypeStruct((head_count, flat), F32),
            jax.ShapeDtypeStruct((head_count, var_count), F32),
            piece,
            piece,
        ),
        scratch_shapes=[pltpu.VMEM((rows, local_width), BF), pltpu.VMEM((rows, flat), F32)],
        cost_estimate=LONG,
        compiler_params=vmem_limit(20 << 20),
        name="pool_back",
    )(low, out_weight, value_flat, value_var, pix_low, probs, scores)


class Links:
    def __init__(self, dp, mp):
        self.dp, self.mp = dp, mp
        self.dp_index = lax.axis_index("dp")
        self.mp_index = lax.axis_index("mp")

    def dp_bit(self, bit):
        return (self.dp_index >> bit) & 1

    def mp_bit(self, bit):
        return (self.mp_index >> bit) & 1

    def ordered_sum(self, clock, own, send):
        send = clock.one(send)
        got = exchange(send, "mp", self.mp, 0)
        clock.hold()
        mine = clock.one(own() + clock.one(got))
        last = bit_count(self.mp) - 1
        for bit in range(1, last):
            mine = clock.one(mine + exchange(mine, "mp", self.mp, bit))
        return mine, exchange(mine, "mp", self.mp, last)

    def begin_sum(self, own, send):
        mine = own + exchange(send, "mp", self.mp, 0)
        last = bit_count(self.mp) - 1
        for bit in range(1, last):
            mine = mine + exchange(mine, "mp", self.mp, bit)
        return mine, exchange(mine, "mp", self.mp, last)

    def begin_product(self, left, right, product=matmul):
        half = left.shape[0] // 2
        send = product(left[half:], right)
        return self.begin_sum(product(left[:half], right), send)

    def sum_rows(self, partial):
        half = partial.shape[0] // 2
        mine, got = self.begin_sum(partial[:half], partial[half:])
        return mine + got

    def other_rows(self, own):
        return exchange(own, "mp", self.mp, 0)

    def split_rows(self, tensor):
        half = tensor.shape[0] // 2
        core = self.mp_bit(0)
        own = lax.dynamic_slice_in_dim(tensor, core * half, half, 0)
        other = lax.dynamic_slice_in_dim(tensor, (1 - core) * half, half, 0)
        return own, other

    def global_rows(self, own, other):
        core = self.mp_bit(0)
        return jnp.concatenate(
            [jnp.where(core == 0, own, other), jnp.where(core == 0, other, own)], axis=0
        )

    def order(self, bits):
        masks = []
        for place in range(self.dp):
            mask = 0
            for i, bit in enumerate(bits):
                if not (place >> (len(bits) - 1 - i)) & 1:
                    mask |= 1 << bit
            masks.append(mask)
        return jnp.array(masks, jnp.int32) ^ self.dp_index


class Merge:
    def __init__(self, links, pairs, bits):
        self.links, self.pairs, self.bits = links, pairs, bits
        self.blocks = pairs[0][0].shape[1] // 128
        self.step = 0

    def advance(self, clock):
        if self.step == len(self.bits):
            self.total = clock.one(self.keep + clock.one(self.got))
            self.step += 1
            return
        got, pairs = None, self.pairs
        if self.step:
            got = clock.one(self.got)
        else:
            pairs = [(clock.one(pairs[0][0]), pairs[0][1])] + pairs[1:]
        if self.step == 0:
            send = product_rows(pairs, clock.cell, 0, self.blocks // 2, 0)[0]
        elif self.step == 1:
            send, self.keep = product_rows(
                pairs, clock.cell, self.blocks // 2, self.blocks // 4, self.blocks // 4, got
            )
        else:
            send, self.keep = add_split(self.keep, got)
        send = clock.one(send)
        self.got = exchange(send, "dp", self.links.dp, self.bits[self.step])
        self.step += 1

    @property
    def open(self):
        return self.step <= len(self.bits)


class ShardMerge:
    def __init__(self, links, shards):
        self.links, self.shards = links, shards
        self.step = 0

    def split(self, total):
        pairs = total.reshape((total.shape[0] // 2, 2) + total.shape[1:])
        own = self.links.dp_bit(self.step)
        self.keep = pick(pairs, own, 1)
        return pick(pairs, 1 - own, 1)

    def advance(self, clock):
        if self.step == bit_count(self.links.dp):
            self.total = clock.one(self.keep + clock.one(self.got))
            self.step += 1
            return
        total = self.shards
        if self.step:
            total = self.keep + clock.one(self.got)
        send = clock.one(self.split(clock.one(total)))
        self.got = exchange(send, "dp", self.links.dp, self.step)
        clock.hold()
        self.step += 1

    @property
    def open(self):
        return self.step <= bit_count(self.links.dp)


def norm_parts(rows):
    row_mean = jnp.mean(rows, axis=-1, keepdims=True)
    centred = rows - row_mean
    spread = jnp.mean(centred * centred, axis=-1, keepdims=True)
    inverse = lax.rsqrt(spread + 1e-05)
    return centred * inverse, jnp.broadcast_to(inverse, (rows.shape[0], 128))


def make_per_device(dp, mp):
    def per_device(
        pixels,
        dataset_id,
        variable_mask,
        lead_hours,
        token_counts,
        dataset_weight,
        patch_weight,
        variable_embed,
        position_embed,
        pool_query,
        pool_query_weight,
        pool_key_weight,
        pool_value_weight,
        pool_value_bias,
        pool_output_weight,
        pool_output_bias,
        lead_weight,
        lead_bias,
        norm_gain,
        norm_bias,
        attention_weight,
        attention_bias,
        output_weight,
        output_bias,
        up_weight,
        up_bias,
        down_weight,
        down_bias,
        cotangent,
    ):
        links = Links(dp, mp)
        var_count, pix_count, row_count = pixels.shape[1:]
        flat_count = var_count * pix_count
        model_width = patch_weight.shape[2]
        local_width = pool_query_weight.shape[1]
        head_count = local_width // HEAD_DIM
        layer_count = attention_weight.shape[0]
        shard = model_width // dp

        def heads_first(tensor):
            return tensor.reshape(row_count, head_count, HEAD_DIM).transpose(1, 0, 2)

        def heads_last(tensor):
            return tensor.transpose(1, 0, 2).reshape(row_count, local_width)

        dataset_pick = jnp.arange(variable_mask.shape[0], dtype=jnp.int32) == dataset_id[0]
        mask_row = jnp.sum(jnp.where(dataset_pick[:, None], variable_mask, 0), axis=0)
        item_weight = jnp.sum(jnp.where(dataset_pick, dataset_weight, 0)).astype(F32)
        own_count = token_counts[0].astype(F32)
        lead_scale = lead_hours[0].astype(F32) / 24.0

        patch_flat = patch_weight.reshape(flat_count, model_width)
        (
            pix_low,
            query_row,
            key_rows,
            score_rows,
            value_flat,
            value_var,
            pool_probs,
            pooled,
            part_own,
            part_send,
        ) = pool_front(
            links.mp_bit(0).reshape(1),
            pixels[0].reshape(flat_count, row_count),
            patch_flat,
            variable_embed,
            pool_query[None],
            pool_query_weight,
            pool_key_weight,
            pool_value_weight,
            pool_value_bias[None],
            mask_row[None],
            pool_output_weight,
        )
        mine, got = links.begin_sum(part_own, part_send)
        count_total = after(jnp.full((8, 128), own_count, F32), mine)
        for bit in range(bit_count(dp)):
            count_total = count_total + exchange(count_total, "dp", dp, bit)
        scale_cell = item_weight * own_count / count_total
        item_scale = scale_cell[0, 0]
        position_own = links.split_rows(position_embed)[0]
        offset_rows = pool_output_bias + position_own + lead_scale * lead_weight + lead_bias
        mine, scale_cell = lax.optimization_barrier((mine, scale_cell))
        hidden = mine + got + offset_rows

        bits = list(range(bit_count(dp)))
        bits_late = bits[1:] + bits[:1]
        shards, shards_late = links.order(bits), links.order(bits_late)
        top = layer_count - 1
        kept = []
        for layer in range(layer_count):
            unit_one, inverse_one = norm_parts(hidden)
            unit_other = links.other_rows(unit_one)
            qkv, mixed, totals, part_own, part_send = attend_forward(
                unit_one,
                unit_other,
                norm_gain[layer, 0],
                norm_bias[layer, 0],
                attention_weight[layer],
                attention_bias[layer],
                output_weight[layer],
            )
            mine, got = links.begin_sum(part_own, part_send)
            normed = norm_rows(
                after(unit_one, mine), unit_other, norm_gain[layer, 0], norm_bias[layer, 0], shards
            )
            mine, normed = lax.optimization_barrier((mine, normed))
            if layer == 0:
                grad_own, grad_other = links.split_rows(after(cotangent[0], mine))
                grad_other, down_low, down_left = merge_rows(
                    grad_own, grad_other, jnp.zeros_like(grad_other), shards_late
                )
                mine, down_low = lax.optimization_barrier((mine, down_low))
            hidden = hidden + (mine + got) + output_bias[layer]
            unit_two, inverse_two = norm_parts(hidden)
            unit_other = links.other_rows(unit_two)
            normed_two = jnp.concatenate([unit_two, unit_other], axis=0)
            normed_two = (normed_two * norm_gain[layer, 1] + norm_bias[layer, 1]).astype(BF)
            pre_act = matmul(normed_two, up_weight[layer]) + up_bias[layer]
            activation = gelu_exact(pre_act).astype(BF)
            marker = activation
            if layer < top:
                mine, got = links.begin_product(activation, down_weight[layer])
                marker = mine
            normed_two = norm_rows(
                after(unit_two, marker), unit_other, norm_gain[layer, 1], norm_bias[layer, 1], shards
            )
            if layer < top:
                if layer == 0:
                    top_grad = matmul_nt(after(down_low, mine), down_weight[top])
                    embed_high, embed_rest = two_part(variable_embed)
                    embed_all = jnp.concatenate([patch_flat, embed_high, embed_rest], axis=0)
                    mine, embed_all = lax.optimization_barrier((mine, embed_all))
                    embed_left = take_columns(embed_all, shards, shard)
                    key_high, key_rest = two_part(key_rows)
                    left_side = jnp.concatenate(
                        [
                            pool_value_weight,
                            pool_query_weight,
                            jnp.concatenate([key_high, key_high, key_rest], axis=0).T,
                        ],
                        axis=1,
                    )
                    sides = left_side.reshape(dp, mp // 2, 2, shard // mp, left_side.shape[1])
                    side_own, side_send = [
                        pick(sides, which, 2)
                        .transpose(1, 0, 2, 3)
                        .reshape(model_width // 2, left_side.shape[1])
                        for which in (links.mp_bit(0), 1 - links.mp_bit(0))
                    ]
                    mine, top_grad, embed_left, side_own, side_send = lax.optimization_barrier(
                        (mine, top_grad, embed_left, side_own, side_send)
                    )
                mine, normed_two = lax.optimization_barrier((mine, normed_two))
                hidden = hidden + (mine + got) + down_bias[layer]
            kept.append(
                (
                    unit_one,
                    inverse_one,
                    normed,
                    qkv,
                    totals,
                    mixed,
                    unit_two,
                    inverse_two,
                    normed_two,
                    pre_act,
                    activation,
                )
            )

        activation_top = kept[top][-1]
        row_sums = {}
        local_sums = {}
        merges = {}
        row_sums["down_bias", top] = jnp.sum(grad_own, axis=0)

        head_of = jnp.arange(local_width, dtype=jnp.int32) // HEAD_DIM
        head_pick = head_of[:, None] == jnp.arange(head_count, dtype=jnp.int32)[None, :]
        clock = Clock(scale_cell)

        def advance(spot):
            for name in PLAN.get(spot, ()):
                if name in merges and merges[name].open:
                    merges[name].advance(clock)

        for layer in reversed(range(layer_count)):
            depth = top - layer
            (
                unit_one,
                inverse_one,
                normed,
                qkv,
                totals,
                mixed,
                unit_two,
                inverse_two,
                normed_two,
                pre_act,
                activation,
            ) = kept[layer]
            merges["down", depth] = Merge(
                links, [(down_left, activation)], bits if depth else bits_late
            )
            grad_activation = top_grad if layer == top else matmul_nt(down_low, down_weight[layer])
            grad_pre = jax.vjp(gelu_exact, pre_act)[1](grad_activation)[0]
            local_sums["up_bias", layer] = jnp.sum(grad_pre, axis=0)
            pre_low = clock.one(grad_pre.astype(BF))
            merges["up", depth] = Merge(links, [(normed_two, pre_low)], bits)
            advance(("pre", depth))
            pre_low = clock.one(pre_low)
            half = row_count // 2
            mine, got = links.ordered_sum(
                clock,
                lambda: matmul_nt(pre_low[:half], up_weight[layer]),
                matmul_nt(pre_low[half:], up_weight[layer]),
            )
            if not PLAN.get(("wait_two", depth)):
                clock.hold()
            advance(("wait_two", depth))
            mine, got = clock.both(mine, got)
            change, grad_own, sums = norm_back(
                mine, got, unit_two, inverse_two, norm_gain[layer, 1], grad_own
            )
            change, sums = clock.both(change, sums)
            row_sums["gain", layer, 1] = sums[0]
            row_sums["bias", layer, 1] = sums[1]
            row_sums["out_bias", layer] = sums[2]
            other_change = links.other_rows(change)
            clock.hold()
            grad_other, out_low, out_left = merge_rows(
                grad_own, grad_other, clock.one(other_change), shards
            )
            out_low = clock.one(out_low)
            advance(("mid", depth))
            grads, qv_sums, part_own, part_send = attend_back(
                clock.one(out_low), qkv, totals, attention_weight[layer], output_weight[layer]
            )
            local_sums["qv", layer] = qv_sums
            mine, got = links.ordered_sum(clock, lambda: part_own, part_send)
            if not PLAN.get(("wait_one", depth)):
                clock.hold()
            merges["att", depth] = Merge(links, [(out_left, mixed), (normed, grads)], bits)
            advance(("wait_one", depth))
            mine, got = clock.both(mine, got)
            change, grad_own, sums = norm_back(
                mine, got, unit_one, inverse_one, norm_gain[layer, 0], grad_own
            )
            change, sums = clock.both(change, sums)
            row_sums["gain", layer, 0] = sums[0]
            row_sums["bias", layer, 0] = sums[1]
            if layer:
                row_sums["down_bias", layer - 1] = sums[2]
            other_change = links.other_rows(change)
            clock.hold()
            grad_other, down_low, down_left = merge_rows(
                grad_own, grad_other, clock.one(other_change), shards
            )
            down_low = clock.one(down_low)
            advance(("end", depth))
            down_low = clock.one(down_low)

        row_sums["column"] = sums[2]
        row_sums["lead"] = lead_scale * sums[2]
        value_grad, key_grad, key_grad_var, pixel_own, pixel_send = pool_back(
            clock.one(down_low), pool_output_weight, value_flat, value_var, pix_low, pool_probs, score_rows
        )
        value_grad = clock.one(value_grad)
        embed_all, embed_left = clock.both(embed_all, embed_left)
        value_low = value_grad.astype(BF)
        merges["tail"] = Merge(
            links,
            [
                (down_left, pooled),
                (embed_left, jnp.concatenate([value_low, value_low[flat_count:]], axis=0)),
            ],
            bits,
        )
        advance("values")

        flat_all = flat_count + var_count
        item_scale = clock.cell[0, 0]
        value_scaled = (clock.one(value_grad) * item_scale).astype(BF)
        key_scaled = jnp.concatenate([key_grad, key_grad_var], axis=1) * item_scale
        key_high, key_rest = two_part(key_scaled)
        key_twice = jnp.concatenate([key_high, key_rest], axis=0)
        summed_key = matmul(
            jnp.concatenate([key_twice, key_twice[:, flat_count:]], axis=1), embed_all
        )
        summed_key = summed_key[:head_count] + summed_key[head_count:]
        summed_high, summed_rest = two_part(summed_key)
        query_grad = matmul(
            jnp.concatenate([summed_high, summed_rest], axis=0), pool_key_weight
        )
        query_grad = query_grad[:head_count] + query_grad[head_count:]
        query_grad = jnp.sum(jnp.where(head_pick.T, query_grad, 0.0), axis=0) / ROOT_DIM
        query_high, query_rest = two_part(query_grad[None])
        right_side = jnp.concatenate([key_high, key_rest, key_high], axis=0)
        sub = shard // mp
        core = links.mp_bit(0)

        def embed_side(side):
            block = matmul_nt(side[:, :local_width], value_scaled)
            block = block + matmul(side[:, 2 * local_width :], right_side)
            weight = side[:, local_width : 2 * local_width]
            part = matmul_nt(weight, query_high) + matmul_nt(weight, query_rest)
            block = jnp.concatenate([block, part], axis=1)
            return block.reshape(mp // 2, dp, sub, flat_all + 1)

        embed_send = clock.one(embed_side(side_send))
        embed_got = exchange(embed_send, "mp", mp, 0)
        clock.hold()
        embed_grad = embed_side(clock.one(side_own)) + clock.one(embed_got)
        own = links.mp_bit(1)
        for bit in range(1, bit_count(mp)):
            own = links.mp_bit(bit)
            count = embed_grad.shape[0] // 2
            pairs = embed_grad.reshape((count, 2) + embed_grad.shape[1:])
            embed_keep = pick(pairs, own, 1)
            embed_send = clock.one(pick(pairs, 1 - own, 1))
            embed_got = exchange(embed_send, "mp", mp, bit)
            if bit + 1 < bit_count(mp):
                embed_grad = embed_keep + embed_got
        clock.hold()
        advance("embed")

        names = []
        for layer in range(layer_count):
            names += [("gain", layer, 0), ("gain", layer, 1), ("bias", layer, 0), ("bias", layer, 1)]
        for layer in range(layer_count):
            names += [("out_bias", layer), ("down_bias", layer)]
        names += ["column", "lead"]
        own_sums = clock.one(jnp.stack([row_sums[name] for name in names]) * item_scale)
        other_sums = exchange(own_sums, "mp", mp, 0)
        clock.hold()
        full_sums = own_sums + clock.one(other_sums)
        local = jnp.stack([local_sums["up_bias", layer] for layer in range(layer_count)]) * item_scale
        thin = [local_sums["qv", layer] for layer in range(layer_count)]
        pool_bias = jnp.sum(value_grad[flat_count:], axis=0, keepdims=True)
        thin = jnp.concatenate(thin + [pool_bias], axis=0) * item_scale
        packed = jnp.concatenate(
            [
                full_sums.reshape(len(names), dp, shard).transpose(1, 0, 2).reshape(dp, -1),
                summed_key.reshape(head_count, dp, shard).transpose(1, 0, 2).reshape(dp, -1),
                local.reshape(layer_count, dp, -1).transpose(1, 0, 2).reshape(dp, -1),
                thin.reshape(2 * layer_count + 1, dp, -1).transpose(1, 0, 2).reshape(dp, -1),
                jnp.broadcast_to(query_grad[None, :], (dp, local_width)),
            ],
            axis=1,
        )
        packed_size = packed.shape[1]
        packed_rows = -(-packed_size // 1024) * 8
        packed = jnp.pad(packed, ((0, 0), (0, packed_rows * 128 - packed_size)))
        packed = packed.reshape(dp, packed_rows, 128)
        position = (grad_own * item_scale).reshape(row_count // 2, dp, shard).transpose(1, 0, 2)
        position, packed = clock.both(position, packed)
        advance("vectors")
        embed_grad = (embed_keep + clock.one(embed_got)).reshape(dp, sub, flat_all + 1)
        lane_blocks = -(-(flat_all + 1) // 128)
        embed_grad = jnp.pad(
            embed_grad, ((0, 0), (0, 0), (0, lane_blocks * 128 - flat_all - 1))
        )
        if shard == 128:
            tall = jnp.concatenate(
                [embed_grad[:, :, i * 128 : (i + 1) * 128] for i in range(lane_blocks)]
                + [packed, position],
                axis=1,
            )
            merges["small"] = ShardMerge(links, tall)
        else:
            merges["small"] = ShardMerge(
                links,
                jnp.concatenate(
                    [part.reshape(dp, 1, -1) for part in (embed_grad, packed, position)], axis=2
                ),
            )
        advance("small")

        activation_top = clock.one(activation_top)
        half = row_count // 2
        last_mine, last_got = links.ordered_sum(
            clock,
            lambda: matmul(activation_top[:half], down_weight[top]),
            matmul(activation_top[half:], down_weight[top]),
        )
        clock.hold()
        advance("output")
        pixel_mine, pixel_got = links.ordered_sum(clock, lambda: pixel_own, pixel_send)
        clock.hold()
        advance("pixels")
        last_mine, last_got = clock.both(last_mine, last_got)
        hidden = clock.one(hidden + (last_mine + last_got) + down_bias[top])
        hidden_other = links.other_rows(hidden)
        clock.hold()
        layer_out = clock.one(links.global_rows(hidden, clock.one(hidden_other)))
        advance("rows")
        pixel_mine, pixel_got = clock.both(pixel_mine, pixel_got)
        pixel_mine = clock.one(pixel_mine + pixel_got)
        pixel_other = links.other_rows(pixel_mine)
        clock.hold()
        pixel_grad = links.global_rows(pixel_mine, clock.one(pixel_other))
        pixel_grad = clock.one(pixel_grad.T.reshape(1, var_count, pix_count, row_count))
        for name in DRAIN:
            if merges[name].open:
                merges[name].advance(clock)
        for merge in merges.values():
            while merge.open:
                merge.advance(clock)
        finished = {}
        for kind in ("down", "up", "att"):
            parts = [merges[kind, top - layer].total for layer in range(layer_count)]
            finished[kind] = finish_layers(kind, parts, layer_count, shard, local_width)
        tail_total = merges["tail"].total
        small = merges["small"].total[0]
        if shard == 128:
            embed_rows = sub * lane_blocks
            embed_grad = jnp.concatenate(
                [small[i * sub : (i + 1) * sub] for i in range(lane_blocks)], axis=1
            )
            packed = small[embed_rows : embed_rows + packed_rows].reshape(-1)
            position = small[embed_rows + packed_rows :]
        else:
            size = sub * lane_blocks * 128
            embed_grad = small[0, :size].reshape(sub, lane_blocks * 128)
            packed = small[0, size : size + packed_rows * 128]
            position = small[0, size + packed_rows * 128 :].reshape(row_count // 2, shard)
        packed, position, _ = lax.optimization_barrier((packed, position, clock.cell))
        position = links.global_rows(position, links.other_rows(position))
        offset = 0

        def take(*shape):
            nonlocal offset
            size = math.prod(shape)
            piece = packed[offset : offset + size].reshape(shape)
            offset += size
            return piece

        gains = take(layer_count, 2, shard)
        biases = []
        gain_list = []
        offset = 0
        norm_all = take(layer_count, 2, 2, shard)
        gain_list = norm_all[:, 0]
        biases = norm_all[:, 1]
        dense_bias = take(layer_count, 2, shard)
        column_total = take(shard)
        lead_total = take(shard)
        key_shard = take(head_count, shard)
        up_bias_total = take(layer_count, local.shape[1] // dp)
        thin_total = take(2 * layer_count + 1, local_width // dp)
        query_total = take(local_width)

        query_low = pool_query.astype(BF)
        query_rows = lax.dynamic_slice_in_dim(query_low, links.dp_index * shard, shard, 0)
        query_weight_grad = query_rows.astype(F32)[:, None] * query_total[None, :]
        key_weight_grad = (
            jnp.repeat(key_shard.T, HEAD_DIM, axis=1) * query_row / ROOT_DIM
        )
        embed_turned = embed_grad.T
        return (
            layer_out[None],
            pixel_grad,
            embed_turned[:flat_count].reshape(var_count, pix_count, sub),
            embed_turned[flat_count:flat_all],
            position,
            embed_turned[flat_all],
            query_weight_grad,
            key_weight_grad,
            tail_total[:, local_width:],
            thin_total[-1],
            tail_total[:, :local_width].T,
            column_total,
            lead_total,
            column_total,
            gain_list,
            biases,
            finished["att"][1],
            thin_total[:-1].reshape(layer_count, 2, local_width // dp),
            finished["att"][0],
            dense_bias[:, 0],
            finished["up"][0],
            up_bias_total,
            finished["down"][0],
            dense_bias[:, 1],
        )

    return per_device


def solution(mesh):
    return jax.shard_map(
        make_per_device(mesh.shape["dp"], mesh.shape["mp"]),
        mesh=mesh,
        in_specs=(
            P("dp", None, None, None),
            P("dp"),
            P(),
            P("dp"),
            P("dp"),
            P(),
            P(),
            P(),
            P(),
            P(),
            P(None, "mp"),
            P(None, "mp"),
            P(None, "mp"),
            P("mp"),
            P("mp", None),
            P(),
            P(),
            P(),
            P(),
            P(),
            P(None, None, None, "mp"),
            P(None, None, "mp"),
            P(None, "mp", None),
            P(),
            P(None, None, "mp"),
            P(None, "mp"),
            P(None, "mp", None),
            P(),
            P("dp", None, None),
        ),
        out_specs=(
            P("dp", None, None),
            P("dp", None, None, None),
            P(None, None, ("dp", "mp")),
            P(None, ("dp", "mp")),
            P(None, "dp"),
            P(("dp", "mp")),
            P("dp", "mp"),
            P("dp", "mp"),
            P("dp", "mp"),
            P(("mp", "dp")),
            P("mp", "dp"),
            P("dp"),
            P("dp"),
            P("dp"),
            P(None, None, "dp"),
            P(None, None, "dp"),
            P(None, None, "dp", "mp"),
            P(None, None, ("mp", "dp")),
            P(None, "mp", "dp"),
            P(None, "dp"),
            P(None, "dp", "mp"),
            P(None, ("mp", "dp")),
            P(None, "mp", "dp"),
            P(None, "dp"),
        ),
        check_vma=False,
    )
```

```python
import math

import jax
import jax.numpy as jnp
from jax import lax
from jax.experimental import pallas as pl
from jax.experimental.pallas import tpu as pltpu
from jax.sharding import PartitionSpec as P

HEAD_DIM = 64
PLAN = {
    ("top", 0): [("down", 0)],
    ("pre", 0): [("up", 0)],
    ("wait_one", 0): [("att", 0), ("down", 0), ("up", 0)],
    ("wait_two", 1): [("down", 1), ("up", 0)],
    ("mid", 1): [("down", 0), ("att", 0)],
    ("wait_one", 1): [("up", 0), ("up", 1), ("att", 0), ("down", 1)],
    ("end", 1): [("down", 0), ("att", 1)],
    "back": [("down", 1), ("att", 0), ("up", 1)],
    "small": ["small"],
    "values": ["tail", ("down", 1), ("up", 1), ("att", 1)],
    "pixels": ["small", ("up", 1), "tail", ("att", 1)],
    "rows": ["small", ("att", 1), "tail", "small", "tail"],
}
DRAIN = []
ROOT_DIM = math.sqrt(HEAD_DIM)
PRODUCT_BLOCKS = 2
BF = jnp.bfloat16
F32 = jnp.float32


def matmul(left, right):
    return jnp.dot(left, right, preferred_element_type=F32)


def matmul_tn(left, right):
    return lax.dot_general(left, right, (((0,), (0,)), ((), ())), preferred_element_type=F32)


def matmul_nt(left, right):
    return lax.dot_general(left, right, (((1,), (1,)), ((), ())), preferred_element_type=F32)


def two_part(tensor):
    high = tensor.astype(BF)
    return high, (tensor - high.astype(F32)).astype(BF)


def gelu_exact(pre_act):
    return jax.nn.gelu(pre_act, approximate=False)


def bit_count(size):
    bits = size.bit_length() - 1
    assert 1 << bits == size
    return bits


def exchange(tensor, axis, size, bit):
    return lax.ppermute(tensor, axis, [(i, i ^ (1 << bit)) for i in range(size)])


def pick(tensor, index, axis):
    return lax.dynamic_index_in_dim(tensor, index, axis, keepdims=False)


def after(value, *earlier):
    return lax.optimization_barrier((value,) + earlier)[0]


def vmem_limit(size):
    return pltpu.CompilerParams(vmem_limit_bytes=int(size * 1.25) + (2 << 20))


LONG = pl.CostEstimate(flops=10**12, bytes_accessed=8, transcendentals=0)


def step_cell(cell):
    def kernel(cell_ref, out_ref):
        out_ref[...] = cell_ref[...]

    return pl.pallas_call(
        kernel,
        out_shape=jax.ShapeDtypeStruct(cell.shape, F32),
        cost_estimate=LONG,
        compiler_params=vmem_limit(0),
        name="step_cell",
    )(cell)


class Clock:
    def __init__(self, cell):
        self.cell = cell

    def both(self, *values):
        *values, self.cell = lax.optimization_barrier((*values, self.cell))
        return values

    def one(self, value):
        return self.both(value)[0]

    def hold(self):
        self.cell = step_cell(self.cell)


def ordered_columns(source, target, shards_ref, count, shard):
    for place in range(count):
        column = pl.multiple_of(shards_ref[place] * shard, shard)
        target[:, place * shard : (place + 1) * shard] = source[:, pl.ds(column, shard)]


def take_columns(rows, shards, shard):
    pieces = rows.reshape(rows.shape[0], -1, shard)[:, shards]
    return pieces.reshape(rows.shape)


def norm_rows(own, other, gain, bias, shards):
    half, width = own.shape
    count = shards.shape[0]
    shard = width // count
    if shard % 128:
        rows = jnp.concatenate([own, other], axis=0) * gain + bias
        return take_columns(rows.astype(BF), shards, shard)

    def kernel(shards_ref, own_ref, other_ref, gain_ref, bias_ref, out_ref, low_ref):
        low_ref[:half] = (own_ref[...] * gain_ref[...] + bias_ref[...]).astype(BF)
        low_ref[half:] = (other_ref[...] * gain_ref[...] + bias_ref[...]).astype(BF)
        ordered_columns(low_ref, out_ref, shards_ref, count, shard)

    return pl.pallas_call(
        kernel,
        out_shape=jax.ShapeDtypeStruct((2 * half, width), BF),
        in_specs=[pl.BlockSpec(memory_space=pltpu.SMEM)] + [pl.BlockSpec()] * 4,
        scratch_shapes=[pltpu.VMEM((2 * half, width), BF)],
        cost_estimate=pl.CostEstimate(
            flops=4 * half * width, bytes_accessed=12 * half * width, transcendentals=0
        ),
        compiler_params=vmem_limit(16 * half * width),
        name="norm_rows",
    )(shards, own, other, gain[None], bias[None])


def merge_rows(own, other, change, shards):
    half, width = own.shape
    count = shards.shape[0]
    shard = width // count
    if shard % 128:
        total = other + change
        low = jnp.concatenate([own, total], axis=0).astype(BF)
        return total, low, take_columns(low, shards, shard)

    def kernel(shards_ref, own_ref, other_ref, change_ref, other_out, low_out, ordered_out):
        low_out[:half] = own_ref[...].astype(BF)
        total = other_ref[...] + change_ref[...]
        other_out[...] = total
        low_out[half:] = total.astype(BF)
        ordered_columns(low_out, ordered_out, shards_ref, count, shard)

    return pl.pallas_call(
        kernel,
        out_shape=(
            jax.ShapeDtypeStruct((half, width), F32),
            jax.ShapeDtypeStruct((2 * half, width), BF),
            jax.ShapeDtypeStruct((2 * half, width), BF),
        ),
        in_specs=[pl.BlockSpec(memory_space=pltpu.SMEM)] + [pl.BlockSpec()] * 3,
        cost_estimate=LONG,
        compiler_params=vmem_limit(26 * half * width),
        name="merge_rows",
    )(shards, own, other, change)


def norm_back(mine, got, unit, inverse, gains, place, grad):
    half, width = mine.shape
    size = half

    def kernel(mine_ref, got_ref, unit_ref, inverse_ref, gain_ref, grad_ref, change_out, grad_out, sums_out):
        pull = mine_ref[...] + got_ref[...]
        unit_rows = unit_ref[...]
        scaled = pull * gain_ref[place[0], place[1] : place[1] + 1]
        first = jnp.mean(scaled, axis=-1, keepdims=True)
        second = jnp.mean(scaled * unit_rows, axis=-1, keepdims=True)
        change = inverse_ref[:, :1] * (scaled - first - unit_rows * second)
        change_out[...] = change
        total = grad_ref[...] + change
        grad_out[...] = total

        @pl.when(pl.program_id(0) == 0)
        def _():
            sums_out[...] = jnp.zeros_like(sums_out)

        sums_out[0:1] += jnp.sum(pull * unit_rows, axis=0, keepdims=True)
        sums_out[1:2] += jnp.sum(pull, axis=0, keepdims=True)
        sums_out[2:3] += jnp.sum(total, axis=0, keepdims=True)

    rows = jax.ShapeDtypeStruct((half, width), F32)
    block = pl.BlockSpec((size, width), lambda j: (j, 0))
    return pl.pallas_call(
        kernel,
        out_shape=(rows, rows, jax.ShapeDtypeStruct((3, width), F32)),
        grid=(half // size,),
        in_specs=[
            block,
            block,
            block,
            pl.BlockSpec((size, 128), lambda j: (j, 0)),
            pl.BlockSpec(gains.shape, lambda j: (0, 0, 0)),
            block,
        ],
        out_specs=(block, block, pl.BlockSpec((3, width), lambda j: (0, 0))),
        cost_estimate=LONG,
        compiler_params=vmem_limit(64 * size * width),
        name="norm_back",
    )(mine, got, unit, inverse, gains, grad)


def feed_forward(unit_own, unit_other, gains, biases, place, up_weight, up_bias, down_weight):
    half, width = unit_own.shape
    rows = 2 * half
    layer, which = place
    hidden = up_weight.shape[2]
    size = hidden // 4
    spread_of = math.sqrt(2.0)
    peak = 1.0 / math.sqrt(2.0 * math.pi)

    def kernel(own_ref, other_ref, gain_ref, bias_ref, up_ref, up_bias_ref, down_ref,
               activation_out, slope_out, own_out, send_out, normed_ref):
        step = pl.program_id(0)

        @pl.when(step == 0)
        def _():
            gain = gain_ref[layer, which : which + 1]
            bias = bias_ref[layer, which : which + 1]
            normed_ref[:half] = (own_ref[...] * gain + bias).astype(BF)
            normed_ref[half:] = (other_ref[...] * gain + bias).astype(BF)
            own_out[...] = jnp.zeros_like(own_out)
            send_out[...] = jnp.zeros_like(send_out)

        pre = matmul(normed_ref[...], up_ref[0]) + up_bias_ref[layer : layer + 1]
        below = 0.5 + 0.5 * lax.erf(pre / spread_of)
        slope_out[...] = below + pre * (jnp.exp(-0.5 * pre * pre) * peak)
        activation = (pre * below).astype(BF)
        activation_out[...] = activation
        send_out[...] += matmul(activation[half:], down_ref[0])
        own_out[...] += matmul(activation[:half], down_ref[0])

    piece = jax.ShapeDtypeStruct((half, width), F32)
    whole = pl.BlockSpec((half, width), lambda j: (0, 0))
    return pl.pallas_call(
        kernel,
        out_shape=(
            jax.ShapeDtypeStruct((rows, hidden), BF),
            jax.ShapeDtypeStruct((rows, hidden), F32),
            piece,
            piece,
        ),
        grid=(hidden // size,),
        in_specs=[
            whole,
            whole,
            pl.BlockSpec(gains.shape, lambda j: (0, 0, 0)),
            pl.BlockSpec(biases.shape, lambda j: (0, 0, 0)),
            pl.BlockSpec((1, width, size), lambda j: (layer, 0, j)),
            pl.BlockSpec((up_bias.shape[0], size), lambda j: (0, j)),
            pl.BlockSpec((1, size, width), lambda j: (layer, j, 0)),
        ],
        out_specs=(
            pl.BlockSpec((rows, size), lambda j: (0, j)),
            pl.BlockSpec((rows, size), lambda j: (0, j)),
            whole,
            whole,
        ),
        scratch_shapes=[pltpu.VMEM((rows, width), BF)],
        cost_estimate=LONG,
        compiler_params=vmem_limit(30 * rows * width),
        name="feed_forward",
    )(unit_own, unit_other, gains, biases, up_weight, up_bias, down_weight)


def feed_back(low, slope, down_weight, up_weight, layer):
    rows, width = low.shape
    half = rows // 2
    hidden = slope.shape[1]
    size = hidden // 4

    def kernel(low_ref, slope_ref, down_ref, up_ref, pre_out, sums_out, own_out, send_out):
        @pl.when(pl.program_id(0) == 0)
        def _():
            own_out[...] = jnp.zeros_like(own_out)
            send_out[...] = jnp.zeros_like(send_out)

        grad = matmul_nt(low_ref[...], down_ref[0]) * slope_ref[...]
        sums_out[...] = jnp.sum(grad, axis=0, keepdims=True)
        grad_low = grad.astype(BF)
        pre_out[...] = grad_low
        send_out[...] += matmul_nt(grad_low[half:], up_ref[0])
        own_out[...] += matmul_nt(grad_low[:half], up_ref[0])

    piece = jax.ShapeDtypeStruct((half, width), F32)
    whole = pl.BlockSpec((half, width), lambda j: (0, 0))
    return pl.pallas_call(
        kernel,
        out_shape=(
            jax.ShapeDtypeStruct((rows, hidden), BF),
            jax.ShapeDtypeStruct((1, hidden), F32),
            piece,
            piece,
        ),
        grid=(hidden // size,),
        in_specs=[
            pl.BlockSpec((rows, width), lambda j: (0, 0)),
            pl.BlockSpec((rows, size), lambda j: (0, j)),
            pl.BlockSpec((1, size, width), lambda j: (layer, j, 0)),
            pl.BlockSpec((1, width, size), lambda j: (layer, 0, j)),
        ],
        out_specs=(
            pl.BlockSpec((rows, size), lambda j: (0, j)),
            pl.BlockSpec((1, size), lambda j: (0, j)),
            whole,
            whole,
        ),
        cost_estimate=LONG,
        compiler_params=vmem_limit(26 * rows * width),
        name="feed_back",
    )(low, slope, down_weight, up_weight)


def embed_terms(side_send, side_own, value_grad, key_grad, key_var, cell, patch, embed, key_weight):
    count, _ = side_send.shape
    flat_all, local_width = value_grad.shape
    head_count, flat = key_grad.shape
    model_width = patch.shape[1]
    lanes = -(-(flat_all + 1) // 128) * 128

    def kernel(send_ref, own_ref, value_ref, key_ref, var_ref, cell_ref, patch_ref, embed_ref, weight_ref,
               send_out, own_out, sum_out, query_out, bias_out, value_low_ref):
        scale = cell_ref[0:1, 0:1]
        value_low_ref[...] = (value_ref[...] * scale).astype(BF)
        bias_out[...] = jnp.sum(value_ref[flat:], axis=0, keepdims=True) * scale
        key_high, key_rest = two_part(key_ref[...] * scale)
        var_high, var_rest = two_part(var_ref[...] * scale)
        embed_high, embed_rest = two_part(embed_ref[...])
        total = matmul(key_high, patch_ref[...]) + matmul(key_rest, patch_ref[...])
        total = total + matmul(var_high, embed_high) + matmul(var_rest, embed_high)
        total = total + matmul(var_high, embed_rest)
        sum_out[...] = total
        high, rest = two_part(total)
        query = matmul(high, weight_ref[...]) + matmul(rest, weight_ref[...])
        head = lax.broadcasted_iota(jnp.int32, (head_count, local_width), 0)
        column = lax.broadcasted_iota(jnp.int32, (head_count, local_width), 1)
        inside = (column >= head * HEAD_DIM) & (column < (head + 1) * HEAD_DIM)
        query = jnp.sum(jnp.where(inside, query, 0.0), axis=0, keepdims=True) / ROOT_DIM
        query_out[...] = query
        query_high, query_rest = two_part(query)
        query_rows = jnp.concatenate(
            [query_high.astype(F32), query_rest.astype(F32), jnp.zeros((6, local_width), F32)], axis=0
        ).astype(BF)
        flat_rows, var_rows = [
            jnp.concatenate(
                [part.astype(F32) for part in (first, second, first, jnp.zeros_like(first))], axis=0
            ).astype(BF)
            for first, second in ((key_high, key_rest), (var_high, var_rest))
        ]
        for side_ref, out_ref in ((send_ref, send_out), (own_ref, own_out)):
            keys = side_ref[:, 2 * local_width :]
            values = side_ref[:, :local_width]
            weight = side_ref[:, local_width : 2 * local_width]
            out_ref[...] = jnp.zeros_like(out_ref)
            out_ref[:, :flat] = matmul_nt(values, value_low_ref[:flat]) + matmul(keys, flat_rows)
            out_ref[:, flat:flat_all] = matmul_nt(values, value_low_ref[flat:]) + matmul(keys, var_rows)
            part = matmul_nt(weight, query_rows)
            out_ref[:, flat_all : flat_all + 1] = jnp.sum(part, axis=1, keepdims=True)

    block = jax.ShapeDtypeStruct((count, lanes), F32)
    return pl.pallas_call(
        kernel,
        out_shape=(
            block,
            block,
            jax.ShapeDtypeStruct((head_count, model_width), F32),
            jax.ShapeDtypeStruct((1, local_width), F32),
            jax.ShapeDtypeStruct((1, local_width), F32),
        ),
        scratch_shapes=[pltpu.VMEM((flat_all, local_width), BF)],
        cost_estimate=LONG,
        compiler_params=vmem_limit(14 << 20),
        name="embed_terms",
    )(side_send, side_own, value_grad, key_grad, key_var, cell, patch, embed, key_weight)


def product_rows(pairs, scale, start, first, second, got=None):
    widths = [right.shape[1] for _, right in pairs]
    total = sum(widths)
    has_got = got is not None
    count = first + second
    size = 128 * PRODUCT_BLOCKS
    start, first, second, count = [n // PRODUCT_BLOCKS for n in (start, first, second, count)]

    def kernel(scale_ref, *refs):
        ins = refs[: 2 * len(pairs)]
        outs = refs[2 * len(pairs) + has_got :]
        step = pl.program_id(0)

        def fill(out_ref):
            column = 0
            for i, width in enumerate(widths):
                block = (
                    lax.dot_general(
                        ins[2 * i][...],
                        ins[2 * i + 1][...],
                        (((0,), (0,)), ((), ())),
                        preferred_element_type=F32,
                    )
                    * scale_ref[0:1, 0:1]
                )
                if has_got:
                    block = block + refs[2 * len(pairs)][:, column : column + width]
                out_ref[:, column : column + width] = block
                column += width

        if second:
            pl.when(step < first)(lambda: fill(outs[0]))
            pl.when(step >= first)(lambda: fill(outs[1]))
        else:
            fill(outs[0])

    in_specs = [pl.BlockSpec(scale.shape, lambda j: (0, 0))]
    operands = [scale]
    traffic = 0
    for left, right in pairs:
        rows = left.shape[0]
        in_specs.append(pl.BlockSpec((rows, size), lambda j: (0, start + j)))
        in_specs.append(pl.BlockSpec(right.shape, lambda j: (0, 0)))
        operands += [left, right]
        traffic += 2 * 2 * rows * (size + right.shape[1])
    if has_got:
        in_specs.append(pl.BlockSpec((size, total), lambda j: (j, 0)))
        operands.append(got)
    out_shape = [jax.ShapeDtypeStruct((first * size, total), F32)]
    out_specs = [pl.BlockSpec((size, total), lambda j: (jnp.minimum(j, first - 1), 0))]
    if second:
        out_shape.append(jax.ShapeDtypeStruct((second * size, total), F32))
        out_specs.append(pl.BlockSpec((size, total), lambda j: (jnp.maximum(j - first, 0), 0)))
    return pl.pallas_call(
        kernel,
        out_shape=out_shape,
        grid=(count,),
        in_specs=in_specs,
        out_specs=out_specs,
        cost_estimate=LONG,
        compiler_params=vmem_limit(traffic + 2 * 4 * size * total * 4),
        name="product_rows",
    )(*operands)


def add_split(keep, got):
    rows, width = keep.shape
    half = rows // 2
    size = min(128, half)
    count = half // size

    def kernel(keep_ref, got_ref, first_out, second_out):
        total = keep_ref[...] + got_ref[...]

        @pl.when(pl.program_id(0) < count)
        def _():
            first_out[...] = total

        @pl.when(pl.program_id(0) >= count)
        def _():
            second_out[...] = total

    block = (size, width)
    return pl.pallas_call(
        kernel,
        out_shape=[jax.ShapeDtypeStruct((half, width), F32)] * 2,
        grid=(2 * count,),
        in_specs=[pl.BlockSpec(block, lambda j: (j, 0))] * 2,
        out_specs=[
            pl.BlockSpec(block, lambda j: (jnp.minimum(j, count - 1), 0)),
            pl.BlockSpec(block, lambda j: (jnp.maximum(j - count, 0), 0)),
        ],
        cost_estimate=LONG,
        compiler_params=vmem_limit(32 * size * width),
        name="add_split",
    )(keep, got)


def attend_forward(unit_own, unit_other, gain, bias, weights, biases, out_weight):
    half, model_width = unit_own.shape
    rows = 2 * half
    local_width = weights.shape[2]
    head_count = local_width // HEAD_DIM

    def kernel(own_ref, other_ref, gain_ref, bias_ref, weight_ref, biases_ref, out_weight_ref,
               qkv_out, mixed_out, total_out, own_out, send_out, normed_ref):
        normed_ref[:half] = (own_ref[...] * gain_ref[...] + bias_ref[...]).astype(BF)
        normed_ref[half:] = (other_ref[...] * gain_ref[...] + bias_ref[...]).astype(BF)
        normed = normed_ref[...]
        qkv_out[:, :local_width] = (matmul(normed, weight_ref[0]) + biases_ref[0:1]).astype(BF)
        qkv_out[:, local_width : 2 * local_width] = matmul(normed, weight_ref[1]).astype(BF)
        qkv_out[:, 2 * local_width :] = (matmul(normed, weight_ref[2]) + biases_ref[1:2]).astype(BF)
        for head in range(head_count):
            one = slice(head * HEAD_DIM, (head + 1) * HEAD_DIM)
            query = qkv_out[:, one]
            key = qkv_out[:, local_width + head * HEAD_DIM : local_width + (head + 1) * HEAD_DIM]
            value = qkv_out[:, 2 * local_width + head * HEAD_DIM : 2 * local_width + (head + 1) * HEAD_DIM]
            scores = matmul_nt(query, key) / ROOT_DIM
            top = jnp.max(scores, axis=-1, keepdims=True)
            exponent = jnp.exp(scores - top)
            row_sum = jnp.sum(exponent, axis=-1, keepdims=True)
            attend = (exponent / row_sum).astype(BF)
            mixed_out[:, one] = matmul(attend, value).astype(BF)
            total_out[:, head : head + 1] = top + jnp.log(row_sum)
        send_out[...] = matmul(mixed_out[half:], out_weight_ref[...])
        own_out[...] = matmul(mixed_out[:half], out_weight_ref[...])

    piece = jax.ShapeDtypeStruct((half, model_width), F32)
    return pl.pallas_call(
        kernel,
        out_shape=(
            jax.ShapeDtypeStruct((rows, 3 * local_width), BF),
            jax.ShapeDtypeStruct((rows, local_width), BF),
            jax.ShapeDtypeStruct((rows, 128), F32),
            piece,
            piece,
        ),
        scratch_shapes=[pltpu.VMEM((rows, model_width), BF)],
        cost_estimate=pl.CostEstimate(
            flops=2 * rows * local_width * (4 * model_width + 2 * rows),
            bytes_accessed=8 * rows * model_width + 8 * local_width * model_width,
            transcendentals=rows * rows * head_count,
        ),
        compiler_params=vmem_limit(22 * rows * model_width),
        name="attend_forward",
    )(unit_own, unit_other, gain[None], bias[None], weights, biases, out_weight)


def attend_back(low, qkv, totals, weights, out_weight):
    rows, model_width = low.shape
    half = rows // 2
    local_width = weights.shape[2]
    head_count = local_width // HEAD_DIM

    def kernel(low_ref, qkv_ref, total_ref, weight_ref, out_weight_ref,
               grads_out, sums_out, own_out, send_out, mix_ref):
        mix_ref[...] = matmul_nt(low_ref[...], out_weight_ref[...]).astype(BF)
        for head in range(head_count):
            one = slice(head * HEAD_DIM, (head + 1) * HEAD_DIM)
            two = slice(local_width + head * HEAD_DIM, local_width + (head + 1) * HEAD_DIM)
            three = slice(2 * local_width + head * HEAD_DIM, 2 * local_width + (head + 1) * HEAD_DIM)
            query, key, value = qkv_ref[:, one], qkv_ref[:, two], qkv_ref[:, three]
            mix = mix_ref[:, one]
            attend = jnp.exp(matmul_nt(query, key) / ROOT_DIM - total_ref[:, head : head + 1])
            grad_attend = matmul_nt(mix, value)
            grad_value = matmul_tn(attend.astype(BF), mix)
            weighted = attend * grad_attend
            grad_scores = weighted - attend * jnp.sum(weighted, axis=-1, keepdims=True)
            grad_low = grad_scores.astype(BF)
            grad_query = matmul(grad_low, key) / ROOT_DIM
            grad_key = matmul_tn(grad_low, query) / ROOT_DIM
            grads_out[:, one] = grad_query.astype(BF)
            grads_out[:, two] = grad_key.astype(BF)
            grads_out[:, three] = grad_value.astype(BF)
            sums_out[0:1, one] = jnp.sum(grad_query, axis=0, keepdims=True)
            sums_out[1:2, one] = jnp.sum(grad_value, axis=0, keepdims=True)

        def pull(part):
            total = matmul_nt(grads_out[part, :local_width], weight_ref[0])
            total = total + matmul_nt(grads_out[part, local_width : 2 * local_width], weight_ref[1])
            return total + matmul_nt(grads_out[part, 2 * local_width :], weight_ref[2])

        send_out[...] = pull(slice(half, rows))
        own_out[...] = pull(slice(0, half))

    piece = jax.ShapeDtypeStruct((half, model_width), F32)
    return pl.pallas_call(
        kernel,
        out_shape=(
            jax.ShapeDtypeStruct((rows, 3 * local_width), BF),
            jax.ShapeDtypeStruct((2, local_width), F32),
            piece,
            piece,
        ),
        scratch_shapes=[pltpu.VMEM((rows, local_width), BF)],
        cost_estimate=LONG,
        compiler_params=vmem_limit(24 * rows * model_width),
        name="attend_back",
    )(low, qkv, totals, weights, out_weight)


def finish_layers(kind, pieces, cell, layer_count, shard, local_width):
    width = pieces[0].shape[1]
    shapes = {
        "down": [(layer_count, width, shard)],
        "up": [(layer_count, shard, width)],
        "att": [
            (layer_count, local_width, shard),
            (layer_count, 3, shard, local_width),
        ],
    }[kind]

    def store(values, outs):
        for layer, value in enumerate(values):
            if kind == "down":
                outs[0][layer] = value.T
            elif kind == "up":
                outs[0][layer] = value
            else:
                outs[0][layer] = value[:, :local_width].T
                for which in range(3):
                    begin = (1 + which) * local_width
                    outs[1][layer, which] = value[:, begin : begin + local_width]

    if shard % 128:
        values = pieces
        if kind == "down":
            return [jnp.stack([value.T for value in values])]
        if kind == "up":
            return [jnp.stack(values)]
        rest = [
            value[:, local_width:].reshape(shard, 3, local_width).transpose(1, 0, 2)
            for value in values
        ]
        return [jnp.stack([value[:, :local_width].T for value in values]), jnp.stack(rest)]

    def kernel(*refs):
        store([ref[...] for ref in refs[:layer_count]], refs[layer_count + 1 :])

    return pl.pallas_call(
        kernel,
        out_shape=[jax.ShapeDtypeStruct(shape, F32) for shape in shapes],
        cost_estimate=pl.CostEstimate(
            flops=layer_count * shard * width,
            bytes_accessed=12 * layer_count * shard * width,
            transcendentals=0,
        ),
        compiler_params=vmem_limit(20 * layer_count * shard * width),
        name="finish_layers",
    )(*pieces, cell)


def one_hot_segments(var_count, pix_count):
    flat = var_count * pix_count
    rows = lax.broadcasted_iota(jnp.int32, (var_count, flat), 0)
    columns = lax.broadcasted_iota(jnp.int32, (var_count, flat), 1)
    inside = (columns >= rows * pix_count) & (columns < (rows + 1) * pix_count)
    return jnp.where(inside, 1.0, 0.0).astype(BF)


def pool_front(core, pixels, patch, embed, query, query_weight, key_weight, value_weight,
               value_bias, mask, out_weight):
    var_count = embed.shape[0]
    flat, rows = pixels.shape
    pix_count = flat // var_count
    model_width, local_width = key_weight.shape
    head_count = local_width // HEAD_DIM
    half = rows // 2

    large = (query_weight, key_weight, pixels, patch, embed, value_weight, out_weight)

    def kernel(core_ref, query_ref, bias_ref, mask_ref, *refs):
        sources, refs = refs[: len(large)], refs[len(large) :]
        (low_out, query_out, key_out, score_out, flat_out, var_out, probs_out, pooled_out,
         own_out, send_out, turned_ref) = refs[:11]
        held, sems = refs[11 : 11 + len(large)], refs[11 + len(large)]
        copies = [
            pltpu.make_async_copy(source, target, sems.at[i])
            for i, (source, target) in enumerate(zip(sources, held))
        ]
        for copy in copies:
            copy.start()
        (query_weight_ref, key_weight_ref, pixels_ref, patch_ref, embed_ref, value_weight_ref,
         out_weight_ref) = held
        copies[0].wait()
        query = matmul(query_ref[...].astype(BF), query_weight_ref[...]).astype(BF)
        query_out[...] = query.astype(F32)
        copies[1].wait()
        for head in range(head_count):
            one = slice(head * HEAD_DIM, (head + 1) * HEAD_DIM)
            key_out[head : head + 1] = matmul_nt(query[:, one], key_weight_ref[:, one]) / ROOT_DIM
        copies[2].wait()
        turned_ref[...] = pixels_ref[...].T
        mine = pl.multiple_of(core_ref[0] * half, 8)
        theirs = pl.multiple_of(half - core_ref[0] * half, 8)
        low_out[:half] = turned_ref[pl.ds(mine, half)].astype(BF)
        low_out[half:] = turned_ref[pl.ds(theirs, half)].astype(BF)
        for copy in copies[3:]:
            copy.wait()
        key_high, key_rest = two_part(key_out[...])
        embed_high, embed_rest = two_part(embed_ref[...])
        score_out[...] = matmul_nt(key_high, patch_ref[...]) + matmul_nt(key_rest, patch_ref[...])
        score_var = (
            matmul_nt(key_high, embed_high)
            + matmul_nt(key_rest, embed_high)
            + matmul_nt(key_high, embed_rest)
        )
        flat_out[...] = matmul(patch_ref[...], value_weight_ref[...]).astype(BF)
        value_var = matmul(embed_high, value_weight_ref[...]) + matmul(embed_rest, value_weight_ref[...])
        var_out[...] = (value_var + bias_ref[...]).astype(BF)
        segment = one_hot_segments(var_count, pix_count)
        for head in range(head_count):
            one = slice(head * HEAD_DIM, (head + 1) * HEAD_DIM)
            pix = low_out[...].astype(F32)
            high, rest = two_part(pix * score_out[head : head + 1])
            scores = matmul_nt(high, segment) + matmul_nt(rest, segment) + score_var[head : head + 1]
            scores = jnp.where(mask_ref[...] > 0, scores, -1000000000.0)
            exponent = jnp.exp(scores - jnp.max(scores, axis=-1, keepdims=True))
            probs = exponent / jnp.sum(exponent, axis=-1, keepdims=True)
            probs_out[head] = probs
            low = probs.astype(BF)
            mixed = (matmul(low, segment) * pix).astype(BF)
            pooled_out[:, one] = (matmul(mixed, flat_out[:, one]) + matmul(low, var_out[:, one])).astype(BF)
        send_out[...] = matmul(pooled_out[half:], out_weight_ref[...])
        own_out[...] = matmul(pooled_out[:half], out_weight_ref[...])

    piece = jax.ShapeDtypeStruct((half, model_width), F32)
    return pl.pallas_call(
        kernel,
        out_shape=(
            jax.ShapeDtypeStruct((rows, flat), BF),
            jax.ShapeDtypeStruct((1, local_width), F32),
            jax.ShapeDtypeStruct((head_count, model_width), F32),
            jax.ShapeDtypeStruct((head_count, flat), F32),
            jax.ShapeDtypeStruct((flat, local_width), BF),
            jax.ShapeDtypeStruct((var_count, local_width), BF),
            jax.ShapeDtypeStruct((head_count, rows, var_count), F32),
            jax.ShapeDtypeStruct((rows, local_width), BF),
            piece,
            piece,
        ),
        in_specs=[pl.BlockSpec(memory_space=pltpu.SMEM)]
        + [pl.BlockSpec()] * 3
        + [pl.BlockSpec(memory_space=pltpu.HBM)] * len(large),
        scratch_shapes=[pltpu.VMEM((rows, flat), F32)]
        + [pltpu.VMEM(array.shape, array.dtype) for array in large]
        + [pltpu.SemaphoreType.DMA((len(large),))],
        cost_estimate=LONG,
        compiler_params=vmem_limit(46 << 20),
        name="pool_front",
    )(core, query, value_bias, mask, *large)


def pool_back(low, out_weight, value_flat, value_var, pix_low, probs, scores):
    rows, flat = pix_low.shape
    head_count, _, var_count = probs.shape
    pix_count = flat // var_count
    local_width = value_flat.shape[1]
    half = rows // 2

    def kernel(low_ref, out_weight_ref, flat_ref, var_ref, pix_ref, probs_ref, score_ref,
               value_out, key_out, key_var_out, own_out, send_out, pooled_ref, pixel_ref):
        pooled_ref[...] = matmul_nt(low_ref[...], out_weight_ref[...]).astype(BF)
        segment = one_hot_segments(var_count, pix_count)
        for head in range(head_count):
            one = slice(head * HEAD_DIM, (head + 1) * HEAD_DIM)
            pix = pix_ref[...].astype(F32)
            pooled = pooled_ref[:, one]
            pull = matmul_nt(pooled, flat_ref[:, one])
            high, rest = two_part(pull * pix)
            grad_probs = (
                matmul_nt(high, segment) + matmul_nt(rest, segment) + matmul_nt(pooled, var_ref[:, one])
            )
            probs_one = probs_ref[head]
            weighted = probs_one * grad_probs
            grad_scores = weighted - probs_one * jnp.sum(weighted, axis=-1, keepdims=True)
            high, rest = two_part(grad_scores)
            wide = matmul(high, segment) + matmul(rest, segment)
            key_out[head : head + 1] = jnp.sum(wide * pix, axis=0, keepdims=True)
            key_var_out[head : head + 1] = jnp.sum(grad_scores, axis=0, keepdims=True)
            probs_low = probs_one.astype(BF)
            probs_wide = matmul(probs_low, segment)
            term = wide * score_ref[head : head + 1] + probs_wide * pull
            if head:
                pixel_ref[...] += term
            else:
                pixel_ref[...] = term
            mixed = (probs_wide * pix).astype(BF)
            value_out[:flat, one] = matmul_tn(mixed, pooled)
            value_out[flat:, one] = matmul_tn(probs_low, pooled)
        own_out[...] = pixel_ref[:half]
        send_out[...] = pixel_ref[half:]

    piece = jax.ShapeDtypeStruct((half, flat), F32)
    return pl.pallas_call(
        kernel,
        out_shape=(
            jax.ShapeDtypeStruct((flat + var_count, local_width), F32),
            jax.ShapeDtypeStruct((head_count, flat), F32),
            jax.ShapeDtypeStruct((head_count, var_count), F32),
            piece,
            piece,
        ),
        scratch_shapes=[pltpu.VMEM((rows, local_width), BF), pltpu.VMEM((rows, flat), F32)],
        cost_estimate=LONG,
        compiler_params=vmem_limit(20 << 20),
        name="pool_back",
    )(low, out_weight, value_flat, value_var, pix_low, probs, scores)


class Links:
    def __init__(self, dp, mp):
        self.dp, self.mp = dp, mp
        self.dp_index = lax.axis_index("dp")
        self.mp_index = lax.axis_index("mp")

    def dp_bit(self, bit):
        return (self.dp_index >> bit) & 1

    def mp_bit(self, bit):
        return (self.mp_index >> bit) & 1

    def ordered_sum(self, clock, own, send):
        send = clock.one(send)
        got = exchange(send, "mp", self.mp, 0)
        clock.hold()
        mine = clock.one(own() + clock.one(got))
        last = bit_count(self.mp) - 1
        for bit in range(1, last):
            mine = clock.one(mine + exchange(mine, "mp", self.mp, bit))
        return mine, exchange(mine, "mp", self.mp, last)

    def begin_sum(self, own, send):
        mine = own + exchange(send, "mp", self.mp, 0)
        last = bit_count(self.mp) - 1
        for bit in range(1, last):
            mine = mine + exchange(mine, "mp", self.mp, bit)
        return mine, exchange(mine, "mp", self.mp, last)

    def begin_product(self, left, right, product=matmul):
        half = left.shape[0] // 2
        send = product(left[half:], right)
        return self.begin_sum(product(left[:half], right), send)

    def sum_rows(self, partial):
        half = partial.shape[0] // 2
        mine, got = self.begin_sum(partial[:half], partial[half:])
        return mine + got

    def other_rows(self, own):
        return exchange(own, "mp", self.mp, 0)

    def split_rows(self, tensor):
        half = tensor.shape[0] // 2
        core = self.mp_bit(0)
        own = lax.dynamic_slice_in_dim(tensor, core * half, half, 0)
        other = lax.dynamic_slice_in_dim(tensor, (1 - core) * half, half, 0)
        return own, other

    def global_rows(self, own, other):
        core = self.mp_bit(0)
        return jnp.concatenate(
            [jnp.where(core == 0, own, other), jnp.where(core == 0, other, own)], axis=0
        )

    def order(self, bits):
        masks = []
        for place in range(self.dp):
            mask = 0
            for i, bit in enumerate(bits):
                if not (place >> (len(bits) - 1 - i)) & 1:
                    mask |= 1 << bit
            masks.append(mask)
        return jnp.array(masks, jnp.int32) ^ self.dp_index


class Merge:
    def __init__(self, links, pairs, bits):
        self.links, self.pairs, self.bits = links, pairs, bits
        self.blocks = pairs[0][0].shape[1] // 128
        self.step = 0

    def advance(self, clock):
        if self.step == len(self.bits):
            self.total = clock.one(self.keep + clock.one(self.got))
            self.step += 1
            return
        got, pairs = None, self.pairs
        if self.step:
            got = clock.one(self.got)
        else:
            pairs = [(clock.one(pairs[0][0]), pairs[0][1])] + pairs[1:]
        if self.step == 0:
            send = product_rows(pairs, clock.cell, 0, self.blocks // 2, 0)[0]
        elif self.step == 1:
            send, self.keep = product_rows(
                pairs, clock.cell, self.blocks // 2, self.blocks // 4, self.blocks // 4, got
            )
        else:
            send, self.keep = add_split(self.keep, got)
        send = clock.one(send)
        self.got = exchange(send, "dp", self.links.dp, self.bits[self.step])
        self.step += 1

    @property
    def open(self):
        return self.step <= len(self.bits)


class ShardMerge:
    def __init__(self, links, shards):
        self.links, self.shards = links, shards
        self.step = 0

    def split(self, total):
        pairs = total.reshape((total.shape[0] // 2, 2) + total.shape[1:])
        own = self.links.dp_bit(self.step)
        self.keep = pick(pairs, own, 1)
        return pick(pairs, 1 - own, 1)

    def advance(self, clock):
        if self.step == bit_count(self.links.dp):
            self.total = clock.one(self.keep + clock.one(self.got))
            self.step += 1
            return
        total = self.shards
        if self.step:
            total = self.keep + clock.one(self.got)
        send = clock.one(self.split(clock.one(total)))
        self.got = exchange(send, "dp", self.links.dp, self.step)
        clock.hold()
        self.step += 1

    @property
    def open(self):
        return self.step <= bit_count(self.links.dp)


def norm_parts(rows):
    row_mean = jnp.mean(rows, axis=-1, keepdims=True)
    centred = rows - row_mean
    spread = jnp.mean(centred * centred, axis=-1, keepdims=True)
    inverse = lax.rsqrt(spread + 1e-05)
    return centred * inverse, jnp.broadcast_to(inverse, (rows.shape[0], 128))


def make_per_device(dp, mp):
    def per_device(
        pixels,
        dataset_id,
        variable_mask,
        lead_hours,
        token_counts,
        dataset_weight,
        patch_weight,
        variable_embed,
        position_embed,
        pool_query,
        pool_query_weight,
        pool_key_weight,
        pool_value_weight,
        pool_value_bias,
        pool_output_weight,
        pool_output_bias,
        lead_weight,
        lead_bias,
        norm_gain,
        norm_bias,
        attention_weight,
        attention_bias,
        output_weight,
        output_bias,
        up_weight,
        up_bias,
        down_weight,
        down_bias,
        cotangent,
    ):
        links = Links(dp, mp)
        var_count, pix_count, row_count = pixels.shape[1:]
        flat_count = var_count * pix_count
        model_width = patch_weight.shape[2]
        local_width = pool_query_weight.shape[1]
        head_count = local_width // HEAD_DIM
        layer_count = attention_weight.shape[0]
        shard = model_width // dp

        def heads_first(tensor):
            return tensor.reshape(row_count, head_count, HEAD_DIM).transpose(1, 0, 2)

        def heads_last(tensor):
            return tensor.transpose(1, 0, 2).reshape(row_count, local_width)

        dataset_pick = jnp.arange(variable_mask.shape[0], dtype=jnp.int32) == dataset_id[0]
        mask_row = jnp.sum(jnp.where(dataset_pick[:, None], variable_mask, 0), axis=0)
        item_weight = jnp.sum(jnp.where(dataset_pick, dataset_weight, 0)).astype(F32)
        own_count = token_counts[0].astype(F32)
        lead_scale = lead_hours[0].astype(F32) / 24.0

        patch_flat = patch_weight.reshape(flat_count, model_width)
        (
            pix_low,
            query_row,
            key_rows,
            score_rows,
            value_flat,
            value_var,
            pool_probs,
            pooled,
            part_own,
            part_send,
        ) = pool_front(
            links.mp_bit(0).reshape(1),
            pixels[0].reshape(flat_count, row_count),
            patch_flat,
            variable_embed,
            pool_query[None],
            pool_query_weight,
            pool_key_weight,
            pool_value_weight,
            pool_value_bias[None],
            mask_row[None],
            pool_output_weight,
        )
        mine, got = links.begin_sum(part_own, part_send)
        count_total = after(jnp.full((8, 128), own_count, F32), mine)
        for bit in range(bit_count(dp)):
            count_total = count_total + exchange(count_total, "dp", dp, bit)
        scale_cell = item_weight * own_count / count_total
        item_scale = scale_cell[0, 0]
        position_own = links.split_rows(position_embed)[0]
        offset_rows = pool_output_bias + position_own + lead_scale * lead_weight + lead_bias
        mine, scale_cell = lax.optimization_barrier((mine, scale_cell))
        hidden = mine + got + offset_rows

        bits = list(range(bit_count(dp)))
        bits_late = bits[1:] + bits[:1]
        shards, shards_late = links.order(bits), links.order(bits_late)
        top = layer_count - 1
        kept = []
        for layer in range(layer_count):
            unit_one, inverse_one = norm_parts(hidden)
            unit_other = links.other_rows(unit_one)
            qkv, mixed, totals, part_own, part_send = attend_forward(
                unit_one,
                unit_other,
                norm_gain[layer, 0],
                norm_bias[layer, 0],
                attention_weight[layer],
                attention_bias[layer],
                output_weight[layer],
            )
            mine, got = links.begin_sum(part_own, part_send)
            normed = norm_rows(
                after(unit_one, mine), unit_other, norm_gain[layer, 0], norm_bias[layer, 0], shards
            )
            mine, normed = lax.optimization_barrier((mine, normed))
            if layer == 0:
                grad_own, grad_other = links.split_rows(after(cotangent[0], mine))
                grad_other, down_low, down_left = merge_rows(
                    grad_own, grad_other, jnp.zeros_like(grad_other), shards_late
                )
                mine, down_low = lax.optimization_barrier((mine, down_low))
            hidden = hidden + (mine + got) + output_bias[layer]
            unit_two, inverse_two = norm_parts(hidden)
            unit_other = links.other_rows(unit_two)
            activation, slope, part_own, part_send = feed_forward(
                unit_two,
                unit_other,
                norm_gain,
                norm_bias,
                (layer, 1),
                up_weight,
                up_bias,
                down_weight,
            )
            marker = activation
            if layer < top:
                mine, got = links.begin_sum(part_own, part_send)
                marker = mine
            normed_two = norm_rows(
                after(unit_two, marker), unit_other, norm_gain[layer, 1], norm_bias[layer, 1], shards
            )
            if layer < top:
                if layer == 0:
                    embed_high, embed_rest = two_part(variable_embed)
                    embed_all = jnp.concatenate([patch_flat, embed_high, embed_rest], axis=0)
                    mine, embed_all = lax.optimization_barrier((mine, embed_all))
                    embed_left = take_columns(embed_all, shards, shard)
                    key_high, key_rest = two_part(key_rows)
                    left_side = jnp.concatenate(
                        [
                            pool_value_weight,
                            pool_query_weight,
                            jnp.concatenate(
                                [key_high, key_high, key_rest, jnp.zeros_like(key_high)], axis=0
                            ).T,
                        ],
                        axis=1,
                    )
                    sides = left_side.reshape(dp, mp, shard // mp, left_side.shape[1])
                    mp_bits = range(bit_count(mp))
                    masks = [
                        sum((1 - ((i >> (len(mp_bits) - 1 - b)) & 1)) << b for b in mp_bits)
                        for i in range(mp)
                    ]
                    sides = jnp.stack(
                        [pick(sides, links.mp_index ^ mask, 1) for mask in masks]
                    ).reshape(2, model_width // 2, left_side.shape[1])
                    side_send, side_own = sides[0], sides[1]
                    mine, embed_left, side_own, side_send = lax.optimization_barrier(
                        (mine, embed_left, side_own, side_send)
                    )
                mine, normed_two = lax.optimization_barrier((mine, normed_two))
                hidden = hidden + (mine + got) + down_bias[layer]
            kept.append(
                (
                    unit_one,
                    inverse_one,
                    normed,
                    qkv,
                    totals,
                    mixed,
                    unit_two,
                    inverse_two,
                    normed_two,
                    slope,
                    activation,
                )
            )

        last_own, last_send = part_own, part_send
        row_sums = {}
        local_sums = {}
        merges = {}
        row_sums["down_bias", top] = jnp.sum(grad_own, axis=0)

        head_of = jnp.arange(local_width, dtype=jnp.int32) // HEAD_DIM
        head_pick = head_of[:, None] == jnp.arange(head_count, dtype=jnp.int32)[None, :]
        clock = Clock(scale_cell)

        def advance(spot):
            for name in PLAN.get(spot, ()):
                if name in merges and merges[name].open:
                    merges[name].advance(clock)

        for layer in reversed(range(layer_count)):
            depth = top - layer
            (
                unit_one,
                inverse_one,
                normed,
                qkv,
                totals,
                mixed,
                unit_two,
                inverse_two,
                normed_two,
                slope,
                activation,
            ) = kept[layer]
            merges["down", depth] = Merge(
                links, [(down_left, activation)], bits if depth else bits_late
            )
            advance(("top", depth))
            pre_low, up_sums, part_own, part_send = feed_back(
                clock.one(down_low), slope, down_weight, up_weight, layer
            )
            local_sums["up_bias", layer] = up_sums[0]
            pre_low, part_send = clock.both(pre_low, part_send)
            merges["up", depth] = Merge(links, [(normed_two, pre_low)], bits)
            advance(("pre", depth))
            mine, got = links.ordered_sum(clock, lambda: part_own, part_send)
            if not PLAN.get(("wait_two", depth)):
                clock.hold()
            advance(("wait_two", depth))
            if layer == top:
                last_send = clock.one(last_send)
                last_other = exchange(last_send, "mp", mp, 0)
                clock.hold()
                last_mine = clock.one(last_own + clock.one(last_other))
            mine, got = clock.both(mine, got)
            if layer == top:
                for bit in range(1, bit_count(mp)):
                    last_mine = clock.one(last_mine)
                    last_other = exchange(last_mine, "mp", mp, bit)
                    if bit + 1 < bit_count(mp):
                        last_mine = last_mine + last_other
            change, grad_own, sums = norm_back(
                mine, got, unit_two, inverse_two, norm_gain, (layer, 1), grad_own
            )
            change, sums = clock.both(change, sums)
            row_sums["gain", layer, 1] = sums[0]
            row_sums["bias", layer, 1] = sums[1]
            row_sums["out_bias", layer] = sums[2]
            other_change = links.other_rows(change)
            clock.hold()
            grad_other, out_low, out_left = merge_rows(
                grad_own, grad_other, clock.one(other_change), shards
            )
            out_low = clock.one(out_low)
            advance(("mid", depth))
            grads, qv_sums, part_own, part_send = attend_back(
                clock.one(out_low), qkv, totals, attention_weight[layer], output_weight[layer]
            )
            local_sums["qv", layer] = qv_sums
            mine, got = links.ordered_sum(clock, lambda: part_own, part_send)
            if not PLAN.get(("wait_one", depth)):
                clock.hold()
            merges["att", depth] = Merge(links, [(out_left, mixed), (normed, grads)], bits)
            advance(("wait_one", depth))
            if layer == top:
                hidden = clock.one(hidden + (last_mine + clock.one(last_other)) + down_bias[top])
                hidden_other = links.other_rows(hidden)
                clock.hold()
                layer_out = clock.one(links.global_rows(hidden, clock.one(hidden_other)))
            mine, got = clock.both(mine, got)
            change, grad_own, sums = norm_back(
                mine, got, unit_one, inverse_one, norm_gain, (layer, 0), grad_own
            )
            change, sums = clock.both(change, sums)
            row_sums["gain", layer, 0] = sums[0]
            row_sums["bias", layer, 0] = sums[1]
            if layer:
                row_sums["down_bias", layer - 1] = sums[2]
            other_change = links.other_rows(change)
            clock.hold()
            grad_other, down_low, down_left = merge_rows(
                grad_own, grad_other, clock.one(other_change), shards
            )
            down_low = clock.one(down_low)
            advance(("end", depth))
            down_low = clock.one(down_low)

        row_sums["column"] = sums[2]
        row_sums["lead"] = lead_scale * sums[2]
        clock.hold()
        value_grad, key_grad, key_grad_var, pixel_own, pixel_send = pool_back(
            clock.one(down_low), pool_output_weight, value_flat, value_var, pix_low, pool_probs, score_rows
        )
        flat_all = flat_count + var_count
        item_scale = clock.cell[0, 0]
        sub = shard // mp
        embed_send, embed_own, summed_key, query_grad, pool_bias = embed_terms(
            side_send,
            side_own,
            clock.one(value_grad),
            key_grad,
            key_grad_var,
            clock.cell,
            patch_flat,
            variable_embed,
            pool_key_weight,
        )
        embed_all, embed_left = clock.both(embed_all, embed_left)
        value_low = value_grad.astype(BF)
        merges["tail"] = Merge(
            links,
            [
                (down_left, pooled),
                (embed_left, jnp.concatenate([value_low, value_low[flat_count:]], axis=0)),
            ],
            bits,
        )
        query_grad = query_grad[0]
        embed_send = clock.one(embed_send)
        embed_got = exchange(embed_send, "mp", mp, 0)
        clock.hold()
        embed_got = clock.one(embed_got)
        for bit in range(1, bit_count(mp)):
            embed_send, embed_own = add_split(embed_own, embed_got)
            embed_send = clock.one(embed_send)
            embed_got = exchange(embed_send, "mp", mp, bit)
        advance("back")
        lanes = embed_own.shape[1]

        names = []
        for layer in range(layer_count):
            names += [("gain", layer, 0), ("gain", layer, 1), ("bias", layer, 0), ("bias", layer, 1)]
        for layer in range(layer_count):
            names += [("out_bias", layer), ("down_bias", layer)]
        names += ["column", "lead"]
        own_sums = clock.one(jnp.stack([row_sums[name] for name in names]) * item_scale)
        other_sums = exchange(own_sums, "mp", mp, 0)
        clock.hold()
        full_sums = own_sums + clock.one(other_sums)
        local = jnp.stack([local_sums["up_bias", layer] for layer in range(layer_count)]) * item_scale
        thin = [local_sums["qv", layer] for layer in range(layer_count)]
        thin = jnp.concatenate([jnp.concatenate(thin, axis=0) * item_scale, pool_bias], axis=0)
        packed = jnp.concatenate(
            [
                full_sums.reshape(len(names), dp, shard).transpose(1, 0, 2).reshape(dp, -1),
                summed_key.reshape(head_count, dp, shard).transpose(1, 0, 2).reshape(dp, -1),
                local.reshape(layer_count, dp, -1).transpose(1, 0, 2).reshape(dp, -1),
                thin.reshape(2 * layer_count + 1, dp, -1).transpose(1, 0, 2).reshape(dp, -1),
                jnp.broadcast_to(query_grad[None, :], (dp, local_width)),
            ],
            axis=1,
        )
        packed_size = packed.shape[1]
        packed_rows = -(-packed_size // 1024) * 8
        packed = jnp.pad(packed, ((0, 0), (0, packed_rows * 128 - packed_size)))
        packed = packed.reshape(dp, packed_rows, 128)
        position = (grad_own * item_scale).reshape(row_count // 2, dp, shard).transpose(1, 0, 2)
        position, packed = clock.both(position, packed)
        advance("vectors")
        embed_grad = (embed_own + clock.one(embed_got)).reshape(dp, sub, lanes)
        lane_blocks = lanes // 128
        if shard == 128:
            tall = jnp.concatenate(
                [embed_grad[:, :, i * 128 : (i + 1) * 128] for i in range(lane_blocks)]
                + [packed, position],
                axis=1,
            )
            merges["small"] = ShardMerge(links, tall)
        else:
            merges["small"] = ShardMerge(
                links,
                jnp.concatenate(
                    [part.reshape(dp, 1, -1) for part in (embed_grad, packed, position)], axis=2
                ),
            )
        advance("small")

        pixel_mine, pixel_got = links.ordered_sum(clock, lambda: pixel_own, pixel_send)
        clock.hold()
        advance("values")
        pixel_mine, pixel_got = clock.both(pixel_mine, pixel_got)
        pixel_mine = clock.one(pixel_mine + pixel_got)
        pixel_other = links.other_rows(pixel_mine)
        clock.hold()
        advance("pixels")
        pixel_grad = links.global_rows(pixel_mine, clock.one(pixel_other))
        pixel_grad = clock.one(pixel_grad.T.reshape(1, var_count, pix_count, row_count))
        advance("rows")
        for name in DRAIN:
            if merges[name].open:
                merges[name].advance(clock)
        for merge in merges.values():
            while merge.open:
                merge.advance(clock)
        finished = {}
        for kind in ("down", "up", "att"):
            parts = [merges[kind, top - layer].total for layer in range(layer_count)]
            finished[kind] = finish_layers(
                kind, parts, clock.cell, layer_count, shard, local_width
            )
        tail_total = merges["tail"].total
        small = merges["small"].total[0]
        if shard == 128:
            embed_rows = sub * lane_blocks
            embed_grad = jnp.concatenate(
                [small[i * sub : (i + 1) * sub] for i in range(lane_blocks)], axis=1
            )
            packed = small[embed_rows : embed_rows + packed_rows].reshape(-1)
            position = small[embed_rows + packed_rows :]
        else:
            size = sub * lane_blocks * 128
            embed_grad = small[0, :size].reshape(sub, lane_blocks * 128)
            packed = small[0, size : size + packed_rows * 128]
            position = small[0, size + packed_rows * 128 :].reshape(row_count // 2, shard)
        packed, position, _ = lax.optimization_barrier((packed, position, clock.cell))
        position = links.global_rows(position, links.other_rows(position))
        offset = 0

        def take(*shape):
            nonlocal offset
            size = math.prod(shape)
            piece = packed[offset : offset + size].reshape(shape)
            offset += size
            return piece

        gains = take(layer_count, 2, shard)
        biases = []
        gain_list = []
        offset = 0
        norm_all = take(layer_count, 2, 2, shard)
        gain_list = norm_all[:, 0]
        biases = norm_all[:, 1]
        dense_bias = take(layer_count, 2, shard)
        column_total = take(shard)
        lead_total = take(shard)
        key_shard = take(head_count, shard)
        up_bias_total = take(layer_count, local.shape[1] // dp)
        thin_total = take(2 * layer_count + 1, local_width // dp)
        query_total = take(local_width)

        query_low = pool_query.astype(BF)
        query_rows = lax.dynamic_slice_in_dim(query_low, links.dp_index * shard, shard, 0)
        query_weight_grad = query_rows.astype(F32)[:, None] * query_total[None, :]
        key_weight_grad = (
            jnp.repeat(key_shard.T, HEAD_DIM, axis=1) * query_row / ROOT_DIM
        )
        embed_turned = embed_grad.T
        return (
            layer_out[None],
            pixel_grad,
            embed_turned[:flat_count].reshape(var_count, pix_count, sub),
            embed_turned[flat_count:flat_all],
            position,
            embed_turned[flat_all],
            query_weight_grad,
            key_weight_grad,
            tail_total[:, local_width:],
            thin_total[-1],
            tail_total[:, :local_width].T,
            column_total,
            lead_total,
            column_total,
            gain_list,
            biases,
            finished["att"][1],
            thin_total[:-1].reshape(layer_count, 2, local_width // dp),
            finished["att"][0],
            dense_bias[:, 0],
            finished["up"][0],
            up_bias_total,
            finished["down"][0],
            dense_bias[:, 1],
        )

    return per_device


def solution(mesh):
    return jax.shard_map(
        make_per_device(mesh.shape["dp"], mesh.shape["mp"]),
        mesh=mesh,
        in_specs=(
            P("dp", None, None, None),
            P("dp"),
            P(),
            P("dp"),
            P("dp"),
            P(),
            P(),
            P(),
            P(),
            P(),
            P(None, "mp"),
            P(None, "mp"),
            P(None, "mp"),
            P("mp"),
            P("mp", None),
            P(),
            P(),
            P(),
            P(),
            P(),
            P(None, None, None, "mp"),
            P(None, None, "mp"),
            P(None, "mp", None),
            P(),
            P(None, None, "mp"),
            P(None, "mp"),
            P(None, "mp", None),
            P(),
            P("dp", None, None),
        ),
        out_specs=(
            P("dp", None, None),
            P("dp", None, None, None),
            P(None, None, ("dp", "mp")),
            P(None, ("dp", "mp")),
            P(None, "dp"),
            P(("dp", "mp")),
            P("dp", "mp"),
            P("dp", "mp"),
            P("dp", "mp"),
            P(("mp", "dp")),
            P("mp", "dp"),
            P("dp"),
            P("dp"),
            P("dp"),
            P(None, None, "dp"),
            P(None, None, "dp"),
            P(None, None, "dp", "mp"),
            P(None, None, ("mp", "dp")),
            P(None, "mp", "dp"),
            P(None, "dp"),
            P(None, "dp", "mp"),
            P(None, ("mp", "dp")),
            P(None, "mp", "dp"),
            P(None, "dp"),
        ),
        check_vma=False,
    )
```

```python
import math

import jax
import jax.numpy as jnp
from jax import lax
from jax.experimental import pallas as pl
from jax.experimental.pallas import tpu as pltpu
from jax.sharding import PartitionSpec as P

HEAD_DIM = 64
PLAN = {
    ("top", 0): [("down", 0)],
    ("pre", 0): [("up", 0)],
    ("wait_one", 0): [("att", 0), ("down", 0), ("up", 0)],
    ("wait_two", 1): [("down", 1), ("up", 0)],
    ("mid", 1): [("down", 0), ("att", 0)],
    ("wait_one", 1): [("up", 0), ("up", 1), ("att", 0), ("down", 1)],
    ("end", 1): [("down", 0), ("att", 1)],
    "back": [("down", 1), ("att", 0), ("up", 1)],
    "small": ["small"],
    "values": ["tail", ("down", 1), ("up", 1), ("att", 1)],
    "pixels": ["small", ("up", 1), "tail", ("att", 1)],
    "rows": ["small", ("att", 1), "tail", "small", "tail"],
}
DRAIN = []
ROOT_DIM = math.sqrt(HEAD_DIM)
PRODUCT_BLOCKS = 2
BF = jnp.bfloat16
F32 = jnp.float32


def matmul(left, right):
    return jnp.dot(left, right, preferred_element_type=F32)


def matmul_tn(left, right):
    return lax.dot_general(left, right, (((0,), (0,)), ((), ())), preferred_element_type=F32)


def matmul_nt(left, right):
    return lax.dot_general(left, right, (((1,), (1,)), ((), ())), preferred_element_type=F32)


def two_part(tensor):
    high = tensor.astype(BF)
    return high, (tensor - high.astype(F32)).astype(BF)


def gelu_exact(pre_act):
    return jax.nn.gelu(pre_act, approximate=False)


def bit_count(size):
    bits = size.bit_length() - 1
    assert 1 << bits == size
    return bits


def exchange(tensor, axis, size, bit):
    return lax.ppermute(tensor, axis, [(i, i ^ (1 << bit)) for i in range(size)])


def pick(tensor, index, axis):
    return lax.dynamic_index_in_dim(tensor, index, axis, keepdims=False)


def after(value, *earlier):
    return lax.optimization_barrier((value,) + earlier)[0]


def vmem_limit(size):
    return pltpu.CompilerParams(vmem_limit_bytes=int(size * 1.25) + (2 << 20))


LONG = pl.CostEstimate(flops=10**12, bytes_accessed=8, transcendentals=0)


def step_cell(cell):
    def kernel(cell_ref, out_ref):
        out_ref[...] = cell_ref[...]

    return pl.pallas_call(
        kernel,
        out_shape=jax.ShapeDtypeStruct(cell.shape, F32),
        cost_estimate=LONG,
        compiler_params=vmem_limit(0),
        name="step_cell",
    )(cell)


class Clock:
    def __init__(self, cell):
        self.cell = cell

    def both(self, *values):
        *values, self.cell = lax.optimization_barrier((*values, self.cell))
        return values

    def one(self, value):
        return self.both(value)[0]

    def hold(self):
        self.cell = step_cell(self.cell)


def ordered_columns(source, target, shards_ref, count, shard):
    for place in range(count):
        column = pl.multiple_of(shards_ref[place] * shard, shard)
        target[:, place * shard : (place + 1) * shard] = source[:, pl.ds(column, shard)]


def take_columns(rows, shards, shard):
    pieces = rows.reshape(rows.shape[0], -1, shard)[:, shards]
    return pieces.reshape(rows.shape)


def norm_rows(own, other, gain, bias, shards):
    half, width = own.shape
    count = shards.shape[0]
    shard = width // count
    if shard % 128:
        rows = jnp.concatenate([own, other], axis=0) * gain + bias
        return take_columns(rows.astype(BF), shards, shard)

    def kernel(shards_ref, own_ref, other_ref, gain_ref, bias_ref, out_ref, low_ref):
        low_ref[:half] = (own_ref[...] * gain_ref[...] + bias_ref[...]).astype(BF)
        low_ref[half:] = (other_ref[...] * gain_ref[...] + bias_ref[...]).astype(BF)
        ordered_columns(low_ref, out_ref, shards_ref, count, shard)

    return pl.pallas_call(
        kernel,
        out_shape=jax.ShapeDtypeStruct((2 * half, width), BF),
        in_specs=[pl.BlockSpec(memory_space=pltpu.SMEM)] + [pl.BlockSpec()] * 4,
        scratch_shapes=[pltpu.VMEM((2 * half, width), BF)],
        cost_estimate=pl.CostEstimate(
            flops=4 * half * width, bytes_accessed=12 * half * width, transcendentals=0
        ),
        compiler_params=vmem_limit(16 * half * width),
        name="norm_rows",
    )(shards, own, other, gain[None], bias[None])


def embed_columns(patch, embed, shards):
    flat, width = patch.shape
    var_count = embed.shape[0]
    count = shards.shape[0]
    shard = width // count
    if shard % 128:
        high, rest = two_part(embed)
        return take_columns(jnp.concatenate([patch, high, rest], axis=0), shards, shard)

    def kernel(shards_ref, patch_ref, embed_ref, out_ref):
        for place in range(count):
            column = pl.ds(pl.multiple_of(shards_ref[place] * shard, shard), shard)
            target = slice(place * shard, (place + 1) * shard)
            high, rest = two_part(embed_ref[:, column])
            out_ref[:flat, target] = patch_ref[:, column]
            out_ref[flat : flat + var_count, target] = high
            out_ref[flat + var_count :, target] = rest

    return pl.pallas_call(
        kernel,
        out_shape=jax.ShapeDtypeStruct((flat + 2 * var_count, width), BF),
        in_specs=[pl.BlockSpec(memory_space=pltpu.SMEM)] + [pl.BlockSpec()] * 2,
        compiler_params=vmem_limit(8 << 20),
        name="embed_columns",
    )(shards, patch, embed)


def merge_rows(own, other, change, shards):
    half, width = own.shape
    count = shards.shape[0]
    shard = width // count
    if shard % 128:
        total = other + change
        low = jnp.concatenate([own, total], axis=0).astype(BF)
        return total, low, take_columns(low, shards, shard)

    def kernel(shards_ref, own_ref, other_ref, change_ref, other_out, low_out, ordered_out):
        low_out[:half] = own_ref[...].astype(BF)
        total = other_ref[...] + change_ref[...]
        other_out[...] = total
        low_out[half:] = total.astype(BF)
        ordered_columns(low_out, ordered_out, shards_ref, count, shard)

    return pl.pallas_call(
        kernel,
        out_shape=(
            jax.ShapeDtypeStruct((half, width), F32),
            jax.ShapeDtypeStruct((2 * half, width), BF),
            jax.ShapeDtypeStruct((2 * half, width), BF),
        ),
        in_specs=[pl.BlockSpec(memory_space=pltpu.SMEM)] + [pl.BlockSpec()] * 3,
        cost_estimate=LONG,
        compiler_params=vmem_limit(26 * half * width),
        name="merge_rows",
    )(shards, own, other, change)


def norm_back(mine, got, unit, inverse, gains, place, grad):
    half, width = mine.shape
    size = half

    def kernel(mine_ref, got_ref, unit_ref, inverse_ref, gain_ref, grad_ref, change_out, grad_out, sums_out):
        pull = mine_ref[...] + got_ref[...]
        unit_rows = unit_ref[...]
        scaled = pull * gain_ref[place[0], place[1] : place[1] + 1]
        first = jnp.mean(scaled, axis=-1, keepdims=True)
        second = jnp.mean(scaled * unit_rows, axis=-1, keepdims=True)
        change = inverse_ref[:, :1] * (scaled - first - unit_rows * second)
        change_out[...] = change
        total = grad_ref[...] + change
        grad_out[...] = total

        @pl.when(pl.program_id(0) == 0)
        def _():
            sums_out[...] = jnp.zeros_like(sums_out)

        sums_out[0:1] += jnp.sum(pull * unit_rows, axis=0, keepdims=True)
        sums_out[1:2] += jnp.sum(pull, axis=0, keepdims=True)
        sums_out[2:3] += jnp.sum(total, axis=0, keepdims=True)

    rows = jax.ShapeDtypeStruct((half, width), F32)
    block = pl.BlockSpec((size, width), lambda j: (j, 0))
    return pl.pallas_call(
        kernel,
        out_shape=(rows, rows, jax.ShapeDtypeStruct((3, width), F32)),
        grid=(half // size,),
        in_specs=[
            block,
            block,
            block,
            pl.BlockSpec((size, 128), lambda j: (j, 0)),
            pl.BlockSpec(gains.shape, lambda j: (0, 0, 0)),
            block,
        ],
        out_specs=(block, block, pl.BlockSpec((3, width), lambda j: (0, 0))),
        cost_estimate=LONG,
        compiler_params=vmem_limit(64 * size * width),
        name="norm_back",
    )(mine, got, unit, inverse, gains, grad)


def feed_forward(unit_own, unit_other, gains, biases, place, up_weight, up_bias, down_weight):
    half, width = unit_own.shape
    rows = 2 * half
    layer, which = place
    hidden = up_weight.shape[2]
    size = hidden // 4
    spread_of = math.sqrt(2.0)
    peak = 1.0 / math.sqrt(2.0 * math.pi)

    def kernel(own_ref, other_ref, gain_ref, bias_ref, up_ref, up_bias_ref, down_ref,
               activation_out, slope_out, own_out, send_out, normed_ref):
        step = pl.program_id(0)

        @pl.when(step == 0)
        def _():
            gain = gain_ref[layer, which : which + 1]
            bias = bias_ref[layer, which : which + 1]
            normed_ref[:half] = (own_ref[...] * gain + bias).astype(BF)
            normed_ref[half:] = (other_ref[...] * gain + bias).astype(BF)
            own_out[...] = jnp.zeros_like(own_out)
            send_out[...] = jnp.zeros_like(send_out)

        pre = matmul(normed_ref[...], up_ref[0]) + up_bias_ref[layer : layer + 1]
        below = 0.5 + 0.5 * lax.erf(pre / spread_of)
        slope_out[...] = below + pre * (jnp.exp(-0.5 * pre * pre) * peak)
        activation = (pre * below).astype(BF)
        activation_out[...] = activation
        send_out[...] += matmul(activation[half:], down_ref[0])
        own_out[...] += matmul(activation[:half], down_ref[0])

    piece = jax.ShapeDtypeStruct((half, width), F32)
    whole = pl.BlockSpec((half, width), lambda j: (0, 0))
    return pl.pallas_call(
        kernel,
        out_shape=(
            jax.ShapeDtypeStruct((rows, hidden), BF),
            jax.ShapeDtypeStruct((rows, hidden), F32),
            piece,
            piece,
        ),
        grid=(hidden // size,),
        in_specs=[
            whole,
            whole,
            pl.BlockSpec(gains.shape, lambda j: (0, 0, 0)),
            pl.BlockSpec(biases.shape, lambda j: (0, 0, 0)),
            pl.BlockSpec((1, width, size), lambda j: (layer, 0, j)),
            pl.BlockSpec((up_bias.shape[0], size), lambda j: (0, j)),
            pl.BlockSpec((1, size, width), lambda j: (layer, j, 0)),
        ],
        out_specs=(
            pl.BlockSpec((rows, size), lambda j: (0, j)),
            pl.BlockSpec((rows, size), lambda j: (0, j)),
            whole,
            whole,
        ),
        scratch_shapes=[pltpu.VMEM((rows, width), BF)],
        cost_estimate=LONG,
        compiler_params=vmem_limit(44 << 20),
        name="feed_forward",
    )(unit_own, unit_other, gains, biases, up_weight, up_bias, down_weight)


def feed_back(low, slope, down_weight, up_weight, layer):
    rows, width = low.shape
    half = rows // 2
    hidden = slope.shape[1]
    size = hidden // 4

    def kernel(low_ref, slope_ref, down_ref, up_ref, pre_out, sums_out, own_out, send_out):
        @pl.when(pl.program_id(0) == 0)
        def _():
            own_out[...] = jnp.zeros_like(own_out)
            send_out[...] = jnp.zeros_like(send_out)

        grad = matmul_nt(low_ref[...], down_ref[0]) * slope_ref[...]
        sums_out[...] = jnp.sum(grad, axis=0, keepdims=True)
        grad_low = grad.astype(BF)
        pre_out[...] = grad_low
        send_out[...] += matmul_nt(grad_low[half:], up_ref[0])
        own_out[...] += matmul_nt(grad_low[:half], up_ref[0])

    piece = jax.ShapeDtypeStruct((half, width), F32)
    whole = pl.BlockSpec((half, width), lambda j: (0, 0))
    return pl.pallas_call(
        kernel,
        out_shape=(
            jax.ShapeDtypeStruct((rows, hidden), BF),
            jax.ShapeDtypeStruct((1, hidden), F32),
            piece,
            piece,
        ),
        grid=(hidden // size,),
        in_specs=[
            pl.BlockSpec((rows, width), lambda j: (0, 0)),
            pl.BlockSpec((rows, size), lambda j: (0, j)),
            pl.BlockSpec((1, size, width), lambda j: (layer, j, 0)),
            pl.BlockSpec((1, width, size), lambda j: (layer, 0, j)),
        ],
        out_specs=(
            pl.BlockSpec((rows, size), lambda j: (0, j)),
            pl.BlockSpec((1, size), lambda j: (0, j)),
            whole,
            whole,
        ),
        cost_estimate=LONG,
        compiler_params=vmem_limit(26 * rows * width),
        name="feed_back",
    )(low, slope, down_weight, up_weight)


def embed_terms(side_send, side_own, value_grad, key_grad, key_var, cell, patch, embed, key_weight):
    count, _ = side_send.shape
    flat_all, local_width = value_grad.shape
    head_count, flat = key_grad.shape
    model_width = patch.shape[1]
    lanes = -(-(flat_all + 1) // 128) * 128

    def kernel(send_ref, own_ref, value_ref, key_ref, var_ref, cell_ref, patch_ref, embed_ref, weight_ref,
               send_out, own_out, sum_out, query_out, bias_out, value_low_ref):
        scale = cell_ref[0:1, 0:1]
        value_low_ref[...] = (value_ref[...] * scale).astype(BF)
        bias_out[...] = jnp.sum(value_ref[flat:], axis=0, keepdims=True) * scale
        key_high, key_rest = two_part(key_ref[...] * scale)
        var_high, var_rest = two_part(var_ref[...] * scale)
        embed_high, embed_rest = two_part(embed_ref[...])
        total = matmul(key_high, patch_ref[...]) + matmul(key_rest, patch_ref[...])
        total = total + matmul(var_high, embed_high) + matmul(var_rest, embed_high)
        total = total + matmul(var_high, embed_rest)
        sum_out[...] = total
        high, rest = two_part(total)
        query = matmul(high, weight_ref[...]) + matmul(rest, weight_ref[...])
        head = lax.broadcasted_iota(jnp.int32, (head_count, local_width), 0)
        column = lax.broadcasted_iota(jnp.int32, (head_count, local_width), 1)
        inside = (column >= head * HEAD_DIM) & (column < (head + 1) * HEAD_DIM)
        query = jnp.sum(jnp.where(inside, query, 0.0), axis=0, keepdims=True) / ROOT_DIM
        query_out[...] = query
        query_high, query_rest = two_part(query)
        query_rows = jnp.concatenate(
            [query_high.astype(F32), query_rest.astype(F32), jnp.zeros((6, local_width), F32)], axis=0
        ).astype(BF)
        flat_rows, var_rows = [
            jnp.concatenate(
                [part.astype(F32) for part in (first, second, first, jnp.zeros_like(first))], axis=0
            ).astype(BF)
            for first, second in ((key_high, key_rest), (var_high, var_rest))
        ]
        for side_ref, out_ref in ((send_ref, send_out), (own_ref, own_out)):
            keys = side_ref[:, 2 * local_width :]
            values = side_ref[:, :local_width]
            weight = side_ref[:, local_width : 2 * local_width]
            out_ref[...] = jnp.zeros_like(out_ref)
            out_ref[:, :flat] = matmul_nt(values, value_low_ref[:flat]) + matmul(keys, flat_rows)
            out_ref[:, flat:flat_all] = matmul_nt(values, value_low_ref[flat:]) + matmul(keys, var_rows)
            part = matmul_nt(weight, query_rows)
            out_ref[:, flat_all : flat_all + 1] = jnp.sum(part, axis=1, keepdims=True)

    block = jax.ShapeDtypeStruct((count, lanes), F32)
    return pl.pallas_call(
        kernel,
        out_shape=(
            block,
            block,
            jax.ShapeDtypeStruct((head_count, model_width), F32),
            jax.ShapeDtypeStruct((1, local_width), F32),
            jax.ShapeDtypeStruct((1, local_width), F32),
        ),
        scratch_shapes=[pltpu.VMEM((flat_all, local_width), BF)],
        cost_estimate=LONG,
        compiler_params=vmem_limit(14 << 20),
        name="embed_terms",
    )(side_send, side_own, value_grad, key_grad, key_var, cell, patch, embed, key_weight)


def product_rows(pairs, scale, start, first, second, got=None):
    widths = [right.shape[1] for _, right in pairs]
    total = sum(widths)
    has_got = got is not None
    count = first + second
    size = 128 * PRODUCT_BLOCKS
    start, first, second, count = [n // PRODUCT_BLOCKS for n in (start, first, second, count)]

    def kernel(scale_ref, *refs):
        ins = refs[: 2 * len(pairs)]
        outs = refs[2 * len(pairs) + has_got :]
        step = pl.program_id(0)

        def fill(out_ref):
            column = 0
            for i, width in enumerate(widths):
                block = (
                    lax.dot_general(
                        ins[2 * i][...],
                        ins[2 * i + 1][...],
                        (((0,), (0,)), ((), ())),
                        preferred_element_type=F32,
                    )
                    * scale_ref[0:1, 0:1]
                )
                if has_got:
                    block = block + refs[2 * len(pairs)][:, column : column + width]
                out_ref[:, column : column + width] = block
                column += width

        if second:
            pl.when(step < first)(lambda: fill(outs[0]))
            pl.when(step >= first)(lambda: fill(outs[1]))
        else:
            fill(outs[0])

    in_specs = [pl.BlockSpec(scale.shape, lambda j: (0, 0))]
    operands = [scale]
    traffic = 0
    for left, right in pairs:
        rows = left.shape[0]
        in_specs.append(pl.BlockSpec((rows, size), lambda j: (0, start + j)))
        in_specs.append(pl.BlockSpec(right.shape, lambda j: (0, 0)))
        operands += [left, right]
        traffic += 2 * 2 * rows * (size + right.shape[1])
    if has_got:
        in_specs.append(pl.BlockSpec((size, total), lambda j: (j, 0)))
        operands.append(got)
    out_shape = [jax.ShapeDtypeStruct((first * size, total), F32)]
    out_specs = [pl.BlockSpec((size, total), lambda j: (jnp.minimum(j, first - 1), 0))]
    if second:
        out_shape.append(jax.ShapeDtypeStruct((second * size, total), F32))
        out_specs.append(pl.BlockSpec((size, total), lambda j: (jnp.maximum(j - first, 0), 0)))
    return pl.pallas_call(
        kernel,
        out_shape=out_shape,
        grid=(count,),
        in_specs=in_specs,
        out_specs=out_specs,
        cost_estimate=LONG,
        compiler_params=vmem_limit(traffic + 2 * 4 * size * total * 4),
        name="product_rows",
    )(*operands)


def add_rows(own, got):
    rows, width = own.shape
    size = rows // 2

    def kernel(own_ref, got_ref, out_ref):
        out_ref[...] = own_ref[...] + got_ref[...]

    block = pl.BlockSpec((size, width), lambda j: (j, 0))
    return pl.pallas_call(
        kernel,
        out_shape=jax.ShapeDtypeStruct((rows, width), F32),
        grid=(rows // size,),
        in_specs=[block, block],
        out_specs=block,
        cost_estimate=LONG,
        compiler_params=vmem_limit(32 * size * width),
        name="add_rows",
    )(own, got)


def add_split(keep, got):
    rows, width = keep.shape
    half = rows // 2
    size = min(128, half)
    count = half // size

    def kernel(keep_ref, got_ref, first_out, second_out):
        total = keep_ref[...] + got_ref[...]

        @pl.when(pl.program_id(0) < count)
        def _():
            first_out[...] = total

        @pl.when(pl.program_id(0) >= count)
        def _():
            second_out[...] = total

    block = (size, width)
    return pl.pallas_call(
        kernel,
        out_shape=[jax.ShapeDtypeStruct((half, width), F32)] * 2,
        grid=(2 * count,),
        in_specs=[pl.BlockSpec(block, lambda j: (j, 0))] * 2,
        out_specs=[
            pl.BlockSpec(block, lambda j: (jnp.minimum(j, count - 1), 0)),
            pl.BlockSpec(block, lambda j: (jnp.maximum(j - count, 0), 0)),
        ],
        cost_estimate=LONG,
        compiler_params=vmem_limit(32 * size * width),
        name="add_split",
    )(keep, got)


def attend_forward(unit_own, unit_other, gain, bias, weights, biases, out_weight):
    half, model_width = unit_own.shape
    rows = 2 * half
    local_width = weights.shape[2]
    head_count = local_width // HEAD_DIM

    def kernel(own_ref, other_ref, gain_ref, bias_ref, weight_ref, biases_ref, out_weight_ref,
               qkv_out, mixed_out, total_out, own_out, send_out, normed_ref):
        normed_ref[:half] = (own_ref[...] * gain_ref[...] + bias_ref[...]).astype(BF)
        normed_ref[half:] = (other_ref[...] * gain_ref[...] + bias_ref[...]).astype(BF)
        normed = normed_ref[...]
        qkv_out[:, :local_width] = (matmul(normed, weight_ref[0]) + biases_ref[0:1]).astype(BF)
        qkv_out[:, local_width : 2 * local_width] = matmul(normed, weight_ref[1]).astype(BF)
        qkv_out[:, 2 * local_width :] = (matmul(normed, weight_ref[2]) + biases_ref[1:2]).astype(BF)
        for head in range(head_count):
            one = slice(head * HEAD_DIM, (head + 1) * HEAD_DIM)
            query = qkv_out[:, one]
            key = qkv_out[:, local_width + head * HEAD_DIM : local_width + (head + 1) * HEAD_DIM]
            value = qkv_out[:, 2 * local_width + head * HEAD_DIM : 2 * local_width + (head + 1) * HEAD_DIM]
            scores = matmul_nt(query, key) / ROOT_DIM
            top = jnp.max(scores, axis=-1, keepdims=True)
            exponent = jnp.exp(scores - top)
            row_sum = jnp.sum(exponent, axis=-1, keepdims=True)
            attend = (exponent / row_sum).astype(BF)
            mixed_out[:, one] = matmul(attend, value).astype(BF)
            total_out[:, head : head + 1] = top + jnp.log(row_sum)
        send_out[...] = matmul(mixed_out[half:], out_weight_ref[...])
        own_out[...] = matmul(mixed_out[:half], out_weight_ref[...])

    piece = jax.ShapeDtypeStruct((half, model_width), F32)
    return pl.pallas_call(
        kernel,
        out_shape=(
            jax.ShapeDtypeStruct((rows, 3 * local_width), BF),
            jax.ShapeDtypeStruct((rows, local_width), BF),
            jax.ShapeDtypeStruct((rows, 128), F32),
            piece,
            piece,
        ),
        scratch_shapes=[pltpu.VMEM((rows, model_width), BF)],
        cost_estimate=pl.CostEstimate(
            flops=2 * rows * local_width * (4 * model_width + 2 * rows),
            bytes_accessed=8 * rows * model_width + 8 * local_width * model_width,
            transcendentals=rows * rows * head_count,
        ),
        compiler_params=vmem_limit(22 * rows * model_width),
        name="attend_forward",
    )(unit_own, unit_other, gain[None], bias[None], weights, biases, out_weight)


def attend_back(low, qkv, totals, weights, out_weight):
    rows, model_width = low.shape
    half = rows // 2
    local_width = weights.shape[2]
    head_count = local_width // HEAD_DIM

    def kernel(low_ref, qkv_ref, total_ref, weight_ref, out_weight_ref,
               grads_out, sums_out, own_out, send_out, mix_ref):
        mix_ref[...] = matmul_nt(low_ref[...], out_weight_ref[...]).astype(BF)
        for head in range(head_count):
            one = slice(head * HEAD_DIM, (head + 1) * HEAD_DIM)
            two = slice(local_width + head * HEAD_DIM, local_width + (head + 1) * HEAD_DIM)
            three = slice(2 * local_width + head * HEAD_DIM, 2 * local_width + (head + 1) * HEAD_DIM)
            query, key, value = qkv_ref[:, one], qkv_ref[:, two], qkv_ref[:, three]
            mix = mix_ref[:, one]
            attend = jnp.exp(matmul_nt(query, key) / ROOT_DIM - total_ref[:, head : head + 1])
            grad_attend = matmul_nt(mix, value)
            grad_value = matmul_tn(attend.astype(BF), mix)
            weighted = attend * grad_attend
            grad_scores = weighted - attend * jnp.sum(weighted, axis=-1, keepdims=True)
            grad_low = grad_scores.astype(BF)
            grad_query = matmul(grad_low, key) / ROOT_DIM
            grad_key = matmul_tn(grad_low, query) / ROOT_DIM
            grads_out[:, one] = grad_query.astype(BF)
            grads_out[:, two] = grad_key.astype(BF)
            grads_out[:, three] = grad_value.astype(BF)
            sums_out[0:1, one] = jnp.sum(grad_query, axis=0, keepdims=True)
            sums_out[1:2, one] = jnp.sum(grad_value, axis=0, keepdims=True)

        def pull(part):
            total = matmul_nt(grads_out[part, :local_width], weight_ref[0])
            total = total + matmul_nt(grads_out[part, local_width : 2 * local_width], weight_ref[1])
            return total + matmul_nt(grads_out[part, 2 * local_width :], weight_ref[2])

        send_out[...] = pull(slice(half, rows))
        own_out[...] = pull(slice(0, half))

    piece = jax.ShapeDtypeStruct((half, model_width), F32)
    return pl.pallas_call(
        kernel,
        out_shape=(
            jax.ShapeDtypeStruct((rows, 3 * local_width), BF),
            jax.ShapeDtypeStruct((2, local_width), F32),
            piece,
            piece,
        ),
        scratch_shapes=[pltpu.VMEM((rows, local_width), BF)],
        cost_estimate=LONG,
        compiler_params=vmem_limit(24 * rows * model_width),
        name="attend_back",
    )(low, qkv, totals, weights, out_weight)


def finish_layers(kind, pieces, cell, layer_count, shard, local_width):
    width = pieces[0].shape[1]
    shapes = {
        "down": [(layer_count, width, shard)],
        "up": [(layer_count, shard, width)],
        "att": [
            (layer_count, local_width, shard),
            (layer_count, 3, shard, local_width),
        ],
    }[kind]

    def store(values, outs):
        for layer, value in enumerate(values):
            if kind == "down":
                outs[0][layer] = value.T
            elif kind == "up":
                outs[0][layer] = value
            else:
                outs[0][layer] = value[:, :local_width].T
                for which in range(3):
                    begin = (1 + which) * local_width
                    outs[1][layer, which] = value[:, begin : begin + local_width]

    if shard % 128:
        values = pieces
        if kind == "down":
            return [jnp.stack([value.T for value in values])]
        if kind == "up":
            return [jnp.stack(values)]
        rest = [
            value[:, local_width:].reshape(shard, 3, local_width).transpose(1, 0, 2)
            for value in values
        ]
        return [jnp.stack([value[:, :local_width].T for value in values]), jnp.stack(rest)]

    def kernel(*refs):
        store([ref[...] for ref in refs[:layer_count]], refs[layer_count + 1 :])

    return pl.pallas_call(
        kernel,
        out_shape=[jax.ShapeDtypeStruct(shape, F32) for shape in shapes],
        cost_estimate=pl.CostEstimate(
            flops=layer_count * shard * width,
            bytes_accessed=12 * layer_count * shard * width,
            transcendentals=0,
        ),
        compiler_params=vmem_limit(20 * layer_count * shard * width),
        name="finish_layers",
    )(*pieces, cell)


def one_hot_segments(var_count, pix_count):
    flat = var_count * pix_count
    rows = lax.broadcasted_iota(jnp.int32, (var_count, flat), 0)
    columns = lax.broadcasted_iota(jnp.int32, (var_count, flat), 1)
    inside = (columns >= rows * pix_count) & (columns < (rows + 1) * pix_count)
    return jnp.where(inside, 1.0, 0.0).astype(BF)


def pool_front(core, pixels, patch, embed, query, query_weight, key_weight, value_weight,
               value_bias, mask, out_weight):
    var_count = embed.shape[0]
    flat, rows = pixels.shape
    pix_count = flat // var_count
    model_width, local_width = key_weight.shape
    head_count = local_width // HEAD_DIM
    half = rows // 2

    large = (query_weight, key_weight, pixels, patch, embed, value_weight, out_weight)

    def kernel(core_ref, query_ref, bias_ref, mask_ref, *refs):
        sources, refs = refs[: len(large)], refs[len(large) :]
        (low_out, query_out, key_out, score_out, flat_out, var_out, probs_out, pooled_out,
         own_out, send_out, turned_ref) = refs[:11]
        held, sems = refs[11 : 11 + len(large)], refs[11 + len(large)]
        copies = [
            pltpu.make_async_copy(source, target, sems.at[i])
            for i, (source, target) in enumerate(zip(sources, held))
        ]
        for copy in copies:
            copy.start()
        (query_weight_ref, key_weight_ref, pixels_ref, patch_ref, embed_ref, value_weight_ref,
         out_weight_ref) = held
        copies[0].wait()
        query = matmul(query_ref[...].astype(BF), query_weight_ref[...]).astype(BF)
        query_out[...] = query.astype(F32)
        copies[1].wait()
        for head in range(head_count):
            one = slice(head * HEAD_DIM, (head + 1) * HEAD_DIM)
            key_out[head : head + 1] = matmul_nt(query[:, one], key_weight_ref[:, one]) / ROOT_DIM
        copies[2].wait()
        turned_ref[...] = pixels_ref[...].T
        mine = pl.multiple_of(core_ref[0] * half, 8)
        theirs = pl.multiple_of(half - core_ref[0] * half, 8)
        low_out[:half] = turned_ref[pl.ds(mine, half)].astype(BF)
        low_out[half:] = turned_ref[pl.ds(theirs, half)].astype(BF)
        for copy in copies[3:]:
            copy.wait()
        key_high, key_rest = two_part(key_out[...])
        embed_high, embed_rest = two_part(embed_ref[...])
        score_out[...] = matmul_nt(key_high, patch_ref[...]) + matmul_nt(key_rest, patch_ref[...])
        score_var = (
            matmul_nt(key_high, embed_high)
            + matmul_nt(key_rest, embed_high)
            + matmul_nt(key_high, embed_rest)
        )
        flat_out[...] = matmul(patch_ref[...], value_weight_ref[...]).astype(BF)
        value_var = matmul(embed_high, value_weight_ref[...]) + matmul(embed_rest, value_weight_ref[...])
        var_out[...] = (value_var + bias_ref[...]).astype(BF)
        segment = one_hot_segments(var_count, pix_count)
        for head in range(head_count):
            one = slice(head * HEAD_DIM, (head + 1) * HEAD_DIM)
            pix = low_out[...].astype(F32)
            high, rest = two_part(pix * score_out[head : head + 1])
            scores = matmul_nt(high, segment) + matmul_nt(rest, segment) + score_var[head : head + 1]
            scores = jnp.where(mask_ref[...] > 0, scores, -1000000000.0)
            exponent = jnp.exp(scores - jnp.max(scores, axis=-1, keepdims=True))
            probs = exponent / jnp.sum(exponent, axis=-1, keepdims=True)
            probs_out[head] = probs
            low = probs.astype(BF)
            mixed = (matmul(low, segment) * pix).astype(BF)
            pooled_out[:, one] = (matmul(mixed, flat_out[:, one]) + matmul(low, var_out[:, one])).astype(BF)
        send_out[...] = matmul(pooled_out[half:], out_weight_ref[...])
        own_out[...] = matmul(pooled_out[:half], out_weight_ref[...])

    piece = jax.ShapeDtypeStruct((half, model_width), F32)
    return pl.pallas_call(
        kernel,
        out_shape=(
            jax.ShapeDtypeStruct((rows, flat), BF),
            jax.ShapeDtypeStruct((1, local_width), F32),
            jax.ShapeDtypeStruct((head_count, model_width), F32),
            jax.ShapeDtypeStruct((head_count, flat), F32),
            jax.ShapeDtypeStruct((flat, local_width), BF),
            jax.ShapeDtypeStruct((var_count, local_width), BF),
            jax.ShapeDtypeStruct((head_count, rows, var_count), F32),
            jax.ShapeDtypeStruct((rows, local_width), BF),
            piece,
            piece,
        ),
        in_specs=[pl.BlockSpec(memory_space=pltpu.SMEM)]
        + [pl.BlockSpec()] * 3
        + [pl.BlockSpec(memory_space=pltpu.HBM)] * len(large),
        scratch_shapes=[pltpu.VMEM((rows, flat), F32)]
        + [pltpu.VMEM(array.shape, array.dtype) for array in large]
        + [pltpu.SemaphoreType.DMA((len(large),))],
        cost_estimate=LONG,
        compiler_params=vmem_limit(46 << 20),
        name="pool_front",
    )(core, query, value_bias, mask, *large)


def pool_back(low, out_weight, value_flat, value_var, pix_low, probs, scores):
    rows, flat = pix_low.shape
    head_count, _, var_count = probs.shape
    pix_count = flat // var_count
    local_width = value_flat.shape[1]
    half = rows // 2

    def kernel(low_ref, out_weight_ref, flat_ref, var_ref, pix_ref, probs_ref, score_ref,
               value_out, key_out, key_var_out, own_out, send_out, pooled_ref, pixel_ref):
        pooled_ref[...] = matmul_nt(low_ref[...], out_weight_ref[...]).astype(BF)
        segment = one_hot_segments(var_count, pix_count)
        for head in range(head_count):
            one = slice(head * HEAD_DIM, (head + 1) * HEAD_DIM)
            pix = pix_ref[...].astype(F32)
            pooled = pooled_ref[:, one]
            pull = matmul_nt(pooled, flat_ref[:, one])
            high, rest = two_part(pull * pix)
            grad_probs = (
                matmul_nt(high, segment) + matmul_nt(rest, segment) + matmul_nt(pooled, var_ref[:, one])
            )
            probs_one = probs_ref[head]
            weighted = probs_one * grad_probs
            grad_scores = weighted - probs_one * jnp.sum(weighted, axis=-1, keepdims=True)
            high, rest = two_part(grad_scores)
            wide = matmul(high, segment) + matmul(rest, segment)
            key_out[head : head + 1] = jnp.sum(wide * pix, axis=0, keepdims=True)
            key_var_out[head : head + 1] = jnp.sum(grad_scores, axis=0, keepdims=True)
            probs_low = probs_one.astype(BF)
            probs_wide = matmul(probs_low, segment)
            term = wide * score_ref[head : head + 1] + probs_wide * pull
            if head:
                pixel_ref[...] += term
            else:
                pixel_ref[...] = term
            mixed = (probs_wide * pix).astype(BF)
            value_out[:flat, one] = matmul_tn(mixed, pooled)
            value_out[flat:, one] = matmul_tn(probs_low, pooled)
        own_out[...] = pixel_ref[:half]
        send_out[...] = pixel_ref[half:]

    piece = jax.ShapeDtypeStruct((half, flat), F32)
    return pl.pallas_call(
        kernel,
        out_shape=(
            jax.ShapeDtypeStruct((flat + var_count, local_width), F32),
            jax.ShapeDtypeStruct((head_count, flat), F32),
            jax.ShapeDtypeStruct((head_count, var_count), F32),
            piece,
            piece,
        ),
        scratch_shapes=[pltpu.VMEM((rows, local_width), BF), pltpu.VMEM((rows, flat), F32)],
        cost_estimate=LONG,
        compiler_params=vmem_limit(20 << 20),
        name="pool_back",
    )(low, out_weight, value_flat, value_var, pix_low, probs, scores)


class Links:
    def __init__(self, dp, mp):
        self.dp, self.mp = dp, mp
        self.dp_index = lax.axis_index("dp")
        self.mp_index = lax.axis_index("mp")

    def dp_bit(self, bit):
        return (self.dp_index >> bit) & 1

    def mp_bit(self, bit):
        return (self.mp_index >> bit) & 1

    def ordered_sum(self, clock, own, send):
        send = clock.one(send)
        got = exchange(send, "mp", self.mp, 0)
        clock.hold()
        mine = clock.one(add_rows(own(), clock.one(got)))
        last = bit_count(self.mp) - 1
        for bit in range(1, last):
            mine = clock.one(mine + exchange(mine, "mp", self.mp, bit))
        return mine, exchange(mine, "mp", self.mp, last)

    def begin_sum(self, own, send):
        mine = add_rows(own, exchange(send, "mp", self.mp, 0))
        last = bit_count(self.mp) - 1
        for bit in range(1, last):
            mine = mine + exchange(mine, "mp", self.mp, bit)
        return mine, exchange(mine, "mp", self.mp, last)

    def begin_product(self, left, right, product=matmul):
        half = left.shape[0] // 2
        send = product(left[half:], right)
        return self.begin_sum(product(left[:half], right), send)

    def sum_rows(self, partial):
        half = partial.shape[0] // 2
        mine, got = self.begin_sum(partial[:half], partial[half:])
        return mine + got

    def other_rows(self, own):
        return exchange(own, "mp", self.mp, 0)

    def split_rows(self, tensor):
        half = tensor.shape[0] // 2
        core = self.mp_bit(0)
        own = lax.dynamic_slice_in_dim(tensor, core * half, half, 0)
        other = lax.dynamic_slice_in_dim(tensor, (1 - core) * half, half, 0)
        return own, other

    def global_rows(self, own, other):
        core = self.mp_bit(0)
        return jnp.concatenate(
            [jnp.where(core == 0, own, other), jnp.where(core == 0, other, own)], axis=0
        )

    def order(self, bits):
        masks = []
        for place in range(self.dp):
            mask = 0
            for i, bit in enumerate(bits):
                if not (place >> (len(bits) - 1 - i)) & 1:
                    mask |= 1 << bit
            masks.append(mask)
        return jnp.array(masks, jnp.int32) ^ self.dp_index


class Merge:
    def __init__(self, links, pairs, bits):
        self.links, self.pairs, self.bits = links, pairs, bits
        self.blocks = pairs[0][0].shape[1] // 128
        self.step = 0

    def advance(self, clock):
        if self.step == len(self.bits):
            self.total = clock.one(self.keep + clock.one(self.got))
            self.step += 1
            return
        got, pairs = None, self.pairs
        if self.step:
            got = clock.one(self.got)
        else:
            pairs = [(clock.one(pairs[0][0]), pairs[0][1])] + pairs[1:]
        if self.step == 0:
            send = product_rows(pairs, clock.cell, 0, self.blocks // 2, 0)[0]
        elif self.step == 1:
            send, self.keep = product_rows(
                pairs, clock.cell, self.blocks // 2, self.blocks // 4, self.blocks // 4, got
            )
        else:
            send, self.keep = add_split(self.keep, got)
        send = clock.one(send)
        self.got = exchange(send, "dp", self.links.dp, self.bits[self.step])
        self.step += 1

    @property
    def open(self):
        return self.step <= len(self.bits)


class ShardMerge:
    def __init__(self, links, shards):
        self.links, self.shards = links, shards
        self.step = 0

    def split(self, total):
        pairs = total.reshape((total.shape[0] // 2, 2) + total.shape[1:])
        own = self.links.dp_bit(self.step)
        self.keep = pick(pairs, own, 1)
        return pick(pairs, 1 - own, 1)

    def advance(self, clock):
        if self.step == bit_count(self.links.dp):
            self.total = clock.one(self.keep + clock.one(self.got))
            self.step += 1
            return
        total = self.shards
        if self.step:
            total = self.keep + clock.one(self.got)
        send = clock.one(self.split(clock.one(total)))
        self.got = exchange(send, "dp", self.links.dp, self.step)
        clock.hold()
        self.step += 1

    @property
    def open(self):
        return self.step <= bit_count(self.links.dp)


def norm_parts(rows):
    row_mean = jnp.mean(rows, axis=-1, keepdims=True)
    centred = rows - row_mean
    spread = jnp.mean(centred * centred, axis=-1, keepdims=True)
    inverse = lax.rsqrt(spread + 1e-05)
    return centred * inverse, jnp.broadcast_to(inverse, (rows.shape[0], 128))


def make_per_device(dp, mp):
    def per_device(
        pixels,
        dataset_id,
        variable_mask,
        lead_hours,
        token_counts,
        dataset_weight,
        patch_weight,
        variable_embed,
        position_embed,
        pool_query,
        pool_query_weight,
        pool_key_weight,
        pool_value_weight,
        pool_value_bias,
        pool_output_weight,
        pool_output_bias,
        lead_weight,
        lead_bias,
        norm_gain,
        norm_bias,
        attention_weight,
        attention_bias,
        output_weight,
        output_bias,
        up_weight,
        up_bias,
        down_weight,
        down_bias,
        cotangent,
    ):
        links = Links(dp, mp)
        var_count, pix_count, row_count = pixels.shape[1:]
        flat_count = var_count * pix_count
        model_width = patch_weight.shape[2]
        local_width = pool_query_weight.shape[1]
        head_count = local_width // HEAD_DIM
        layer_count = attention_weight.shape[0]
        shard = model_width // dp

        def heads_first(tensor):
            return tensor.reshape(row_count, head_count, HEAD_DIM).transpose(1, 0, 2)

        def heads_last(tensor):
            return tensor.transpose(1, 0, 2).reshape(row_count, local_width)

        dataset_pick = jnp.arange(variable_mask.shape[0], dtype=jnp.int32) == dataset_id[0]
        mask_row = jnp.sum(jnp.where(dataset_pick[:, None], variable_mask, 0), axis=0)
        item_weight = jnp.sum(jnp.where(dataset_pick, dataset_weight, 0)).astype(F32)
        own_count = token_counts[0].astype(F32)
        lead_scale = lead_hours[0].astype(F32) / 24.0

        patch_flat = patch_weight.reshape(flat_count, model_width)
        (
            pix_low,
            query_row,
            key_rows,
            score_rows,
            value_flat,
            value_var,
            pool_probs,
            pooled,
            part_own,
            part_send,
        ) = pool_front(
            links.mp_bit(0).reshape(1),
            pixels[0].reshape(flat_count, row_count),
            patch_flat,
            variable_embed,
            pool_query[None],
            pool_query_weight,
            pool_key_weight,
            pool_value_weight,
            pool_value_bias[None],
            mask_row[None],
            pool_output_weight,
        )
        mine, got = links.begin_sum(part_own, part_send)
        count_total = after(jnp.full((8, 128), own_count, F32), mine)
        for bit in range(bit_count(dp)):
            count_total = count_total + exchange(count_total, "dp", dp, bit)
        scale_cell = item_weight * own_count / count_total
        item_scale = scale_cell[0, 0]
        position_own = links.split_rows(position_embed)[0]
        offset_rows = pool_output_bias + position_own + lead_scale * lead_weight + lead_bias
        mine, scale_cell = lax.optimization_barrier((mine, scale_cell))
        hidden = mine + got + offset_rows

        bits = list(range(bit_count(dp)))
        bits_late = bits[1:] + bits[:1]
        shards, shards_late = links.order(bits), links.order(bits_late)
        top = layer_count - 1
        kept = []
        for layer in range(layer_count):
            unit_one, inverse_one = norm_parts(hidden)
            unit_other = links.other_rows(unit_one)
            qkv, mixed, totals, part_own, part_send = attend_forward(
                unit_one,
                unit_other,
                norm_gain[layer, 0],
                norm_bias[layer, 0],
                attention_weight[layer],
                attention_bias[layer],
                output_weight[layer],
            )
            mine, got = links.begin_sum(part_own, part_send)
            normed = norm_rows(
                after(unit_one, mine), unit_other, norm_gain[layer, 0], norm_bias[layer, 0], shards
            )
            mine, normed = lax.optimization_barrier((mine, normed))
            if layer == 0:
                grad_own, grad_other = links.split_rows(after(cotangent[0], mine))
                grad_other, down_low, down_left = merge_rows(
                    grad_own, grad_other, jnp.zeros_like(grad_other), shards_late
                )
                mine, down_low = lax.optimization_barrier((mine, down_low))
            hidden = hidden + (mine + got) + output_bias[layer]
            unit_two, inverse_two = norm_parts(hidden)
            unit_other = links.other_rows(unit_two)
            activation, slope, part_own, part_send = feed_forward(
                unit_two,
                unit_other,
                norm_gain,
                norm_bias,
                (layer, 1),
                up_weight,
                up_bias,
                down_weight,
            )
            marker = activation
            if layer < top:
                mine, got = links.begin_sum(part_own, part_send)
                marker = mine
            normed_two = norm_rows(
                after(unit_two, marker), unit_other, norm_gain[layer, 1], norm_bias[layer, 1], shards
            )
            if layer < top:
                if layer == 0:
                    mine, embed_late, key_late = lax.optimization_barrier(
                        (mine, variable_embed, key_rows)
                    )
                    embed_left = embed_columns(patch_flat, embed_late, shards)
                    key_high, key_rest = two_part(key_late)
                    left_side = jnp.concatenate(
                        [
                            pool_value_weight,
                            pool_query_weight,
                            jnp.concatenate(
                                [key_high, key_high, key_rest, jnp.zeros_like(key_high)], axis=0
                            ).T,
                        ],
                        axis=1,
                    )
                    sides = left_side.reshape(dp, mp, shard // mp, left_side.shape[1])
                    mp_bits = range(bit_count(mp))
                    masks = [
                        sum((1 - ((i >> (len(mp_bits) - 1 - b)) & 1)) << b for b in mp_bits)
                        for i in range(mp)
                    ]
                    sides = jnp.stack(
                        [pick(sides, links.mp_index ^ mask, 1) for mask in masks]
                    ).reshape(2, model_width // 2, left_side.shape[1])
                    side_send, side_own = sides[0], sides[1]
                    mine, embed_left, side_own, side_send = lax.optimization_barrier(
                        (mine, embed_left, side_own, side_send)
                    )
                mine, normed_two = lax.optimization_barrier((mine, normed_two))
                hidden = hidden + (mine + got) + down_bias[layer]
            kept.append(
                (
                    unit_one,
                    inverse_one,
                    normed,
                    qkv,
                    totals,
                    mixed,
                    unit_two,
                    inverse_two,
                    normed_two,
                    slope,
                    activation,
                )
            )

        last_own, last_send = part_own, part_send
        row_sums = {}
        local_sums = {}
        merges = {}
        row_sums["down_bias", top] = jnp.sum(grad_own, axis=0)

        head_of = jnp.arange(local_width, dtype=jnp.int32) // HEAD_DIM
        head_pick = head_of[:, None] == jnp.arange(head_count, dtype=jnp.int32)[None, :]
        clock = Clock(scale_cell)

        def advance(spot):
            for name in PLAN.get(spot, ()):
                if name in merges and merges[name].open:
                    merges[name].advance(clock)

        for layer in reversed(range(layer_count)):
            depth = top - layer
            (
                unit_one,
                inverse_one,
                normed,
                qkv,
                totals,
                mixed,
                unit_two,
                inverse_two,
                normed_two,
                slope,
                activation,
            ) = kept[layer]
            merges["down", depth] = Merge(
                links, [(down_left, activation)], bits if depth else bits_late
            )
            advance(("top", depth))
            pre_low, up_sums, part_own, part_send = feed_back(
                clock.one(down_low), slope, down_weight, up_weight, layer
            )
            local_sums["up_bias", layer] = up_sums[0]
            pre_low, part_send = clock.both(pre_low, part_send)
            merges["up", depth] = Merge(links, [(normed_two, pre_low)], bits)
            advance(("pre", depth))
            mine, got = links.ordered_sum(clock, lambda: part_own, part_send)
            if not PLAN.get(("wait_two", depth)):
                clock.hold()
            advance(("wait_two", depth))
            if layer == top:
                last_send = clock.one(last_send)
                last_other = exchange(last_send, "mp", mp, 0)
                clock.hold()
                last_mine = clock.one(last_own + clock.one(last_other))
            mine, got = clock.both(mine, got)
            if layer == top:
                for bit in range(1, bit_count(mp)):
                    last_mine = clock.one(last_mine)
                    last_other = exchange(last_mine, "mp", mp, bit)
                    if bit + 1 < bit_count(mp):
                        last_mine = last_mine + last_other
            change, grad_own, sums = norm_back(
                mine, got, unit_two, inverse_two, norm_gain, (layer, 1), grad_own
            )
            change, sums = clock.both(change, sums)
            row_sums["gain", layer, 1] = sums[0]
            row_sums["bias", layer, 1] = sums[1]
            row_sums["out_bias", layer] = sums[2]
            other_change = links.other_rows(change)
            clock.hold()
            grad_other, out_low, out_left = merge_rows(
                grad_own, grad_other, clock.one(other_change), shards
            )
            out_low = clock.one(out_low)
            advance(("mid", depth))
            grads, qv_sums, part_own, part_send = attend_back(
                clock.one(out_low), qkv, totals, attention_weight[layer], output_weight[layer]
            )
            local_sums["qv", layer] = qv_sums
            mine, got = links.ordered_sum(clock, lambda: part_own, part_send)
            if not PLAN.get(("wait_one", depth)):
                clock.hold()
            merges["att", depth] = Merge(links, [(out_left, mixed), (normed, grads)], bits)
            advance(("wait_one", depth))
            if layer == top:
                hidden = clock.one(hidden + (last_mine + clock.one(last_other)) + down_bias[top])
                hidden_other = links.other_rows(hidden)
                clock.hold()
                layer_out = clock.one(links.global_rows(hidden, clock.one(hidden_other)))
            mine, got = clock.both(mine, got)
            change, grad_own, sums = norm_back(
                mine, got, unit_one, inverse_one, norm_gain, (layer, 0), grad_own
            )
            change, sums = clock.both(change, sums)
            row_sums["gain", layer, 0] = sums[0]
            row_sums["bias", layer, 0] = sums[1]
            if layer:
                row_sums["down_bias", layer - 1] = sums[2]
            other_change = links.other_rows(change)
            clock.hold()
            grad_other, down_low, down_left = merge_rows(
                grad_own, grad_other, clock.one(other_change), shards
            )
            down_low = clock.one(down_low)
            advance(("end", depth))
            down_low = clock.one(down_low)

        row_sums["column"] = sums[2]
        row_sums["lead"] = lead_scale * sums[2]
        clock.hold()
        value_grad, key_grad, key_grad_var, pixel_own, pixel_send = pool_back(
            clock.one(down_low), pool_output_weight, value_flat, value_var, pix_low, pool_probs, score_rows
        )
        flat_all = flat_count + var_count
        item_scale = clock.cell[0, 0]
        sub = shard // mp
        embed_send, embed_own, summed_key, query_grad, pool_bias = embed_terms(
            side_send,
            side_own,
            clock.one(value_grad),
            key_grad,
            key_grad_var,
            clock.cell,
            patch_flat,
            variable_embed,
            pool_key_weight,
        )
        value_low = value_grad.astype(BF)
        query_late = clock.one(pool_query)
        merges["tail"] = Merge(
            links,
            [
                (down_left, pooled),
                (embed_left, jnp.concatenate([value_low, value_low[flat_count:]], axis=0)),
            ],
            bits,
        )
        query_grad = query_grad[0]
        embed_send = clock.one(embed_send)
        embed_got = exchange(embed_send, "mp", mp, 0)
        clock.hold()
        embed_got = clock.one(embed_got)
        for bit in range(1, bit_count(mp)):
            embed_send, embed_own = add_split(embed_own, embed_got)
            embed_send = clock.one(embed_send)
            embed_got = exchange(embed_send, "mp", mp, bit)
        advance("back")
        lanes = embed_own.shape[1]

        names = []
        for layer in range(layer_count):
            names += [("gain", layer, 0), ("gain", layer, 1), ("bias", layer, 0), ("bias", layer, 1)]
        for layer in range(layer_count):
            names += [("out_bias", layer), ("down_bias", layer)]
        names += ["column", "lead"]
        own_sums = clock.one(jnp.stack([row_sums[name] for name in names]) * item_scale)
        other_sums = exchange(own_sums, "mp", mp, 0)
        clock.hold()
        full_sums = own_sums + clock.one(other_sums)
        local = jnp.stack([local_sums["up_bias", layer] for layer in range(layer_count)]) * item_scale
        thin = [local_sums["qv", layer] for layer in range(layer_count)]
        thin = jnp.concatenate([jnp.concatenate(thin, axis=0) * item_scale, pool_bias], axis=0)
        packed = jnp.concatenate(
            [
                full_sums.reshape(len(names), dp, shard).transpose(1, 0, 2).reshape(dp, -1),
                summed_key.reshape(head_count, dp, shard).transpose(1, 0, 2).reshape(dp, -1),
                local.reshape(layer_count, dp, -1).transpose(1, 0, 2).reshape(dp, -1),
                thin.reshape(2 * layer_count + 1, dp, -1).transpose(1, 0, 2).reshape(dp, -1),
                jnp.broadcast_to(query_grad[None, :], (dp, local_width)),
            ],
            axis=1,
        )
        packed_size = packed.shape[1]
        packed_rows = -(-packed_size // 1024) * 8
        packed = jnp.pad(packed, ((0, 0), (0, packed_rows * 128 - packed_size)))
        packed = packed.reshape(dp, packed_rows, 128)
        position = (grad_own * item_scale).reshape(row_count // 2, dp, shard).transpose(1, 0, 2)
        position, packed = clock.both(position, packed)
        advance("vectors")
        embed_grad = (embed_own + clock.one(embed_got)).reshape(dp, sub, lanes)
        lane_blocks = lanes // 128
        if shard == 128:
            tall = jnp.concatenate(
                [embed_grad[:, :, i * 128 : (i + 1) * 128] for i in range(lane_blocks)]
                + [packed, position],
                axis=1,
            )
            merges["small"] = ShardMerge(links, tall)
        else:
            merges["small"] = ShardMerge(
                links,
                jnp.concatenate(
                    [part.reshape(dp, 1, -1) for part in (embed_grad, packed, position)], axis=2
                ),
            )
        advance("small")

        pixel_mine, pixel_got = links.ordered_sum(clock, lambda: pixel_own, pixel_send)
        clock.hold()
        advance("values")
        pixel_mine, pixel_got = clock.both(pixel_mine, pixel_got)
        pixel_mine = clock.one(pixel_mine + pixel_got)
        pixel_other = links.other_rows(pixel_mine)
        clock.hold()
        advance("pixels")
        pixel_grad = links.global_rows(pixel_mine, clock.one(pixel_other))
        pixel_grad = clock.one(pixel_grad.T.reshape(1, var_count, pix_count, row_count))
        advance("rows")
        for name in DRAIN:
            if merges[name].open:
                merges[name].advance(clock)
        for merge in merges.values():
            while merge.open:
                merge.advance(clock)
        finished = {}
        for kind in ("down", "up", "att"):
            parts = [merges[kind, top - layer].total for layer in range(layer_count)]
            finished[kind] = finish_layers(
                kind, parts, clock.cell, layer_count, shard, local_width
            )
        tail_total = merges["tail"].total
        small = merges["small"].total[0]
        if shard == 128:
            embed_rows = sub * lane_blocks
            embed_grad = jnp.concatenate(
                [small[i * sub : (i + 1) * sub] for i in range(lane_blocks)], axis=1
            )
            packed = small[embed_rows : embed_rows + packed_rows].reshape(-1)
            position = small[embed_rows + packed_rows :]
        else:
            size = sub * lane_blocks * 128
            embed_grad = small[0, :size].reshape(sub, lane_blocks * 128)
            packed = small[0, size : size + packed_rows * 128]
            position = small[0, size + packed_rows * 128 :].reshape(row_count // 2, shard)
        position = links.global_rows(position, links.other_rows(position))
        offset = 0

        def take(*shape):
            nonlocal offset
            size = math.prod(shape)
            piece = packed[offset : offset + size].reshape(shape)
            offset += size
            return piece

        gains = take(layer_count, 2, shard)
        biases = []
        gain_list = []
        offset = 0
        norm_all = take(layer_count, 2, 2, shard)
        gain_list = norm_all[:, 0]
        biases = norm_all[:, 1]
        dense_bias = take(layer_count, 2, shard)
        column_total = take(shard)
        lead_total = take(shard)
        key_shard = take(head_count, shard)
        up_bias_total = take(layer_count, local.shape[1] // dp)
        thin_total = take(2 * layer_count + 1, local_width // dp)
        query_total = take(local_width)

        query_low = query_late.astype(BF)
        query_rows = lax.dynamic_slice_in_dim(query_low, links.dp_index * shard, shard, 0)
        query_weight_grad = query_rows.astype(F32)[:, None] * query_total[None, :]
        key_weight_grad = (
            jnp.repeat(key_shard.T, HEAD_DIM, axis=1) * query_row / ROOT_DIM
        )
        embed_turned = embed_grad.T
        return (
            layer_out[None],
            pixel_grad,
            embed_turned[:flat_count].reshape(var_count, pix_count, sub),
            embed_turned[flat_count:flat_all],
            position,
            embed_turned[flat_all],
            query_weight_grad,
            key_weight_grad,
            tail_total[:, local_width:],
            thin_total[-1],
            tail_total[:, :local_width].T,
            column_total,
            lead_total,
            column_total,
            gain_list,
            biases,
            finished["att"][1],
            thin_total[:-1].reshape(layer_count, 2, local_width // dp),
            finished["att"][0],
            dense_bias[:, 0],
            finished["up"][0],
            up_bias_total,
            finished["down"][0],
            dense_bias[:, 1],
        )

    return per_device


def solution(mesh):
    return jax.shard_map(
        make_per_device(mesh.shape["dp"], mesh.shape["mp"]),
        mesh=mesh,
        in_specs=(
            P("dp", None, None, None),
            P("dp"),
            P(),
            P("dp"),
            P("dp"),
            P(),
            P(),
            P(),
            P(),
            P(),
            P(None, "mp"),
            P(None, "mp"),
            P(None, "mp"),
            P("mp"),
            P("mp", None),
            P(),
            P(),
            P(),
            P(),
            P(),
            P(None, None, None, "mp"),
            P(None, None, "mp"),
            P(None, "mp", None),
            P(),
            P(None, None, "mp"),
            P(None, "mp"),
            P(None, "mp", None),
            P(),
            P("dp", None, None),
        ),
        out_specs=(
            P("dp", None, None),
            P("dp", None, None, None),
            P(None, None, ("dp", "mp")),
            P(None, ("dp", "mp")),
            P(None, "dp"),
            P(("dp", "mp")),
            P("dp", "mp"),
            P("dp", "mp"),
            P("dp", "mp"),
            P(("mp", "dp")),
            P("mp", "dp"),
            P("dp"),
            P("dp"),
            P("dp"),
            P(None, None, "dp"),
            P(None, None, "dp"),
            P(None, None, "dp", "mp"),
            P(None, None, ("mp", "dp")),
            P(None, "mp", "dp"),
            P(None, "dp"),
            P(None, "dp", "mp"),
            P(None, ("mp", "dp")),
            P(None, "mp", "dp"),
            P(None, "dp"),
        ),
        check_vma=False,
    )
```

```python
import math

import jax
import jax.numpy as jnp
from jax import lax
from jax.experimental import pallas as pl
from jax.experimental.pallas import tpu as pltpu
from jax.sharding import PartitionSpec as P

HEAD_DIM = 64
PLAN = {
    ("top", 0): [("down", 0)],
    ("pre", 0): [("up", 0)],
    ("core_one", 0): [("att", 0)],
    ("wait_one", 0): [("down", 0), ("up", 0)],
    ("core_two", 1): [("down", 1)],
    ("wait_two", 1): [("up", 0)],
    ("mid", 1): [("down", 0), ("att", 0)],
    ("wait_one", 1): [("up", 0), ("up", 1), ("att", 0), ("down", 1)],
    ("end", 1): [("down", 0), ("att", 1)],
    "back": [("down", 1), ("att", 0), ("up", 1)],
    "small": ["small"],
    "values": ["tail", ("down", 1), ("up", 1), ("att", 1)],
    "pixels": ["small", ("up", 1), "tail", ("att", 1)],
    "rows": ["small", ("att", 1), "tail", "small", "tail"],
}
DRAIN = []
ROOT_DIM = math.sqrt(HEAD_DIM)
PRODUCT_BLOCKS = 2
BF = jnp.bfloat16
F32 = jnp.float32


def matmul(left, right):
    return jnp.dot(left, right, preferred_element_type=F32)


def matmul_tn(left, right):
    return lax.dot_general(left, right, (((0,), (0,)), ((), ())), preferred_element_type=F32)


def matmul_nt(left, right):
    return lax.dot_general(left, right, (((1,), (1,)), ((), ())), preferred_element_type=F32)


def two_part(tensor):
    high = tensor.astype(BF)
    return high, (tensor - high.astype(F32)).astype(BF)


def gelu_exact(pre_act):
    return jax.nn.gelu(pre_act, approximate=False)


def bit_count(size):
    bits = size.bit_length() - 1
    assert 1 << bits == size
    return bits


def exchange(tensor, axis, size, bit):
    return lax.ppermute(tensor, axis, [(i, i ^ (1 << bit)) for i in range(size)])


def pick(tensor, index, axis):
    return lax.dynamic_index_in_dim(tensor, index, axis, keepdims=False)


def after(value, *earlier):
    return lax.optimization_barrier((value,) + earlier)[0]


def vmem_limit(size):
    return pltpu.CompilerParams(vmem_limit_bytes=int(size * 1.25) + (2 << 20))


LONG = pl.CostEstimate(flops=10**12, bytes_accessed=8, transcendentals=0)


def step_cell(cell):
    def kernel(cell_ref, out_ref):
        out_ref[...] = cell_ref[...]

    return pl.pallas_call(
        kernel,
        out_shape=jax.ShapeDtypeStruct(cell.shape, F32),
        cost_estimate=LONG,
        compiler_params=vmem_limit(0),
        name="step_cell",
    )(cell)


class Clock:
    def __init__(self, cell):
        self.cell = cell

    def both(self, *values):
        *values, self.cell = lax.optimization_barrier((*values, self.cell))
        return values

    def one(self, value):
        return self.both(value)[0]

    def hold(self):
        self.cell = step_cell(self.cell)


def ordered_columns(source, target, shards_ref, count, shard):
    for place in range(count):
        column = pl.multiple_of(shards_ref[place] * shard, shard)
        target[:, place * shard : (place + 1) * shard] = source[:, pl.ds(column, shard)]


def take_columns(rows, shards, shard):
    pieces = rows.reshape(rows.shape[0], -1, shard)[:, shards]
    return pieces.reshape(rows.shape)


def norm_rows(own, other, gain, bias, shards):
    half, width = own.shape
    count = shards.shape[0]
    shard = width // count
    if shard % 128:
        rows = jnp.concatenate([own, other], axis=0) * gain + bias
        return take_columns(rows.astype(BF), shards, shard)

    def kernel(shards_ref, own_ref, other_ref, gain_ref, bias_ref, out_ref, low_ref):
        low_ref[:half] = (own_ref[...] * gain_ref[...] + bias_ref[...]).astype(BF)
        low_ref[half:] = (other_ref[...] * gain_ref[...] + bias_ref[...]).astype(BF)
        ordered_columns(low_ref, out_ref, shards_ref, count, shard)

    return pl.pallas_call(
        kernel,
        out_shape=jax.ShapeDtypeStruct((2 * half, width), BF),
        in_specs=[pl.BlockSpec(memory_space=pltpu.SMEM)] + [pl.BlockSpec()] * 4,
        scratch_shapes=[pltpu.VMEM((2 * half, width), BF)],
        cost_estimate=pl.CostEstimate(
            flops=4 * half * width, bytes_accessed=12 * half * width, transcendentals=0
        ),
        compiler_params=vmem_limit(16 * half * width),
        name="norm_rows",
    )(shards, own, other, gain[None], bias[None])


def embed_columns(patch, embed, shards):
    flat, width = patch.shape
    var_count = embed.shape[0]
    count = shards.shape[0]
    shard = width // count
    if shard % 128:
        high, rest = two_part(embed)
        return take_columns(jnp.concatenate([patch, high, rest], axis=0), shards, shard)

    def kernel(shards_ref, patch_ref, embed_ref, out_ref):
        for place in range(count):
            column = pl.ds(pl.multiple_of(shards_ref[place] * shard, shard), shard)
            target = slice(place * shard, (place + 1) * shard)
            high, rest = two_part(embed_ref[:, column])
            out_ref[:flat, target] = patch_ref[:, column]
            out_ref[flat : flat + var_count, target] = high
            out_ref[flat + var_count :, target] = rest

    return pl.pallas_call(
        kernel,
        out_shape=jax.ShapeDtypeStruct((flat + 2 * var_count, width), BF),
        in_specs=[pl.BlockSpec(memory_space=pltpu.SMEM)] + [pl.BlockSpec()] * 2,
        compiler_params=vmem_limit(8 << 20),
        name="embed_columns",
    )(shards, patch, embed)


def merge_rows(own, other, change, shards):
    half, width = own.shape
    count = shards.shape[0]
    shard = width // count
    if shard % 128:
        total = other + change
        low = jnp.concatenate([own, total], axis=0).astype(BF)
        return total, low, take_columns(low, shards, shard)

    def kernel(shards_ref, own_ref, other_ref, change_ref, other_out, low_out, ordered_out):
        low_out[:half] = own_ref[...].astype(BF)
        total = other_ref[...] + change_ref[...]
        other_out[...] = total
        low_out[half:] = total.astype(BF)
        ordered_columns(low_out, ordered_out, shards_ref, count, shard)

    return pl.pallas_call(
        kernel,
        out_shape=(
            jax.ShapeDtypeStruct((half, width), F32),
            jax.ShapeDtypeStruct((2 * half, width), BF),
            jax.ShapeDtypeStruct((2 * half, width), BF),
        ),
        in_specs=[pl.BlockSpec(memory_space=pltpu.SMEM)] + [pl.BlockSpec()] * 3,
        cost_estimate=LONG,
        compiler_params=vmem_limit(26 * half * width),
        name="merge_rows",
    )(shards, own, other, change)


def norm_back(mine, got, unit, inverse, gains, place, grad):
    half, width = mine.shape
    size = half

    def kernel(mine_ref, got_ref, unit_ref, inverse_ref, gain_ref, grad_ref, change_out, grad_out, sums_out):
        pull = mine_ref[...] + got_ref[...]
        unit_rows = unit_ref[...]
        scaled = pull * gain_ref[place[0], place[1] : place[1] + 1]
        first = jnp.mean(scaled, axis=-1, keepdims=True)
        second = jnp.mean(scaled * unit_rows, axis=-1, keepdims=True)
        change = inverse_ref[:, :1] * (scaled - first - unit_rows * second)
        change_out[...] = change
        total = grad_ref[...] + change
        grad_out[...] = total

        @pl.when(pl.program_id(0) == 0)
        def _():
            sums_out[...] = jnp.zeros_like(sums_out)

        sums_out[0:1] += jnp.sum(pull * unit_rows, axis=0, keepdims=True)
        sums_out[1:2] += jnp.sum(pull, axis=0, keepdims=True)
        sums_out[2:3] += jnp.sum(total, axis=0, keepdims=True)

    rows = jax.ShapeDtypeStruct((half, width), F32)
    block = pl.BlockSpec((size, width), lambda j: (j, 0))
    return pl.pallas_call(
        kernel,
        out_shape=(rows, rows, jax.ShapeDtypeStruct((3, width), F32)),
        grid=(half // size,),
        in_specs=[
            block,
            block,
            block,
            pl.BlockSpec((size, 128), lambda j: (j, 0)),
            pl.BlockSpec(gains.shape, lambda j: (0, 0, 0)),
            block,
        ],
        out_specs=(block, block, pl.BlockSpec((3, width), lambda j: (0, 0))),
        cost_estimate=LONG,
        compiler_params=vmem_limit(64 * size * width),
        name="norm_back",
    )(mine, got, unit, inverse, gains, grad)


def feed_forward(unit_own, unit_other, gains, biases, place, up_weight, up_bias, down_weight, shards):
    half, width = unit_own.shape
    rows = 2 * half
    layer, which = place
    hidden = up_weight.shape[2]
    size = hidden // 4
    spread_of = math.sqrt(2.0)
    peak = 1.0 / math.sqrt(2.0 * math.pi)

    count = shards.shape[0]
    shard = width // count

    def kernel(shards_ref, own_ref, other_ref, gain_ref, bias_ref, up_ref, up_bias_ref, down_ref,
               activation_out, slope_out, own_out, send_out, ordered_out, normed_ref):
        step = pl.program_id(0)

        @pl.when(step == 0)
        def _():
            gain = gain_ref[layer, which : which + 1]
            bias = bias_ref[layer, which : which + 1]
            normed_ref[:half] = (own_ref[...] * gain + bias).astype(BF)
            normed_ref[half:] = (other_ref[...] * gain + bias).astype(BF)
            own_out[...] = jnp.zeros_like(own_out)
            send_out[...] = jnp.zeros_like(send_out)
            if shard % 128:
                ordered_out[...] = normed_ref[...]
            else:
                ordered_columns(normed_ref, ordered_out, shards_ref, count, shard)

        pre = matmul(normed_ref[...], up_ref[0]) + up_bias_ref[layer : layer + 1]
        below = 0.5 + 0.5 * lax.erf(pre / spread_of)
        slope_out[...] = below + pre * (jnp.exp(-0.5 * pre * pre) * peak)
        activation = (pre * below).astype(BF)
        activation_out[...] = activation
        send_out[...] += matmul(activation[half:], down_ref[0])
        own_out[...] += matmul(activation[:half], down_ref[0])

    piece = jax.ShapeDtypeStruct((half, width), F32)
    whole = pl.BlockSpec((half, width), lambda j: (0, 0))
    return pl.pallas_call(
        kernel,
        out_shape=(
            jax.ShapeDtypeStruct((rows, hidden), BF),
            jax.ShapeDtypeStruct((rows, hidden), F32),
            piece,
            piece,
            jax.ShapeDtypeStruct((rows, width), BF),
        ),
        grid=(hidden // size,),
        in_specs=[
            pl.BlockSpec(memory_space=pltpu.SMEM),
            whole,
            whole,
            pl.BlockSpec(gains.shape, lambda j: (0, 0, 0)),
            pl.BlockSpec(biases.shape, lambda j: (0, 0, 0)),
            pl.BlockSpec((1, width, size), lambda j: (layer, 0, j)),
            pl.BlockSpec((up_bias.shape[0], size), lambda j: (0, j)),
            pl.BlockSpec((1, size, width), lambda j: (layer, j, 0)),
        ],
        out_specs=(
            pl.BlockSpec((rows, size), lambda j: (0, j)),
            pl.BlockSpec((rows, size), lambda j: (0, j)),
            whole,
            whole,
            pl.BlockSpec((rows, width), lambda j: (0, 0)),
        ),
        scratch_shapes=[pltpu.VMEM((rows, width), BF)],
        cost_estimate=LONG,
        compiler_params=vmem_limit(44 << 20),
        name="feed_forward",
    )(shards, unit_own, unit_other, gains, biases, up_weight, up_bias, down_weight)


def feed_back(low, slope, down_weight, up_weight, layer):
    rows, width = low.shape
    half = rows // 2
    hidden = slope.shape[1]
    size = hidden // 4

    def kernel(low_ref, slope_ref, down_ref, up_ref, pre_out, sums_out, own_out, send_out):
        @pl.when(pl.program_id(0) == 0)
        def _():
            own_out[...] = jnp.zeros_like(own_out)
            send_out[...] = jnp.zeros_like(send_out)

        grad = matmul_nt(low_ref[...], down_ref[0]) * slope_ref[...]
        sums_out[...] = jnp.sum(grad, axis=0, keepdims=True)
        grad_low = grad.astype(BF)
        pre_out[...] = grad_low
        send_out[...] += matmul_nt(grad_low[half:], up_ref[0])
        own_out[...] += matmul_nt(grad_low[:half], up_ref[0])

    piece = jax.ShapeDtypeStruct((half, width), F32)
    whole = pl.BlockSpec((half, width), lambda j: (0, 0))
    return pl.pallas_call(
        kernel,
        out_shape=(
            jax.ShapeDtypeStruct((rows, hidden), BF),
            jax.ShapeDtypeStruct((1, hidden), F32),
            piece,
            piece,
        ),
        grid=(hidden // size,),
        in_specs=[
            pl.BlockSpec((rows, width), lambda j: (0, 0)),
            pl.BlockSpec((rows, size), lambda j: (0, j)),
            pl.BlockSpec((1, size, width), lambda j: (layer, j, 0)),
            pl.BlockSpec((1, width, size), lambda j: (layer, 0, j)),
        ],
        out_specs=(
            pl.BlockSpec((rows, size), lambda j: (0, j)),
            pl.BlockSpec((1, size), lambda j: (0, j)),
            whole,
            whole,
        ),
        cost_estimate=LONG,
        compiler_params=vmem_limit(26 * rows * width),
        name="feed_back",
    )(low, slope, down_weight, up_weight)


def embed_terms(side_send, side_own, value_grad, key_grad, key_var, cell, patch, embed, key_weight):
    count, _ = side_send.shape
    flat_all, local_width = value_grad.shape
    head_count, flat = key_grad.shape
    model_width = patch.shape[1]
    lanes = -(-(flat_all + 1) // 128) * 128

    def kernel(send_ref, own_ref, value_ref, key_ref, var_ref, cell_ref, patch_ref, embed_ref, weight_ref,
               send_out, own_out, sum_out, query_out, bias_out, value_low_ref):
        scale = cell_ref[0:1, 0:1]
        value_low_ref[...] = (value_ref[...] * scale).astype(BF)
        bias_out[...] = jnp.sum(value_ref[flat:], axis=0, keepdims=True) * scale
        key_high, key_rest = two_part(key_ref[...] * scale)
        var_high, var_rest = two_part(var_ref[...] * scale)
        embed_high, embed_rest = two_part(embed_ref[...])
        total = matmul(key_high, patch_ref[...]) + matmul(key_rest, patch_ref[...])
        total = total + matmul(var_high, embed_high) + matmul(var_rest, embed_high)
        total = total + matmul(var_high, embed_rest)
        sum_out[...] = total
        high, rest = two_part(total)
        query = matmul(high, weight_ref[...]) + matmul(rest, weight_ref[...])
        head = lax.broadcasted_iota(jnp.int32, (head_count, local_width), 0)
        column = lax.broadcasted_iota(jnp.int32, (head_count, local_width), 1)
        inside = (column >= head * HEAD_DIM) & (column < (head + 1) * HEAD_DIM)
        query = jnp.sum(jnp.where(inside, query, 0.0), axis=0, keepdims=True) / ROOT_DIM
        query_out[...] = query
        query_high, query_rest = two_part(query)
        query_rows = jnp.concatenate(
            [query_high.astype(F32), query_rest.astype(F32), jnp.zeros((6, local_width), F32)], axis=0
        ).astype(BF)
        flat_rows, var_rows = [
            jnp.concatenate(
                [part.astype(F32) for part in (first, second, first, jnp.zeros_like(first))], axis=0
            ).astype(BF)
            for first, second in ((key_high, key_rest), (var_high, var_rest))
        ]
        for side_ref, out_ref in ((send_ref, send_out), (own_ref, own_out)):
            keys = side_ref[:, 2 * local_width :]
            values = side_ref[:, :local_width]
            weight = side_ref[:, local_width : 2 * local_width]
            out_ref[...] = jnp.zeros_like(out_ref)
            out_ref[:, :flat] = matmul_nt(values, value_low_ref[:flat]) + matmul(keys, flat_rows)
            out_ref[:, flat:flat_all] = matmul_nt(values, value_low_ref[flat:]) + matmul(keys, var_rows)
            part = matmul_nt(weight, query_rows)
            out_ref[:, flat_all : flat_all + 1] = jnp.sum(part, axis=1, keepdims=True)

    block = jax.ShapeDtypeStruct((count, lanes), F32)
    return pl.pallas_call(
        kernel,
        out_shape=(
            block,
            block,
            jax.ShapeDtypeStruct((head_count, model_width), F32),
            jax.ShapeDtypeStruct((1, local_width), F32),
            jax.ShapeDtypeStruct((1, local_width), F32),
        ),
        scratch_shapes=[pltpu.VMEM((flat_all, local_width), BF)],
        cost_estimate=LONG,
        compiler_params=vmem_limit(14 << 20),
        name="embed_terms",
    )(side_send, side_own, value_grad, key_grad, key_var, cell, patch, embed, key_weight)


def product_rows(pairs, scale, start, first, second, got=None):
    widths = [right.shape[1] for _, right in pairs]
    total = sum(widths)
    has_got = got is not None
    count = first + second
    size = 128 * PRODUCT_BLOCKS
    start, first, second, count = [n // PRODUCT_BLOCKS for n in (start, first, second, count)]

    def kernel(scale_ref, *refs):
        ins = refs[: 2 * len(pairs)]
        outs = refs[2 * len(pairs) + has_got :]
        step = pl.program_id(0)

        def fill(out_ref):
            column = 0
            for i, width in enumerate(widths):
                block = (
                    lax.dot_general(
                        ins[2 * i][...],
                        ins[2 * i + 1][...],
                        (((0,), (0,)), ((), ())),
                        preferred_element_type=F32,
                    )
                    * scale_ref[0:1, 0:1]
                )
                if has_got:
                    block = block + refs[2 * len(pairs)][:, column : column + width]
                out_ref[:, column : column + width] = block
                column += width

        if second:
            pl.when(step < first)(lambda: fill(outs[0]))
            pl.when(step >= first)(lambda: fill(outs[1]))
        else:
            fill(outs[0])

    in_specs = [pl.BlockSpec(scale.shape, lambda j: (0, 0))]
    operands = [scale]
    traffic = 0
    for left, right in pairs:
        rows = left.shape[0]
        in_specs.append(pl.BlockSpec((rows, size), lambda j: (0, start + j)))
        in_specs.append(pl.BlockSpec(right.shape, lambda j: (0, 0)))
        operands += [left, right]
        traffic += 2 * 2 * rows * (size + right.shape[1])
    if has_got:
        in_specs.append(pl.BlockSpec((size, total), lambda j: (j, 0)))
        operands.append(got)
    out_shape = [jax.ShapeDtypeStruct((first * size, total), F32)]
    out_specs = [pl.BlockSpec((size, total), lambda j: (jnp.minimum(j, first - 1), 0))]
    if second:
        out_shape.append(jax.ShapeDtypeStruct((second * size, total), F32))
        out_specs.append(pl.BlockSpec((size, total), lambda j: (jnp.maximum(j - first, 0), 0)))
    return pl.pallas_call(
        kernel,
        out_shape=out_shape,
        grid=(count,),
        in_specs=in_specs,
        out_specs=out_specs,
        cost_estimate=LONG,
        compiler_params=vmem_limit(traffic + 2 * 4 * size * total * 4),
        name="product_rows",
    )(*operands)


def add_rows(own, got):
    rows, width = own.shape
    size = rows // 2

    def kernel(own_ref, got_ref, out_ref):
        out_ref[...] = own_ref[...] + got_ref[...]

    block = pl.BlockSpec((size, width), lambda j: (j, 0))
    return pl.pallas_call(
        kernel,
        out_shape=jax.ShapeDtypeStruct((rows, width), F32),
        grid=(rows // size,),
        in_specs=[block, block],
        out_specs=block,
        cost_estimate=LONG,
        compiler_params=vmem_limit(32 * size * width),
        name="add_rows",
    )(own, got)


def add_split(keep, got):
    rows, width = keep.shape
    half = rows // 2
    size = min(128, half)
    count = half // size

    def kernel(keep_ref, got_ref, first_out, second_out):
        total = keep_ref[...] + got_ref[...]

        @pl.when(pl.program_id(0) < count)
        def _():
            first_out[...] = total

        @pl.when(pl.program_id(0) >= count)
        def _():
            second_out[...] = total

    block = (size, width)
    return pl.pallas_call(
        kernel,
        out_shape=[jax.ShapeDtypeStruct((half, width), F32)] * 2,
        grid=(2 * count,),
        in_specs=[pl.BlockSpec(block, lambda j: (j, 0))] * 2,
        out_specs=[
            pl.BlockSpec(block, lambda j: (jnp.minimum(j, count - 1), 0)),
            pl.BlockSpec(block, lambda j: (jnp.maximum(j - count, 0), 0)),
        ],
        cost_estimate=LONG,
        compiler_params=vmem_limit(32 * size * width),
        name="add_split",
    )(keep, got)


def attend_forward(unit_own, unit_other, gain, bias, weights, biases, out_weight):
    half, model_width = unit_own.shape
    rows = 2 * half
    local_width = weights.shape[2]
    head_count = local_width // HEAD_DIM

    def kernel(own_ref, other_ref, gain_ref, bias_ref, weight_ref, biases_ref, out_weight_ref,
               qkv_out, mixed_out, total_out, own_out, send_out, normed_ref):
        normed_ref[:half] = (own_ref[...] * gain_ref[...] + bias_ref[...]).astype(BF)
        normed_ref[half:] = (other_ref[...] * gain_ref[...] + bias_ref[...]).astype(BF)
        normed = normed_ref[...]
        qkv_out[:, :local_width] = (matmul(normed, weight_ref[0]) + biases_ref[0:1]).astype(BF)
        qkv_out[:, local_width : 2 * local_width] = matmul(normed, weight_ref[1]).astype(BF)
        qkv_out[:, 2 * local_width :] = (matmul(normed, weight_ref[2]) + biases_ref[1:2]).astype(BF)
        for head in range(head_count):
            one = slice(head * HEAD_DIM, (head + 1) * HEAD_DIM)
            query = qkv_out[:, one]
            key = qkv_out[:, local_width + head * HEAD_DIM : local_width + (head + 1) * HEAD_DIM]
            value = qkv_out[:, 2 * local_width + head * HEAD_DIM : 2 * local_width + (head + 1) * HEAD_DIM]
            scores = matmul_nt(query, key) / ROOT_DIM
            top = jnp.max(scores, axis=-1, keepdims=True)
            exponent = jnp.exp(scores - top)
            row_sum = jnp.sum(exponent, axis=-1, keepdims=True)
            attend = (exponent / row_sum).astype(BF)
            mixed_out[:, one] = matmul(attend, value).astype(BF)
            total_out[:, head : head + 1] = top + jnp.log(row_sum)
        send_out[...] = matmul(mixed_out[half:], out_weight_ref[...])
        own_out[...] = matmul(mixed_out[:half], out_weight_ref[...])

    piece = jax.ShapeDtypeStruct((half, model_width), F32)
    return pl.pallas_call(
        kernel,
        out_shape=(
            jax.ShapeDtypeStruct((rows, 3 * local_width), BF),
            jax.ShapeDtypeStruct((rows, local_width), BF),
            jax.ShapeDtypeStruct((rows, 128), F32),
            piece,
            piece,
        ),
        scratch_shapes=[pltpu.VMEM((rows, model_width), BF)],
        cost_estimate=pl.CostEstimate(
            flops=2 * rows * local_width * (4 * model_width + 2 * rows),
            bytes_accessed=8 * rows * model_width + 8 * local_width * model_width,
            transcendentals=rows * rows * head_count,
        ),
        compiler_params=vmem_limit(22 * rows * model_width),
        name="attend_forward",
    )(unit_own, unit_other, gain[None], bias[None], weights, biases, out_weight)


def attend_back(low, qkv, totals, weights, out_weight):
    rows, model_width = low.shape
    half = rows // 2
    local_width = weights.shape[2]
    head_count = local_width // HEAD_DIM

    def kernel(low_ref, qkv_ref, total_ref, weight_ref, out_weight_ref,
               grads_out, sums_out, own_out, send_out, mix_ref):
        mix_ref[...] = matmul_nt(low_ref[...], out_weight_ref[...]).astype(BF)
        for head in range(head_count):
            one = slice(head * HEAD_DIM, (head + 1) * HEAD_DIM)
            two = slice(local_width + head * HEAD_DIM, local_width + (head + 1) * HEAD_DIM)
            three = slice(2 * local_width + head * HEAD_DIM, 2 * local_width + (head + 1) * HEAD_DIM)
            query, key, value = qkv_ref[:, one], qkv_ref[:, two], qkv_ref[:, three]
            mix = mix_ref[:, one]
            attend = jnp.exp(matmul_nt(query, key) / ROOT_DIM - total_ref[:, head : head + 1])
            grad_attend = matmul_nt(mix, value)
            grad_value = matmul_tn(attend.astype(BF), mix)
            weighted = attend * grad_attend
            grad_scores = weighted - attend * jnp.sum(weighted, axis=-1, keepdims=True)
            grad_low = grad_scores.astype(BF)
            grad_query = matmul(grad_low, key) / ROOT_DIM
            grad_key = matmul_tn(grad_low, query) / ROOT_DIM
            grads_out[:, one] = grad_query.astype(BF)
            grads_out[:, two] = grad_key.astype(BF)
            grads_out[:, three] = grad_value.astype(BF)
            sums_out[0:1, one] = jnp.sum(grad_query, axis=0, keepdims=True)
            sums_out[1:2, one] = jnp.sum(grad_value, axis=0, keepdims=True)

        def pull(part):
            total = matmul_nt(grads_out[part, :local_width], weight_ref[0])
            total = total + matmul_nt(grads_out[part, local_width : 2 * local_width], weight_ref[1])
            return total + matmul_nt(grads_out[part, 2 * local_width :], weight_ref[2])

        send_out[...] = pull(slice(half, rows))
        own_out[...] = pull(slice(0, half))

    piece = jax.ShapeDtypeStruct((half, model_width), F32)
    return pl.pallas_call(
        kernel,
        out_shape=(
            jax.ShapeDtypeStruct((rows, 3 * local_width), BF),
            jax.ShapeDtypeStruct((2, local_width), F32),
            piece,
            piece,
        ),
        scratch_shapes=[pltpu.VMEM((rows, local_width), BF)],
        cost_estimate=LONG,
        compiler_params=vmem_limit(24 * rows * model_width),
        name="attend_back",
    )(low, qkv, totals, weights, out_weight)


def finish_layers(kind, pieces, cell, layer_count, shard, local_width):
    width = pieces[0].shape[1]
    shapes = {
        "down": [(layer_count, width, shard)],
        "up": [(layer_count, shard, width)],
        "att": [
            (layer_count, local_width, shard),
            (layer_count, 3, shard, local_width),
        ],
    }[kind]

    def store(values, outs):
        for layer, value in enumerate(values):
            if kind == "down":
                outs[0][layer] = value.T
            elif kind == "up":
                outs[0][layer] = value
            else:
                outs[0][layer] = value[:, :local_width].T
                for which in range(3):
                    begin = (1 + which) * local_width
                    outs[1][layer, which] = value[:, begin : begin + local_width]

    if shard % 128:
        values = pieces
        if kind == "down":
            return [jnp.stack([value.T for value in values])]
        if kind == "up":
            return [jnp.stack(values)]
        rest = [
            value[:, local_width:].reshape(shard, 3, local_width).transpose(1, 0, 2)
            for value in values
        ]
        return [jnp.stack([value[:, :local_width].T for value in values]), jnp.stack(rest)]

    def kernel(*refs):
        store([ref[...] for ref in refs[:layer_count]], refs[layer_count + 1 :])

    return pl.pallas_call(
        kernel,
        out_shape=[jax.ShapeDtypeStruct(shape, F32) for shape in shapes],
        cost_estimate=pl.CostEstimate(
            flops=layer_count * shard * width,
            bytes_accessed=12 * layer_count * shard * width,
            transcendentals=0,
        ),
        compiler_params=vmem_limit(20 * layer_count * shard * width),
        name="finish_layers",
    )(*pieces, cell)


def one_hot_segments(var_count, pix_count):
    flat = var_count * pix_count
    rows = lax.broadcasted_iota(jnp.int32, (var_count, flat), 0)
    columns = lax.broadcasted_iota(jnp.int32, (var_count, flat), 1)
    inside = (columns >= rows * pix_count) & (columns < (rows + 1) * pix_count)
    return jnp.where(inside, 1.0, 0.0).astype(BF)


def pool_front(core, pixels, patch, embed, query, query_weight, key_weight, value_weight,
               value_bias, mask, out_weight):
    var_count = embed.shape[0]
    flat, rows = pixels.shape
    pix_count = flat // var_count
    model_width, local_width = key_weight.shape
    head_count = local_width // HEAD_DIM
    half = rows // 2

    large = (query_weight, key_weight, pixels, patch, embed, value_weight, out_weight)

    def kernel(core_ref, query_ref, bias_ref, mask_ref, *refs):
        sources, refs = refs[: len(large)], refs[len(large) :]
        (low_out, query_out, key_out, score_out, flat_out, var_out, probs_out, pooled_out,
         own_out, send_out, turned_ref) = refs[:11]
        held, sems = refs[11 : 11 + len(large)], refs[11 + len(large)]
        copies = [
            pltpu.make_async_copy(source, target, sems.at[i])
            for i, (source, target) in enumerate(zip(sources, held))
        ]
        for copy in copies:
            copy.start()
        (query_weight_ref, key_weight_ref, pixels_ref, patch_ref, embed_ref, value_weight_ref,
         out_weight_ref) = held
        copies[0].wait()
        query = matmul(query_ref[...].astype(BF), query_weight_ref[...]).astype(BF)
        query_out[...] = query.astype(F32)
        copies[1].wait()
        for head in range(head_count):
            one = slice(head * HEAD_DIM, (head + 1) * HEAD_DIM)
            key_out[head : head + 1] = matmul_nt(query[:, one], key_weight_ref[:, one]) / ROOT_DIM
        copies[2].wait()
        turned_ref[...] = pixels_ref[...].T
        mine = pl.multiple_of(core_ref[0] * half, 8)
        theirs = pl.multiple_of(half - core_ref[0] * half, 8)
        low_out[:half] = turned_ref[pl.ds(mine, half)].astype(BF)
        low_out[half:] = turned_ref[pl.ds(theirs, half)].astype(BF)
        for copy in copies[3:]:
            copy.wait()
        key_high, key_rest = two_part(key_out[...])
        embed_high, embed_rest = two_part(embed_ref[...])
        score_out[...] = matmul_nt(key_high, patch_ref[...]) + matmul_nt(key_rest, patch_ref[...])
        score_var = (
            matmul_nt(key_high, embed_high)
            + matmul_nt(key_rest, embed_high)
            + matmul_nt(key_high, embed_rest)
        )
        flat_out[...] = matmul(patch_ref[...], value_weight_ref[...]).astype(BF)
        value_var = matmul(embed_high, value_weight_ref[...]) + matmul(embed_rest, value_weight_ref[...])
        var_out[...] = (value_var + bias_ref[...]).astype(BF)
        segment = one_hot_segments(var_count, pix_count)
        for head in range(head_count):
            one = slice(head * HEAD_DIM, (head + 1) * HEAD_DIM)
            pix = low_out[...].astype(F32)
            high, rest = two_part(pix * score_out[head : head + 1])
            scores = matmul_nt(high, segment) + matmul_nt(rest, segment) + score_var[head : head + 1]
            scores = jnp.where(mask_ref[...] > 0, scores, -1000000000.0)
            exponent = jnp.exp(scores - jnp.max(scores, axis=-1, keepdims=True))
            probs = exponent / jnp.sum(exponent, axis=-1, keepdims=True)
            probs_out[head] = probs
            low = probs.astype(BF)
            mixed = (matmul(low, segment) * pix).astype(BF)
            pooled_out[:, one] = (matmul(mixed, flat_out[:, one]) + matmul(low, var_out[:, one])).astype(BF)
        send_out[...] = matmul(pooled_out[half:], out_weight_ref[...])
        own_out[...] = matmul(pooled_out[:half], out_weight_ref[...])

    piece = jax.ShapeDtypeStruct((half, model_width), F32)
    return pl.pallas_call(
        kernel,
        out_shape=(
            jax.ShapeDtypeStruct((rows, flat), BF),
            jax.ShapeDtypeStruct((1, local_width), F32),
            jax.ShapeDtypeStruct((head_count, model_width), F32),
            jax.ShapeDtypeStruct((head_count, flat), F32),
            jax.ShapeDtypeStruct((flat, local_width), BF),
            jax.ShapeDtypeStruct((var_count, local_width), BF),
            jax.ShapeDtypeStruct((head_count, rows, var_count), F32),
            jax.ShapeDtypeStruct((rows, local_width), BF),
            piece,
            piece,
        ),
        in_specs=[pl.BlockSpec(memory_space=pltpu.SMEM)]
        + [pl.BlockSpec()] * 3
        + [pl.BlockSpec(memory_space=pltpu.HBM)] * len(large),
        scratch_shapes=[pltpu.VMEM((rows, flat), F32)]
        + [pltpu.VMEM(array.shape, array.dtype) for array in large]
        + [pltpu.SemaphoreType.DMA((len(large),))],
        cost_estimate=LONG,
        compiler_params=vmem_limit(46 << 20),
        name="pool_front",
    )(core, query, value_bias, mask, *large)


def pool_back(low, out_weight, value_flat, value_var, pix_low, probs, scores):
    rows, flat = pix_low.shape
    head_count, _, var_count = probs.shape
    pix_count = flat // var_count
    local_width = value_flat.shape[1]
    half = rows // 2

    def kernel(low_ref, out_weight_ref, flat_ref, var_ref, pix_ref, probs_ref, score_ref,
               value_out, key_out, key_var_out, own_out, send_out, pooled_ref, pixel_ref):
        pooled_ref[...] = matmul_nt(low_ref[...], out_weight_ref[...]).astype(BF)
        segment = one_hot_segments(var_count, pix_count)
        for head in range(head_count):
            one = slice(head * HEAD_DIM, (head + 1) * HEAD_DIM)
            pix = pix_ref[...].astype(F32)
            pooled = pooled_ref[:, one]
            pull = matmul_nt(pooled, flat_ref[:, one])
            high, rest = two_part(pull * pix)
            grad_probs = (
                matmul_nt(high, segment) + matmul_nt(rest, segment) + matmul_nt(pooled, var_ref[:, one])
            )
            probs_one = probs_ref[head]
            weighted = probs_one * grad_probs
            grad_scores = weighted - probs_one * jnp.sum(weighted, axis=-1, keepdims=True)
            high, rest = two_part(grad_scores)
            wide = matmul(high, segment) + matmul(rest, segment)
            key_out[head : head + 1] = jnp.sum(wide * pix, axis=0, keepdims=True)
            key_var_out[head : head + 1] = jnp.sum(grad_scores, axis=0, keepdims=True)
            probs_low = probs_one.astype(BF)
            probs_wide = matmul(probs_low, segment)
            term = wide * score_ref[head : head + 1] + probs_wide * pull
            if head:
                pixel_ref[...] += term
            else:
                pixel_ref[...] = term
            mixed = (probs_wide * pix).astype(BF)
            value_out[:flat, one] = matmul_tn(mixed, pooled)
            value_out[flat:, one] = matmul_tn(probs_low, pooled)
        own_out[...] = pixel_ref[:half]
        send_out[...] = pixel_ref[half:]

    piece = jax.ShapeDtypeStruct((half, flat), F32)
    return pl.pallas_call(
        kernel,
        out_shape=(
            jax.ShapeDtypeStruct((flat + var_count, local_width), F32),
            jax.ShapeDtypeStruct((head_count, flat), F32),
            jax.ShapeDtypeStruct((head_count, var_count), F32),
            piece,
            piece,
        ),
        scratch_shapes=[pltpu.VMEM((rows, local_width), BF), pltpu.VMEM((rows, flat), F32)],
        cost_estimate=LONG,
        compiler_params=vmem_limit(20 << 20),
        name="pool_back",
    )(low, out_weight, value_flat, value_var, pix_low, probs, scores)


class Links:
    def __init__(self, dp, mp):
        self.dp, self.mp = dp, mp
        self.dp_index = lax.axis_index("dp")
        self.mp_index = lax.axis_index("mp")

    def dp_bit(self, bit):
        return (self.dp_index >> bit) & 1

    def mp_bit(self, bit):
        return (self.mp_index >> bit) & 1

    def ordered_sum(self, clock, own, send, fill=None):
        send = clock.one(send)
        got = exchange(send, "mp", self.mp, 0)
        if fill:
            fill()
        else:
            clock.hold()
        mine = clock.one(add_rows(own(), clock.one(got)))
        last = bit_count(self.mp) - 1
        for bit in range(1, last):
            mine = clock.one(mine + exchange(mine, "mp", self.mp, bit))
        return mine, exchange(mine, "mp", self.mp, last)

    def begin_sum(self, own, send):
        mine = add_rows(own, exchange(send, "mp", self.mp, 0))
        last = bit_count(self.mp) - 1
        for bit in range(1, last):
            mine = mine + exchange(mine, "mp", self.mp, bit)
        return mine, exchange(mine, "mp", self.mp, last)

    def begin_product(self, left, right, product=matmul):
        half = left.shape[0] // 2
        send = product(left[half:], right)
        return self.begin_sum(product(left[:half], right), send)

    def sum_rows(self, partial):
        half = partial.shape[0] // 2
        mine, got = self.begin_sum(partial[:half], partial[half:])
        return mine + got

    def other_rows(self, own):
        return exchange(own, "mp", self.mp, 0)

    def split_rows(self, tensor):
        half = tensor.shape[0] // 2
        core = self.mp_bit(0)
        own = lax.dynamic_slice_in_dim(tensor, core * half, half, 0)
        other = lax.dynamic_slice_in_dim(tensor, (1 - core) * half, half, 0)
        return own, other

    def global_rows(self, own, other):
        core = self.mp_bit(0)
        return jnp.concatenate(
            [jnp.where(core == 0, own, other), jnp.where(core == 0, other, own)], axis=0
        )

    def order(self, bits):
        masks = []
        for place in range(self.dp):
            mask = 0
            for i, bit in enumerate(bits):
                if not (place >> (len(bits) - 1 - i)) & 1:
                    mask |= 1 << bit
            masks.append(mask)
        return jnp.array(masks, jnp.int32) ^ self.dp_index


class Merge:
    def __init__(self, links, pairs, bits):
        self.links, self.pairs, self.bits = links, pairs, bits
        self.blocks = pairs[0][0].shape[1] // 128
        self.step = 0

    def advance(self, clock):
        if self.step == len(self.bits):
            self.total = clock.one(self.keep + clock.one(self.got))
            self.step += 1
            return
        got, pairs = None, self.pairs
        if self.step:
            got = clock.one(self.got)
        else:
            pairs = [(clock.one(pairs[0][0]), pairs[0][1])] + pairs[1:]
        if self.step == 0:
            send = product_rows(pairs, clock.cell, 0, self.blocks // 2, 0)[0]
        elif self.step == 1:
            send, self.keep = product_rows(
                pairs, clock.cell, self.blocks // 2, self.blocks // 4, self.blocks // 4, got
            )
        else:
            send, self.keep = add_split(self.keep, got)
        send = clock.one(send)
        self.got = exchange(send, "dp", self.links.dp, self.bits[self.step])
        self.step += 1

    @property
    def open(self):
        return self.step <= len(self.bits)


class ShardMerge:
    def __init__(self, links, shards):
        self.links, self.shards = links, shards
        self.step = 0

    def split(self, total):
        pairs = total.reshape((total.shape[0] // 2, 2) + total.shape[1:])
        own = self.links.dp_bit(self.step)
        self.keep = pick(pairs, own, 1)
        return pick(pairs, 1 - own, 1)

    def advance(self, clock):
        if self.step == bit_count(self.links.dp):
            self.total = clock.one(self.keep + clock.one(self.got))
            self.step += 1
            return
        total = self.shards
        if self.step:
            total = self.keep + clock.one(self.got)
        send = clock.one(self.split(clock.one(total)))
        self.got = exchange(send, "dp", self.links.dp, self.step)
        clock.hold()
        self.step += 1

    @property
    def open(self):
        return self.step <= bit_count(self.links.dp)


def norm_parts(rows):
    row_mean = jnp.mean(rows, axis=-1, keepdims=True)
    centred = rows - row_mean
    spread = jnp.mean(centred * centred, axis=-1, keepdims=True)
    inverse = lax.rsqrt(spread + 1e-05)
    return centred * inverse, jnp.broadcast_to(inverse, (rows.shape[0], 128))


def make_per_device(dp, mp):
    def per_device(
        pixels,
        dataset_id,
        variable_mask,
        lead_hours,
        token_counts,
        dataset_weight,
        patch_weight,
        variable_embed,
        position_embed,
        pool_query,
        pool_query_weight,
        pool_key_weight,
        pool_value_weight,
        pool_value_bias,
        pool_output_weight,
        pool_output_bias,
        lead_weight,
        lead_bias,
        norm_gain,
        norm_bias,
        attention_weight,
        attention_bias,
        output_weight,
        output_bias,
        up_weight,
        up_bias,
        down_weight,
        down_bias,
        cotangent,
    ):
        links = Links(dp, mp)
        var_count, pix_count, row_count = pixels.shape[1:]
        flat_count = var_count * pix_count
        model_width = patch_weight.shape[2]
        local_width = pool_query_weight.shape[1]
        head_count = local_width // HEAD_DIM
        layer_count = attention_weight.shape[0]
        shard = model_width // dp

        def heads_first(tensor):
            return tensor.reshape(row_count, head_count, HEAD_DIM).transpose(1, 0, 2)

        def heads_last(tensor):
            return tensor.transpose(1, 0, 2).reshape(row_count, local_width)

        dataset_pick = jnp.arange(variable_mask.shape[0], dtype=jnp.int32) == dataset_id[0]
        mask_row = jnp.sum(jnp.where(dataset_pick[:, None], variable_mask, 0), axis=0)
        item_weight = jnp.sum(jnp.where(dataset_pick, dataset_weight, 0)).astype(F32)
        own_count = token_counts[0].astype(F32)
        lead_scale = lead_hours[0].astype(F32) / 24.0

        patch_flat = patch_weight.reshape(flat_count, model_width)
        (
            pix_low,
            query_row,
            key_rows,
            score_rows,
            value_flat,
            value_var,
            pool_probs,
            pooled,
            part_own,
            part_send,
        ) = pool_front(
            links.mp_bit(0).reshape(1),
            pixels[0].reshape(flat_count, row_count),
            patch_flat,
            variable_embed,
            pool_query[None],
            pool_query_weight,
            pool_key_weight,
            pool_value_weight,
            pool_value_bias[None],
            mask_row[None],
            pool_output_weight,
        )
        mine, got = links.begin_sum(part_own, part_send)
        count_total = after(jnp.full((8, 128), own_count, F32), mine)
        for bit in range(bit_count(dp)):
            count_total = count_total + exchange(count_total, "dp", dp, bit)
        scale_cell = item_weight * own_count / count_total
        item_scale = scale_cell[0, 0]
        position_own = links.split_rows(position_embed)[0]
        offset_rows = pool_output_bias + position_own + lead_scale * lead_weight + lead_bias
        mine, scale_cell = lax.optimization_barrier((mine, scale_cell))
        hidden = mine + got + offset_rows

        bits = list(range(bit_count(dp)))
        bits_late = bits[1:] + bits[:1]
        shards, shards_late = links.order(bits), links.order(bits_late)
        top = layer_count - 1
        kept = []
        for layer in range(layer_count):
            unit_one, inverse_one = norm_parts(hidden)
            unit_other = links.other_rows(unit_one)
            qkv, mixed, totals, part_own, part_send = attend_forward(
                unit_one,
                unit_other,
                norm_gain[layer, 0],
                norm_bias[layer, 0],
                attention_weight[layer],
                attention_bias[layer],
                output_weight[layer],
            )
            mine, got = links.begin_sum(part_own, part_send)
            normed = norm_rows(
                after(unit_one, mine), unit_other, norm_gain[layer, 0], norm_bias[layer, 0], shards
            )
            mine, normed = lax.optimization_barrier((mine, normed))
            if layer == 0:
                grad_own, grad_other = links.split_rows(after(cotangent[0], mine))
                grad_other, down_low, down_left = merge_rows(
                    grad_own, grad_other, jnp.zeros_like(grad_other), shards_late
                )
                mine, down_low = lax.optimization_barrier((mine, down_low))
            hidden = hidden + (mine + got) + output_bias[layer]
            unit_two, inverse_two = norm_parts(hidden)
            unit_other = links.other_rows(unit_two)
            activation, slope, part_own, part_send, normed_two = feed_forward(
                unit_two,
                unit_other,
                norm_gain,
                norm_bias,
                (layer, 1),
                up_weight,
                up_bias,
                down_weight,
                shards,
            )
            if shard % 128:
                normed_two = take_columns(normed_two, shards, shard)
            if layer < top:
                mine, got = links.begin_sum(part_own, part_send)
            if layer < top:
                if layer == 0:
                    mine, embed_late, key_late = lax.optimization_barrier(
                        (mine, variable_embed, key_rows)
                    )
                    embed_left = embed_columns(patch_flat, embed_late, shards)
                    key_high, key_rest = two_part(key_late)
                    left_side = jnp.concatenate(
                        [
                            pool_value_weight,
                            pool_query_weight,
                            jnp.concatenate(
                                [key_high, key_high, key_rest, jnp.zeros_like(key_high)], axis=0
                            ).T,
                        ],
                        axis=1,
                    )
                    sides = left_side.reshape(dp, mp, shard // mp, left_side.shape[1])
                    mp_bits = range(bit_count(mp))
                    masks = [
                        sum((1 - ((i >> (len(mp_bits) - 1 - b)) & 1)) << b for b in mp_bits)
                        for i in range(mp)
                    ]
                    sides = jnp.stack(
                        [pick(sides, links.mp_index ^ mask, 1) for mask in masks]
                    ).reshape(2, model_width // 2, left_side.shape[1])
                    side_send, side_own = sides[0], sides[1]
                    mine, embed_left, side_own, side_send = lax.optimization_barrier(
                        (mine, embed_left, side_own, side_send)
                    )
                mine, normed_two = lax.optimization_barrier((mine, normed_two))
                hidden = hidden + (mine + got) + down_bias[layer]
            kept.append(
                (
                    unit_one,
                    inverse_one,
                    normed,
                    qkv,
                    totals,
                    mixed,
                    unit_two,
                    inverse_two,
                    normed_two,
                    slope,
                    activation,
                )
            )

        last_own, last_send = part_own, part_send
        row_sums = {}
        local_sums = {}
        merges = {}
        row_sums["down_bias", top] = jnp.sum(grad_own, axis=0)

        head_of = jnp.arange(local_width, dtype=jnp.int32) // HEAD_DIM
        head_pick = head_of[:, None] == jnp.arange(head_count, dtype=jnp.int32)[None, :]
        clock = Clock(scale_cell)

        def advance(spot):
            for name in PLAN.get(spot, ()):
                if name in merges and merges[name].open:
                    merges[name].advance(clock)

        def fill(spot):
            return (lambda: advance(spot)) if PLAN.get(spot) else None

        for layer in reversed(range(layer_count)):
            depth = top - layer
            (
                unit_one,
                inverse_one,
                normed,
                qkv,
                totals,
                mixed,
                unit_two,
                inverse_two,
                normed_two,
                slope,
                activation,
            ) = kept[layer]
            merges["down", depth] = Merge(
                links, [(down_left, activation)], bits if depth else bits_late
            )
            advance(("top", depth))
            if layer == top:
                last_send = clock.one(last_send)
                last_other = exchange(last_send, "mp", mp, 0)
            pre_low, up_sums, part_own, part_send = feed_back(
                clock.one(down_low), slope, down_weight, up_weight, layer
            )
            local_sums["up_bias", layer] = up_sums[0]
            pre_low, part_send = clock.both(pre_low, part_send)
            merges["up", depth] = Merge(links, [(normed_two, pre_low)], bits)
            advance(("pre", depth))
            mine, got = links.ordered_sum(clock, lambda: part_own, part_send, fill(("core_two", depth)))
            if not PLAN.get(("wait_two", depth)):
                clock.hold()
            advance(("wait_two", depth))
            if layer == top:
                last_mine = clock.one(last_own + clock.one(last_other))
            mine, got = clock.both(mine, got)
            if layer == top:
                for bit in range(1, bit_count(mp)):
                    last_mine = clock.one(last_mine)
                    last_other = exchange(last_mine, "mp", mp, bit)
                    if bit + 1 < bit_count(mp):
                        last_mine = last_mine + last_other
            change, grad_own, sums = norm_back(
                mine, got, unit_two, inverse_two, norm_gain, (layer, 1), grad_own
            )
            change, sums = clock.both(change, sums)
            row_sums["gain", layer, 1] = sums[0]
            row_sums["bias", layer, 1] = sums[1]
            row_sums["out_bias", layer] = sums[2]
            other_change = links.other_rows(change)
            clock.hold()
            grad_other, out_low, out_left = merge_rows(
                grad_own, grad_other, clock.one(other_change), shards
            )
            out_low = clock.one(out_low)
            advance(("mid", depth))
            grads, qv_sums, part_own, part_send = attend_back(
                clock.one(out_low), qkv, totals, attention_weight[layer], output_weight[layer]
            )
            local_sums["qv", layer] = qv_sums
            merges["att", depth] = Merge(links, [(out_left, mixed), (normed, grads)], bits)
            mine, got = links.ordered_sum(clock, lambda: part_own, part_send, fill(("core_one", depth)))
            if not PLAN.get(("wait_one", depth)):
                clock.hold()
            advance(("wait_one", depth))
            if layer == top:
                hidden = clock.one(hidden + (last_mine + clock.one(last_other)) + down_bias[top])
                hidden_other = links.other_rows(hidden)
                clock.hold()
                layer_out = clock.one(links.global_rows(hidden, clock.one(hidden_other)))
            mine, got = clock.both(mine, got)
            change, grad_own, sums = norm_back(
                mine, got, unit_one, inverse_one, norm_gain, (layer, 0), grad_own
            )
            change, sums = clock.both(change, sums)
            row_sums["gain", layer, 0] = sums[0]
            row_sums["bias", layer, 0] = sums[1]
            if layer:
                row_sums["down_bias", layer - 1] = sums[2]
            other_change = links.other_rows(change)
            clock.hold()
            grad_other, down_low, down_left = merge_rows(
                grad_own, grad_other, clock.one(other_change), shards
            )
            down_low = clock.one(down_low)
            advance(("end", depth))
            down_low = clock.one(down_low)

        row_sums["column"] = sums[2]
        row_sums["lead"] = lead_scale * sums[2]
        clock.hold()
        value_grad, key_grad, key_grad_var, pixel_own, pixel_send = pool_back(
            clock.one(down_low), pool_output_weight, value_flat, value_var, pix_low, pool_probs, score_rows
        )
        flat_all = flat_count + var_count
        item_scale = clock.cell[0, 0]
        sub = shard // mp
        embed_send, embed_own, summed_key, query_grad, pool_bias = embed_terms(
            side_send,
            side_own,
            clock.one(value_grad),
            key_grad,
            key_grad_var,
            clock.cell,
            patch_flat,
            variable_embed,
            pool_key_weight,
        )
        value_low = value_grad.astype(BF)
        query_late = clock.one(pool_query)
        merges["tail"] = Merge(
            links,
            [
                (down_left, pooled),
                (embed_left, jnp.concatenate([value_low, value_low[flat_count:]], axis=0)),
            ],
            bits,
        )
        query_grad = query_grad[0]
        embed_send = clock.one(embed_send)
        embed_got = exchange(embed_send, "mp", mp, 0)
        clock.hold()
        embed_got = clock.one(embed_got)
        for bit in range(1, bit_count(mp)):
            embed_send, embed_own = add_split(embed_own, embed_got)
            embed_send = clock.one(embed_send)
            embed_got = exchange(embed_send, "mp", mp, bit)
        names = []
        for layer in range(layer_count):
            names += [("gain", layer, 0), ("gain", layer, 1), ("bias", layer, 0), ("bias", layer, 1)]
        for layer in range(layer_count):
            names += [("out_bias", layer), ("down_bias", layer)]
        names += ["column", "lead"]
        own_sums = clock.one(jnp.stack([row_sums[name] for name in names]) * item_scale)
        other_sums = exchange(own_sums, "mp", mp, 0)
        advance("back")
        lanes = embed_own.shape[1]

        full_sums = own_sums + clock.one(other_sums)
        local = jnp.stack([local_sums["up_bias", layer] for layer in range(layer_count)]) * item_scale
        thin = [local_sums["qv", layer] for layer in range(layer_count)]
        thin = jnp.concatenate([jnp.concatenate(thin, axis=0) * item_scale, pool_bias], axis=0)
        packed = jnp.concatenate(
            [
                full_sums.reshape(len(names), dp, shard).transpose(1, 0, 2).reshape(dp, -1),
                summed_key.reshape(head_count, dp, shard).transpose(1, 0, 2).reshape(dp, -1),
                local.reshape(layer_count, dp, -1).transpose(1, 0, 2).reshape(dp, -1),
                thin.reshape(2 * layer_count + 1, dp, -1).transpose(1, 0, 2).reshape(dp, -1),
                jnp.broadcast_to(query_grad[None, :], (dp, local_width)),
            ],
            axis=1,
        )
        packed_size = packed.shape[1]
        packed_rows = -(-packed_size // 1024) * 8
        packed = jnp.pad(packed, ((0, 0), (0, packed_rows * 128 - packed_size)))
        packed = packed.reshape(dp, packed_rows, 128)
        position = (grad_own * item_scale).reshape(row_count // 2, dp, shard).transpose(1, 0, 2)
        position, packed = clock.both(position, packed)
        advance("vectors")
        embed_grad = (embed_own + clock.one(embed_got)).reshape(dp, sub, lanes)
        lane_blocks = lanes // 128
        if shard == 128:
            tall = jnp.concatenate(
                [embed_grad[:, :, i * 128 : (i + 1) * 128] for i in range(lane_blocks)]
                + [packed, position],
                axis=1,
            )
            merges["small"] = ShardMerge(links, tall)
        else:
            merges["small"] = ShardMerge(
                links,
                jnp.concatenate(
                    [part.reshape(dp, 1, -1) for part in (embed_grad, packed, position)], axis=2
                ),
            )
        advance("small")

        pixel_mine, pixel_got = links.ordered_sum(clock, lambda: pixel_own, pixel_send)
        clock.hold()
        advance("values")
        pixel_mine, pixel_got = clock.both(pixel_mine, pixel_got)
        pixel_mine = clock.one(pixel_mine + pixel_got)
        pixel_other = links.other_rows(pixel_mine)
        clock.hold()
        advance("pixels")
        pixel_grad = links.global_rows(pixel_mine, clock.one(pixel_other))
        pixel_grad = clock.one(pixel_grad.T.reshape(1, var_count, pix_count, row_count))
        advance("rows")
        for name in DRAIN:
            if merges[name].open:
                merges[name].advance(clock)
        for merge in merges.values():
            while merge.open:
                merge.advance(clock)
        finished = {}
        for kind in ("down", "up", "att"):
            parts = [merges[kind, top - layer].total for layer in range(layer_count)]
            finished[kind] = finish_layers(
                kind, parts, clock.cell if kind == "att" else scale_cell, layer_count, shard, local_width
            )
        tail_total = merges["tail"].total
        small = merges["small"].total[0]
        if shard == 128:
            embed_rows = sub * lane_blocks
            embed_grad = jnp.concatenate(
                [small[i * sub : (i + 1) * sub] for i in range(lane_blocks)], axis=1
            )
            packed = small[embed_rows : embed_rows + packed_rows].reshape(-1)
            position = small[embed_rows + packed_rows :]
        else:
            size = sub * lane_blocks * 128
            embed_grad = small[0, :size].reshape(sub, lane_blocks * 128)
            packed = small[0, size : size + packed_rows * 128]
            position = small[0, size + packed_rows * 128 :].reshape(row_count // 2, shard)
        position = links.global_rows(position, links.other_rows(position))
        offset = 0

        def take(*shape):
            nonlocal offset
            size = math.prod(shape)
            piece = packed[offset : offset + size].reshape(shape)
            offset += size
            return piece

        gains = take(layer_count, 2, shard)
        biases = []
        gain_list = []
        offset = 0
        norm_all = take(layer_count, 2, 2, shard)
        gain_list = norm_all[:, 0]
        biases = norm_all[:, 1]
        dense_bias = take(layer_count, 2, shard)
        column_total = take(shard)
        lead_total = take(shard)
        key_shard = take(head_count, shard)
        up_bias_total = take(layer_count, local.shape[1] // dp)
        thin_total = take(2 * layer_count + 1, local_width // dp)
        query_total = take(local_width)

        query_low = query_late.astype(BF)
        query_rows = lax.dynamic_slice_in_dim(query_low, links.dp_index * shard, shard, 0)
        query_weight_grad = query_rows.astype(F32)[:, None] * query_total[None, :]
        key_weight_grad = (
            jnp.repeat(key_shard.T, HEAD_DIM, axis=1) * query_row / ROOT_DIM
        )
        embed_turned = embed_grad.T
        return (
            layer_out[None],
            pixel_grad,
            embed_turned[:flat_count].reshape(var_count, pix_count, sub),
            embed_turned[flat_count:flat_all],
            position,
            embed_turned[flat_all],
            query_weight_grad,
            key_weight_grad,
            tail_total[:, local_width:],
            thin_total[-1],
            tail_total[:, :local_width].T,
            column_total,
            lead_total,
            column_total,
            gain_list,
            biases,
            finished["att"][1],
            thin_total[:-1].reshape(layer_count, 2, local_width // dp),
            finished["att"][0],
            dense_bias[:, 0],
            finished["up"][0],
            up_bias_total,
            finished["down"][0],
            dense_bias[:, 1],
        )

    return per_device


def solution(mesh):
    return jax.shard_map(
        make_per_device(mesh.shape["dp"], mesh.shape["mp"]),
        mesh=mesh,
        in_specs=(
            P("dp", None, None, None),
            P("dp"),
            P(),
            P("dp"),
            P("dp"),
            P(),
            P(),
            P(),
            P(),
            P(),
            P(None, "mp"),
            P(None, "mp"),
            P(None, "mp"),
            P("mp"),
            P("mp", None),
            P(),
            P(),
            P(),
            P(),
            P(),
            P(None, None, None, "mp"),
            P(None, None, "mp"),
            P(None, "mp", None),
            P(),
            P(None, None, "mp"),
            P(None, "mp"),
            P(None, "mp", None),
            P(),
            P("dp", None, None),
        ),
        out_specs=(
            P("dp", None, None),
            P("dp", None, None, None),
            P(None, None, ("dp", "mp")),
            P(None, ("dp", "mp")),
            P(None, "dp"),
            P(("dp", "mp")),
            P("dp", "mp"),
            P("dp", "mp"),
            P("dp", "mp"),
            P(("mp", "dp")),
            P("mp", "dp"),
            P("dp"),
            P("dp"),
            P("dp"),
            P(None, None, "dp"),
            P(None, None, "dp"),
            P(None, None, "dp", "mp"),
            P(None, None, ("mp", "dp")),
            P(None, "mp", "dp"),
            P(None, "dp"),
            P(None, "dp", "mp"),
            P(None, ("mp", "dp")),
            P(None, "mp", "dp"),
            P(None, "dp"),
        ),
        check_vma=False,
    )
```

```python
import math

import jax
import jax.numpy as jnp
from jax import lax
from jax.experimental import pallas as pl
from jax.experimental.pallas import tpu as pltpu
from jax.sharding import PartitionSpec as P

HEAD_DIM = 64
PLAN = {
    ("pre", 0): [("up", 0), ("down", 0)],
    ("core_one", 0): [("att", 0)],
    ("wait_one", 0): [("down", 0), ("up", 0)],
    ("core_two", 1): [("down", 1)],
    ("wait_two", 1): [("up", 0)],
    ("mid", 1): [("down", 0), ("att", 0)],
    ("wait_one", 1): [("up", 0), ("up", 1), ("att", 0), ("down", 1)],
    ("end", 1): [("down", 0), ("att", 1)],
    "back": [("down", 1), ("att", 0), ("up", 1)],
    "small": ["small"],
    "values": ["tail", ("down", 1), ("up", 1), ("att", 1)],
    "pixels": ["small", ("up", 1), "tail", ("att", 1)],
    "rows": ["small", ("att", 1), "tail", "small", "tail"],
}
DRAIN = []
ROOT_DIM = math.sqrt(HEAD_DIM)
PRODUCT_BLOCKS = 2
BF = jnp.bfloat16
F32 = jnp.float32


def matmul(left, right):
    return jnp.dot(left, right, preferred_element_type=F32)


def matmul_tn(left, right):
    return lax.dot_general(left, right, (((0,), (0,)), ((), ())), preferred_element_type=F32)


def matmul_nt(left, right):
    return lax.dot_general(left, right, (((1,), (1,)), ((), ())), preferred_element_type=F32)


def two_part(tensor):
    high = tensor.astype(BF)
    return high, (tensor - high.astype(F32)).astype(BF)


def gelu_exact(pre_act):
    return jax.nn.gelu(pre_act, approximate=False)


def bit_count(size):
    bits = size.bit_length() - 1
    assert 1 << bits == size
    return bits


def exchange(tensor, axis, size, bit):
    return lax.ppermute(tensor, axis, [(i, i ^ (1 << bit)) for i in range(size)])


def pick(tensor, index, axis):
    return lax.dynamic_index_in_dim(tensor, index, axis, keepdims=False)


def after(value, *earlier):
    return lax.optimization_barrier((value,) + earlier)[0]


def vmem_limit(size):
    return pltpu.CompilerParams(vmem_limit_bytes=int(size * 1.25) + (2 << 20))


LONG = pl.CostEstimate(flops=10**12, bytes_accessed=8, transcendentals=0)


def step_cell(cell):
    def kernel(cell_ref, out_ref):
        out_ref[...] = cell_ref[...]

    return pl.pallas_call(
        kernel,
        out_shape=jax.ShapeDtypeStruct(cell.shape, F32),
        cost_estimate=LONG,
        compiler_params=vmem_limit(0),
        name="step_cell",
    )(cell)


class Clock:
    def __init__(self, cell):
        self.cell = cell

    def both(self, *values):
        *values, self.cell = lax.optimization_barrier((*values, self.cell))
        return values

    def one(self, value):
        return self.both(value)[0]

    def hold(self):
        self.cell = step_cell(self.cell)


def ordered_columns(source, target, shards_ref, count, shard):
    for place in range(count):
        column = pl.multiple_of(shards_ref[place] * shard, shard)
        target[:, place * shard : (place + 1) * shard] = source[:, pl.ds(column, shard)]


def take_columns(rows, shards, shard):
    pieces = rows.reshape(rows.shape[0], -1, shard)[:, shards]
    return pieces.reshape(rows.shape)


def norm_rows(own, other, gain, bias, shards):
    half, width = own.shape
    count = shards.shape[0]
    shard = width // count
    if shard % 128:
        rows = jnp.concatenate([own, other], axis=0) * gain + bias
        return take_columns(rows.astype(BF), shards, shard)

    def kernel(shards_ref, own_ref, other_ref, gain_ref, bias_ref, out_ref, low_ref):
        low_ref[:half] = (own_ref[...] * gain_ref[...] + bias_ref[...]).astype(BF)
        low_ref[half:] = (other_ref[...] * gain_ref[...] + bias_ref[...]).astype(BF)
        ordered_columns(low_ref, out_ref, shards_ref, count, shard)

    return pl.pallas_call(
        kernel,
        out_shape=jax.ShapeDtypeStruct((2 * half, width), BF),
        in_specs=[pl.BlockSpec(memory_space=pltpu.SMEM)] + [pl.BlockSpec()] * 4,
        scratch_shapes=[pltpu.VMEM((2 * half, width), BF)],
        cost_estimate=pl.CostEstimate(
            flops=4 * half * width, bytes_accessed=12 * half * width, transcendentals=0
        ),
        compiler_params=vmem_limit(16 * half * width),
        name="norm_rows",
    )(shards, own, other, gain[None], bias[None])


def embed_columns(patch, embed, shards):
    flat, width = patch.shape
    var_count = embed.shape[0]
    count = shards.shape[0]
    shard = width // count
    if shard % 128:
        high, rest = two_part(embed)
        return take_columns(jnp.concatenate([patch, high, rest], axis=0), shards, shard)

    def kernel(shards_ref, patch_ref, embed_ref, out_ref):
        for place in range(count):
            column = pl.ds(pl.multiple_of(shards_ref[place] * shard, shard), shard)
            target = slice(place * shard, (place + 1) * shard)
            high, rest = two_part(embed_ref[:, column])
            out_ref[:flat, target] = patch_ref[:, column]
            out_ref[flat : flat + var_count, target] = high
            out_ref[flat + var_count :, target] = rest

    return pl.pallas_call(
        kernel,
        out_shape=jax.ShapeDtypeStruct((flat + 2 * var_count, width), BF),
        in_specs=[pl.BlockSpec(memory_space=pltpu.SMEM)] + [pl.BlockSpec()] * 2,
        compiler_params=vmem_limit(8 << 20),
        name="embed_columns",
    )(shards, patch, embed)


def merge_rows(own, other, change, shards):
    half, width = own.shape
    count = shards.shape[0]
    shard = width // count
    if shard % 128:
        total = other + change
        low = jnp.concatenate([own, total], axis=0).astype(BF)
        return total, low, take_columns(low, shards, shard)

    def kernel(shards_ref, own_ref, other_ref, change_ref, other_out, low_out, ordered_out):
        low_out[:half] = own_ref[...].astype(BF)
        total = other_ref[...] + change_ref[...]
        other_out[...] = total
        low_out[half:] = total.astype(BF)
        ordered_columns(low_out, ordered_out, shards_ref, count, shard)

    return pl.pallas_call(
        kernel,
        out_shape=(
            jax.ShapeDtypeStruct((half, width), F32),
            jax.ShapeDtypeStruct((2 * half, width), BF),
            jax.ShapeDtypeStruct((2 * half, width), BF),
        ),
        in_specs=[pl.BlockSpec(memory_space=pltpu.SMEM)] + [pl.BlockSpec()] * 3,
        cost_estimate=LONG,
        compiler_params=vmem_limit(26 * half * width),
        name="merge_rows",
    )(shards, own, other, change)


def norm_back(mine, got, unit, inverse, gains, place, grad):
    half, width = mine.shape
    size = half

    def kernel(mine_ref, got_ref, unit_ref, inverse_ref, gain_ref, grad_ref, change_out, grad_out, sums_out):
        pull = mine_ref[...] + got_ref[...]
        unit_rows = unit_ref[...]
        scaled = pull * gain_ref[place[0], place[1] : place[1] + 1]
        first = jnp.mean(scaled, axis=-1, keepdims=True)
        second = jnp.mean(scaled * unit_rows, axis=-1, keepdims=True)
        change = inverse_ref[:, :1] * (scaled - first - unit_rows * second)
        change_out[...] = change
        total = grad_ref[...] + change
        grad_out[...] = total

        @pl.when(pl.program_id(0) == 0)
        def _():
            sums_out[...] = jnp.zeros_like(sums_out)

        sums_out[0:1] += jnp.sum(pull * unit_rows, axis=0, keepdims=True)
        sums_out[1:2] += jnp.sum(pull, axis=0, keepdims=True)
        sums_out[2:3] += jnp.sum(total, axis=0, keepdims=True)

    rows = jax.ShapeDtypeStruct((half, width), F32)
    block = pl.BlockSpec((size, width), lambda j: (j, 0))
    return pl.pallas_call(
        kernel,
        out_shape=(rows, rows, jax.ShapeDtypeStruct((3, width), F32)),
        grid=(half // size,),
        in_specs=[
            block,
            block,
            block,
            pl.BlockSpec((size, 128), lambda j: (j, 0)),
            pl.BlockSpec(gains.shape, lambda j: (0, 0, 0)),
            block,
        ],
        out_specs=(block, block, pl.BlockSpec((3, width), lambda j: (0, 0))),
        cost_estimate=LONG,
        compiler_params=vmem_limit(64 * size * width),
        name="norm_back",
    )(mine, got, unit, inverse, gains, grad)


def feed_forward(unit_own, unit_other, gains, biases, place, up_weight, up_bias, down_weight, shards, with_down):
    half, width = unit_own.shape
    rows = 2 * half
    layer, which = place
    hidden = up_weight.shape[2]
    size = hidden // 4
    spread_of = math.sqrt(2.0)
    peak = 1.0 / math.sqrt(2.0 * math.pi)

    count = shards.shape[0]
    shard = width // count

    def kernel(shards_ref, own_ref, other_ref, gain_ref, bias_ref, up_ref, up_bias_ref, down_ref,
               activation_out, slope_out, *refs):
        *parts, ordered_out, normed_ref = refs
        own_out, send_out = parts if with_down else (None, None)
        step = pl.program_id(0)

        @pl.when(step == 0)
        def _():
            gain = gain_ref[layer, which : which + 1]
            bias = bias_ref[layer, which : which + 1]
            normed_ref[:half] = (own_ref[...] * gain + bias).astype(BF)
            normed_ref[half:] = (other_ref[...] * gain + bias).astype(BF)
            if with_down:
                own_out[...] = jnp.zeros_like(own_out)
                send_out[...] = jnp.zeros_like(send_out)
            if shard % 128:
                ordered_out[...] = normed_ref[...]
            else:
                ordered_columns(normed_ref, ordered_out, shards_ref, count, shard)

        pre = matmul(normed_ref[...], up_ref[0]) + up_bias_ref[layer : layer + 1]
        below = 0.5 + 0.5 * lax.erf(pre / spread_of)
        slope_out[...] = below + pre * (jnp.exp(-0.5 * pre * pre) * peak)
        activation = (pre * below).astype(BF)
        activation_out[...] = activation
        if with_down:
            send_out[...] += matmul(activation[half:], down_ref[0])
            own_out[...] += matmul(activation[:half], down_ref[0])

    piece = jax.ShapeDtypeStruct((half, width), F32)
    whole = pl.BlockSpec((half, width), lambda j: (0, 0))
    return pl.pallas_call(
        kernel,
        out_shape=(
            jax.ShapeDtypeStruct((rows, hidden), BF),
            jax.ShapeDtypeStruct((rows, hidden), F32),
            *([piece, piece] if with_down else []),
            jax.ShapeDtypeStruct((rows, width), BF),
        ),
        grid=(hidden // size,),
        in_specs=[
            pl.BlockSpec(memory_space=pltpu.SMEM),
            whole,
            whole,
            pl.BlockSpec(gains.shape, lambda j: (0, 0, 0)),
            pl.BlockSpec(biases.shape, lambda j: (0, 0, 0)),
            pl.BlockSpec((1, width, size), lambda j: (layer, 0, j)),
            pl.BlockSpec((up_bias.shape[0], size), lambda j: (0, j)),
            pl.BlockSpec((1, size, width), lambda j: (layer, j, 0)),
        ],
        out_specs=(
            pl.BlockSpec((rows, size), lambda j: (0, j)),
            pl.BlockSpec((rows, size), lambda j: (0, j)),
            *([whole, whole] if with_down else []),
            pl.BlockSpec((rows, width), lambda j: (0, 0)),
        ),
        scratch_shapes=[pltpu.VMEM((rows, width), BF)],
        cost_estimate=LONG,
        compiler_params=vmem_limit(44 << 20),
        name="feed_forward",
    )(shards, unit_own, unit_other, gains, biases, up_weight, up_bias, down_weight)


def feed_back(low, slope, down_weight, up_weight, layer, stream):
    rows, width = low.shape
    half = rows // 2
    hidden = slope.shape[1]
    size = hidden // 4

    def kernel(low_ref, slope_ref, down_ref, up_ref, pre_out, sums_out, own_out, send_out):
        @pl.when(pl.program_id(0) == 0)
        def _():
            own_out[...] = jnp.zeros_like(own_out)
            send_out[...] = jnp.zeros_like(send_out)

        grad = matmul_nt(low_ref[...], down_ref[0]) * slope_ref[...]
        sums_out[...] = jnp.sum(grad, axis=0, keepdims=True)
        grad_low = grad.astype(BF)
        pre_out[...] = grad_low
        send_out[...] += matmul_nt(grad_low[half:], up_ref[0])
        own_out[...] += matmul_nt(grad_low[:half], up_ref[0])

    piece = jax.ShapeDtypeStruct((half, width), F32)
    whole = pl.BlockSpec((half, width), lambda j: (0, 0))
    return pl.pallas_call(
        kernel,
        out_shape=(
            jax.ShapeDtypeStruct((rows, hidden), BF),
            jax.ShapeDtypeStruct((1, hidden), F32),
            piece,
            piece,
        ),
        grid=(hidden // size,),
        in_specs=[
            pl.BlockSpec((rows, width), lambda j: (0, 0)),
            pl.BlockSpec((rows, size), lambda j: (0, j)),
            pl.BlockSpec((1, size, width), lambda j: (layer, j, 0)),
            pl.BlockSpec((1, width, size), lambda j: (layer, 0, j)),
        ],
        out_specs=(
            pl.BlockSpec((rows, size), lambda j: (0, j)),
            pl.BlockSpec((1, size), lambda j: (0, j)),
            whole,
            whole,
        ),
        cost_estimate=LONG,
        compiler_params=vmem_limit((44 << 20) if stream else 26 * rows * width),
        name="feed_back",
    )(low, slope, down_weight, up_weight)


def embed_terms(side_send, side_own, value_grad, key_grad, key_var, cell, patch, embed, key_weight):
    count, _ = side_send.shape
    flat_all, local_width = value_grad.shape
    head_count, flat = key_grad.shape
    model_width = patch.shape[1]
    lanes = -(-(flat_all + 1) // 128) * 128

    def kernel(send_ref, own_ref, value_ref, key_ref, var_ref, cell_ref, patch_ref, embed_ref, weight_ref,
               send_out, own_out, sum_out, query_out, bias_out, value_low_ref):
        scale = cell_ref[0:1, 0:1]
        value_low_ref[...] = (value_ref[...] * scale).astype(BF)
        bias_out[...] = jnp.sum(value_ref[flat:], axis=0, keepdims=True) * scale
        key_high, key_rest = two_part(key_ref[...] * scale)
        var_high, var_rest = two_part(var_ref[...] * scale)
        embed_high, embed_rest = two_part(embed_ref[...])
        total = matmul(key_high, patch_ref[...]) + matmul(key_rest, patch_ref[...])
        total = total + matmul(var_high, embed_high) + matmul(var_rest, embed_high)
        total = total + matmul(var_high, embed_rest)
        sum_out[...] = total
        high, rest = two_part(total)
        query = matmul(high, weight_ref[...]) + matmul(rest, weight_ref[...])
        head = lax.broadcasted_iota(jnp.int32, (head_count, local_width), 0)
        column = lax.broadcasted_iota(jnp.int32, (head_count, local_width), 1)
        inside = (column >= head * HEAD_DIM) & (column < (head + 1) * HEAD_DIM)
        query = jnp.sum(jnp.where(inside, query, 0.0), axis=0, keepdims=True) / ROOT_DIM
        query_out[...] = query
        query_high, query_rest = two_part(query)
        query_rows = jnp.concatenate(
            [query_high.astype(F32), query_rest.astype(F32), jnp.zeros((6, local_width), F32)], axis=0
        ).astype(BF)
        flat_rows, var_rows = [
            jnp.concatenate(
                [part.astype(F32) for part in (first, second, first, jnp.zeros_like(first))], axis=0
            ).astype(BF)
            for first, second in ((key_high, key_rest), (var_high, var_rest))
        ]
        for side_ref, out_ref in ((send_ref, send_out), (own_ref, own_out)):
            keys = side_ref[:, 2 * local_width :]
            values = side_ref[:, :local_width]
            weight = side_ref[:, local_width : 2 * local_width]
            out_ref[...] = jnp.zeros_like(out_ref)
            out_ref[:, :flat] = matmul_nt(values, value_low_ref[:flat]) + matmul(keys, flat_rows)
            out_ref[:, flat:flat_all] = matmul_nt(values, value_low_ref[flat:]) + matmul(keys, var_rows)
            part = matmul_nt(weight, query_rows)
            out_ref[:, flat_all : flat_all + 1] = jnp.sum(part, axis=1, keepdims=True)

    block = jax.ShapeDtypeStruct((count, lanes), F32)
    return pl.pallas_call(
        kernel,
        out_shape=(
            block,
            block,
            jax.ShapeDtypeStruct((head_count, model_width), F32),
            jax.ShapeDtypeStruct((1, local_width), F32),
            jax.ShapeDtypeStruct((1, local_width), F32),
        ),
        scratch_shapes=[pltpu.VMEM((flat_all, local_width), BF)],
        cost_estimate=LONG,
        compiler_params=vmem_limit(14 << 20),
        name="embed_terms",
    )(side_send, side_own, value_grad, key_grad, key_var, cell, patch, embed, key_weight)


def product_rows(pairs, scale, start, first, second, got=None):
    widths = [right.shape[1] for _, right in pairs]
    total = sum(widths)
    has_got = got is not None
    count = first + second
    size = 128 * PRODUCT_BLOCKS
    start, first, second, count = [n // PRODUCT_BLOCKS for n in (start, first, second, count)]

    def kernel(scale_ref, *refs):
        ins = refs[: 2 * len(pairs)]
        outs = refs[2 * len(pairs) + has_got :]
        step = pl.program_id(0)

        def fill(out_ref):
            column = 0
            for i, width in enumerate(widths):
                block = (
                    lax.dot_general(
                        ins[2 * i][...],
                        ins[2 * i + 1][...],
                        (((0,), (0,)), ((), ())),
                        preferred_element_type=F32,
                    )
                    * scale_ref[0:1, 0:1]
                )
                if has_got:
                    block = block + refs[2 * len(pairs)][:, column : column + width]
                out_ref[:, column : column + width] = block
                column += width

        if second:
            pl.when(step < first)(lambda: fill(outs[0]))
            pl.when(step >= first)(lambda: fill(outs[1]))
        else:
            fill(outs[0])

    in_specs = [pl.BlockSpec(scale.shape, lambda j: (0, 0))]
    operands = [scale]
    traffic = 0
    for left, right in pairs:
        rows = left.shape[0]
        in_specs.append(pl.BlockSpec((rows, size), lambda j: (0, start + j)))
        in_specs.append(pl.BlockSpec(right.shape, lambda j: (0, 0)))
        operands += [left, right]
        traffic += 2 * 2 * rows * (size + right.shape[1])
    if has_got:
        in_specs.append(pl.BlockSpec((size, total), lambda j: (j, 0)))
        operands.append(got)
    out_shape = [jax.ShapeDtypeStruct((first * size, total), F32)]
    out_specs = [pl.BlockSpec((size, total), lambda j: (jnp.minimum(j, first - 1), 0))]
    if second:
        out_shape.append(jax.ShapeDtypeStruct((second * size, total), F32))
        out_specs.append(pl.BlockSpec((size, total), lambda j: (jnp.maximum(j - first, 0), 0)))
    return pl.pallas_call(
        kernel,
        out_shape=out_shape,
        grid=(count,),
        in_specs=in_specs,
        out_specs=out_specs,
        cost_estimate=LONG,
        compiler_params=vmem_limit(traffic + 2 * 4 * size * total * 4),
        name="product_rows",
    )(*operands)


def add_rows(own, got):
    rows, width = own.shape
    size = rows // 2

    def kernel(own_ref, got_ref, out_ref):
        out_ref[...] = own_ref[...] + got_ref[...]

    block = pl.BlockSpec((size, width), lambda j: (j, 0))
    return pl.pallas_call(
        kernel,
        out_shape=jax.ShapeDtypeStruct((rows, width), F32),
        grid=(rows // size,),
        in_specs=[block, block],
        out_specs=block,
        cost_estimate=LONG,
        compiler_params=vmem_limit(32 * size * width),
        name="add_rows",
    )(own, got)


def add_split(keep, got):
    rows, width = keep.shape
    half = rows // 2
    size = min(128, half)
    count = half // size

    def kernel(keep_ref, got_ref, first_out, second_out):
        total = keep_ref[...] + got_ref[...]

        @pl.when(pl.program_id(0) < count)
        def _():
            first_out[...] = total

        @pl.when(pl.program_id(0) >= count)
        def _():
            second_out[...] = total

    block = (size, width)
    return pl.pallas_call(
        kernel,
        out_shape=[jax.ShapeDtypeStruct((half, width), F32)] * 2,
        grid=(2 * count,),
        in_specs=[pl.BlockSpec(block, lambda j: (j, 0))] * 2,
        out_specs=[
            pl.BlockSpec(block, lambda j: (jnp.minimum(j, count - 1), 0)),
            pl.BlockSpec(block, lambda j: (jnp.maximum(j - count, 0), 0)),
        ],
        cost_estimate=LONG,
        compiler_params=vmem_limit(32 * size * width),
        name="add_split",
    )(keep, got)


def attend_forward(unit_own, unit_other, gain, bias, weights, biases, out_weight):
    half, model_width = unit_own.shape
    rows = 2 * half
    local_width = weights.shape[2]
    head_count = local_width // HEAD_DIM

    def kernel(own_ref, other_ref, gain_ref, bias_ref, weight_ref, biases_ref, out_weight_ref,
               qkv_out, mixed_out, total_out, own_out, send_out, normed_ref):
        normed_ref[:half] = (own_ref[...] * gain_ref[...] + bias_ref[...]).astype(BF)
        normed_ref[half:] = (other_ref[...] * gain_ref[...] + bias_ref[...]).astype(BF)
        normed = normed_ref[...]
        qkv_out[:, :local_width] = (matmul(normed, weight_ref[0]) + biases_ref[0:1]).astype(BF)
        qkv_out[:, local_width : 2 * local_width] = matmul(normed, weight_ref[1]).astype(BF)
        qkv_out[:, 2 * local_width :] = (matmul(normed, weight_ref[2]) + biases_ref[1:2]).astype(BF)
        for head in range(head_count):
            one = slice(head * HEAD_DIM, (head + 1) * HEAD_DIM)
            query = qkv_out[:, one]
            key = qkv_out[:, local_width + head * HEAD_DIM : local_width + (head + 1) * HEAD_DIM]
            value = qkv_out[:, 2 * local_width + head * HEAD_DIM : 2 * local_width + (head + 1) * HEAD_DIM]
            scores = matmul_nt(query, key) / ROOT_DIM
            top = jnp.max(scores, axis=-1, keepdims=True)
            exponent = jnp.exp(scores - top)
            row_sum = jnp.sum(exponent, axis=-1, keepdims=True)
            attend = (exponent / row_sum).astype(BF)
            mixed_out[:, one] = matmul(attend, value).astype(BF)
            total_out[:, head : head + 1] = top + jnp.log(row_sum)
        send_out[...] = matmul(mixed_out[half:], out_weight_ref[...])
        own_out[...] = matmul(mixed_out[:half], out_weight_ref[...])

    piece = jax.ShapeDtypeStruct((half, model_width), F32)
    return pl.pallas_call(
        kernel,
        out_shape=(
            jax.ShapeDtypeStruct((rows, 3 * local_width), BF),
            jax.ShapeDtypeStruct((rows, local_width), BF),
            jax.ShapeDtypeStruct((rows, 128), F32),
            piece,
            piece,
        ),
        scratch_shapes=[pltpu.VMEM((rows, model_width), BF)],
        cost_estimate=pl.CostEstimate(
            flops=2 * rows * local_width * (4 * model_width + 2 * rows),
            bytes_accessed=8 * rows * model_width + 8 * local_width * model_width,
            transcendentals=rows * rows * head_count,
        ),
        compiler_params=vmem_limit(22 * rows * model_width),
        name="attend_forward",
    )(unit_own, unit_other, gain[None], bias[None], weights, biases, out_weight)


def attend_back(low, qkv, totals, weights, out_weight):
    rows, model_width = low.shape
    half = rows // 2
    local_width = weights.shape[2]
    head_count = local_width // HEAD_DIM

    def kernel(low_ref, qkv_ref, total_ref, weight_ref, out_weight_ref,
               grads_out, sums_out, own_out, send_out, mix_ref):
        mix_ref[...] = matmul_nt(low_ref[...], out_weight_ref[...]).astype(BF)
        for head in range(head_count):
            one = slice(head * HEAD_DIM, (head + 1) * HEAD_DIM)
            two = slice(local_width + head * HEAD_DIM, local_width + (head + 1) * HEAD_DIM)
            three = slice(2 * local_width + head * HEAD_DIM, 2 * local_width + (head + 1) * HEAD_DIM)
            query, key, value = qkv_ref[:, one], qkv_ref[:, two], qkv_ref[:, three]
            mix = mix_ref[:, one]
            attend = jnp.exp(matmul_nt(query, key) / ROOT_DIM - total_ref[:, head : head + 1])
            grad_attend = matmul_nt(mix, value)
            grad_value = matmul_tn(attend.astype(BF), mix)
            weighted = attend * grad_attend
            grad_scores = weighted - attend * jnp.sum(weighted, axis=-1, keepdims=True)
            grad_low = grad_scores.astype(BF)
            grad_query = matmul(grad_low, key) / ROOT_DIM
            grad_key = matmul_tn(grad_low, query) / ROOT_DIM
            grads_out[:, one] = grad_query.astype(BF)
            grads_out[:, two] = grad_key.astype(BF)
            grads_out[:, three] = grad_value.astype(BF)
            sums_out[0:1, one] = jnp.sum(grad_query, axis=0, keepdims=True)
            sums_out[1:2, one] = jnp.sum(grad_value, axis=0, keepdims=True)

        def pull(part):
            total = matmul_nt(grads_out[part, :local_width], weight_ref[0])
            total = total + matmul_nt(grads_out[part, local_width : 2 * local_width], weight_ref[1])
            return total + matmul_nt(grads_out[part, 2 * local_width :], weight_ref[2])

        send_out[...] = pull(slice(half, rows))
        own_out[...] = pull(slice(0, half))

    piece = jax.ShapeDtypeStruct((half, model_width), F32)
    return pl.pallas_call(
        kernel,
        out_shape=(
            jax.ShapeDtypeStruct((rows, 3 * local_width), BF),
            jax.ShapeDtypeStruct((2, local_width), F32),
            piece,
            piece,
        ),
        scratch_shapes=[pltpu.VMEM((rows, local_width), BF)],
        cost_estimate=LONG,
        compiler_params=vmem_limit(24 * rows * model_width),
        name="attend_back",
    )(low, qkv, totals, weights, out_weight)


def finish_layers(kind, pieces, cell, layer_count, shard, local_width):
    width = pieces[0].shape[1]
    shapes = {
        "down": [(layer_count, width, shard)],
        "up": [(layer_count, shard, width)],
        "att": [
            (layer_count, local_width, shard),
            (layer_count, 3, shard, local_width),
        ],
    }[kind]

    def store(values, outs):
        for layer, value in enumerate(values):
            if kind == "down":
                outs[0][layer] = value.T
            elif kind == "up":
                outs[0][layer] = value
            else:
                outs[0][layer] = value[:, :local_width].T
                for which in range(3):
                    begin = (1 + which) * local_width
                    outs[1][layer, which] = value[:, begin : begin + local_width]

    if shard % 128:
        values = pieces
        if kind == "down":
            return [jnp.stack([value.T for value in values])]
        if kind == "up":
            return [jnp.stack(values)]
        rest = [
            value[:, local_width:].reshape(shard, 3, local_width).transpose(1, 0, 2)
            for value in values
        ]
        return [jnp.stack([value[:, :local_width].T for value in values]), jnp.stack(rest)]

    def kernel(*refs):
        store([ref[...] for ref in refs[:layer_count]], refs[layer_count + 1 :])

    return pl.pallas_call(
        kernel,
        out_shape=[jax.ShapeDtypeStruct(shape, F32) for shape in shapes],
        cost_estimate=pl.CostEstimate(
            flops=layer_count * shard * width,
            bytes_accessed=12 * layer_count * shard * width,
            transcendentals=0,
        ),
        compiler_params=vmem_limit(20 * layer_count * shard * width),
        name="finish_layers",
    )(*pieces, cell)


def one_hot_segments(var_count, pix_count):
    flat = var_count * pix_count
    rows = lax.broadcasted_iota(jnp.int32, (var_count, flat), 0)
    columns = lax.broadcasted_iota(jnp.int32, (var_count, flat), 1)
    inside = (columns >= rows * pix_count) & (columns < (rows + 1) * pix_count)
    return jnp.where(inside, 1.0, 0.0).astype(BF)


def pool_front(core, pixels, patch, embed, query, query_weight, key_weight, value_weight,
               value_bias, mask, out_weight):
    var_count = embed.shape[0]
    flat, rows = pixels.shape
    pix_count = flat // var_count
    model_width, local_width = key_weight.shape
    head_count = local_width // HEAD_DIM
    half = rows // 2

    large = (query_weight, key_weight, pixels, patch, embed, value_weight, out_weight)

    def kernel(core_ref, query_ref, bias_ref, mask_ref, *refs):
        sources, refs = refs[: len(large)], refs[len(large) :]
        (low_out, query_out, key_out, score_out, flat_out, var_out, probs_out, pooled_out,
         own_out, send_out, turned_ref) = refs[:11]
        held, sems = refs[11 : 11 + len(large)], refs[11 + len(large)]
        copies = [
            pltpu.make_async_copy(source, target, sems.at[i])
            for i, (source, target) in enumerate(zip(sources, held))
        ]
        for copy in copies:
            copy.start()
        (query_weight_ref, key_weight_ref, pixels_ref, patch_ref, embed_ref, value_weight_ref,
         out_weight_ref) = held
        copies[0].wait()
        query = matmul(query_ref[...].astype(BF), query_weight_ref[...]).astype(BF)
        query_out[...] = query.astype(F32)
        copies[1].wait()
        for head in range(head_count):
            one = slice(head * HEAD_DIM, (head + 1) * HEAD_DIM)
            key_out[head : head + 1] = matmul_nt(query[:, one], key_weight_ref[:, one]) / ROOT_DIM
        copies[2].wait()
        turned_ref[...] = pixels_ref[...].T
        mine = pl.multiple_of(core_ref[0] * half, 8)
        theirs = pl.multiple_of(half - core_ref[0] * half, 8)
        low_out[:half] = turned_ref[pl.ds(mine, half)].astype(BF)
        low_out[half:] = turned_ref[pl.ds(theirs, half)].astype(BF)
        for copy in copies[3:]:
            copy.wait()
        key_high, key_rest = two_part(key_out[...])
        embed_high, embed_rest = two_part(embed_ref[...])
        score_out[...] = matmul_nt(key_high, patch_ref[...]) + matmul_nt(key_rest, patch_ref[...])
        score_var = (
            matmul_nt(key_high, embed_high)
            + matmul_nt(key_rest, embed_high)
            + matmul_nt(key_high, embed_rest)
        )
        flat_out[...] = matmul(patch_ref[...], value_weight_ref[...]).astype(BF)
        value_var = matmul(embed_high, value_weight_ref[...]) + matmul(embed_rest, value_weight_ref[...])
        var_out[...] = (value_var + bias_ref[...]).astype(BF)
        segment = one_hot_segments(var_count, pix_count)
        for head in range(head_count):
            one = slice(head * HEAD_DIM, (head + 1) * HEAD_DIM)
            pix = low_out[...].astype(F32)
            high, rest = two_part(pix * score_out[head : head + 1])
            scores = matmul_nt(high, segment) + matmul_nt(rest, segment) + score_var[head : head + 1]
            scores = jnp.where(mask_ref[...] > 0, scores, -1000000000.0)
            exponent = jnp.exp(scores - jnp.max(scores, axis=-1, keepdims=True))
            probs = exponent / jnp.sum(exponent, axis=-1, keepdims=True)
            probs_out[head] = probs
            low = probs.astype(BF)
            mixed = (matmul(low, segment) * pix).astype(BF)
            pooled_out[:, one] = (matmul(mixed, flat_out[:, one]) + matmul(low, var_out[:, one])).astype(BF)
        send_out[...] = matmul(pooled_out[half:], out_weight_ref[...])
        own_out[...] = matmul(pooled_out[:half], out_weight_ref[...])

    piece = jax.ShapeDtypeStruct((half, model_width), F32)
    return pl.pallas_call(
        kernel,
        out_shape=(
            jax.ShapeDtypeStruct((rows, flat), BF),
            jax.ShapeDtypeStruct((1, local_width), F32),
            jax.ShapeDtypeStruct((head_count, model_width), F32),
            jax.ShapeDtypeStruct((head_count, flat), F32),
            jax.ShapeDtypeStruct((flat, local_width), BF),
            jax.ShapeDtypeStruct((var_count, local_width), BF),
            jax.ShapeDtypeStruct((head_count, rows, var_count), F32),
            jax.ShapeDtypeStruct((rows, local_width), BF),
            piece,
            piece,
        ),
        in_specs=[pl.BlockSpec(memory_space=pltpu.SMEM)]
        + [pl.BlockSpec()] * 3
        + [pl.BlockSpec(memory_space=pltpu.HBM)] * len(large),
        scratch_shapes=[pltpu.VMEM((rows, flat), F32)]
        + [pltpu.VMEM(array.shape, array.dtype) for array in large]
        + [pltpu.SemaphoreType.DMA((len(large),))],
        cost_estimate=LONG,
        compiler_params=vmem_limit(46 << 20),
        name="pool_front",
    )(core, query, value_bias, mask, *large)


def pool_back(low, out_weight, value_flat, value_var, pix_low, probs, scores):
    rows, flat = pix_low.shape
    head_count, _, var_count = probs.shape
    pix_count = flat // var_count
    local_width = value_flat.shape[1]
    half = rows // 2

    def kernel(low_ref, out_weight_ref, flat_ref, var_ref, pix_ref, probs_ref, score_ref,
               value_out, key_out, key_var_out, own_out, send_out, pooled_ref, pixel_ref):
        pooled_ref[...] = matmul_nt(low_ref[...], out_weight_ref[...]).astype(BF)
        segment = one_hot_segments(var_count, pix_count)
        for head in range(head_count):
            one = slice(head * HEAD_DIM, (head + 1) * HEAD_DIM)
            pix = pix_ref[...].astype(F32)
            pooled = pooled_ref[:, one]
            pull = matmul_nt(pooled, flat_ref[:, one])
            high, rest = two_part(pull * pix)
            grad_probs = (
                matmul_nt(high, segment) + matmul_nt(rest, segment) + matmul_nt(pooled, var_ref[:, one])
            )
            probs_one = probs_ref[head]
            weighted = probs_one * grad_probs
            grad_scores = weighted - probs_one * jnp.sum(weighted, axis=-1, keepdims=True)
            high, rest = two_part(grad_scores)
            wide = matmul(high, segment) + matmul(rest, segment)
            key_out[head : head + 1] = jnp.sum(wide * pix, axis=0, keepdims=True)
            key_var_out[head : head + 1] = jnp.sum(grad_scores, axis=0, keepdims=True)
            probs_low = probs_one.astype(BF)
            probs_wide = matmul(probs_low, segment)
            term = wide * score_ref[head : head + 1] + probs_wide * pull
            if head:
                pixel_ref[...] += term
            else:
                pixel_ref[...] = term
            mixed = (probs_wide * pix).astype(BF)
            value_out[:flat, one] = matmul_tn(mixed, pooled)
            value_out[flat:, one] = matmul_tn(probs_low, pooled)
        own_out[...] = pixel_ref[:half]
        send_out[...] = pixel_ref[half:]

    piece = jax.ShapeDtypeStruct((half, flat), F32)
    return pl.pallas_call(
        kernel,
        out_shape=(
            jax.ShapeDtypeStruct((flat + var_count, local_width), F32),
            jax.ShapeDtypeStruct((head_count, flat), F32),
            jax.ShapeDtypeStruct((head_count, var_count), F32),
            piece,
            piece,
        ),
        scratch_shapes=[pltpu.VMEM((rows, local_width), BF), pltpu.VMEM((rows, flat), F32)],
        cost_estimate=LONG,
        compiler_params=vmem_limit(20 << 20),
        name="pool_back",
    )(low, out_weight, value_flat, value_var, pix_low, probs, scores)


class Links:
    def __init__(self, dp, mp):
        self.dp, self.mp = dp, mp
        self.dp_index = lax.axis_index("dp")
        self.mp_index = lax.axis_index("mp")

    def dp_bit(self, bit):
        return (self.dp_index >> bit) & 1

    def mp_bit(self, bit):
        return (self.mp_index >> bit) & 1

    def ordered_sum(self, clock, own, send, fill=None):
        send = clock.one(send)
        got = exchange(send, "mp", self.mp, 0)
        if fill:
            fill()
        else:
            clock.hold()
        mine = clock.one(add_rows(own(), clock.one(got)))
        last = bit_count(self.mp) - 1
        for bit in range(1, last):
            mine = clock.one(mine + exchange(mine, "mp", self.mp, bit))
        return mine, exchange(mine, "mp", self.mp, last)

    def begin_sum(self, own, send):
        mine = add_rows(own, exchange(send, "mp", self.mp, 0))
        last = bit_count(self.mp) - 1
        for bit in range(1, last):
            mine = mine + exchange(mine, "mp", self.mp, bit)
        return mine, exchange(mine, "mp", self.mp, last)

    def begin_product(self, left, right, product=matmul):
        half = left.shape[0] // 2
        send = product(left[half:], right)
        return self.begin_sum(product(left[:half], right), send)

    def sum_rows(self, partial):
        half = partial.shape[0] // 2
        mine, got = self.begin_sum(partial[:half], partial[half:])
        return mine + got

    def other_rows(self, own):
        return exchange(own, "mp", self.mp, 0)

    def split_rows(self, tensor):
        half = tensor.shape[0] // 2
        core = self.mp_bit(0)
        own = lax.dynamic_slice_in_dim(tensor, core * half, half, 0)
        other = lax.dynamic_slice_in_dim(tensor, (1 - core) * half, half, 0)
        return own, other

    def global_rows(self, own, other):
        core = self.mp_bit(0)
        return jnp.concatenate(
            [jnp.where(core == 0, own, other), jnp.where(core == 0, other, own)], axis=0
        )

    def order(self, bits):
        masks = []
        for place in range(self.dp):
            mask = 0
            for i, bit in enumerate(bits):
                if not (place >> (len(bits) - 1 - i)) & 1:
                    mask |= 1 << bit
            masks.append(mask)
        return jnp.array(masks, jnp.int32) ^ self.dp_index


class Merge:
    def __init__(self, links, pairs, bits):
        self.links, self.pairs, self.bits = links, pairs, bits
        self.blocks = pairs[0][0].shape[1] // 128
        self.step = 0

    def advance(self, clock):
        if self.step == len(self.bits):
            self.total = clock.one(self.keep + clock.one(self.got))
            self.step += 1
            return
        got, pairs = None, self.pairs
        if self.step:
            got = clock.one(self.got)
        else:
            pairs = [(clock.one(pairs[0][0]), pairs[0][1])] + pairs[1:]
        if self.step == 0:
            send = product_rows(pairs, clock.cell, 0, self.blocks // 2, 0)[0]
        elif self.step == 1:
            send, self.keep = product_rows(
                pairs, clock.cell, self.blocks // 2, self.blocks // 4, self.blocks // 4, got
            )
        else:
            send, self.keep = add_split(self.keep, got)
        send = clock.one(send)
        self.got = exchange(send, "dp", self.links.dp, self.bits[self.step])
        self.step += 1

    @property
    def open(self):
        return self.step <= len(self.bits)


class ShardMerge:
    def __init__(self, links, shards):
        self.links, self.shards = links, shards
        self.step = 0

    def split(self, total):
        pairs = total.reshape((total.shape[0] // 2, 2) + total.shape[1:])
        own = self.links.dp_bit(self.step)
        self.keep = pick(pairs, own, 1)
        return pick(pairs, 1 - own, 1)

    def advance(self, clock):
        if self.step == bit_count(self.links.dp):
            self.total = clock.one(self.keep + clock.one(self.got))
            self.step += 1
            return
        total = self.shards
        if self.step:
            total = self.keep + clock.one(self.got)
        send = clock.one(self.split(clock.one(total)))
        self.got = exchange(send, "dp", self.links.dp, self.step)
        clock.hold()
        self.step += 1

    @property
    def open(self):
        return self.step <= bit_count(self.links.dp)


def norm_parts(rows):
    row_mean = jnp.mean(rows, axis=-1, keepdims=True)
    centred = rows - row_mean
    spread = jnp.mean(centred * centred, axis=-1, keepdims=True)
    inverse = lax.rsqrt(spread + 1e-05)
    return centred * inverse, jnp.broadcast_to(inverse, (rows.shape[0], 128))


def make_per_device(dp, mp):
    def per_device(
        pixels,
        dataset_id,
        variable_mask,
        lead_hours,
        token_counts,
        dataset_weight,
        patch_weight,
        variable_embed,
        position_embed,
        pool_query,
        pool_query_weight,
        pool_key_weight,
        pool_value_weight,
        pool_value_bias,
        pool_output_weight,
        pool_output_bias,
        lead_weight,
        lead_bias,
        norm_gain,
        norm_bias,
        attention_weight,
        attention_bias,
        output_weight,
        output_bias,
        up_weight,
        up_bias,
        down_weight,
        down_bias,
        cotangent,
    ):
        links = Links(dp, mp)
        var_count, pix_count, row_count = pixels.shape[1:]
        flat_count = var_count * pix_count
        model_width = patch_weight.shape[2]
        local_width = pool_query_weight.shape[1]
        head_count = local_width // HEAD_DIM
        layer_count = attention_weight.shape[0]
        shard = model_width // dp

        def heads_first(tensor):
            return tensor.reshape(row_count, head_count, HEAD_DIM).transpose(1, 0, 2)

        def heads_last(tensor):
            return tensor.transpose(1, 0, 2).reshape(row_count, local_width)

        dataset_pick = jnp.arange(variable_mask.shape[0], dtype=jnp.int32) == dataset_id[0]
        mask_row = jnp.sum(jnp.where(dataset_pick[:, None], variable_mask, 0), axis=0)
        item_weight = jnp.sum(jnp.where(dataset_pick, dataset_weight, 0)).astype(F32)
        own_count = token_counts[0].astype(F32)
        lead_scale = lead_hours[0].astype(F32) / 24.0

        patch_flat = patch_weight.reshape(flat_count, model_width)
        (
            pix_low,
            query_row,
            key_rows,
            score_rows,
            value_flat,
            value_var,
            pool_probs,
            pooled,
            part_own,
            part_send,
        ) = pool_front(
            links.mp_bit(0).reshape(1),
            pixels[0].reshape(flat_count, row_count),
            patch_flat,
            variable_embed,
            pool_query[None],
            pool_query_weight,
            pool_key_weight,
            pool_value_weight,
            pool_value_bias[None],
            mask_row[None],
            pool_output_weight,
        )
        mine, got = links.begin_sum(part_own, part_send)
        count_total = after(jnp.full((8, 128), own_count, F32), mine)
        for bit in range(bit_count(dp)):
            count_total = count_total + exchange(count_total, "dp", dp, bit)
        scale_cell = item_weight * own_count / count_total
        item_scale = scale_cell[0, 0]
        position_own = links.split_rows(position_embed)[0]
        offset_rows = pool_output_bias + position_own + lead_scale * lead_weight + lead_bias
        mine, scale_cell = lax.optimization_barrier((mine, scale_cell))
        hidden = mine + got + offset_rows

        bits = list(range(bit_count(dp)))
        bits_late = bits[1:] + bits[:1]
        shards, shards_late = links.order(bits), links.order(bits_late)
        top = layer_count - 1
        kept = []
        for layer in range(layer_count):
            unit_one, inverse_one = norm_parts(hidden)
            unit_other = links.other_rows(unit_one)
            qkv, mixed, totals, part_own, part_send = attend_forward(
                unit_one,
                unit_other,
                norm_gain[layer, 0],
                norm_bias[layer, 0],
                attention_weight[layer],
                attention_bias[layer],
                output_weight[layer],
            )
            mine, got = links.begin_sum(part_own, part_send)
            normed = norm_rows(
                after(unit_one, mine), unit_other, norm_gain[layer, 0], norm_bias[layer, 0], shards
            )
            mine, normed = lax.optimization_barrier((mine, normed))
            if layer == 0:
                grad_own, grad_other = links.split_rows(after(cotangent[0], mine))
                grad_other, down_low, down_left = merge_rows(
                    grad_own, grad_other, jnp.zeros_like(grad_other), shards_late
                )
                mine, down_low = lax.optimization_barrier((mine, down_low))
            hidden = hidden + (mine + got) + output_bias[layer]
            unit_two, inverse_two = norm_parts(hidden)
            unit_other = links.other_rows(unit_two)
            activation, slope, *parts, normed_two = feed_forward(
                unit_two,
                unit_other,
                norm_gain,
                norm_bias,
                (layer, 1),
                up_weight,
                up_bias,
                down_weight,
                shards,
                layer < top,
            )
            if shard % 128:
                normed_two = take_columns(normed_two, shards, shard)
            if layer < top:
                mine, got = links.begin_sum(*parts)
            if layer < top:
                if layer == 0:
                    mine, embed_late, key_late = lax.optimization_barrier(
                        (mine, variable_embed, key_rows)
                    )
                    embed_left = embed_columns(patch_flat, embed_late, shards)
                    key_high, key_rest = two_part(key_late)
                    left_side = jnp.concatenate(
                        [
                            pool_value_weight,
                            pool_query_weight,
                            jnp.concatenate(
                                [key_high, key_high, key_rest, jnp.zeros_like(key_high)], axis=0
                            ).T,
                        ],
                        axis=1,
                    )
                    sides = left_side.reshape(dp, mp, shard // mp, left_side.shape[1])
                    mp_bits = range(bit_count(mp))
                    masks = [
                        sum((1 - ((i >> (len(mp_bits) - 1 - b)) & 1)) << b for b in mp_bits)
                        for i in range(mp)
                    ]
                    sides = jnp.stack(
                        [pick(sides, links.mp_index ^ mask, 1) for mask in masks]
                    ).reshape(2, model_width // 2, left_side.shape[1])
                    side_send, side_own = sides[0], sides[1]
                    mine, embed_left, side_own, side_send = lax.optimization_barrier(
                        (mine, embed_left, side_own, side_send)
                    )
                mine, normed_two = lax.optimization_barrier((mine, normed_two))
                hidden = hidden + (mine + got) + down_bias[layer]
            kept.append(
                (
                    unit_one,
                    inverse_one,
                    normed,
                    qkv,
                    totals,
                    mixed,
                    unit_two,
                    inverse_two,
                    normed_two,
                    slope,
                    activation,
                )
            )

        activation_top = activation
        row_sums = {}
        local_sums = {}
        merges = {}
        row_sums["down_bias", top] = jnp.sum(grad_own, axis=0)

        head_of = jnp.arange(local_width, dtype=jnp.int32) // HEAD_DIM
        head_pick = head_of[:, None] == jnp.arange(head_count, dtype=jnp.int32)[None, :]
        clock = Clock(scale_cell)

        def advance(spot):
            for name in PLAN.get(spot, ()):
                if name in merges and merges[name].open:
                    merges[name].advance(clock)

        def fill(spot):
            return (lambda: advance(spot)) if PLAN.get(spot) else None

        for layer in reversed(range(layer_count)):
            depth = top - layer
            (
                unit_one,
                inverse_one,
                normed,
                qkv,
                totals,
                mixed,
                unit_two,
                inverse_two,
                normed_two,
                slope,
                activation,
            ) = kept[layer]
            merges["down", depth] = Merge(
                links, [(down_left, activation)], bits if depth else bits_late
            )
            advance(("top", depth))
            pre_low, up_sums, part_own, part_send = feed_back(
                clock.one(down_low), slope, down_weight, up_weight, layer, layer == top
            )
            local_sums["up_bias", layer] = up_sums[0]
            pre_low, part_send = clock.both(pre_low, part_send)
            merges["up", depth] = Merge(links, [(normed_two, pre_low)], bits)
            advance(("pre", depth))
            mine, got = links.ordered_sum(clock, lambda: part_own, part_send, fill(("core_two", depth)))
            if not PLAN.get(("wait_two", depth)):
                clock.hold()
            advance(("wait_two", depth))
            if layer == top:
                half = row_count // 2
                activation_top = clock.one(activation_top)
                last_send = clock.one(matmul(activation_top[half:], down_weight[top]))
                last_other = exchange(last_send, "mp", mp, 0)
                last_own = matmul(activation_top[:half], down_weight[top])
                last_own = clock.one(last_own)
                clock.hold()
                last_mine = clock.one(last_own + clock.one(last_other))
            mine, got = clock.both(mine, got)
            if layer == top:
                for bit in range(1, bit_count(mp)):
                    last_mine = clock.one(last_mine)
                    last_other = exchange(last_mine, "mp", mp, bit)
                    if bit + 1 < bit_count(mp):
                        last_mine = last_mine + last_other
            change, grad_own, sums = norm_back(
                mine, got, unit_two, inverse_two, norm_gain, (layer, 1), grad_own
            )
            change, sums = clock.both(change, sums)
            row_sums["gain", layer, 1] = sums[0]
            row_sums["bias", layer, 1] = sums[1]
            row_sums["out_bias", layer] = sums[2]
            other_change = links.other_rows(change)
            clock.hold()
            grad_other, out_low, out_left = merge_rows(
                grad_own, grad_other, clock.one(other_change), shards
            )
            out_low = clock.one(out_low)
            advance(("mid", depth))
            grads, qv_sums, part_own, part_send = attend_back(
                clock.one(out_low), qkv, totals, attention_weight[layer], output_weight[layer]
            )
            local_sums["qv", layer] = qv_sums
            merges["att", depth] = Merge(links, [(out_left, mixed), (normed, grads)], bits)
            mine, got = links.ordered_sum(clock, lambda: part_own, part_send, fill(("core_one", depth)))
            if not PLAN.get(("wait_one", depth)):
                clock.hold()
            advance(("wait_one", depth))
            if layer == top:
                hidden = clock.one(hidden + (last_mine + clock.one(last_other)) + down_bias[top])
                hidden_other = links.other_rows(hidden)
                clock.hold()
                layer_out = clock.one(links.global_rows(hidden, clock.one(hidden_other)))
            mine, got = clock.both(mine, got)
            change, grad_own, sums = norm_back(
                mine, got, unit_one, inverse_one, norm_gain, (layer, 0), grad_own
            )
            change, sums = clock.both(change, sums)
            row_sums["gain", layer, 0] = sums[0]
            row_sums["bias", layer, 0] = sums[1]
            if layer:
                row_sums["down_bias", layer - 1] = sums[2]
            other_change = links.other_rows(change)
            clock.hold()
            grad_other, down_low, down_left = merge_rows(
                grad_own, grad_other, clock.one(other_change), shards
            )
            down_low = clock.one(down_low)
            advance(("end", depth))
            down_low = clock.one(down_low)

        row_sums["column"] = sums[2]
        row_sums["lead"] = lead_scale * sums[2]
        clock.hold()
        value_grad, key_grad, key_grad_var, pixel_own, pixel_send = pool_back(
            clock.one(down_low), pool_output_weight, value_flat, value_var, pix_low, pool_probs, score_rows
        )
        flat_all = flat_count + var_count
        item_scale = clock.cell[0, 0]
        sub = shard // mp
        embed_send, embed_own, summed_key, query_grad, pool_bias = embed_terms(
            side_send,
            side_own,
            clock.one(value_grad),
            key_grad,
            key_grad_var,
            clock.cell,
            patch_flat,
            variable_embed,
            pool_key_weight,
        )
        value_low = value_grad.astype(BF)
        query_late = clock.one(pool_query)
        merges["tail"] = Merge(
            links,
            [
                (down_left, pooled),
                (embed_left, jnp.concatenate([value_low, value_low[flat_count:]], axis=0)),
            ],
            bits,
        )
        query_grad = query_grad[0]
        embed_send = clock.one(embed_send)
        embed_got = exchange(embed_send, "mp", mp, 0)
        clock.hold()
        embed_got = clock.one(embed_got)
        for bit in range(1, bit_count(mp)):
            embed_send, embed_own = add_split(embed_own, embed_got)
            embed_send = clock.one(embed_send)
            embed_got = exchange(embed_send, "mp", mp, bit)
        names = []
        for layer in range(layer_count):
            names += [("gain", layer, 0), ("gain", layer, 1), ("bias", layer, 0), ("bias", layer, 1)]
        for layer in range(layer_count):
            names += [("out_bias", layer), ("down_bias", layer)]
        names += ["column", "lead"]
        own_sums = clock.one(jnp.stack([row_sums[name] for name in names]) * item_scale)
        other_sums = exchange(own_sums, "mp", mp, 0)
        advance("back")
        lanes = embed_own.shape[1]

        full_sums = own_sums + clock.one(other_sums)
        local = jnp.stack([local_sums["up_bias", layer] for layer in range(layer_count)]) * item_scale
        thin = [local_sums["qv", layer] for layer in range(layer_count)]
        thin = jnp.concatenate([jnp.concatenate(thin, axis=0) * item_scale, pool_bias], axis=0)
        packed = jnp.concatenate(
            [
                full_sums.reshape(len(names), dp, shard).transpose(1, 0, 2).reshape(dp, -1),
                summed_key.reshape(head_count, dp, shard).transpose(1, 0, 2).reshape(dp, -1),
                local.reshape(layer_count, dp, -1).transpose(1, 0, 2).reshape(dp, -1),
                thin.reshape(2 * layer_count + 1, dp, -1).transpose(1, 0, 2).reshape(dp, -1),
                jnp.broadcast_to(query_grad[None, :], (dp, local_width)),
            ],
            axis=1,
        )
        packed_size = packed.shape[1]
        packed_rows = -(-packed_size // 1024) * 8
        packed = jnp.pad(packed, ((0, 0), (0, packed_rows * 128 - packed_size)))
        packed = packed.reshape(dp, packed_rows, 128)
        position = (grad_own * item_scale).reshape(row_count // 2, dp, shard).transpose(1, 0, 2)
        position, packed = clock.both(position, packed)
        advance("vectors")
        embed_grad = (embed_own + clock.one(embed_got)).reshape(dp, sub, lanes)
        lane_blocks = lanes // 128
        if shard == 128:
            tall = jnp.concatenate(
                [embed_grad[:, :, i * 128 : (i + 1) * 128] for i in range(lane_blocks)]
                + [packed, position],
                axis=1,
            )
            merges["small"] = ShardMerge(links, tall)
        else:
            merges["small"] = ShardMerge(
                links,
                jnp.concatenate(
                    [part.reshape(dp, 1, -1) for part in (embed_grad, packed, position)], axis=2
                ),
            )
        advance("small")

        pixel_mine, pixel_got = links.ordered_sum(clock, lambda: pixel_own, pixel_send)
        clock.hold()
        advance("values")
        pixel_mine, pixel_got = clock.both(pixel_mine, pixel_got)
        pixel_mine = clock.one(pixel_mine + pixel_got)
        pixel_other = links.other_rows(pixel_mine)
        clock.hold()
        advance("pixels")
        pixel_grad = links.global_rows(pixel_mine, clock.one(pixel_other))
        pixel_grad = clock.one(pixel_grad.T.reshape(1, var_count, pix_count, row_count))
        advance("rows")
        for name in DRAIN:
            if merges[name].open:
                merges[name].advance(clock)
        for merge in merges.values():
            while merge.open:
                merge.advance(clock)
        finished = {}
        for kind in ("down", "up", "att"):
            parts = [merges[kind, top - layer].total for layer in range(layer_count)]
            finished[kind] = finish_layers(
                kind, parts, clock.cell if kind == "att" else scale_cell, layer_count, shard, local_width
            )
        tail_total = merges["tail"].total
        small = merges["small"].total[0]
        if shard == 128:
            embed_rows = sub * lane_blocks
            embed_grad = jnp.concatenate(
                [small[i * sub : (i + 1) * sub] for i in range(lane_blocks)], axis=1
            )
            packed = small[embed_rows : embed_rows + packed_rows].reshape(-1)
            position = small[embed_rows + packed_rows :]
        else:
            size = sub * lane_blocks * 128
            embed_grad = small[0, :size].reshape(sub, lane_blocks * 128)
            packed = small[0, size : size + packed_rows * 128]
            position = small[0, size + packed_rows * 128 :].reshape(row_count // 2, shard)
        position = links.global_rows(position, links.other_rows(position))
        offset = 0

        def take(*shape):
            nonlocal offset
            size = math.prod(shape)
            piece = packed[offset : offset + size].reshape(shape)
            offset += size
            return piece

        gains = take(layer_count, 2, shard)
        biases = []
        gain_list = []
        offset = 0
        norm_all = take(layer_count, 2, 2, shard)
        gain_list = norm_all[:, 0]
        biases = norm_all[:, 1]
        dense_bias = take(layer_count, 2, shard)
        column_total = take(shard)
        lead_total = take(shard)
        key_shard = take(head_count, shard)
        up_bias_total = take(layer_count, local.shape[1] // dp)
        thin_total = take(2 * layer_count + 1, local_width // dp)
        query_total = take(local_width)

        query_low = query_late.astype(BF)
        query_rows = lax.dynamic_slice_in_dim(query_low, links.dp_index * shard, shard, 0)
        query_weight_grad = query_rows.astype(F32)[:, None] * query_total[None, :]
        key_weight_grad = (
            jnp.repeat(key_shard.T, HEAD_DIM, axis=1) * query_row / ROOT_DIM
        )
        embed_turned = embed_grad.T
        return (
            layer_out[None],
            pixel_grad,
            embed_turned[:flat_count].reshape(var_count, pix_count, sub),
            embed_turned[flat_count:flat_all],
            position,
            embed_turned[flat_all],
            query_weight_grad,
            key_weight_grad,
            tail_total[:, local_width:],
            thin_total[-1],
            tail_total[:, :local_width].T,
            column_total,
            lead_total,
            column_total,
            gain_list,
            biases,
            finished["att"][1],
            thin_total[:-1].reshape(layer_count, 2, local_width // dp),
            finished["att"][0],
            dense_bias[:, 0],
            finished["up"][0],
            up_bias_total,
            finished["down"][0],
            dense_bias[:, 1],
        )

    return per_device


def solution(mesh):
    return jax.shard_map(
        make_per_device(mesh.shape["dp"], mesh.shape["mp"]),
        mesh=mesh,
        in_specs=(
            P("dp", None, None, None),
            P("dp"),
            P(),
            P("dp"),
            P("dp"),
            P(),
            P(),
            P(),
            P(),
            P(),
            P(None, "mp"),
            P(None, "mp"),
            P(None, "mp"),
            P("mp"),
            P("mp", None),
            P(),
            P(),
            P(),
            P(),
            P(),
            P(None, None, None, "mp"),
            P(None, None, "mp"),
            P(None, "mp", None),
            P(),
            P(None, None, "mp"),
            P(None, "mp"),
            P(None, "mp", None),
            P(),
            P("dp", None, None),
        ),
        out_specs=(
            P("dp", None, None),
            P("dp", None, None, None),
            P(None, None, ("dp", "mp")),
            P(None, ("dp", "mp")),
            P(None, "dp"),
            P(("dp", "mp")),
            P("dp", "mp"),
            P("dp", "mp"),
            P("dp", "mp"),
            P(("mp", "dp")),
            P("mp", "dp"),
            P("dp"),
            P("dp"),
            P("dp"),
            P(None, None, "dp"),
            P(None, None, "dp"),
            P(None, None, "dp", "mp"),
            P(None, None, ("mp", "dp")),
            P(None, "mp", "dp"),
            P(None, "dp"),
            P(None, "dp", "mp"),
            P(None, ("mp", "dp")),
            P(None, "mp", "dp"),
            P(None, "dp"),
        ),
        check_vma=False,
    )
```

```python
import math

import jax
import jax.numpy as jnp
from jax import lax
from jax.experimental import pallas as pl
from jax.experimental.pallas import tpu as pltpu
from jax.sharding import PartitionSpec as P

HEAD_DIM = 64
PLAN = {
    ("pre", 0): [("up", 0), ("down", 0)],
    ("core_one", 0): [("att", 0)],
    ("wait_one", 0): [("down", 0), ("up", 0)],
    ("core_two", 1): [("down", 1)],
    ("wait_two", 1): [("up", 0)],
    ("mid", 1): [("down", 0), ("att", 0)],
    ("wait_one", 1): [("up", 0), ("up", 1), ("att", 0), ("down", 1)],
    ("end", 1): [("down", 0), ("att", 1)],
    "back": [("down", 1), ("att", 0), ("up", 1)],
    "small": ["small"],
    "values": ["tail", ("down", 1), ("up", 1), ("att", 1)],
    "pixels": ["small", ("up", 1), "tail", ("att", 1)],
    "rows": ["small", ("att", 1), "tail", "small", "tail"],
}
DRAIN = []
ROOT_DIM = math.sqrt(HEAD_DIM)
PRODUCT_BLOCKS = 2
BF = jnp.bfloat16
F32 = jnp.float32


def matmul(left, right):
    return jnp.dot(left, right, preferred_element_type=F32)


def matmul_tn(left, right):
    return lax.dot_general(left, right, (((0,), (0,)), ((), ())), preferred_element_type=F32)


def matmul_nt(left, right):
    return lax.dot_general(left, right, (((1,), (1,)), ((), ())), preferred_element_type=F32)


def two_part(tensor):
    high = tensor.astype(BF)
    return high, (tensor - high.astype(F32)).astype(BF)


def gelu_exact(pre_act):
    return jax.nn.gelu(pre_act, approximate=False)


def bit_count(size):
    bits = size.bit_length() - 1
    assert 1 << bits == size
    return bits


def exchange(tensor, axis, size, bit):
    return lax.ppermute(tensor, axis, [(i, i ^ (1 << bit)) for i in range(size)])


def pick(tensor, index, axis):
    return lax.dynamic_index_in_dim(tensor, index, axis, keepdims=False)


def after(value, *earlier):
    return lax.optimization_barrier((value,) + earlier)[0]


def vmem_limit(size):
    return pltpu.CompilerParams(vmem_limit_bytes=int(size * 1.25) + (2 << 20))


LONG = pl.CostEstimate(flops=10**12, bytes_accessed=8, transcendentals=0)


def step_cell(cell):
    def kernel(cell_ref, out_ref):
        out_ref[...] = cell_ref[...]

    return pl.pallas_call(
        kernel,
        out_shape=jax.ShapeDtypeStruct(cell.shape, F32),
        cost_estimate=LONG,
        compiler_params=vmem_limit(0),
        name="step_cell",
    )(cell)


class Clock:
    def __init__(self, cell):
        self.cell = cell

    def both(self, *values):
        *values, self.cell = lax.optimization_barrier((*values, self.cell))
        return values

    def one(self, value):
        return self.both(value)[0]

    def hold(self):
        self.cell = step_cell(self.cell)


def ordered_columns(source, target, shards_ref, count, shard):
    for place in range(count):
        column = pl.multiple_of(shards_ref[place] * shard, shard)
        target[:, place * shard : (place + 1) * shard] = source[:, pl.ds(column, shard)]


def take_columns(rows, shards, shard):
    pieces = rows.reshape(rows.shape[0], -1, shard)[:, shards]
    return pieces.reshape(rows.shape)


def norm_rows(own, other, gain, bias, shards):
    half, width = own.shape
    count = shards.shape[0]
    shard = width // count
    if shard % 128:
        rows = jnp.concatenate([own, other], axis=0) * gain + bias
        return take_columns(rows.astype(BF), shards, shard)

    def kernel(shards_ref, own_ref, other_ref, gain_ref, bias_ref, out_ref, low_ref):
        low_ref[:half] = (own_ref[...] * gain_ref[...] + bias_ref[...]).astype(BF)
        low_ref[half:] = (other_ref[...] * gain_ref[...] + bias_ref[...]).astype(BF)
        ordered_columns(low_ref, out_ref, shards_ref, count, shard)

    return pl.pallas_call(
        kernel,
        out_shape=jax.ShapeDtypeStruct((2 * half, width), BF),
        in_specs=[pl.BlockSpec(memory_space=pltpu.SMEM)] + [pl.BlockSpec()] * 4,
        scratch_shapes=[pltpu.VMEM((2 * half, width), BF)],
        cost_estimate=pl.CostEstimate(
            flops=4 * half * width, bytes_accessed=12 * half * width, transcendentals=0
        ),
        compiler_params=vmem_limit(16 * half * width),
        name="norm_rows",
    )(shards, own, other, gain[None], bias[None])


def embed_columns(patch, embed, shards):
    flat, width = patch.shape
    var_count = embed.shape[0]
    count = shards.shape[0]
    shard = width // count
    if shard % 128:
        high, rest = two_part(embed)
        return take_columns(jnp.concatenate([patch, high, rest], axis=0), shards, shard)

    def kernel(shards_ref, patch_ref, embed_ref, out_ref):
        for place in range(count):
            column = pl.ds(pl.multiple_of(shards_ref[place] * shard, shard), shard)
            target = slice(place * shard, (place + 1) * shard)
            high, rest = two_part(embed_ref[:, column])
            out_ref[:flat, target] = patch_ref[:, column]
            out_ref[flat : flat + var_count, target] = high
            out_ref[flat + var_count :, target] = rest

    return pl.pallas_call(
        kernel,
        out_shape=jax.ShapeDtypeStruct((flat + 2 * var_count, width), BF),
        in_specs=[pl.BlockSpec(memory_space=pltpu.SMEM)] + [pl.BlockSpec()] * 2,
        compiler_params=vmem_limit(8 << 20),
        name="embed_columns",
    )(shards, patch, embed)


def merge_rows(own, other, change, shards):
    half, width = own.shape
    count = shards.shape[0]
    shard = width // count
    if shard % 128:
        total = other + change
        low = jnp.concatenate([own, total], axis=0).astype(BF)
        return total, low, take_columns(low, shards, shard)

    def kernel(shards_ref, own_ref, other_ref, change_ref, other_out, low_out, ordered_out):
        low_out[:half] = own_ref[...].astype(BF)
        total = other_ref[...] + change_ref[...]
        other_out[...] = total
        low_out[half:] = total.astype(BF)
        ordered_columns(low_out, ordered_out, shards_ref, count, shard)

    return pl.pallas_call(
        kernel,
        out_shape=(
            jax.ShapeDtypeStruct((half, width), F32),
            jax.ShapeDtypeStruct((2 * half, width), BF),
            jax.ShapeDtypeStruct((2 * half, width), BF),
        ),
        in_specs=[pl.BlockSpec(memory_space=pltpu.SMEM)] + [pl.BlockSpec()] * 3,
        cost_estimate=LONG,
        compiler_params=vmem_limit(26 * half * width),
        name="merge_rows",
    )(shards, own, other, change)


def norm_back(mine, got, unit, inverse, gains, place, grad):
    half, width = mine.shape
    size = half

    def kernel(mine_ref, got_ref, unit_ref, inverse_ref, gain_ref, grad_ref, change_out, grad_out, sums_out):
        pull = mine_ref[...] + got_ref[...]
        unit_rows = unit_ref[...]
        scaled = pull * gain_ref[place[0], place[1] : place[1] + 1]
        first = jnp.mean(scaled, axis=-1, keepdims=True)
        second = jnp.mean(scaled * unit_rows, axis=-1, keepdims=True)
        change = inverse_ref[:, :1] * (scaled - first - unit_rows * second)
        change_out[...] = change
        total = grad_ref[...] + change
        grad_out[...] = total

        @pl.when(pl.program_id(0) == 0)
        def _():
            sums_out[...] = jnp.zeros_like(sums_out)

        sums_out[0:1] += jnp.sum(pull * unit_rows, axis=0, keepdims=True)
        sums_out[1:2] += jnp.sum(pull, axis=0, keepdims=True)
        sums_out[2:3] += jnp.sum(total, axis=0, keepdims=True)

    rows = jax.ShapeDtypeStruct((half, width), F32)
    block = pl.BlockSpec((size, width), lambda j: (j, 0))
    return pl.pallas_call(
        kernel,
        out_shape=(rows, rows, jax.ShapeDtypeStruct((3, width), F32)),
        grid=(half // size,),
        in_specs=[
            block,
            block,
            block,
            pl.BlockSpec((size, 128), lambda j: (j, 0)),
            pl.BlockSpec(gains.shape, lambda j: (0, 0, 0)),
            block,
        ],
        out_specs=(block, block, pl.BlockSpec((3, width), lambda j: (0, 0))),
        cost_estimate=LONG,
        compiler_params=vmem_limit(64 * size * width),
        name="norm_back",
    )(mine, got, unit, inverse, gains, grad)


def feed_forward(unit_own, unit_other, gains, biases, place, up_weight, up_bias, down_weight, shards, with_down):
    half, width = unit_own.shape
    rows = 2 * half
    layer, which = place
    hidden = up_weight.shape[2]
    size = hidden // 4
    spread_of = math.sqrt(2.0)
    peak = 1.0 / math.sqrt(2.0 * math.pi)

    count = shards.shape[0]
    shard = width // count

    def kernel(shards_ref, own_ref, other_ref, gain_ref, bias_ref, up_ref, up_bias_ref, down_ref,
               activation_out, slope_out, *refs):
        *parts, ordered_out, normed_ref = refs
        own_out, send_out = parts if with_down else (None, None)
        step = pl.program_id(0)

        @pl.when(step == 0)
        def _():
            gain = gain_ref[layer, which : which + 1]
            bias = bias_ref[layer, which : which + 1]
            normed_ref[:half] = (own_ref[...] * gain + bias).astype(BF)
            normed_ref[half:] = (other_ref[...] * gain + bias).astype(BF)
            if with_down:
                own_out[...] = jnp.zeros_like(own_out)
                send_out[...] = jnp.zeros_like(send_out)
            if shard % 128:
                ordered_out[...] = normed_ref[...]
            else:
                ordered_columns(normed_ref, ordered_out, shards_ref, count, shard)

        pre = matmul(normed_ref[...], up_ref[0]) + up_bias_ref[layer : layer + 1]
        below = 0.5 + 0.5 * lax.erf(pre / spread_of)
        slope_out[...] = below + pre * (jnp.exp(-0.5 * pre * pre) * peak)
        activation = (pre * below).astype(BF)
        activation_out[...] = activation
        if with_down:
            send_out[...] += matmul(activation[half:], down_ref[0])
            own_out[...] += matmul(activation[:half], down_ref[0])

    piece = jax.ShapeDtypeStruct((half, width), F32)
    whole = pl.BlockSpec((half, width), lambda j: (0, 0))
    return pl.pallas_call(
        kernel,
        out_shape=(
            jax.ShapeDtypeStruct((rows, hidden), BF),
            jax.ShapeDtypeStruct((rows, hidden), F32),
            *([piece, piece] if with_down else []),
            jax.ShapeDtypeStruct((rows, width), BF),
        ),
        grid=(hidden // size,),
        in_specs=[
            pl.BlockSpec(memory_space=pltpu.SMEM),
            whole,
            whole,
            pl.BlockSpec(gains.shape, lambda j: (0, 0, 0)),
            pl.BlockSpec(biases.shape, lambda j: (0, 0, 0)),
            pl.BlockSpec((1, width, size), lambda j: (layer, 0, j)),
            pl.BlockSpec((up_bias.shape[0], size), lambda j: (0, j)),
            pl.BlockSpec((1, size, width), lambda j: (layer, j, 0)),
        ],
        out_specs=(
            pl.BlockSpec((rows, size), lambda j: (0, j)),
            pl.BlockSpec((rows, size), lambda j: (0, j)),
            *([whole, whole] if with_down else []),
            pl.BlockSpec((rows, width), lambda j: (0, 0)),
        ),
        scratch_shapes=[pltpu.VMEM((rows, width), BF)],
        cost_estimate=LONG,
        compiler_params=vmem_limit(44 << 20),
        name="feed_forward",
    )(shards, unit_own, unit_other, gains, biases, up_weight, up_bias, down_weight)


def feed_back(low, slope, down_weight, up_weight, layer, stream):
    rows, width = low.shape
    half = rows // 2
    hidden = slope.shape[1]
    size = hidden // 4

    def kernel(low_ref, slope_ref, down_ref, up_ref, pre_out, sums_out, own_out, send_out):
        @pl.when(pl.program_id(0) == 0)
        def _():
            own_out[...] = jnp.zeros_like(own_out)
            send_out[...] = jnp.zeros_like(send_out)

        grad = matmul_nt(low_ref[...], down_ref[0]) * slope_ref[...]
        sums_out[...] = jnp.sum(grad, axis=0, keepdims=True)
        grad_low = grad.astype(BF)
        pre_out[...] = grad_low
        send_out[...] += matmul_nt(grad_low[half:], up_ref[0])
        own_out[...] += matmul_nt(grad_low[:half], up_ref[0])

    piece = jax.ShapeDtypeStruct((half, width), F32)
    whole = pl.BlockSpec((half, width), lambda j: (0, 0))
    return pl.pallas_call(
        kernel,
        out_shape=(
            jax.ShapeDtypeStruct((rows, hidden), BF),
            jax.ShapeDtypeStruct((1, hidden), F32),
            piece,
            piece,
        ),
        grid=(hidden // size,),
        in_specs=[
            pl.BlockSpec((rows, width), lambda j: (0, 0)),
            pl.BlockSpec((rows, size), lambda j: (0, j)),
            pl.BlockSpec((1, size, width), lambda j: (layer, j, 0)),
            pl.BlockSpec((1, width, size), lambda j: (layer, 0, j)),
        ],
        out_specs=(
            pl.BlockSpec((rows, size), lambda j: (0, j)),
            pl.BlockSpec((1, size), lambda j: (0, j)),
            whole,
            whole,
        ),
        cost_estimate=LONG,
        compiler_params=vmem_limit((44 << 20) if stream else 26 * rows * width),
        name="feed_back",
    )(low, slope, down_weight, up_weight)


def embed_terms(side_send, side_own, value_grad, key_grad, key_var, cell, patch, embed, key_weight):
    count, _ = side_send.shape
    flat_all, local_width = value_grad.shape
    head_count, flat = key_grad.shape
    model_width = patch.shape[1]
    lanes = -(-(flat_all + 1) // 128) * 128

    def kernel(send_ref, own_ref, value_ref, key_ref, var_ref, cell_ref, patch_ref, embed_ref, weight_ref,
               send_out, own_out, sum_out, query_out, bias_out, value_low_ref):
        scale = cell_ref[0:1, 0:1]
        value_low_ref[...] = (value_ref[...] * scale).astype(BF)
        bias_out[...] = jnp.sum(value_ref[flat:], axis=0, keepdims=True) * scale
        key_high, key_rest = two_part(key_ref[...] * scale)
        var_high, var_rest = two_part(var_ref[...] * scale)
        embed_high, embed_rest = two_part(embed_ref[...])
        total = matmul(key_high, patch_ref[...]) + matmul(key_rest, patch_ref[...])
        total = total + matmul(var_high, embed_high) + matmul(var_rest, embed_high)
        total = total + matmul(var_high, embed_rest)
        sum_out[...] = total
        high, rest = two_part(total)
        query = matmul(high, weight_ref[...]) + matmul(rest, weight_ref[...])
        head = lax.broadcasted_iota(jnp.int32, (head_count, local_width), 0)
        column = lax.broadcasted_iota(jnp.int32, (head_count, local_width), 1)
        inside = (column >= head * HEAD_DIM) & (column < (head + 1) * HEAD_DIM)
        query = jnp.sum(jnp.where(inside, query, 0.0), axis=0, keepdims=True) / ROOT_DIM
        query_out[...] = query
        query_high, query_rest = two_part(query)
        query_rows = jnp.concatenate(
            [query_high.astype(F32), query_rest.astype(F32), jnp.zeros((6, local_width), F32)], axis=0
        ).astype(BF)
        flat_rows, var_rows = [
            jnp.concatenate(
                [part.astype(F32) for part in (first, second, first, jnp.zeros_like(first))], axis=0
            ).astype(BF)
            for first, second in ((key_high, key_rest), (var_high, var_rest))
        ]
        for side_ref, out_ref in ((send_ref, send_out), (own_ref, own_out)):
            keys = side_ref[:, 2 * local_width :]
            values = side_ref[:, :local_width]
            weight = side_ref[:, local_width : 2 * local_width]
            out_ref[...] = jnp.zeros_like(out_ref)
            out_ref[:, :flat] = matmul_nt(values, value_low_ref[:flat]) + matmul(keys, flat_rows)
            out_ref[:, flat:flat_all] = matmul_nt(values, value_low_ref[flat:]) + matmul(keys, var_rows)
            part = matmul_nt(weight, query_rows)
            out_ref[:, flat_all : flat_all + 1] = jnp.sum(part, axis=1, keepdims=True)

    block = jax.ShapeDtypeStruct((count, lanes), F32)
    return pl.pallas_call(
        kernel,
        out_shape=(
            block,
            block,
            jax.ShapeDtypeStruct((head_count, model_width), F32),
            jax.ShapeDtypeStruct((1, local_width), F32),
            jax.ShapeDtypeStruct((1, local_width), F32),
        ),
        scratch_shapes=[pltpu.VMEM((flat_all, local_width), BF)],
        cost_estimate=LONG,
        compiler_params=vmem_limit(14 << 20),
        name="embed_terms",
    )(side_send, side_own, value_grad, key_grad, key_var, cell, patch, embed, key_weight)


def product_rows(pairs, scale, start, first, second, got=None):
    widths = [right.shape[1] for _, right in pairs]
    total = sum(widths)
    has_got = got is not None
    count = first + second
    size = 128 * PRODUCT_BLOCKS
    start, first, second, count = [n // PRODUCT_BLOCKS for n in (start, first, second, count)]

    def kernel(scale_ref, *refs):
        ins = refs[: 2 * len(pairs)]
        outs = refs[2 * len(pairs) + has_got :]
        step = pl.program_id(0)

        def fill(out_ref):
            column = 0
            for i, width in enumerate(widths):
                block = (
                    lax.dot_general(
                        ins[2 * i][...],
                        ins[2 * i + 1][...],
                        (((0,), (0,)), ((), ())),
                        preferred_element_type=F32,
                    )
                    * scale_ref[0:1, 0:1]
                )
                if has_got:
                    block = block + refs[2 * len(pairs)][:, column : column + width]
                out_ref[:, column : column + width] = block
                column += width

        if second:
            pl.when(step < first)(lambda: fill(outs[0]))
            pl.when(step >= first)(lambda: fill(outs[1]))
        else:
            fill(outs[0])

    in_specs = [pl.BlockSpec(scale.shape, lambda j: (0, 0))]
    operands = [scale]
    traffic = 0
    for left, right in pairs:
        rows = left.shape[0]
        in_specs.append(pl.BlockSpec((rows, size), lambda j: (0, start + j)))
        in_specs.append(pl.BlockSpec(right.shape, lambda j: (0, 0)))
        operands += [left, right]
        traffic += 2 * 2 * rows * (size + right.shape[1])
    if has_got:
        in_specs.append(pl.BlockSpec((size, total), lambda j: (j, 0)))
        operands.append(got)
    out_shape = [jax.ShapeDtypeStruct((first * size, total), F32)]
    out_specs = [pl.BlockSpec((size, total), lambda j: (jnp.minimum(j, first - 1), 0))]
    if second:
        out_shape.append(jax.ShapeDtypeStruct((second * size, total), F32))
        out_specs.append(pl.BlockSpec((size, total), lambda j: (jnp.maximum(j - first, 0), 0)))
    return pl.pallas_call(
        kernel,
        out_shape=out_shape,
        grid=(count,),
        in_specs=in_specs,
        out_specs=out_specs,
        cost_estimate=LONG,
        compiler_params=vmem_limit(traffic + 2 * 4 * size * total * 4),
        name="product_rows",
    )(*operands)


def add_rows(own, got):
    rows, width = own.shape
    size = rows // 2

    def kernel(own_ref, got_ref, out_ref):
        out_ref[...] = own_ref[...] + got_ref[...]

    block = pl.BlockSpec((size, width), lambda j: (j, 0))
    return pl.pallas_call(
        kernel,
        out_shape=jax.ShapeDtypeStruct((rows, width), F32),
        grid=(rows // size,),
        in_specs=[block, block],
        out_specs=block,
        cost_estimate=LONG,
        compiler_params=vmem_limit(32 * size * width),
        name="add_rows",
    )(own, got)


def add_split(keep, got):
    rows, width = keep.shape
    half = rows // 2
    size = min(128, half)
    count = half // size

    def kernel(keep_ref, got_ref, first_out, second_out):
        total = keep_ref[...] + got_ref[...]

        @pl.when(pl.program_id(0) < count)
        def _():
            first_out[...] = total

        @pl.when(pl.program_id(0) >= count)
        def _():
            second_out[...] = total

    block = (size, width)
    return pl.pallas_call(
        kernel,
        out_shape=[jax.ShapeDtypeStruct((half, width), F32)] * 2,
        grid=(2 * count,),
        in_specs=[pl.BlockSpec(block, lambda j: (j, 0))] * 2,
        out_specs=[
            pl.BlockSpec(block, lambda j: (jnp.minimum(j, count - 1), 0)),
            pl.BlockSpec(block, lambda j: (jnp.maximum(j - count, 0), 0)),
        ],
        cost_estimate=LONG,
        compiler_params=vmem_limit(32 * size * width),
        name="add_split",
    )(keep, got)


def attend_forward(unit_own, unit_other, gain, bias, weights, biases, out_weight):
    half, model_width = unit_own.shape
    rows = 2 * half
    local_width = weights.shape[2]
    head_count = local_width // HEAD_DIM

    def kernel(own_ref, other_ref, gain_ref, bias_ref, weight_ref, biases_ref, out_weight_ref,
               qkv_out, mixed_out, total_out, own_out, send_out, normed_ref):
        normed_ref[:half] = (own_ref[...] * gain_ref[...] + bias_ref[...]).astype(BF)
        normed_ref[half:] = (other_ref[...] * gain_ref[...] + bias_ref[...]).astype(BF)
        normed = normed_ref[...]
        qkv_out[:, :local_width] = (matmul(normed, weight_ref[0]) + biases_ref[0:1]).astype(BF)
        qkv_out[:, local_width : 2 * local_width] = matmul(normed, weight_ref[1]).astype(BF)
        qkv_out[:, 2 * local_width :] = (matmul(normed, weight_ref[2]) + biases_ref[1:2]).astype(BF)
        for head in range(head_count):
            one = slice(head * HEAD_DIM, (head + 1) * HEAD_DIM)
            query = qkv_out[:, one]
            key = qkv_out[:, local_width + head * HEAD_DIM : local_width + (head + 1) * HEAD_DIM]
            value = qkv_out[:, 2 * local_width + head * HEAD_DIM : 2 * local_width + (head + 1) * HEAD_DIM]
            scores = matmul_nt(query, key) / ROOT_DIM
            top = jnp.max(scores, axis=-1, keepdims=True)
            exponent = jnp.exp(scores - top)
            row_sum = jnp.sum(exponent, axis=-1, keepdims=True)
            attend = (exponent / row_sum).astype(BF)
            mixed_out[:, one] = matmul(attend, value).astype(BF)
            total_out[:, head : head + 1] = top + jnp.log(row_sum)
        send_out[...] = matmul(mixed_out[half:], out_weight_ref[...])
        own_out[...] = matmul(mixed_out[:half], out_weight_ref[...])

    piece = jax.ShapeDtypeStruct((half, model_width), F32)
    return pl.pallas_call(
        kernel,
        out_shape=(
            jax.ShapeDtypeStruct((rows, 3 * local_width), BF),
            jax.ShapeDtypeStruct((rows, local_width), BF),
            jax.ShapeDtypeStruct((rows, 128), F32),
            piece,
            piece,
        ),
        scratch_shapes=[pltpu.VMEM((rows, model_width), BF)],
        cost_estimate=pl.CostEstimate(
            flops=2 * rows * local_width * (4 * model_width + 2 * rows),
            bytes_accessed=8 * rows * model_width + 8 * local_width * model_width,
            transcendentals=rows * rows * head_count,
        ),
        compiler_params=vmem_limit(22 * rows * model_width),
        name="attend_forward",
    )(unit_own, unit_other, gain[None], bias[None], weights, biases, out_weight)


def attend_back(low, qkv, totals, weights, out_weight):
    rows, model_width = low.shape
    half = rows // 2
    local_width = weights.shape[2]
    head_count = local_width // HEAD_DIM

    def kernel(low_ref, qkv_ref, total_ref, weight_ref, out_weight_ref,
               grads_out, sums_out, own_out, send_out, mix_ref):
        mix_ref[...] = matmul_nt(low_ref[...], out_weight_ref[...]).astype(BF)
        for head in range(head_count):
            one = slice(head * HEAD_DIM, (head + 1) * HEAD_DIM)
            two = slice(local_width + head * HEAD_DIM, local_width + (head + 1) * HEAD_DIM)
            three = slice(2 * local_width + head * HEAD_DIM, 2 * local_width + (head + 1) * HEAD_DIM)
            query, key, value = qkv_ref[:, one], qkv_ref[:, two], qkv_ref[:, three]
            mix = mix_ref[:, one]
            attend = jnp.exp(matmul_nt(query, key) / ROOT_DIM - total_ref[:, head : head + 1])
            grad_attend = matmul_nt(mix, value)
            grad_value = matmul_tn(attend.astype(BF), mix)
            weighted = attend * grad_attend
            grad_scores = weighted - attend * jnp.sum(weighted, axis=-1, keepdims=True)
            grad_low = grad_scores.astype(BF)
            grad_query = matmul(grad_low, key) / ROOT_DIM
            grad_key = matmul_tn(grad_low, query) / ROOT_DIM
            grads_out[:, one] = grad_query.astype(BF)
            grads_out[:, two] = grad_key.astype(BF)
            grads_out[:, three] = grad_value.astype(BF)
            sums_out[0:1, one] = jnp.sum(grad_query, axis=0, keepdims=True)
            sums_out[1:2, one] = jnp.sum(grad_value, axis=0, keepdims=True)

        def pull(part):
            total = matmul_nt(grads_out[part, :local_width], weight_ref[0])
            total = total + matmul_nt(grads_out[part, local_width : 2 * local_width], weight_ref[1])
            return total + matmul_nt(grads_out[part, 2 * local_width :], weight_ref[2])

        send_out[...] = pull(slice(half, rows))
        own_out[...] = pull(slice(0, half))

    piece = jax.ShapeDtypeStruct((half, model_width), F32)
    return pl.pallas_call(
        kernel,
        out_shape=(
            jax.ShapeDtypeStruct((rows, 3 * local_width), BF),
            jax.ShapeDtypeStruct((2, local_width), F32),
            piece,
            piece,
        ),
        scratch_shapes=[pltpu.VMEM((rows, local_width), BF)],
        cost_estimate=LONG,
        compiler_params=vmem_limit(24 * rows * model_width),
        name="attend_back",
    )(low, qkv, totals, weights, out_weight)


def finish_layers(kind, pieces, cell, layer_count, shard, local_width):
    width = pieces[0].shape[1]
    shapes = {
        "down": [(layer_count, width, shard)],
        "up": [(layer_count, shard, width)],
        "att": [
            (layer_count, local_width, shard),
            (layer_count, 3, shard, local_width),
        ],
    }[kind]

    def store(values, outs):
        for layer, value in enumerate(values):
            if kind == "down":
                outs[0][layer] = value.T
            elif kind == "up":
                outs[0][layer] = value
            else:
                outs[0][layer] = value[:, :local_width].T
                for which in range(3):
                    begin = (1 + which) * local_width
                    outs[1][layer, which] = value[:, begin : begin + local_width]

    if shard % 128:
        values = pieces
        if kind == "down":
            return [jnp.stack([value.T for value in values])]
        if kind == "up":
            return [jnp.stack(values)]
        rest = [
            value[:, local_width:].reshape(shard, 3, local_width).transpose(1, 0, 2)
            for value in values
        ]
        return [jnp.stack([value[:, :local_width].T for value in values]), jnp.stack(rest)]

    def kernel(*refs):
        store([ref[...] for ref in refs[:layer_count]], refs[layer_count + 1 :])

    return pl.pallas_call(
        kernel,
        out_shape=[jax.ShapeDtypeStruct(shape, F32) for shape in shapes],
        cost_estimate=pl.CostEstimate(
            flops=layer_count * shard * width,
            bytes_accessed=12 * layer_count * shard * width,
            transcendentals=0,
        ),
        compiler_params=vmem_limit(20 * layer_count * shard * width),
        name="finish_layers",
    )(*pieces, cell)


def one_hot_segments(var_count, pix_count):
    flat = var_count * pix_count
    rows = lax.broadcasted_iota(jnp.int32, (var_count, flat), 0)
    columns = lax.broadcasted_iota(jnp.int32, (var_count, flat), 1)
    inside = (columns >= rows * pix_count) & (columns < (rows + 1) * pix_count)
    return jnp.where(inside, 1.0, 0.0).astype(BF)


def pool_front(core, pixels, patch, embed, query, query_weight, key_weight, value_weight,
               value_bias, mask, out_weight):
    var_count = embed.shape[0]
    flat, rows = pixels.shape
    pix_count = flat // var_count
    model_width, local_width = key_weight.shape
    head_count = local_width // HEAD_DIM
    half = rows // 2

    large = (query_weight, key_weight, pixels, patch, embed, value_weight, out_weight)

    def kernel(core_ref, query_ref, bias_ref, mask_ref, *refs):
        sources, refs = refs[: len(large)], refs[len(large) :]
        (low_out, query_out, key_out, score_out, flat_out, var_out, probs_out, pooled_out,
         own_out, send_out, turned_ref) = refs[:11]
        held, sems = refs[11 : 11 + len(large)], refs[11 + len(large)]
        copies = [
            pltpu.make_async_copy(source, target, sems.at[i])
            for i, (source, target) in enumerate(zip(sources, held))
        ]
        for copy in copies:
            copy.start()
        (query_weight_ref, key_weight_ref, pixels_ref, patch_ref, embed_ref, value_weight_ref,
         out_weight_ref) = held
        copies[0].wait()
        query = matmul(query_ref[...].astype(BF), query_weight_ref[...]).astype(BF)
        query_out[...] = query.astype(F32)
        copies[1].wait()
        for head in range(head_count):
            one = slice(head * HEAD_DIM, (head + 1) * HEAD_DIM)
            key_out[head : head + 1] = matmul_nt(query[:, one], key_weight_ref[:, one]) / ROOT_DIM
        copies[2].wait()
        turned_ref[...] = pixels_ref[...].T
        mine = pl.multiple_of(core_ref[0] * half, 8)
        theirs = pl.multiple_of(half - core_ref[0] * half, 8)
        low_out[:half] = turned_ref[pl.ds(mine, half)].astype(BF)
        low_out[half:] = turned_ref[pl.ds(theirs, half)].astype(BF)
        copies[3].wait()
        copies[4].wait()
        key_high, key_rest = two_part(key_out[...])
        embed_high, embed_rest = two_part(embed_ref[...])
        score_out[...] = matmul_nt(key_high, patch_ref[...]) + matmul_nt(key_rest, patch_ref[...])
        score_var = (
            matmul_nt(key_high, embed_high)
            + matmul_nt(key_rest, embed_high)
            + matmul_nt(key_high, embed_rest)
        )
        copies[5].wait()
        flat_out[...] = matmul(patch_ref[...], value_weight_ref[...]).astype(BF)
        value_var = matmul(embed_high, value_weight_ref[...]) + matmul(embed_rest, value_weight_ref[...])
        var_out[...] = (value_var + bias_ref[...]).astype(BF)
        segment = one_hot_segments(var_count, pix_count)
        for head in range(head_count):
            one = slice(head * HEAD_DIM, (head + 1) * HEAD_DIM)
            pix = low_out[...].astype(F32)
            high, rest = two_part(pix * score_out[head : head + 1])
            scores = matmul_nt(high, segment) + matmul_nt(rest, segment) + score_var[head : head + 1]
            scores = jnp.where(mask_ref[...] > 0, scores, -1000000000.0)
            exponent = jnp.exp(scores - jnp.max(scores, axis=-1, keepdims=True))
            probs = exponent / jnp.sum(exponent, axis=-1, keepdims=True)
            probs_out[head] = probs
            low = probs.astype(BF)
            mixed = (matmul(low, segment) * pix).astype(BF)
            pooled_out[:, one] = (matmul(mixed, flat_out[:, one]) + matmul(low, var_out[:, one])).astype(BF)
        copies[6].wait()
        send_out[...] = matmul(pooled_out[half:], out_weight_ref[...])
        own_out[...] = matmul(pooled_out[:half], out_weight_ref[...])

    piece = jax.ShapeDtypeStruct((half, model_width), F32)
    return pl.pallas_call(
        kernel,
        out_shape=(
            jax.ShapeDtypeStruct((rows, flat), BF),
            jax.ShapeDtypeStruct((1, local_width), F32),
            jax.ShapeDtypeStruct((head_count, model_width), F32),
            jax.ShapeDtypeStruct((head_count, flat), F32),
            jax.ShapeDtypeStruct((flat, local_width), BF),
            jax.ShapeDtypeStruct((var_count, local_width), BF),
            jax.ShapeDtypeStruct((head_count, rows, var_count), F32),
            jax.ShapeDtypeStruct((rows, local_width), BF),
            piece,
            piece,
        ),
        in_specs=[pl.BlockSpec(memory_space=pltpu.SMEM)]
        + [pl.BlockSpec()] * 3
        + [pl.BlockSpec(memory_space=pltpu.HBM)] * len(large),
        scratch_shapes=[pltpu.VMEM((rows, flat), F32)]
        + [pltpu.VMEM(array.shape, array.dtype) for array in large]
        + [pltpu.SemaphoreType.DMA((len(large),))],
        cost_estimate=LONG,
        compiler_params=vmem_limit(46 << 20),
        name="pool_front",
    )(core, query, value_bias, mask, *large)


def pool_back(low, out_weight, value_flat, value_var, pix_low, probs, scores):
    rows, flat = pix_low.shape
    head_count, _, var_count = probs.shape
    pix_count = flat // var_count
    local_width = value_flat.shape[1]
    half = rows // 2

    def kernel(low_ref, out_weight_ref, flat_ref, var_ref, pix_ref, probs_ref, score_ref,
               value_out, key_out, key_var_out, own_out, send_out, pooled_ref, pixel_ref):
        pooled_ref[...] = matmul_nt(low_ref[...], out_weight_ref[...]).astype(BF)
        segment = one_hot_segments(var_count, pix_count)
        for head in range(head_count):
            one = slice(head * HEAD_DIM, (head + 1) * HEAD_DIM)
            pix = pix_ref[...].astype(F32)
            pooled = pooled_ref[:, one]
            pull = matmul_nt(pooled, flat_ref[:, one])
            high, rest = two_part(pull * pix)
            grad_probs = (
                matmul_nt(high, segment) + matmul_nt(rest, segment) + matmul_nt(pooled, var_ref[:, one])
            )
            probs_one = probs_ref[head]
            weighted = probs_one * grad_probs
            grad_scores = weighted - probs_one * jnp.sum(weighted, axis=-1, keepdims=True)
            high, rest = two_part(grad_scores)
            wide = matmul(high, segment) + matmul(rest, segment)
            key_out[head : head + 1] = jnp.sum(wide * pix, axis=0, keepdims=True)
            key_var_out[head : head + 1] = jnp.sum(grad_scores, axis=0, keepdims=True)
            probs_low = probs_one.astype(BF)
            probs_wide = matmul(probs_low, segment)
            term = wide * score_ref[head : head + 1] + probs_wide * pull
            if head:
                pixel_ref[...] += term
            else:
                pixel_ref[...] = term
            mixed = (probs_wide * pix).astype(BF)
            value_out[:flat, one] = matmul_tn(mixed, pooled)
            value_out[flat:, one] = matmul_tn(probs_low, pooled)
        own_out[...] = pixel_ref[:half]
        send_out[...] = pixel_ref[half:]

    piece = jax.ShapeDtypeStruct((half, flat), F32)
    return pl.pallas_call(
        kernel,
        out_shape=(
            jax.ShapeDtypeStruct((flat + var_count, local_width), F32),
            jax.ShapeDtypeStruct((head_count, flat), F32),
            jax.ShapeDtypeStruct((head_count, var_count), F32),
            piece,
            piece,
        ),
        scratch_shapes=[pltpu.VMEM((rows, local_width), BF), pltpu.VMEM((rows, flat), F32)],
        cost_estimate=LONG,
        compiler_params=vmem_limit(20 << 20),
        name="pool_back",
    )(low, out_weight, value_flat, value_var, pix_low, probs, scores)


class Links:
    def __init__(self, dp, mp):
        self.dp, self.mp = dp, mp
        self.dp_index = lax.axis_index("dp")
        self.mp_index = lax.axis_index("mp")

    def dp_bit(self, bit):
        return (self.dp_index >> bit) & 1

    def mp_bit(self, bit):
        return (self.mp_index >> bit) & 1

    def ordered_sum(self, clock, own, send, fill=None):
        send = clock.one(send)
        got = exchange(send, "mp", self.mp, 0)
        if fill:
            fill()
        else:
            clock.hold()
        mine = clock.one(add_rows(own(), clock.one(got)))
        last = bit_count(self.mp) - 1
        for bit in range(1, last):
            mine = clock.one(mine + exchange(mine, "mp", self.mp, bit))
        return mine, exchange(mine, "mp", self.mp, last)

    def begin_sum(self, own, send):
        mine = add_rows(own, exchange(send, "mp", self.mp, 0))
        last = bit_count(self.mp) - 1
        for bit in range(1, last):
            mine = mine + exchange(mine, "mp", self.mp, bit)
        return mine, exchange(mine, "mp", self.mp, last)

    def begin_product(self, left, right, product=matmul):
        half = left.shape[0] // 2
        send = product(left[half:], right)
        return self.begin_sum(product(left[:half], right), send)

    def sum_rows(self, partial):
        half = partial.shape[0] // 2
        mine, got = self.begin_sum(partial[:half], partial[half:])
        return mine + got

    def other_rows(self, own):
        return exchange(own, "mp", self.mp, 0)

    def split_rows(self, tensor):
        half = tensor.shape[0] // 2
        core = self.mp_bit(0)
        own = lax.dynamic_slice_in_dim(tensor, core * half, half, 0)
        other = lax.dynamic_slice_in_dim(tensor, (1 - core) * half, half, 0)
        return own, other

    def global_rows(self, own, other):
        core = self.mp_bit(0)
        return jnp.concatenate(
            [jnp.where(core == 0, own, other), jnp.where(core == 0, other, own)], axis=0
        )

    def order(self, bits):
        masks = []
        for place in range(self.dp):
            mask = 0
            for i, bit in enumerate(bits):
                if not (place >> (len(bits) - 1 - i)) & 1:
                    mask |= 1 << bit
            masks.append(mask)
        return jnp.array(masks, jnp.int32) ^ self.dp_index


class Merge:
    def __init__(self, links, pairs, bits):
        self.links, self.pairs, self.bits = links, pairs, bits
        self.blocks = pairs[0][0].shape[1] // 128
        self.step = 0

    def advance(self, clock):
        if self.step == len(self.bits):
            self.total = clock.one(self.keep + clock.one(self.got))
            self.step += 1
            return
        got, pairs = None, self.pairs
        if self.step:
            got = clock.one(self.got)
        else:
            pairs = [(clock.one(pairs[0][0]), pairs[0][1])] + pairs[1:]
        if self.step == 0:
            send = product_rows(pairs, clock.cell, 0, self.blocks // 2, 0)[0]
        elif self.step == 1:
            send, self.keep = product_rows(
                pairs, clock.cell, self.blocks // 2, self.blocks // 4, self.blocks // 4, got
            )
        else:
            send, self.keep = add_split(self.keep, got)
        send = clock.one(send)
        self.got = exchange(send, "dp", self.links.dp, self.bits[self.step])
        self.step += 1

    @property
    def open(self):
        return self.step <= len(self.bits)


class ShardMerge:
    def __init__(self, links, shards):
        self.links, self.shards = links, shards
        self.step = 0

    def split(self, total):
        pairs = total.reshape((total.shape[0] // 2, 2) + total.shape[1:])
        own = self.links.dp_bit(self.step)
        self.keep = pick(pairs, own, 1)
        return pick(pairs, 1 - own, 1)

    def advance(self, clock):
        if self.step == bit_count(self.links.dp):
            self.total = clock.one(self.keep + clock.one(self.got))
            self.step += 1
            return
        total = self.shards
        if self.step:
            total = self.keep + clock.one(self.got)
        send = clock.one(self.split(clock.one(total)))
        self.got = exchange(send, "dp", self.links.dp, self.step)
        clock.hold()
        self.step += 1

    @property
    def open(self):
        return self.step <= bit_count(self.links.dp)


def norm_parts(rows):
    row_mean = jnp.mean(rows, axis=-1, keepdims=True)
    centred = rows - row_mean
    spread = jnp.mean(centred * centred, axis=-1, keepdims=True)
    inverse = lax.rsqrt(spread + 1e-05)
    return centred * inverse, jnp.broadcast_to(inverse, (rows.shape[0], 128))


def make_per_device(dp, mp):
    def per_device(
        pixels,
        dataset_id,
        variable_mask,
        lead_hours,
        token_counts,
        dataset_weight,
        patch_weight,
        variable_embed,
        position_embed,
        pool_query,
        pool_query_weight,
        pool_key_weight,
        pool_value_weight,
        pool_value_bias,
        pool_output_weight,
        pool_output_bias,
        lead_weight,
        lead_bias,
        norm_gain,
        norm_bias,
        attention_weight,
        attention_bias,
        output_weight,
        output_bias,
        up_weight,
        up_bias,
        down_weight,
        down_bias,
        cotangent,
    ):
        links = Links(dp, mp)
        var_count, pix_count, row_count = pixels.shape[1:]
        flat_count = var_count * pix_count
        model_width = patch_weight.shape[2]
        local_width = pool_query_weight.shape[1]
        head_count = local_width // HEAD_DIM
        layer_count = attention_weight.shape[0]
        shard = model_width // dp

        def heads_first(tensor):
            return tensor.reshape(row_count, head_count, HEAD_DIM).transpose(1, 0, 2)

        def heads_last(tensor):
            return tensor.transpose(1, 0, 2).reshape(row_count, local_width)

        dataset_pick = jnp.arange(variable_mask.shape[0], dtype=jnp.int32) == dataset_id[0]
        mask_row = jnp.sum(jnp.where(dataset_pick[:, None], variable_mask, 0), axis=0)
        item_weight = jnp.sum(jnp.where(dataset_pick, dataset_weight, 0)).astype(F32)
        own_count = token_counts[0].astype(F32)
        lead_scale = lead_hours[0].astype(F32) / 24.0

        patch_flat = patch_weight.reshape(flat_count, model_width)
        (
            pix_low,
            query_row,
            key_rows,
            score_rows,
            value_flat,
            value_var,
            pool_probs,
            pooled,
            part_own,
            part_send,
        ) = pool_front(
            links.mp_bit(0).reshape(1),
            pixels[0].reshape(flat_count, row_count),
            patch_flat,
            variable_embed,
            pool_query[None],
            pool_query_weight,
            pool_key_weight,
            pool_value_weight,
            pool_value_bias[None],
            mask_row[None],
            pool_output_weight,
        )
        mine, got = links.begin_sum(part_own, part_send)
        count_total = after(jnp.full((8, 128), own_count, F32), mine)
        for bit in range(bit_count(dp)):
            count_total = count_total + exchange(count_total, "dp", dp, bit)
        scale_cell = item_weight * own_count / count_total
        item_scale = scale_cell[0, 0]
        position_own = links.split_rows(position_embed)[0]
        offset_rows = pool_output_bias + position_own + lead_scale * lead_weight + lead_bias
        mine, scale_cell = lax.optimization_barrier((mine, scale_cell))
        hidden = mine + got + offset_rows

        bits = list(range(bit_count(dp)))
        bits_late = bits[1:] + bits[:1]
        shards, shards_late = links.order(bits), links.order(bits_late)
        top = layer_count - 1
        kept = []
        for layer in range(layer_count):
            unit_one, inverse_one = norm_parts(hidden)
            unit_other = links.other_rows(unit_one)
            qkv, mixed, totals, part_own, part_send = attend_forward(
                unit_one,
                unit_other,
                norm_gain[layer, 0],
                norm_bias[layer, 0],
                attention_weight[layer],
                attention_bias[layer],
                output_weight[layer],
            )
            mine, got = links.begin_sum(part_own, part_send)
            normed = norm_rows(
                after(unit_one, mine), unit_other, norm_gain[layer, 0], norm_bias[layer, 0], shards
            )
            mine, normed = lax.optimization_barrier((mine, normed))
            if layer == 0:
                grad_own, grad_other = links.split_rows(after(cotangent[0], mine))
                grad_other, down_low, down_left = merge_rows(
                    grad_own, grad_other, jnp.zeros_like(grad_other), shards_late
                )
                mine, down_low = lax.optimization_barrier((mine, down_low))
            hidden = hidden + (mine + got) + output_bias[layer]
            unit_two, inverse_two = norm_parts(hidden)
            unit_other = links.other_rows(unit_two)
            activation, slope, *parts, normed_two = feed_forward(
                unit_two,
                unit_other,
                norm_gain,
                norm_bias,
                (layer, 1),
                up_weight,
                up_bias,
                down_weight,
                shards,
                layer < top,
            )
            if shard % 128:
                normed_two = take_columns(normed_two, shards, shard)
            if layer < top:
                mine, got = links.begin_sum(*parts)
            if layer < top:
                if layer == 0:
                    mine, embed_late, key_late = lax.optimization_barrier(
                        (mine, variable_embed, key_rows)
                    )
                    embed_left = embed_columns(patch_flat, embed_late, shards)
                    key_high, key_rest = two_part(key_late)
                    left_side = jnp.concatenate(
                        [
                            pool_value_weight,
                            pool_query_weight,
                            jnp.concatenate(
                                [key_high, key_high, key_rest, jnp.zeros_like(key_high)], axis=0
                            ).T,
                        ],
                        axis=1,
                    )
                    sides = left_side.reshape(dp, mp, shard // mp, left_side.shape[1])
                    mp_bits = range(bit_count(mp))
                    masks = [
                        sum((1 - ((i >> (len(mp_bits) - 1 - b)) & 1)) << b for b in mp_bits)
                        for i in range(mp)
                    ]
                    sides = jnp.stack(
                        [pick(sides, links.mp_index ^ mask, 1) for mask in masks]
                    ).reshape(2, model_width // 2, left_side.shape[1])
                    side_send, side_own = sides[0], sides[1]
                    mine, embed_left, side_own, side_send = lax.optimization_barrier(
                        (mine, embed_left, side_own, side_send)
                    )
                mine, normed_two = lax.optimization_barrier((mine, normed_two))
                hidden = hidden + (mine + got) + down_bias[layer]
            kept.append(
                (
                    unit_one,
                    inverse_one,
                    normed,
                    qkv,
                    totals,
                    mixed,
                    unit_two,
                    inverse_two,
                    normed_two,
                    slope,
                    activation,
                )
            )

        activation_top = activation
        row_sums = {}
        local_sums = {}
        merges = {}
        row_sums["down_bias", top] = jnp.sum(grad_own, axis=0)

        head_of = jnp.arange(local_width, dtype=jnp.int32) // HEAD_DIM
        head_pick = head_of[:, None] == jnp.arange(head_count, dtype=jnp.int32)[None, :]
        clock = Clock(scale_cell)

        def advance(spot):
            for name in PLAN.get(spot, ()):
                if name in merges and merges[name].open:
                    merges[name].advance(clock)

        def fill(spot):
            return (lambda: advance(spot)) if PLAN.get(spot) else None

        for layer in reversed(range(layer_count)):
            depth = top - layer
            (
                unit_one,
                inverse_one,
                normed,
                qkv,
                totals,
                mixed,
                unit_two,
                inverse_two,
                normed_two,
                slope,
                activation,
            ) = kept[layer]
            merges["down", depth] = Merge(
                links, [(down_left, activation)], bits if depth else bits_late
            )
            advance(("top", depth))
            pre_low, up_sums, part_own, part_send = feed_back(
                clock.one(down_low), slope, down_weight, up_weight, layer, layer == top
            )
            local_sums["up_bias", layer] = up_sums[0]
            pre_low, part_send = clock.both(pre_low, part_send)
            merges["up", depth] = Merge(links, [(normed_two, pre_low)], bits)
            advance(("pre", depth))
            mine, got = links.ordered_sum(clock, lambda: part_own, part_send, fill(("core_two", depth)))
            if not PLAN.get(("wait_two", depth)):
                clock.hold()
            advance(("wait_two", depth))
            if layer == top:
                half = row_count // 2
                activation_top = clock.one(activation_top)
                last_send = clock.one(matmul(activation_top[half:], down_weight[top]))
                last_other = exchange(last_send, "mp", mp, 0)
                last_own = matmul(activation_top[:half], down_weight[top])
                last_own = clock.one(last_own)
                clock.hold()
                last_mine = clock.one(last_own + clock.one(last_other))
            mine, got = clock.both(mine, got)
            if layer == top:
                for bit in range(1, bit_count(mp)):
                    last_mine = clock.one(last_mine)
                    last_other = exchange(last_mine, "mp", mp, bit)
                    if bit + 1 < bit_count(mp):
                        last_mine = last_mine + last_other
            change, grad_own, sums = norm_back(
                mine, got, unit_two, inverse_two, norm_gain, (layer, 1), grad_own
            )
            change, sums = clock.both(change, sums)
            row_sums["gain", layer, 1] = sums[0]
            row_sums["bias", layer, 1] = sums[1]
            row_sums["out_bias", layer] = sums[2]
            other_change = links.other_rows(change)
            clock.hold()
            grad_other, out_low, out_left = merge_rows(
                grad_own, grad_other, clock.one(other_change), shards
            )
            out_low = clock.one(out_low)
            advance(("mid", depth))
            grads, qv_sums, part_own, part_send = attend_back(
                clock.one(out_low), qkv, totals, attention_weight[layer], output_weight[layer]
            )
            local_sums["qv", layer] = qv_sums
            merges["att", depth] = Merge(links, [(out_left, mixed), (normed, grads)], bits)
            mine, got = links.ordered_sum(clock, lambda: part_own, part_send, fill(("core_one", depth)))
            if not PLAN.get(("wait_one", depth)):
                clock.hold()
            advance(("wait_one", depth))
            if layer == top:
                hidden = clock.one(hidden + (last_mine + clock.one(last_other)) + down_bias[top])
                hidden_other = links.other_rows(hidden)
                clock.hold()
                layer_out = clock.one(links.global_rows(hidden, clock.one(hidden_other)))
            mine, got = clock.both(mine, got)
            change, grad_own, sums = norm_back(
                mine, got, unit_one, inverse_one, norm_gain, (layer, 0), grad_own
            )
            change, sums = clock.both(change, sums)
            row_sums["gain", layer, 0] = sums[0]
            row_sums["bias", layer, 0] = sums[1]
            if layer:
                row_sums["down_bias", layer - 1] = sums[2]
            other_change = links.other_rows(change)
            clock.hold()
            grad_other, down_low, down_left = merge_rows(
                grad_own, grad_other, clock.one(other_change), shards
            )
            down_low = clock.one(down_low)
            advance(("end", depth))
            down_low = clock.one(down_low)

        row_sums["column"] = sums[2]
        row_sums["lead"] = lead_scale * sums[2]
        clock.hold()
        value_grad, key_grad, key_grad_var, pixel_own, pixel_send = pool_back(
            clock.one(down_low), pool_output_weight, value_flat, value_var, pix_low, pool_probs, score_rows
        )
        flat_all = flat_count + var_count
        item_scale = clock.cell[0, 0]
        sub = shard // mp
        embed_send, embed_own, summed_key, query_grad, pool_bias = embed_terms(
            side_send,
            side_own,
            clock.one(value_grad),
            key_grad,
            key_grad_var,
            clock.cell,
            patch_flat,
            variable_embed,
            pool_key_weight,
        )
        value_low = value_grad.astype(BF)
        query_late = clock.one(pool_query)
        merges["tail"] = Merge(
            links,
            [
                (down_left, pooled),
                (embed_left, jnp.concatenate([value_low, value_low[flat_count:]], axis=0)),
            ],
            bits,
        )
        query_grad = query_grad[0]
        embed_send = clock.one(embed_send)
        embed_got = exchange(embed_send, "mp", mp, 0)
        clock.hold()
        embed_got = clock.one(embed_got)
        for bit in range(1, bit_count(mp)):
            embed_send, embed_own = add_split(embed_own, embed_got)
            embed_send = clock.one(embed_send)
            embed_got = exchange(embed_send, "mp", mp, bit)
        names = []
        for layer in range(layer_count):
            names += [("gain", layer, 0), ("gain", layer, 1), ("bias", layer, 0), ("bias", layer, 1)]
        for layer in range(layer_count):
            names += [("out_bias", layer), ("down_bias", layer)]
        names += ["column", "lead"]
        own_sums = clock.one(jnp.stack([row_sums[name] for name in names]) * item_scale)
        other_sums = exchange(own_sums, "mp", mp, 0)
        advance("back")
        lanes = embed_own.shape[1]

        full_sums = own_sums + clock.one(other_sums)
        local = jnp.stack([local_sums["up_bias", layer] for layer in range(layer_count)]) * item_scale
        thin = [local_sums["qv", layer] for layer in range(layer_count)]
        thin = jnp.concatenate([jnp.concatenate(thin, axis=0) * item_scale, pool_bias], axis=0)
        packed = jnp.concatenate(
            [
                full_sums.reshape(len(names), dp, shard).transpose(1, 0, 2).reshape(dp, -1),
                summed_key.reshape(head_count, dp, shard).transpose(1, 0, 2).reshape(dp, -1),
                local.reshape(layer_count, dp, -1).transpose(1, 0, 2).reshape(dp, -1),
                thin.reshape(2 * layer_count + 1, dp, -1).transpose(1, 0, 2).reshape(dp, -1),
                jnp.broadcast_to(query_grad[None, :], (dp, local_width)),
            ],
            axis=1,
        )
        packed_size = packed.shape[1]
        packed_rows = -(-packed_size // 1024) * 8
        packed = jnp.pad(packed, ((0, 0), (0, packed_rows * 128 - packed_size)))
        packed = packed.reshape(dp, packed_rows, 128)
        position = (grad_own * item_scale).reshape(row_count // 2, dp, shard).transpose(1, 0, 2)
        position, packed = clock.both(position, packed)
        advance("vectors")
        embed_grad = (embed_own + clock.one(embed_got)).reshape(dp, sub, lanes)
        lane_blocks = lanes // 128
        if shard == 128:
            tall = jnp.concatenate(
                [embed_grad[:, :, i * 128 : (i + 1) * 128] for i in range(lane_blocks)]
                + [packed, position],
                axis=1,
            )
            merges["small"] = ShardMerge(links, tall)
        else:
            merges["small"] = ShardMerge(
                links,
                jnp.concatenate(
                    [part.reshape(dp, 1, -1) for part in (embed_grad, packed, position)], axis=2
                ),
            )
        advance("small")

        pixel_mine, pixel_got = links.ordered_sum(clock, lambda: pixel_own, pixel_send)
        clock.hold()
        advance("values")
        pixel_mine, pixel_got = clock.both(pixel_mine, pixel_got)
        pixel_mine = clock.one(pixel_mine + pixel_got)
        pixel_other = links.other_rows(pixel_mine)
        clock.hold()
        advance("pixels")
        pixel_grad = links.global_rows(pixel_mine, clock.one(pixel_other))
        pixel_grad = clock.one(pixel_grad.T.reshape(1, var_count, pix_count, row_count))
        advance("rows")
        for name in DRAIN:
            if merges[name].open:
                merges[name].advance(clock)
        for merge in merges.values():
            while merge.open:
                merge.advance(clock)
        finished = {}
        for kind in ("down", "up", "att"):
            parts = [merges[kind, top - layer].total for layer in range(layer_count)]
            finished[kind] = finish_layers(
                kind, parts, clock.cell if kind == "att" else scale_cell, layer_count, shard, local_width
            )
        tail_total = merges["tail"].total
        small = merges["small"].total[0]
        if shard == 128:
            embed_rows = sub * lane_blocks
            embed_grad = jnp.concatenate(
                [small[i * sub : (i + 1) * sub] for i in range(lane_blocks)], axis=1
            )
            packed = small[embed_rows : embed_rows + packed_rows].reshape(-1)
            position = small[embed_rows + packed_rows :]
        else:
            size = sub * lane_blocks * 128
            embed_grad = small[0, :size].reshape(sub, lane_blocks * 128)
            packed = small[0, size : size + packed_rows * 128]
            position = small[0, size + packed_rows * 128 :].reshape(row_count // 2, shard)
        position = links.global_rows(position, links.other_rows(position))
        offset = 0

        def take(*shape):
            nonlocal offset
            size = math.prod(shape)
            piece = packed[offset : offset + size].reshape(shape)
            offset += size
            return piece

        gains = take(layer_count, 2, shard)
        biases = []
        gain_list = []
        offset = 0
        norm_all = take(layer_count, 2, 2, shard)
        gain_list = norm_all[:, 0]
        biases = norm_all[:, 1]
        dense_bias = take(layer_count, 2, shard)
        column_total = take(shard)
        lead_total = take(shard)
        key_shard = take(head_count, shard)
        up_bias_total = take(layer_count, local.shape[1] // dp)
        thin_total = take(2 * layer_count + 1, local_width // dp)
        query_total = take(local_width)

        query_low = query_late.astype(BF)
        query_rows = lax.dynamic_slice_in_dim(query_low, links.dp_index * shard, shard, 0)
        query_weight_grad = query_rows.astype(F32)[:, None] * query_total[None, :]
        key_weight_grad = (
            jnp.repeat(key_shard.T, HEAD_DIM, axis=1) * query_row / ROOT_DIM
        )
        embed_turned = embed_grad.T
        return (
            layer_out[None],
            pixel_grad,
            embed_turned[:flat_count].reshape(var_count, pix_count, sub),
            embed_turned[flat_count:flat_all],
            position,
            embed_turned[flat_all],
            query_weight_grad,
            key_weight_grad,
            tail_total[:, local_width:],
            thin_total[-1],
            tail_total[:, :local_width].T,
            column_total,
            lead_total,
            column_total,
            gain_list,
            biases,
            finished["att"][1],
            thin_total[:-1].reshape(layer_count, 2, local_width // dp),
            finished["att"][0],
            dense_bias[:, 0],
            finished["up"][0],
            up_bias_total,
            finished["down"][0],
            dense_bias[:, 1],
        )

    return per_device


def solution(mesh):
    return jax.shard_map(
        make_per_device(mesh.shape["dp"], mesh.shape["mp"]),
        mesh=mesh,
        in_specs=(
            P("dp", None, None, None),
            P("dp"),
            P(),
            P("dp"),
            P("dp"),
            P(),
            P(),
            P(),
            P(),
            P(),
            P(None, "mp"),
            P(None, "mp"),
            P(None, "mp"),
            P("mp"),
            P("mp", None),
            P(),
            P(),
            P(),
            P(),
            P(),
            P(None, None, None, "mp"),
            P(None, None, "mp"),
            P(None, "mp", None),
            P(),
            P(None, None, "mp"),
            P(None, "mp"),
            P(None, "mp", None),
            P(),
            P("dp", None, None),
        ),
        out_specs=(
            P("dp", None, None),
            P("dp", None, None, None),
            P(None, None, ("dp", "mp")),
            P(None, ("dp", "mp")),
            P(None, "dp"),
            P(("dp", "mp")),
            P("dp", "mp"),
            P("dp", "mp"),
            P("dp", "mp"),
            P(("mp", "dp")),
            P("mp", "dp"),
            P("dp"),
            P("dp"),
            P("dp"),
            P(None, None, "dp"),
            P(None, None, "dp"),
            P(None, None, "dp", "mp"),
            P(None, None, ("mp", "dp")),
            P(None, "mp", "dp"),
            P(None, "dp"),
            P(None, "dp", "mp"),
            P(None, ("mp", "dp")),
            P(None, "mp", "dp"),
            P(None, "dp"),
        ),
        check_vma=False,
    )
```
